32 devices in a mesh: dp: 8 (over z, y), mp: 4 (over x, core).
Axes of the slice: x: 2, y: 2, z: 4, core: 2. Of those that a mesh axis runs over, the one named last changes fastest.
Arguments:
- tokens: bfloat16 [8, 3136, 384], P('dp', 'mp'), may hold values from -6 to 6
- cotangent: bfloat16 [8, 3136, 384], P('dp', 'mp'), may hold values from -6 to 6
- segment_ids: int32 [8, 16], P('dp'), may hold values from 0 to 3, never falling along the last dimension, each value on 1 to 9 neighbouring positions
- padding: int32 [8, 16], P('dp'), may hold values 0 or 1
- pattern: int32 [16, 16], replicated, may hold values from 0 to 1, as said below
- owner_slot: int32 [12], replicated, may hold values from 0 to 15, as said below
- weights: float32 [12, 1152, 128], P(None, 'mp')
- first_moments: float32 [16, 1152, 128], P('dp', 'mp'), may hold values from -0.33 to 0.33
- second_moments: float32 [16, 1152, 128], P('dp', 'mp'), may hold values from 0.0132 to 0.053
- norm_params: float32 [4, 384], replicated
- norm_first: float32 [4, 384], replicated, may hold values from -0.5 to 0.5
- norm_second: float32 [4, 384], replicated, may hold values from 0.026 to 0.1
Outputs:
- out: bfloat16 [8, 3136, 384], P('dp', 'mp')
- grad_in: bfloat16 [8, 3136, 384], P('dp', 'mp')
- grad_norm: float32 [], replicated
- new_weights: float32 [12, 1152, 128], P(None, 'mp')
- new_first: float32 [16, 1152, 128], P('dp', 'mp')
- new_second: float32 [16, 1152, 128], P('dp', 'mp')
- new_norm: float32 [4, 384], replicated
- new_norm_first: float32 [4, 384], replicated
- new_norm_second: float32 [4, 384], replicated
The draws below stay inside these ranges and needn't reach their ends.
Inputs may be any that keep to these rules, and one draw needn't show every extreme that they name: `pattern`: 1 on the diagonal, 0 above it. Distinct values; block b's optimizer state lies in slot owner_slot[b], slot s on index s // 2 of dp.
All inputs are finite; a program needn't handle non-finite values. No bound on the sum of `padding` on one device may be relied on, other than what follows from the above.
Results may differ from the reference program's by a relative error of at most 0.019.
Values may be sent and summed in bfloat16 or wider, within the bound.
A program may use at most 128 MiB of HBM per device.

```python
import math
import jax
import jax.numpy as jnp
import numpy as np
from jax import lax

D = 384
HEADS = 16
HEAD_DIM = 24
FF = 1536
FRAMES = 16
PATCHES = 196
QF = 4
STEP = 10
L = 3136
ROWS = 8
NBLK = 12
SLOTS = 2
BR = 288
NPARAM = 1771008
N_DP = 8
N_MP = 4


def draw_pattern(key, part):
    coin_flips = jax.random.randint(key, (FRAMES, FRAMES), 0, 4)
    lower_part = (coin_flips > 0).astype(jnp.int32)
    row_ids = jnp.arange(FRAMES)[:, None]
    col_ids = jnp.arange(FRAMES)[None, :]
    diagonal = jnp.where(col_ids == row_ids, 1, 0).astype(jnp.int32)
    return jnp.where(col_ids < row_ids, lower_part, diagonal).astype(jnp.int32)


def draw_owner_slot(key, part):
    slot_total = N_DP * SLOTS
    middle = jax.random.permutation(jax.random.fold_in(key, 1), slot_total - 2).astype(jnp.int32) + 1
    ends = jnp.array([0, slot_total - 1], jnp.int32)
    base = jnp.concatenate([ends, middle[:NBLK - 2]])
    order = jax.random.permutation(jax.random.fold_in(key, 2), NBLK)
    return base[order].astype(jnp.int32)


def draw_weights(key, part):
    up_pieces = FF // D
    block_kind = jnp.arange(NBLK)
    base = D ** (-0.5)
    scales = jnp.where(block_kind < 2, 1.4 * base, base)
    scales = jnp.where(block_kind == 3, min(4.0, (FRAMES * PATCHES / 64.0) ** 0.5) * base, scales)
    scales = jnp.where(block_kind >= 4 + up_pieces, FF ** (-0.5), scales)
    shape = (NBLK, N_MP * BR, 128)
    sample = jnp.clip(jax.random.normal(key, shape, jnp.float32), -5.0, 5.0)
    return (sample * scales[:, None, None]).astype(jnp.float32)


def draw_norm_params(key, part):
    gains = jax.random.uniform(jax.random.fold_in(key, 1), (4, D), jnp.float32, 0.7, 1.3)
    shifts = 0.3 * jnp.clip(jax.random.normal(jax.random.fold_in(key, 2), (4, D), jnp.float32), -4.0, 4.0)
    row_kind = jnp.arange(4)[:, None] % 2
    return jnp.where(row_kind == 0, gains, shifts).astype(jnp.float32)


def touch_ends(drawn, key, smallest, largest):
    longest = drawn.shape.index(max(drawn.shape))
    spots = []
    for shift in (0, 1):
        where = [jax.random.randint(jax.random.fold_in(key, axis), (), 0, length) for axis, length in enumerate(drawn.shape)]
        where[longest] = (where[longest] + shift) % drawn.shape[longest]
        spots.append(tuple(where))
    return drawn.at[spots[0]].set(smallest).at[spots[1]].set(largest)


def steps_of(rng, dims, split, low, largest):
    factor_of, own = 1.0, jax.random.fold_in(rng, 6)
    for position, parts in split:
        draws = jnp.exp(jax.random.uniform(jax.random.fold_in(own, position), (parts,), jnp.float32, low / len(split), largest / len(split)))
        factor_of = factor_of * jnp.repeat(draws, dims[position] // parts).reshape([-1 if axis == position else 1 for axis in range(len(dims))])
    return factor_of


def profile(count, total, most, slope):
    weights = [(1 << 20) // math.isqrt(rank ** slope) + 1 for rank in range(2, count + 1)]
    rest, given = total - most - (count - 1), [1] * (count - 1)
    while rest > 0:
        candidates = [i for i in range(count - 1) if given[i] < most]
        whole, left = sum([weights[i] for i in candidates]), rest
        for i in candidates:
            more = min(most - given[i], max(1, left * weights[i] // whole), rest)
            given[i] = given[i] + more
            rest = rest - more
    return np.array([most] + given)


def uneven(own_key, count, total, bound, skew):
    if count == 2:
        one = jax.random.randint(own_key, (), max(1, total - bound), min(bound, total - 1) + 1)
        return jnp.stack([one, total - one])
    tallies = jnp.asarray(profile(count, total, bound, skew), jnp.int32)
    twos = (count - 1) // 2
    source_of, sink = tallies[1:1 + 2 * twos:2], tallies[2:2 + 2 * twos:2]
    room = jnp.minimum(source_of - 1, bound - sink)
    passed = jax.random.randint(jax.random.fold_in(own_key, 1), (twos,), 0, 1 << 20) % (room + 1)
    tallies = tallies.at[1:1 + 2 * twos:2].set(source_of - passed).at[2:2 + 2 * twos:2].set(sink + passed)
    return tallies[jax.random.permutation(jax.random.fold_in(own_key, 2), count)]


def normal_values(stream_key, shape, deviation, most, split=(), held_as=jnp.bfloat16):
    values = jax.random.normal(stream_key, shape, jnp.float32) * deviation
    if len(split) > 0:
        values = steps_of(stream_key, shape, split, -0.22, 0.18) * values
    return jnp.clip(values, min=-most, max=most).astype(held_as)


def setup_inputs(seed: int = 0) -> dict:
    arg_keys = jax.random.split(jax.random.key(seed), 13)
    tokens = normal_values(arg_keys[0], (ROWS, L, D), 1.0, 6.0, ((0, 8), (1, 4)))
    cotangent = normal_values(arg_keys[1], (ROWS, L, D), 1.0, 6.0, ((0, 8), (1, 4)))
    segment_ids = jax.vmap(lambda own: jnp.searchsorted(jnp.cumsum(uneven(own, FRAMES // 4, FRAMES, FRAMES // 2 + 1, 0)), jnp.arange(FRAMES), side="right"))(jax.random.split(arg_keys[2], ROWS)).reshape((ROWS, FRAMES)).astype(jnp.int32)
    padding = touch_ends((jax.random.randint(arg_keys[3], (ROWS, FRAMES), 0, 8) < 1).astype(jnp.int32), jax.random.fold_in(arg_keys[3], 1), 0, 1)
    pattern = draw_pattern(jax.random.fold_in(arg_keys[12], 71), 0)
    owner_slot = draw_owner_slot(jax.random.fold_in(arg_keys[12], 71), 0)
    weights = draw_weights(jax.random.fold_in(arg_keys[12], 71), 0)
    first_moments = normal_values(arg_keys[7], (N_DP * SLOTS, N_MP * BR, 128), 0.055, 0.33, ((0, 8), (1, 4)), jnp.float32)
    second_moments = jnp.clip(jnp.exp(math.log(0.053) - 1.3900751 * jax.random.uniform(arg_keys[8], (N_DP * SLOTS, N_MP * BR, 128), jnp.float32) ** steps_of(arg_keys[8], (N_DP * SLOTS, N_MP * BR, 128), ((0, 8), (1, 4)), -0.2, 0.2)), 0.0132, 0.053)
    norm_params = draw_norm_params(jax.random.fold_in(arg_keys[12], 71), 0)
    norm_first = normal_values(arg_keys[10], (4, D), 0.08, 0.5, (), jnp.float32)
    norm_second = jnp.clip(jnp.exp(jax.random.uniform(arg_keys[11], (4, D), jnp.float32, math.log(0.026), math.log(0.1))), 0.026, 0.1)
    return {"tokens": tokens, "cotangent": cotangent, "segment_ids": segment_ids, "padding": padding, "pattern": pattern, "owner_slot": owner_slot, "weights": weights, "first_moments": first_moments, "second_moments": second_moments, "norm_params": norm_params, "norm_first": norm_first, "norm_second": norm_second}


@jax.custom_vjp
def low(v):
    return lax.optimization_barrier(v.astype(jnp.bfloat16)).astype(jnp.float32)

@jax.custom_vjp
def low_back(v):
    return v

def low_keep(v):
    return (low(v), None)

def low_pass(kept, grad):
    return (grad,)

def back_keep(v):
    return (v, None)

def back_low(kept, grad):
    return (low(grad),)
low.defvjp(low_keep, low_pass)
low_back.defvjp(back_keep, back_low)
NORM_EPS = 1e-05
BETA_ONE = 0.9
BETA_TWO = 0.95
ADAM_EPS = 1e-08
LEARN_RATE = 0.15
NORM_RATE = 0.6
WEIGHT_DECAY = 0.05
MASKED = -1e+30
HIGHEST = lax.Precision.HIGHEST

def layer_norm(values, gain_row, bias_row):
    average = lax.optimization_barrier(jnp.mean(values, axis=-1, keepdims=True))
    centred = values - average
    variance = lax.optimization_barrier(jnp.mean(centred * centred, axis=-1, keepdims=True))
    return centred * lax.rsqrt(variance + NORM_EPS) * gain_row + bias_row

def adam_update(current, gradient, first_moment, second_moment, decay_rate, step_rate):
    first_new = BETA_ONE * first_moment + (1.0 - BETA_ONE) * gradient
    second_new = BETA_TWO * second_moment + (1.0 - BETA_TWO) * gradient * gradient
    first_fix = 1.0 - BETA_ONE ** STEP
    second_fix = 1.0 - BETA_TWO ** STEP
    direction = first_new / first_fix / (jnp.sqrt(second_new / second_fix) + ADAM_EPS)
    return (current - step_rate * (direction + decay_rate * current), first_new, second_new)

def frame_allowed(segment_row, padding_row, pattern):
    frame_ids = jnp.arange(FRAMES)
    same = segment_row[:, None] == segment_row[None, :]
    diagonal = frame_ids[:, None] == frame_ids[None, :]
    live = (padding_row[None, :] == 0) | diagonal
    return (pattern == 1) & same & live

def unpack(weights):
    head_cols = D // N_MP
    hidden_cols = FF // N_MP
    up_pieces = FF // D
    flat_blocks = weights.reshape(NBLK, N_MP, D * head_cols)

    def columns(block_row):
        return block_row.reshape(N_MP, D, head_cols).transpose(1, 0, 2).reshape(D, D)
    w_query = columns(flat_blocks[0])
    w_key = columns(flat_blocks[1])
    w_value = columns(flat_blocks[2])
    output_weight = flat_blocks[3].reshape(D, D)
    up_weight = flat_blocks[4:4 + up_pieces].transpose(1, 0, 2).reshape(N_MP, D, hidden_cols)
    up_weight = up_weight.transpose(1, 0, 2).reshape(D, FF)
    down_weight = flat_blocks[4 + up_pieces:].transpose(1, 0, 2).reshape(FF, D)
    return (w_query, w_key, w_value, output_weight, up_weight, down_weight)

def attend(queries, key_rows, value_rows, allowed):
    score_scale = HEAD_DIM ** (-0.5)
    block_count = FRAMES // QF
    query_heads = queries.reshape(L, HEADS, HEAD_DIM).transpose(1, 0, 2)
    key_heads = key_rows.reshape(L, HEADS, HEAD_DIM).transpose(1, 0, 2)
    value_heads = value_rows.reshape(L, HEADS, HEAD_DIM).transpose(1, 0, 2)
    query_blocks = query_heads.reshape(HEADS, block_count, QF * PATCHES, HEAD_DIM).transpose(1, 0, 2, 3)
    frame_masks = allowed.reshape(block_count, QF, FRAMES)

    def one_block(block_parts):
        query_block, frame_rows = block_parts
        token_mask = jnp.broadcast_to(frame_rows[:, None, :, None], (QF, PATCHES, FRAMES, PATCHES)).reshape(QF * PATCHES, L)
        scores = low_back(jnp.einsum('hqd,hkd->hqk', query_block, key_heads, precision=HIGHEST) * score_scale)
        scores = jnp.where(token_mask[None, :, :], scores, MASKED)
        attn_probs = low(jax.nn.softmax(scores, axis=-1))
        return jnp.einsum('hqk,hkd->hqd', attn_probs, value_heads, precision=HIGHEST)
    outputs = lax.map(jax.checkpoint(one_block), (query_blocks, frame_masks))
    outputs = outputs.transpose(1, 0, 2, 3).reshape(HEADS, L, HEAD_DIM)
    return outputs.transpose(1, 0, 2).reshape(L, D)

def forward(inputs, weights, norm_params, allowed_all):
    w_query, w_key, w_value, output_weight, up_weight, down_weight = [low(matrix) for matrix in unpack(weights)]

    def one_row(running, row_parts):
        row_input, allowed = row_parts
        normed = low(layer_norm(row_input, norm_params[0], norm_params[1]))
        queries = low(low_back(jnp.dot(normed, w_query, precision=HIGHEST)))
        key_rows = low(low_back(jnp.dot(normed, w_key, precision=HIGHEST)))
        value_rows = low(low_back(jnp.dot(normed, w_value, precision=HIGHEST)))
        attended_output = low(low_back(attend(queries, key_rows, value_rows, allowed)))
        middle = row_input + low_back(jnp.dot(attended_output, output_weight, precision=HIGHEST))
        normed_two = low(layer_norm(middle, norm_params[2], norm_params[3]))
        hidden_rows = low_back(jnp.dot(normed_two, up_weight, precision=HIGHEST))
        activated_rows = low(jax.nn.gelu(hidden_rows, approximate=True))
        result = middle + low_back(jnp.dot(activated_rows, down_weight, precision=HIGHEST))
        return (running, result)
    _, outputs = lax.scan(one_row, jnp.zeros((), jnp.float32), (inputs, allowed_all))
    return outputs

def reference(tokens, cotangent, segment_ids, padding, pattern, owner_slot, weights, first_moments, second_moments, norm_params, norm_first, norm_second):
    allowed_all = jax.vmap(frame_allowed, in_axes=(0, 0, None))(segment_ids, padding, pattern)
    keep_frames = (1 - padding).astype(jnp.float32)
    keep_tokens = jnp.repeat(keep_frames, PATCHES, axis=1)
    grad_out = cotangent.astype(jnp.float32) * keep_tokens[:, :, None]
    inputs = tokens.astype(jnp.float32)

    def wrapped(inputs_in, weights_in, norm_in):
        return forward(inputs_in, weights_in, norm_in, allowed_all)
    outputs, pull = jax.vjp(wrapped, inputs, weights, norm_params)
    grad_x, grad_w, grad_n = pull(grad_out)
    total = jnp.sum(grad_w * grad_w) + jnp.sum(grad_n * grad_n)
    grad_norm = jnp.sqrt(total)
    clip_level = 0.5 * NPARAM ** 0.5
    factor = jnp.minimum(1.0, clip_level / grad_norm)
    old_first = first_moments[owner_slot]
    old_second = second_moments[owner_slot]
    new_weights, first_blocks, second_blocks = adam_update(weights, grad_w * factor, old_first, old_second, WEIGHT_DECAY, LEARN_RATE)
    new_first = first_moments.at[owner_slot].set(first_blocks)
    new_second = second_moments.at[owner_slot].set(second_blocks)
    new_norm, new_norm_first, new_norm_second = adam_update(norm_params, grad_n * factor, norm_first, norm_second, 0.0, NORM_RATE)
    return (outputs.astype(jnp.bfloat16), grad_x.astype(jnp.bfloat16), grad_norm, new_weights, new_first, new_second, new_norm, new_norm_first, new_norm_second)
```

```python
import functools
import math

import jax
import jax.numpy as jnp
from jax import lax
from jax.experimental import pallas as pl
from jax.experimental.pallas import tpu as pltpu
from jax.sharding import PartitionSpec as P

D = 384
FF = 1536
STEP = 10
NORM_EPS = 1e-05
BETA_ONE = 0.9
BETA_TWO = 0.95
ADAM_EPS = 1e-08
LEARN_RATE = 0.15
NORM_RATE = 0.6
WEIGHT_DECAY = 0.05

HEAD_DIM = 24
FRAMES = 16
PATCHES = 196
FROWS = 208
FLANES = 256
HW = 32
HEADS_LOCAL = 4
MASKED = -1e30
QSCALE = math.log2(math.e) / math.sqrt(HEAD_DIM)
F32 = jnp.float32
BF16 = jnp.bfloat16
NT = (((1,), (1,)), ((), ()))
TN = (((0,), (0,)), ((), ()))

def dot(a, b):
    return jnp.dot(a, b, preferred_element_type=F32)

def frame_pair(seg_ref, pad_ref, pat_ref, i, j):
    return (pat_ref[i, j] == 1) & (seg_ref[0, i] == seg_ref[0, j]) & ((pad_ref[0, j] == 0) | (i == j))

def fwd_kernel(seg_ref, pad_ref, pat_ref, h_ref, wq_ref, wk_ref, wv_ref,
               o_ref, ot_ref, qa_ref, ka_ref, va_ref, vt_s, qe_s, m_s, acc_s):
    heads = HEADS_LOCAL
    wide = heads * HW
    col = lax.broadcasted_iota(jnp.int32, (FROWS, wide), 1) % HW
    row = lax.broadcasted_iota(jnp.int32, (FROWS, wide), 0)
    kadd = jnp.where((col == 24) | (col == 25), 1.0, 0.0) + jnp.where((col == 26) & (row >= PATCHES), MASKED, 0.0)
    vadd = jnp.where((col == 24) | (col == 25), 1.0, 0.0)
    vrow = lax.broadcasted_iota(jnp.int32, (wide, FROWS), 0) % HW
    vtadd = jnp.where(vrow == 24, 1.0, 0.0)
    zpad = jnp.zeros((wide, FLANES - FROWS), BF16)

    def project(f, _):
        rows = pl.ds(pl.multiple_of(f * FROWS, 16), FROWS)
        hf = h_ref[rows, :]
        qt = (lax.dot_general(wq_ref[...], hf, NT, preferred_element_type=F32) * QSCALE).astype(BF16)
        qa_ref[:, pl.ds(pl.multiple_of(f * FLANES, 128), FLANES)] = jnp.concatenate([qt, zpad], axis=1)
        ka_ref[rows, :] = (lax.dot_general(hf, wk_ref[...], NT, preferred_element_type=F32) + kadd).astype(BF16)
        va_ref[rows, :] = (lax.dot_general(hf, wv_ref[...], NT, preferred_element_type=F32) + vadd).astype(BF16)
        vt = lax.dot_general(wv_ref[...], hf, NT, preferred_element_type=F32) + vtadd
        vt_s[:, pl.ds(pl.multiple_of(f * FLANES, 128), FROWS)] = vt.astype(BF16)
        return 0
    lax.fori_loop(0, FRAMES, project, 0)

    qrow = lax.broadcasted_iota(jnp.int32, (wide, FLANES), 0)
    hrow = qrow % HW

    def queries(i, _):
        lanes = pl.ds(pl.multiple_of(i * FLANES, 128), FLANES)
        qt = qa_ref[:, lanes].astype(F32)
        for h in range(heads):
            mine = (qrow // HW) == h
            qe_s[h] = (jnp.where(mine, qt, 0.0) + jnp.where(mine & (hrow == 26), 1.0, 0.0)).astype(BF16)
        m_s[...] = jnp.full(m_s.shape, MASKED, F32)
        acc_s[...] = jnp.zeros(acc_s.shape, F32)

        def keys(j, _):
            @pl.when(frame_pair(seg_ref, pad_ref, pat_ref, i, j))
            def _():
                kj = ka_ref[pl.ds(pl.multiple_of(j * FROWS, 16), FROWS), :]
                kl = pl.ds(pl.multiple_of(j * FLANES, 128), FROWS)
                for h in range(heads):
                    s = dot(kj, qe_s[h])
                    mo = m_s[h]
                    mn = jnp.maximum(mo, jnp.max(s, axis=0, keepdims=True))
                    p = jnp.exp2(s - mn).astype(BF16)
                    alpha = jnp.exp2(mo - mn)
                    pv = dot(vt_s[HW * h:HW * (h + 1), kl], p)
                    acc_s[h] = acc_s[h] * alpha + pv
                    m_s[h] = mn
            return 0
        lax.fori_loop(0, i + 1, keys, 0)
        outs, augs = [], []
        r32 = lax.broadcasted_iota(jnp.int32, (HW, FLANES), 0)
        for h in range(heads):
            a = acc_s[h]
            l = a[24:25, :]
            o = jnp.where(r32 < HEAD_DIM, a / l, 0.0)
            outs.append(o)
            lse = -(m_s[h] + jnp.log2(l))
            hi = lse.astype(BF16).astype(F32)
            lo = lse - hi
            augs.append(jnp.where(r32 == 24, hi, 0.0) + jnp.where(r32 == 25, lo, 0.0) + jnp.where(r32 == 26, 1.0, 0.0))
        ot = jnp.concatenate(outs, axis=0)
        ot_ref[:, lanes] = ot.astype(BF16)
        qa_ref[:, lanes] = (qt + jnp.concatenate(augs, axis=0)).astype(BF16)
        o_ref[pl.ds(pl.multiple_of(i * FROWS, 16), FROWS), :] = ot.T[:FROWS, :].astype(BF16)
        return 0
    lax.fori_loop(0, FRAMES, queries, 0)

SMEM = pl.BlockSpec(memory_space=pltpu.SMEM)
VM = pl.BlockSpec(memory_space=pltpu.VMEM)

def attn_fwd(seg, pad, pat, h, wqt, wkt, wvt):
    wide = HEADS_LOCAL * HW
    sd = jax.ShapeDtypeStruct
    return pl.pallas_call(
        fwd_kernel,
        out_shape=(sd((FRAMES * FROWS, wide), BF16), sd((wide, FRAMES * FLANES), BF16), sd((wide, FRAMES * FLANES), BF16),
                   sd((FRAMES * FROWS, wide), BF16), sd((FRAMES * FROWS, wide), BF16)),
        in_specs=[SMEM] * 3 + [VM] * 4,
        out_specs=(VM,) * 5,
        scratch_shapes=[pltpu.VMEM((wide, FRAMES * FLANES), BF16), pltpu.VMEM((HEADS_LOCAL, wide, FLANES), BF16),
                        pltpu.VMEM((HEADS_LOCAL, 1, FLANES), F32), pltpu.VMEM((HEADS_LOCAL, HW, FLANES), F32)],
        compiler_params=pltpu.CompilerParams(vmem_limit_bytes=48 << 20),
        cost_estimate=pl.CostEstimate(flops=int(4e9), bytes_accessed=8 << 20, transcendentals=0),
        name="attend_forward",
    )(seg, pad, pat, h, wqt, wkt, wvt)

def bwd_kernel(seg_ref, pad_ref, pat_ref, qa_ref, ka_ref, va_ref, ot_ref, do_ref, h_ref, wq_ref, wk_ref, wv_ref,
               dh_ref, dw_ref, kt_s, qe_s, oe_s, qr_s, or_s, dq_s, p_s, ds_s, dk_s, dv_s, dqr_s):
    heads = HEADS_LOCAL
    wide = heads * HW
    scale = HEAD_DIM ** -0.5
    dk_s[...] = jnp.zeros(dk_s.shape, F32)
    dv_s[...] = jnp.zeros(dv_s.shape, F32)
    qr_s[...] = jnp.zeros(qr_s.shape, BF16)
    or_s[...] = jnp.zeros(or_s.shape, BF16)

    def transposed(f, _):
        kf = ka_ref[pl.ds(pl.multiple_of(f * FROWS, 16), FROWS), :].astype(F32)
        kt_s[:, pl.ds(pl.multiple_of(f * FLANES, 128), FROWS)] = kf.T.astype(BF16)
        return 0
    lax.fori_loop(0, FRAMES, transposed, 0)

    qrow = lax.broadcasted_iota(jnp.int32, (wide, FLANES), 0)
    qcol = lax.broadcasted_iota(jnp.int32, (FROWS, wide), 1)
    r32 = lax.broadcasted_iota(jnp.int32, (HW, FLANES), 0)

    def queries(i, _):
        lanes = pl.ds(pl.multiple_of(i * FLANES, 128), FLANES)
        rows = pl.ds(pl.multiple_of(i * FROWS, 16), FROWS)
        qt = qa_ref[:, lanes].astype(F32)
        dor = do_ref[rows, :].astype(F32)
        dot_ = jnp.concatenate([dor.T, jnp.zeros((wide, FLANES - FROWS), F32)], axis=1)
        prod = dot_ * ot_ref[:, lanes].astype(F32)
        augs = []
        for h in range(heads):
            d = -jnp.sum(prod[HW * h:HW * (h + 1)], axis=0, keepdims=True)
            hi = d.astype(BF16).astype(F32)
            augs.append(jnp.where(r32 == 24, hi, 0.0) + jnp.where(r32 == 25, d - hi, 0.0))
        doa = dot_ + jnp.concatenate(augs, axis=0)
        qrows = qt.T[:FROWS, :]
        for h in range(heads):
            mine = (qrow // HW) == h
            qe_s[h] = jnp.where(mine, qt, 0.0).astype(BF16)
            oe_s[h] = jnp.where(mine, doa, 0.0).astype(BF16)
            cmine = ((qcol // HW) == h) & (qcol % HW < HEAD_DIM)
            qr_s[h * FLANES:h * FLANES + FROWS, :] = jnp.where(cmine, qrows, 0.0).astype(BF16)
            or_s[h * FLANES:h * FLANES + FROWS, :] = jnp.where(cmine, dor, 0.0).astype(BF16)
        dq_s[...] = jnp.zeros(dq_s.shape, F32)

        def keys(j, _):
            @pl.when(frame_pair(seg_ref, pad_ref, pat_ref, i, j))
            def _():
                krows = pl.ds(pl.multiple_of(j * FROWS, 16), FROWS)
                kl = pl.ds(pl.multiple_of(j * FLANES, 128), FROWS)
                kj = ka_ref[krows, :]
                vj = va_ref[krows, :]
                for h in range(heads):
                    p = jnp.exp2(dot(kj, qe_s[h]))
                    ds = (p * dot(vj, oe_s[h])).astype(BF16)
                    p_s[:, h * FLANES:(h + 1) * FLANES] = p.astype(BF16)
                    ds_s[:, h * FLANES:(h + 1) * FLANES] = ds
                    dq_s[HW * h:HW * (h + 1), :] += dot(kt_s[HW * h:HW * (h + 1), kl], ds)
                dv_s[krows, :] += dot(p_s[...], or_s[...])
                dk_s[krows, :] += dot(ds_s[...], qr_s[...])
            return 0
        lax.fori_loop(0, i + 1, keys, 0)
        dq = jnp.where(qrow % HW < HEAD_DIM, dq_s[...] * scale, 0.0)
        dqr_s[rows, :] = dq.T[:FROWS, :].astype(BF16)
        return 0
    lax.fori_loop(0, FRAMES, queries, 0)

    dw_ref[...] = jnp.zeros(dw_ref.shape, F32)
    def finish(f, _):
        rows = pl.ds(pl.multiple_of(f * FROWS, 16), FROWS)
        dq = dqr_s[rows, :]
        dk = (dk_s[rows, :] * math.log(2.0)).astype(BF16)
        dv = dv_s[rows, :].astype(BF16)
        hf = h_ref[rows, :]
        dh = dot(dq, wq_ref[...]) + dot(dk, wk_ref[...]) + dot(dv, wv_ref[...])
        dh_ref[rows, :] = dh.astype(BF16)
        dw_ref[0] += lax.dot_general(dq, hf, TN, preferred_element_type=F32)
        dw_ref[1] += lax.dot_general(dk, hf, TN, preferred_element_type=F32)
        dw_ref[2] += lax.dot_general(dv, hf, TN, preferred_element_type=F32)
        return 0
    lax.fori_loop(0, FRAMES, finish, 0)

def attn_bwd(seg, pad, pat, qa, ka, va, ot, do, h, wqt, wkt, wvt):
    wide = HEADS_LOCAL * HW
    sd = jax.ShapeDtypeStruct
    V = pltpu.VMEM
    return pl.pallas_call(
        bwd_kernel,
        out_shape=(sd((FRAMES * FROWS, D), BF16), sd((3, wide, D), F32)),
        in_specs=[SMEM] * 3 + [VM] * 9,
        out_specs=(VM,) * 2,
        scratch_shapes=[V((wide, FRAMES * FLANES), BF16), V((HEADS_LOCAL, wide, FLANES), BF16), V((HEADS_LOCAL, wide, FLANES), BF16),
                        V((HEADS_LOCAL * FLANES, wide), BF16), V((HEADS_LOCAL * FLANES, wide), BF16), V((wide, FLANES), F32),
                        V((FROWS, HEADS_LOCAL * FLANES), BF16), V((FROWS, HEADS_LOCAL * FLANES), BF16),
                        V((FRAMES * FROWS, wide), F32), V((FRAMES * FROWS, wide), F32), V((FRAMES * FROWS, wide), BF16)],
        compiler_params=pltpu.CompilerParams(vmem_limit_bytes=56 << 20),
        cost_estimate=pl.CostEstimate(flops=int(12e9), bytes_accessed=12 << 20, transcendentals=0),
        name="attend_backward",
    )(seg, pad, pat, qa, ka, va, ot, do, h, wqt, wkt, wvt)


def layer_norm(values, gain_row, bias_row):
    average = jnp.mean(values, axis=-1, keepdims=True)
    centred = values - average
    variance = jnp.mean(centred * centred, axis=-1, keepdims=True)
    return centred * lax.rsqrt(variance + NORM_EPS) * gain_row + bias_row


def adam_update(current, gradient, first_moment, second_moment, decay_rate, step_rate):
    first_new = BETA_ONE * first_moment + (1.0 - BETA_ONE) * gradient
    second_new = BETA_TWO * second_moment + (1.0 - BETA_TWO) * gradient * gradient
    first_fix = 1.0 - BETA_ONE**STEP
    second_fix = 1.0 - BETA_TWO**STEP
    direction = first_new / first_fix / (jnp.sqrt(second_new / second_fix) + ADAM_EPS)
    return (current - step_rate * (direction + decay_rate * current), first_new, second_new)


def pad_frames(rows):
    split = rows.reshape(-1, PATCHES, rows.shape[-1])
    return jnp.pad(split, ((0, 0), (0, FROWS - PATCHES), (0, 0))).reshape(-1, rows.shape[-1])


def drop_pads(rows):
    return rows.reshape(-1, FROWS, rows.shape[-1])[:, :PATCHES].reshape(-1, rows.shape[-1])


def pad_heads(rows):
    split = rows.reshape(-1, HEAD_DIM, rows.shape[-1])
    return jnp.pad(split, ((0, 0), (0, HW - HEAD_DIM), (0, 0))).reshape(-1, rows.shape[-1])


def drop_head_pads(rows):
    return rows.reshape(-1, HW, rows.shape[-1])[:, :HEAD_DIM].reshape(-1, rows.shape[-1])


def pick(stacked, places):
    return jnp.stack([lax.dynamic_index_in_dim(stacked, places[b], 0, keepdims=False) for b in range(places.shape[0])])


def shards(tokens, cotangent, segment_ids, padding, pattern, owner_slot, weights, first_moments, second_moments,
           norm_params, norm_first, norm_second):
    groups = lax.axis_size("mp")
    me = lax.axis_index("mp")
    block_total, block_rows, lanes = weights.shape
    pieces = (block_total - 4) // 2
    head_cols = block_rows * lanes // D
    frames_own = FRAMES // groups
    wide = HEADS_LOCAL * HW

    wb = weights.astype(BF16)
    wqt, wkt, wvt = (pad_heads(wb[b].reshape(D, head_cols).T) for b in range(3))
    shared = lax.all_gather(wb[3:], "mp", axis=0)
    wo = pad_heads(shared[:, 0].reshape(groups * head_cols, D))
    w1 = shared[:, 1:1 + pieces].reshape(groups, D, pieces * head_cols).transpose(1, 0, 2).reshape(D, FF)
    w2 = shared[:, 1 + pieces:].reshape(FF, D)
    moments = lax.all_gather(jnp.stack([first_moments, second_moments]).astype(BF16), "dp", axis=1, tiled=True)

    x = pad_frames(tokens[0]).astype(F32)
    live = jnp.tile(jnp.arange(FROWS) < PATCHES, frames_own)[:, None]
    keep = jnp.repeat(1.0 - lax.dynamic_slice_in_dim(padding[0], me * frames_own, frames_own).astype(F32), FROWS)[:, None]
    grad_out = pad_frames(cotangent[0]).astype(F32) * keep
    h1 = jnp.where(live, layer_norm(x, norm_params[0], norm_params[1]), 0.0).astype(BF16)
    h1_all = lax.all_gather(h1, "mp", axis=0, tiled=True)
    o_heads, ot, qa, ka, va = attn_fwd(segment_ids, padding, pattern, h1_all, wqt, wkt, wvt)
    o_own = lax.all_to_all(o_heads.reshape(groups, frames_own * FROWS, wide), "mp", 0, 0)
    o_own = o_own.transpose(1, 0, 2).reshape(frames_own * FROWS, groups * wide)
    x2 = x + dot(o_own, wo)
    x2 = jnp.where(live, x2, 0.0)
    ln2 = lambda v, g, b: layer_norm(v, g, b)
    h2, pull2 = jax.vjp(ln2, x2, norm_params[2], norm_params[3])
    h2 = h2.astype(BF16)
    u = dot(h2, w1)
    act, gelu_pull = jax.vjp(functools.partial(jax.nn.gelu, approximate=True), u)
    act = act.astype(BF16)
    result = (x2 + dot(act, w2)).astype(BF16)
    g = grad_out.astype(BF16)
    da = lax.dot_general(g, w2, NT, preferred_element_type=F32)
    dw2 = lax.dot_general(act, g, TN, preferred_element_type=F32)
    du = gelu_pull(da)[0].astype(BF16)
    dw1 = lax.dot_general(h2, du, TN, preferred_element_type=F32)
    dh2 = lax.dot_general(du, w1, NT, preferred_element_type=F32)
    dln2, dg2, db2 = pull2(dh2)
    dx2 = grad_out + dln2
    dxa = dx2.astype(BF16)
    do_own = lax.dot_general(dxa, wo, NT, preferred_element_type=F32).astype(BF16)
    dwo = lax.dot_general(o_own, dxa, TN, preferred_element_type=F32)
    do_heads = lax.all_to_all(do_own.reshape(frames_own * FROWS, groups, wide).transpose(1, 0, 2), "mp", 0, 0)
    do_heads = do_heads.reshape(FRAMES * FROWS, wide)
    dwo = drop_head_pads(dwo).reshape(groups, 1, block_rows, lanes)
    dw1 = dw1.reshape(D, groups, pieces * head_cols).transpose(1, 0, 2).reshape(groups, pieces, block_rows, lanes)
    dw2 = dw2.reshape(groups, pieces, block_rows, lanes)
    late = jnp.concatenate([dwo, dw1, dw2], axis=1).astype(BF16)
    late = lax.psum_scatter(late, "mp", scatter_dimension=0, tiled=False)
    late = lax.psum(late, "dp")

    dh_part, dqkv = attn_bwd(segment_ids, padding, pattern, qa, ka, va, ot, do_heads, h1_all, wqt, wkt, wvt)
    early = jnp.stack([drop_head_pads(dqkv[b]).T.reshape(block_rows, lanes) for b in range(3)]).astype(BF16)
    early = lax.psum(early, "dp")
    dh1 = lax.psum_scatter(dh_part, "mp", scatter_dimension=0, tiled=True).astype(F32)
    _, pull1 = jax.vjp(layer_norm, x, norm_params[0], norm_params[1])
    dh1 = jnp.where(live, dh1, 0.0)
    dln1, dg1, db1 = pull1(dh1)
    grad_in = (dx2 + dln1).astype(BF16)

    grads = jnp.concatenate([early, late], axis=0).astype(F32)
    norm_grads, square_sum = lax.psum((jnp.stack([dg1, db1, dg2, db2]),
                                       jnp.sum(grads * grads) / lax.axis_size("dp")), ("dp", "mp"))
    grad_norm = jnp.sqrt(square_sum + jnp.sum(norm_grads * norm_grads))
    clip_level = 0.5 * (4 * D * D + 2 * D * FF + 4 * D) ** 0.5
    factor = jnp.minimum(1.0, clip_level / grad_norm)
    grads = grads * factor
    old = jnp.stack([pick(moments[n], owner_slot) for n in range(2)]).astype(F32)
    new_weights, _, _ = adam_update(weights, grads, old[0], old[1], WEIGHT_DECAY, LEARN_RATE)
    slot_count = first_moments.shape[0]
    slot_ids = lax.axis_index("dp") * slot_count + jnp.arange(slot_count)
    matches = owner_slot[None, :] == slot_ids[:, None]
    in_use = jnp.any(matches, axis=1)[:, None, None]
    owned = pick(grads, jnp.sum(jnp.where(matches, jnp.arange(block_total)[None, :], 0), axis=1))
    _, first_new, second_new = adam_update(0.0, owned, first_moments, second_moments, 0.0, LEARN_RATE)
    new_first = jnp.where(in_use, first_new, first_moments)
    new_second = jnp.where(in_use, second_new, second_moments)
    new_norm, new_norm_first, new_norm_second = adam_update(
        norm_params, norm_grads * factor, norm_first, norm_second, 0.0, NORM_RATE)
    return (drop_pads(result)[None], drop_pads(grad_in)[None], grad_norm, new_weights, new_first, new_second,
            new_norm, new_norm_first, new_norm_second)


def solution(mesh):
    rows, blocks, slots = P("dp", "mp", None), P(None, "mp", None), P("dp", "mp", None)
    return jax.shard_map(
        shards,
        mesh=mesh,
        in_specs=(rows, rows, P("dp", None), P("dp", None), P(), P(), blocks, slots, slots, P(), P(), P()),
        out_specs=(rows, rows, P(), blocks, slots, slots, P(), P(), P()),
        check_vma=False,
    )
```

```python
import functools
import math

import jax
import jax.numpy as jnp
from jax import lax
from jax.experimental import pallas as pl
from jax.experimental.pallas import tpu as pltpu
from jax.sharding import PartitionSpec as P

FF = 1536
STEP = 10
NORM_EPS = 1e-05
BETA_ONE = 0.9
BETA_TWO = 0.95
ADAM_EPS = 1e-08
LEARN_RATE = 0.15
NORM_RATE = 0.6
WEIGHT_DECAY = 0.05

D = 384
HEAD_DIM = 24
FRAMES = 16
PATCHES = 196
FROWS = 208
FLANES = 256
HW = 32
HEADS_LOCAL = 4
WIDE = HEADS_LOCAL * HW
MASKED = -1e30
QSCALE = math.log2(math.e) / math.sqrt(HEAD_DIM)
F32 = jnp.float32
BF16 = jnp.bfloat16
NT = (((1,), (1,)), ((), ()))
TN = (((0,), (0,)), ((), ()))
HEADS = range(HEADS_LOCAL)


def dot(a, b):
    return jnp.dot(a, b, preferred_element_type=F32)


def dot_nt(a, b):
    return lax.dot_general(a, b, NT, preferred_element_type=F32)


def dot_tn(a, b):
    return lax.dot_general(a, b, TN, preferred_element_type=F32)


def frame_rows(f):
    return pl.ds(pl.multiple_of(f * FROWS, 16), FROWS)


def frame_lanes(f, size=FLANES):
    return pl.ds(pl.multiple_of(f * FLANES, 128), size)


def head_rows(h):
    return slice(HW * h, HW * (h + 1))


def seg_start(seg_ref, i, start):
    return jnp.where(seg_ref[0, i] == seg_ref[0, jnp.maximum(i - 1, 0)], start, i)


def fwd_kernel(seg_ref, pad_ref, pat_ref, h_ref, wq_ref, wk_ref, wv_ref,
               o_ref, ot_ref, qa_ref, ka_ref, va_ref, kt_ref, vt_s, qe_s, m_s, acc_s):
    col = lax.broadcasted_iota(jnp.int32, (FROWS, WIDE), 1) % HW
    row = lax.broadcasted_iota(jnp.int32, (FROWS, WIDE), 0)
    ones = jnp.where((col == 24) | (col == 25), 1.0, 0.0)
    kadd = ones + jnp.where((col == 26) & (row >= PATCHES), MASKED, 0.0)
    trow = lax.broadcasted_iota(jnp.int32, (WIDE, FROWS), 0) % HW
    vtadd = jnp.where(trow == 24, 1.0, 0.0)
    qadd = jnp.where(trow == 26, 1.0, 0.0)
    zpad = jnp.zeros((WIDE, FLANES - FROWS), BF16)
    r32 = lax.broadcasted_iota(jnp.int32, (HW, FLANES), 0)
    qe_s[...] = jnp.zeros(qe_s.shape, BF16)

    def project(f):
        hf = h_ref[frame_rows(f), :]
        qt = (dot_nt(wq_ref[...], hf) * QSCALE + qadd).astype(BF16)
        kr = (dot_nt(hf, wk_ref[...]) + kadd).astype(BF16)
        vr = (dot_nt(hf, wv_ref[...]) + ones).astype(BF16)
        kt = dot_nt(wk_ref[...], hf).astype(BF16)
        vt = (dot_nt(wv_ref[...], hf) + vtadd).astype(BF16)
        qt = jnp.concatenate([qt, zpad], axis=1)
        for h in HEADS:
            qe_s[f % 2, h, head_rows(h), :] = qt[head_rows(h)]
        ka_ref[frame_rows(f), :] = kr
        va_ref[frame_rows(f), :] = vr
        kt_ref[:, frame_lanes(f, FROWS)] = kt
        vt_s[:, frame_lanes(f, FROWS)] = vt

    def scores(i, j):
        kj = ka_ref[frame_rows(j), :]
        return [dot(kj, qe_s[i % 2, h]) for h in HEADS]

    def gathered(j, ps):
        return [dot(vt_s[head_rows(h), frame_lanes(j, FROWS)], ps[h]) for h in HEADS]

    def finalize(i):
        outs, augs = [], []
        for h in HEADS:
            a = acc_s[i % 2, h]
            l = a[24:25, :]
            outs.append(jnp.where(r32 < HEAD_DIM, a / l, 0.0))
            lse = -(m_s[i % 2, h] + jnp.log2(l))
            hi = lse.astype(BF16).astype(F32)
            aug = jnp.where(r32 == 24, hi, jnp.where(r32 == 25, lse - hi, 0.0))
            augs.append(qe_s[i % 2, h, head_rows(h), :].astype(F32) + aug)
        ot = jnp.concatenate(outs, axis=0)
        ot_ref[:, frame_lanes(i)] = ot.astype(BF16)
        qa_ref[:, frame_lanes(i)] = jnp.concatenate(augs, axis=0).astype(BF16)
        o_ref[frame_rows(i), :] = ot.T[:FROWS, :].astype(BF16)

    project(0)

    def queries(i, start):
        start = seg_start(seg_ref, i, start)
        finalize(jnp.maximum(i - 1, 0))
        ss = scores(i, i)
        mn = [jnp.max(ss[h], axis=0, keepdims=True) for h in HEADS]
        ps = [jnp.exp2(ss[h] - mn[h]).astype(BF16) for h in HEADS]
        pv = gathered(i, ps)
        for h in HEADS:
            acc_s[i % 2, h] = pv[h]
            m_s[i % 2, h] = mn[h]
        project(jnp.minimum(i + 1, FRAMES - 1))

        def keys(j, _):
            @pl.when((pat_ref[i, j] == 1) & (pad_ref[0, j] == 0))
            def _():
                ss = scores(i, j)
                mo = [m_s[i % 2, h] for h in HEADS]
                mn = [jnp.maximum(mo[h], jnp.max(ss[h], axis=0, keepdims=True)) for h in HEADS]
                ps = [jnp.exp2(ss[h] - mn[h]).astype(BF16) for h in HEADS]
                pv = gathered(j, ps)
                for h in HEADS:
                    acc_s[i % 2, h] = acc_s[i % 2, h] * jnp.exp2(mo[h] - mn[h]) + pv[h]
                    m_s[i % 2, h] = mn[h]
            return 0
        lax.fori_loop(start, i, keys, 0)
        return start
    lax.fori_loop(0, FRAMES, queries, 0)
    finalize(FRAMES - 1)


SMEM = pl.BlockSpec(memory_space=pltpu.SMEM)
VM = pl.BlockSpec(memory_space=pltpu.VMEM)


def attn_fwd(seg, pad, pat, h, wqt, wkt, wvt):
    sd = jax.ShapeDtypeStruct
    V = pltpu.VMEM
    rows, lanes = sd((FRAMES * FROWS, WIDE), BF16), sd((WIDE, FRAMES * FLANES), BF16)
    return pl.pallas_call(
        fwd_kernel,
        out_shape=(rows, lanes, lanes, rows, rows, lanes),
        in_specs=[SMEM] * 3 + [VM] * 4,
        out_specs=(VM,) * 6,
        scratch_shapes=[V((WIDE, FRAMES * FLANES), BF16), V((2, HEADS_LOCAL, WIDE, FLANES), BF16),
                        V((2, HEADS_LOCAL, 1, FLANES), F32), V((2, HEADS_LOCAL, HW, FLANES), F32)],
        compiler_params=pltpu.CompilerParams(vmem_limit_bytes=48 << 20),
        cost_estimate=pl.CostEstimate(flops=int(4e9), bytes_accessed=8 << 20, transcendentals=0),
        name="attend_forward",
    )(seg, pad, pat, h, wqt, wkt, wvt)


def bwd_kernel(seg_ref, pad_ref, pat_ref, qa_ref, ka_ref, va_ref, kt_ref, ot_ref, do_ref, h_ref, wq_ref, wk_ref, wv_ref,
               dh_ref, early_ref, qe_s, oe_s, qr_s, or_s, dq_s, dk_s, dv_s, dw_s, turn_s, blk_s, start_s):
    scale = HEAD_DIM ** -0.5
    for s in (qe_s, oe_s, qr_s, or_s):
        s[...] = jnp.zeros(s.shape, BF16)
    dk_s[...] = jnp.zeros(dk_s.shape, F32)
    dv_s[...] = jnp.zeros(dv_s.shape, F32)
    dq_s[...] = jnp.zeros(dq_s.shape, F32)
    dw_s[...] = jnp.zeros(dw_s.shape, F32)
    qrow = lax.broadcasted_iota(jnp.int32, (WIDE, FLANES), 0) % HW
    qcol = lax.broadcasted_iota(jnp.int32, (FROWS, WIDE), 1)
    r32 = lax.broadcasted_iota(jnp.int32, (HW, FLANES), 0)
    zpad = jnp.zeros((WIDE, FLANES - FROWS), F32)

    def starts(i, start):
        start_s[i] = seg_start(seg_ref, i, start)
        return start_s[i]
    lax.fori_loop(0, FRAMES, starts, 0)

    def prepare(i):
        t = i % 2
        qt = qa_ref[:, frame_lanes(i)]
        dor = do_ref[frame_rows(i), :].astype(F32)
        dot_ = jnp.concatenate([dor.T, zpad], axis=1)
        prod = dot_ * ot_ref[:, frame_lanes(i)].astype(F32)
        qrows = qt.astype(F32).T[:FROWS, :]
        for h in HEADS:
            d = -jnp.sum(prod[head_rows(h)], axis=0, keepdims=True)
            hi = d.astype(BF16).astype(F32)
            aug = jnp.where(r32 == 24, hi, jnp.where(r32 == 25, d - hi, 0.0))
            qe_s[t, h, head_rows(h), :] = qt[head_rows(h)]
            oe_s[t, h, head_rows(h), :] = (dot_[head_rows(h)] + aug).astype(BF16)
            mine = ((qcol // HW) == h) & (qcol % HW < HEAD_DIM)
            qr_s[t, h * FLANES:h * FLANES + FROWS, :] = jnp.where(mine, qrows, 0.0).astype(BF16)
            or_s[t, h * FLANES:h * FLANES + FROWS, :] = jnp.where(mine, dor, 0.0).astype(BF16)

    def pair(i, j):
        t = i % 2
        kj = ka_ref[frame_rows(j), :]
        vj = va_ref[frame_rows(j), :]
        ss = [dot(kj, qe_s[t, h]) for h in HEADS]
        dps = [dot(vj, oe_s[t, h]) for h in HEADS]
        ps = [jnp.exp2(ss[h]) for h in HEADS]
        ds = [(ps[h] * dps[h]).astype(BF16) for h in HEADS]
        pb = [ps[h].astype(BF16) for h in HEADS]
        dq = [dot(kt_ref[head_rows(h), frame_lanes(j, FROWS)], ds[h]) for h in HEADS]
        dv = dot(jnp.concatenate(pb, axis=1), or_s[t])
        dk = dot(jnp.concatenate(ds, axis=1), qr_s[t])
        dv_s[frame_rows(j), :] += dv
        dk_s[frame_rows(j), :] += dk
        return jnp.concatenate(dq, axis=0)

    def finish(f):
        dqt = jnp.where(qrow < HEAD_DIM, dq_s[f % 2] * scale, 0.0).astype(BF16)[:, :FROWS]
        dk = (dk_s[frame_rows(f), :] * math.log(2.0)).astype(BF16)
        dv = dv_s[frame_rows(f), :].astype(BF16)
        hf = h_ref[frame_rows(f), :]
        dh_ref[frame_rows(f), :] = (dot_tn(dqt, wq_ref[...]) + dot(dk, wk_ref[...]) + dot(dv, wv_ref[...])).astype(BF16)
        return dot(dqt, hf), dot_tn(dk, hf), dot_tn(dv, hf)

    prepare(FRAMES - 1)

    def queries(n, _):
        i = FRAMES - 1 - n
        above = jnp.minimum(i + 1, FRAMES - 1)
        dw = finish(above)
        dq_s[i % 2] = pair(i, i)
        for b in range(3):
            dw_s[b] += jnp.where(n > 0, dw[b], 0.0)
        prepare(jnp.maximum(i - 1, 0))

        def keys(j, _):
            @pl.when((pat_ref[i, j] == 1) & (pad_ref[0, j] == 0))
            def _():
                dq_s[i % 2] += pair(i, j)
            return 0
        lax.fori_loop(start_s[i], i, keys, 0)
        return 0
    lax.fori_loop(0, FRAMES, queries, 0)
    dw = finish(0)
    for b in range(3):
        turned = (dw_s[b] + dw[b]).T
        turn_s[:, 0:96] = jnp.concatenate([turned[:, HW * h:HW * h + HEAD_DIM] for h in HEADS], axis=1)
        line = [turn_s[pl.ds(k, 96, stride=4), :][:, 0:96] for k in range(4)]
        blk_s[pl.ds(0, 96, stride=3), :] = jnp.concatenate([line[0], line[1][:, :32]], axis=1)
        blk_s[pl.ds(1, 96, stride=3), :] = jnp.concatenate([line[1][:, 32:], line[2][:, :64]], axis=1)
        blk_s[pl.ds(2, 96, stride=3), :] = jnp.concatenate([line[2][:, 64:], line[3]], axis=1)
        early_ref[288 * b:288 * (b + 1), :] = blk_s[...].astype(BF16)


def attn_bwd(seg, pad, pat, qa, ka, va, kt, ot, do, h, wqt, wkt, wvt):
    sd = jax.ShapeDtypeStruct
    V = pltpu.VMEM
    return pl.pallas_call(
        bwd_kernel,
        out_shape=(sd((FRAMES * FROWS, D), BF16), sd((3 * 288, 128), BF16)),
        in_specs=[SMEM] * 3 + [VM] * 10,
        out_specs=(VM,) * 2,
        scratch_shapes=[V((2, HEADS_LOCAL, WIDE, FLANES), BF16), V((2, HEADS_LOCAL, WIDE, FLANES), BF16),
                        V((2, HEADS_LOCAL * FLANES, WIDE), BF16), V((2, HEADS_LOCAL * FLANES, WIDE), BF16),
                        V((2, WIDE, FLANES), F32), V((FRAMES * FROWS, WIDE), F32), V((FRAMES * FROWS, WIDE), F32),
                        V((3, WIDE, D), F32), V((D, 128), F32), V((288, 128), F32), pltpu.SMEM((FRAMES,), jnp.int32)],
        compiler_params=pltpu.CompilerParams(vmem_limit_bytes=56 << 20),
        cost_estimate=pl.CostEstimate(flops=int(12e9), bytes_accessed=12 << 20, transcendentals=0),
        name="attend_backward",
    )(seg, pad, pat, qa, ka, va, kt, ot, do, h, wqt, wkt, wvt)


MESH = pl.DeviceIdType.MESH
OWN_ROWS = 4 * FROWS


def place(d, m):
    return {"dp": d, "mp": m}


def remote(src, dst, send_sem, recv_sem, device):
    return pltpu.make_async_remote_copy(
        src_ref=src, dst_ref=dst, send_sem=send_sem, recv_sem=recv_sem, device_id=device, device_id_type=MESH
    )


def greet(devices):
    barrier = pltpu.get_barrier_semaphore()
    for device in devices:
        pl.semaphore_signal(barrier, inc=1, device_id=device, device_id_type=MESH)
    pl.semaphore_wait(barrier, len(devices))


def group_peers():
    me = lax.axis_index("mp")
    return me, me ^ 1, me ^ 2, me ^ 3


def frame_part(device, c):
    return pl.ds(pl.multiple_of(device * OWN_ROWS + c * FROWS, 16), FROWS)


def normalised(v):
    centred = v - jnp.mean(v, axis=-1, keepdims=True)
    inv = lax.rsqrt(jnp.mean(centred * centred, axis=-1, keepdims=True) + NORM_EPS)
    return centred * inv, inv


def norm_pull(dy, hat, inv, gain):
    dg = dy * gain
    lead = jnp.mean(dg, axis=-1, keepdims=True)
    along = jnp.mean(dg * hat, axis=-1, keepdims=True)
    return inv * (dg - lead - hat * along)


def col_sum(v):
    return jnp.sum(v, axis=0, keepdims=True)


def live_rows():
    return lax.broadcasted_iota(jnp.int32, (FROWS, 1), 0) < PATCHES


def start_kernel(x_ref, np_ref, w_ref, h_ref, wq_ref, wk_ref, wv_ref, ws_ref, w_s,
                 send_x, recv_x, send_p, recv_p, send_f, recv_f):
    me, near, far, _ = group_peers()
    greet([{"mp": near}, {"mp": far}])
    frames = range(OWN_ROWS // FROWS)
    live = live_rows()
    to_far, to_near = [], []
    for c in frames:
        hat, _ = normalised(x_ref[c * FROWS:(c + 1) * FROWS, :].astype(F32))
        h_ref[frame_part(me, c), :] = jnp.where(live, hat * np_ref[0:1, :] + np_ref[1:2, :], 0.0).astype(BF16)
        rows = h_ref.at[frame_part(me, c), :]
        to_far.append(remote(rows, rows, send_x.at[c], recv_x.at[c], {"mp": far}))
        to_near.append(remote(rows, rows, send_p.at[c], recv_p.at[c], {"mp": near}))
        to_far[c].start()
        to_near[c].start()

    def incoming(device, sends, recvs, c):
        rows = h_ref.at[frame_part(device, c), :]
        return remote(rows, rows, sends.at[c], recvs.at[c], {"mp": near})

    def forward(c):
        incoming(far, send_x, recv_x, c).wait_recv()
        copy = incoming(far, send_f, recv_f, c)
        copy.start()
        return copy

    for b, out in enumerate((wq_ref, wk_ref, wv_ref)):
        a = [w_ref[b, pl.ds(k, 96, stride=3), :] for k in range(3)]
        lines = [a[0][:, :96], jnp.concatenate([a[0][:, 96:], a[1][:, :64]], axis=1),
                 jnp.concatenate([a[1][:, 64:], a[2][:, :32]], axis=1), a[2][:, 32:]]
        gap = jnp.zeros((96, HW - HEAD_DIM), F32)
        for k in range(4):
            parts = []
            for h in HEADS:
                parts += [lines[k][:, HEAD_DIM * h:HEAD_DIM * (h + 1)], gap]
            w_s[pl.ds(k, 96, stride=4), :] = jnp.concatenate(parts, axis=1)
        out[...] = w_s[...].T.astype(BF16)
    copies = [forward(0)]
    for b in range(3, w_ref.shape[0]):
        for k in range(3):
            lanes = slice(128 * k, 128 * (k + 1))
            part = w_ref[b, pl.ds(k, 96, stride=3), :]
            if b == 3:
                gap = jnp.zeros((HW - HEAD_DIM, 128), F32)
                parts = []
                for h in HEADS:
                    parts += [part[HEAD_DIM * h:HEAD_DIM * (h + 1)], gap]
                ws_ref[2 * D:2 * D + WIDE, lanes] = jnp.concatenate(parts, axis=0).astype(BF16)
            else:
                ws_ref[96 * (b - 4):96 * (b - 3), lanes] = part.astype(BF16)
    for c in frames[1:]:
        copies.append(forward(c))
    for c in frames:
        incoming(near, send_p, recv_p, c).wait_recv()
        incoming(near ^ 2, send_f, recv_f, c).wait_recv()
        to_far[c].wait_send()
        to_near[c].wait_send()
        copies[c].wait_send()


def start_call(x, norm_params, weights):
    sd = jax.ShapeDtypeStruct
    blocks = weights.shape[0]
    shared = WIDE + 96 * (blocks - 4)
    turned = sd((WIDE, D), BF16)
    return pl.pallas_call(
        start_kernel,
        out_shape=(sd((FRAMES * FROWS, D), BF16), turned, turned, turned, sd((shared, D), BF16)),
        in_specs=[VM] * 3,
        out_specs=(VM,) * 5,
        scratch_shapes=[pltpu.VMEM((D, WIDE), F32)] + [pltpu.SemaphoreType.DMA((4,))] * 6,
        compiler_params=pltpu.CompilerParams(vmem_limit_bytes=32 << 20, collective_id=1, has_side_effects=True),
        name="norm_and_gather",
    )(x, norm_params, weights)


def gelu_parts(u):
    c = math.sqrt(2.0 / math.pi)
    t = jnp.tanh(c * (u + 0.044715 * u * u * u))
    value = 0.5 * u * (1.0 + t)
    slope = 0.5 * (1.0 + t) + 0.5 * u * (1.0 - t * t) * (c * (1.0 + 3.0 * 0.044715 * u * u))
    return value, slope


def middle_kernel(o_ref, x_ref, ct_ref, keep_ref, w_ref, np_ref,
                  out_ref, dx2_ref, do_ref, late_ref, nb_ref,
                  ob_s, dob_s, g_s, a_s, du_s, da_s, h2_s, dxa_s, blk_s,
                  send_o, recv_o, send_d, recv_d):
    me, near, far, across = group_peers()
    peers = (far, across, near)
    greet([{"mp": p} for p in peers])
    frames = range(OWN_ROWS // FROWS)
    groups = w_ref.shape[0]
    live = live_rows()
    outgoing = []
    for c in frames:
        for n, p in enumerate(peers):
            outgoing.append(remote(o_ref.at[frame_part(p, c), :], ob_s.at[n, pl.ds(c * FROWS, FROWS), :],
                                   send_o.at[n, c], recv_o.at[n, c], {"mp": p}))
            outgoing[-1].start()

    def w_o(m):
        return w_ref[m, 2 * D:2 * D + WIDE, :]

    def w_up(m):
        return w_ref[m, 0:D, :]

    def w_down(m):
        return w_ref[m, D:2 * D, :]

    def cols(m):
        return slice(m * D, (m + 1) * D)

    for c in frames:
        rows = slice(c * FROWS, (c + 1) * FROWS)
        g_s[rows, :] = (ct_ref[rows, :].astype(F32) * keep_ref[0, c]).astype(BF16)
        for m in range(groups):
            da_s[rows, cols(m)] = dot_nt(g_s[rows, :], w_down(m))
    nb_ref[...] = jnp.zeros(nb_ref.shape, F32)
    sent = []
    for c in frames:
        rows = slice(c * FROWS, (c + 1) * FROWS)
        x2 = x_ref[rows, :].astype(F32) + dot(o_ref[frame_part(me, c), :], w_o(me))
        for n, p in enumerate(peers):
            remote(ob_s.at[n, pl.ds(c * FROWS, FROWS), :], ob_s.at[n, pl.ds(c * FROWS, FROWS), :],
                   send_o.at[n, c], recv_o.at[n, c], {"mp": p}).wait_recv()
            x2 = x2 + dot(ob_s[n, rows, :], w_o(p))
        x2 = jnp.where(live, x2, 0.0)
        hat, inv = normalised(x2)
        h2 = (hat * np_ref[2:3, :] + np_ref[3:4, :]).astype(BF16)
        h2_s[rows, :] = h2
        dh2 = jnp.zeros((FROWS, D), F32)
        for m in range(groups):
            value, slope = gelu_parts(dot(h2, w_up(m)))
            act = value.astype(BF16)
            du = (da_s[rows, cols(m)] * slope).astype(BF16)
            a_s[rows, cols(m)] = act
            du_s[rows, cols(m)] = du
            dh2 = dh2 + dot_nt(du, w_up(m))
        down = jnp.concatenate([w_down(m) for m in range(groups)], axis=0)
        out_ref[rows, :] = (x2 + dot(a_s[rows, :], down)).astype(BF16)
        nb_ref[0:1, :] += col_sum(dh2 * hat)
        nb_ref[1:2, :] += col_sum(dh2)
        dx2 = g_s[rows, :].astype(F32) + norm_pull(dh2, hat, inv, np_ref[2:3, :])
        dx2_ref[rows, :] = dx2
        dxa = dx2.astype(BF16)
        dxa_s[rows, :] = dxa
        for n, p in enumerate(peers):
            dob_s[n, rows, :] = dot_nt(dxa, w_o(p)).astype(BF16)
            sent.append(remote(dob_s.at[n, pl.ds(c * FROWS, FROWS), :], do_ref.at[frame_part(me, c), :],
                               send_d.at[n, c], recv_d.at[n, c], {"mp": p}))
            sent[-1].start()
        do_ref[frame_part(me, c), :] = dot_nt(dxa, w_o(me)).astype(BF16)

    def as_block(shard, first, value):
        count = value.shape[0]
        for k in range(3):
            blk_s[pl.ds(k, count, stride=3), :] = value[:, 128 * k:128 * (k + 1)]
        late_ref[shard, first * 288:first * 288 + 3 * count, :] = blk_s[0:3 * count, :].astype(BF16)

    def drop_gaps(value):
        return jnp.concatenate([value[HW * h:HW * h + HEAD_DIM] for h in HEADS], axis=0)

    for m in range(groups):
        as_block(m, 1, dot_tn(h2_s[...], du_s[:, cols(m)]))
        as_block(m, 5, dot_tn(a_s[:, cols(m)], g_s[...]))
    as_block(me, 0, drop_gaps(dot_tn(o_ref[pl.ds(pl.multiple_of(me * OWN_ROWS, 16), OWN_ROWS), :], dxa_s[...])))
    for n, p in enumerate(peers):
        as_block(p, 0, drop_gaps(dot_tn(ob_s[n], dxa_s[...])))
    for copy in outgoing + sent:
        copy.wait_send()
    for c in frames:
        for n, p in enumerate(peers):
            part = do_ref.at[frame_part(p, c), :]
            remote(part, part, send_d.at[n, c], recv_d.at[n, c], {"mp": p}).wait_recv()


def middle_call(o, x, ct, keep, w, norm_params):
    sd = jax.ShapeDtypeStruct
    V = pltpu.VMEM
    groups = w.shape[0]
    sems = [pltpu.SemaphoreType.DMA((3, 4))] * 4
    return pl.pallas_call(
        middle_kernel,
        out_shape=(sd((OWN_ROWS, D), BF16), sd((OWN_ROWS, D), F32), sd((FRAMES * FROWS, WIDE), BF16),
                   sd((groups, 9 * 288, 128), BF16), sd((2, D), F32)),
        in_specs=[VM, VM, VM, SMEM, VM, VM],
        out_specs=(VM,) * 5,
        scratch_shapes=[V((3, OWN_ROWS, WIDE), BF16), V((3, OWN_ROWS, WIDE), BF16), V((OWN_ROWS, D), BF16),
                        V((OWN_ROWS, FF), BF16), V((OWN_ROWS, FF), BF16), V((OWN_ROWS, FF), F32),
                        V((OWN_ROWS, D), BF16), V((OWN_ROWS, D), BF16), V((1152, 128), F32)] + sems,
        compiler_params=pltpu.CompilerParams(vmem_limit_bytes=56 << 20, collective_id=2, has_side_effects=True),
        cost_estimate=pl.CostEstimate(flops=int(6e9), bytes_accessed=12 << 20, transcendentals=0),
        name="feed_forward",
    )(o, x, ct, keep, w, norm_params)


def reduce_kernel(dp, piece, dh_ref, early_ref, late_ref, x_ref, dx2_ref, np_ref, nb_ref,
                  gin_ref, gs_ref, tot_ref,
                  pb_s, xs_s, xb_s, g_s, yb_s, zs_s, zb_s, msg_s, mb_s, dm_s, db_s,
                  send_p, recv_p, send_x, recv_x, send_y, recv_y, send_z, recv_z,
                  send_a, recv_a, send_w, recv_w, send_m, recv_m, send_n, recv_n):
    me, near, far, across = group_peers()
    d = lax.axis_index("dp")
    count = dp // 2
    side, line = d % 2, d // 2
    twin = {"dp": d ^ 1}

    def on_line(n):
        return lax.rem(line + n, count)

    def line_device(q):
        return {"dp": q * 2 + side}

    frames = range(OWN_ROWS // FROWS)
    others = [{"mp": near}, {"mp": far}, {"mp": across}] + [{"dp": lax.rem(d + n, dp)} for n in range(1, dp)]
    greet(others)

    def own(c):
        return pl.ds(c * FROWS, FROWS)

    to_near = []
    for k, target in ((1, across), (0, near)):
        for c in frames:
            to_near.append(remote(dh_ref.at[frame_part(target, c), :], pb_s.at[k, own(c), :],
                                  send_p.at[k, c], recv_p.at[k, c], {"mp": near}))
            to_near[-1].start()

    g_s[0:early_ref.shape[0], :] = early_ref[...]
    g_s[early_ref.shape[0]:early_ref.shape[0] + late_ref.shape[0], :] = late_ref[...]
    total = early_ref.shape[0] + late_ref.shape[0]
    if g_s.shape[0] > total:
        g_s[total:, :] = jnp.zeros((g_s.shape[0] - total, 128), BF16)

    def at(s, q):
        return pl.ds(pl.multiple_of((s * count + q) * piece, 16), piece)

    to_twin = []
    for n in range(count):
        q = on_line(n + 1)
        to_twin.append(remote(g_s.at[at(1 - side, q), :], yb_s.at[q], send_y.at[q], recv_y.at[q], twin))
        to_twin[-1].start()

    to_far = []
    for c in frames:
        remote(pb_s.at[1, own(c), :], pb_s.at[1, own(c), :], send_p.at[1, c], recv_p.at[1, c], {"mp": near}).wait_recv()
        xs_s[own(c), :] = (dh_ref[frame_part(far, c), :].astype(F32) + pb_s[1, own(c), :].astype(F32)).astype(BF16)
        to_far.append(remote(xs_s.at[own(c), :], xb_s.at[own(c), :], send_x.at[c], recv_x.at[c], {"mp": far}))
        to_far[-1].start()

    to_line = []
    for n in range(count):
        q = on_line(n + 1)
        remote(yb_s.at[q], yb_s.at[q], send_y.at[q], recv_y.at[q], twin).wait_recv()
        zs_s[q] = (g_s[at(side, q), :].astype(F32) + yb_s[q].astype(F32)).astype(BF16)
        if n < count - 1:
            to_line.append(remote(zs_s.at[q], zb_s.at[line], send_z.at[q], recv_z.at[line], line_device(q)))
            to_line[-1].start()
    mine = zs_s[line].astype(F32)
    for n in range(1, count):
        q = on_line(n)
        remote(zb_s.at[q], zb_s.at[q], send_z.at[q], recv_z.at[q], line_device(q)).wait_recv()
        mine = mine + zb_s[q].astype(F32)
    mine = mine.astype(BF16)
    gs_ref[at(side, line), :] = mine
    whole = gs_ref.at[at(side, line), :]
    spread = []
    for n in range(1, count):
        q = on_line(n)
        spread.append(remote(whole, whole, send_a.at[q], recv_a.at[line], line_device(q)))
        spread[-1].start()
    passed = [remote(whole, whole, send_w.at[line], recv_w.at[line], twin)]
    passed[0].start()
    mine = mine.astype(F32)
    squares = jnp.sum(mine * mine, axis=0, keepdims=True)

    live = live_rows()
    gain, bias = jnp.zeros((1, D), F32), jnp.zeros((1, D), F32)
    for c in frames:
        remote(pb_s.at[0, own(c), :], pb_s.at[0, own(c), :], send_p.at[0, c], recv_p.at[0, c], {"mp": near}).wait_recv()
        remote(xb_s.at[own(c), :], xb_s.at[own(c), :], send_x.at[c], recv_x.at[c], {"mp": far}).wait_recv()
        dy = dh_ref[frame_part(me, c), :].astype(F32) + pb_s[0, own(c), :].astype(F32) + xb_s[own(c), :].astype(F32)
        dy = jnp.where(live, dy, 0.0)
        hat, inv = normalised(x_ref[own(c), :].astype(F32))
        gain = gain + col_sum(dy * hat)
        bias = bias + col_sum(dy)
        gin_ref[own(c), :] = (dx2_ref[own(c), :] + norm_pull(dy, hat, inv, np_ref[0:1, :])).astype(BF16)

    msg_s[...] = jnp.zeros(msg_s.shape, F32)
    msg_s[0:1, :] = gain
    msg_s[1:2, :] = bias
    msg_s[2:4, :] = nb_ref[...]
    msg_s[4:5, 0:128] = squares
    small = []
    for n, p in enumerate((near, far, across)):
        small.append(remote(msg_s, mb_s.at[n], send_m.at[n], recv_m.at[n], {"mp": p}))
        small[-1].start()

    def pass_on(n):
        q = on_line(n)
        piece_at = gs_ref.at[at(side, q), :]
        remote(piece_at, piece_at, send_a.at[q], recv_a.at[q], line_device(q)).wait_recv()
        passed.append(remote(piece_at, piece_at, send_w.at[q], recv_w.at[q], twin))
        passed[-1].start()

    pass_on(1)
    add = msg_s[...]
    for n, p in enumerate((near, far, across)):
        remote(mb_s.at[n], mb_s.at[n], send_m.at[n], recv_m.at[n], {"mp": p}).wait_recv()
        add = add + mb_s[n]
    dm_s[...] = add
    for n in range(1, dp):
        small.append(remote(dm_s, db_s.at[n], send_n.at[n], recv_n.at[n], {"dp": lax.rem(d + n, dp)}))
        small[-1].start()
    for n in range(2, count):
        pass_on(n)
    for n in range(1, dp):
        remote(db_s.at[n], db_s.at[n], send_n.at[n], recv_n.at[n], {"dp": lax.rem(d + dp - n, dp)}).wait_recv()
        add = add + db_s[n]
    tot_ref[...] = add
    for n in range(count):
        q = on_line(n)
        piece_at = gs_ref.at[at(1 - side, q), :]
        remote(piece_at, piece_at, send_w.at[q], recv_w.at[q], twin).wait_recv()
    for copy in to_near + to_twin + to_far + to_line + spread + passed + small:
        copy.wait_send()


def reduce_call(dp, dh, early, late, x, dx2, norm_params, nb):
    sd = jax.ShapeDtypeStruct
    V, S = pltpu.VMEM, pltpu.SemaphoreType.DMA
    rows = early.shape[0] + late.shape[0]
    count = dp // 2
    piece = -(-rows // (2 * count * 16)) * 16
    held = 2 * count * piece
    return pl.pallas_call(
        functools.partial(reduce_kernel, dp, piece),
        out_shape=(sd((OWN_ROWS, D), BF16), sd((held, 128), BF16), sd((8, D), F32)),
        in_specs=[VM] * 7,
        out_specs=(VM,) * 3,
        scratch_shapes=[V((2, OWN_ROWS, D), BF16), V((OWN_ROWS, D), BF16), V((OWN_ROWS, D), BF16), V((held, 128), BF16),
                        V((count, piece, 128), BF16), V((count, piece, 128), BF16), V((count, piece, 128), BF16),
                        V((8, D), F32), V((3, 8, D), F32), V((8, D), F32), V((dp, 8, D), F32),
                        S((2, 4)), S((2, 4)), S((4,)), S((4,)), S((count,)), S((count,)), S((count,)), S((count,)),
                        S((count,)), S((count,)), S((count,)), S((count,)), S((3,)), S((3,)), S((dp,)), S((dp,))],
        compiler_params=pltpu.CompilerParams(vmem_limit_bytes=48 << 20, collective_id=3, has_side_effects=True),
        name="reduce_gradients",
    )(dh, early, late, x, dx2, norm_params, nb)


def update_kernel(slot_ref, dev_ref, tot_ref, gs_ref, w_ref, m_ref, v_ref, mom_ref, np_ref, nm_ref, nv_ref,
                  norm_ref, nw_ref, nf_ref, ns_ref, nn_ref, nnf_ref, nns_ref):
    blocks, rows, _ = w_ref.shape
    tot = tot_ref[...]
    grads = tot[0:4, :]
    norm = jnp.sqrt(jnp.sum(grads * grads, keepdims=True) + jnp.sum(tot[4:5, 0:128], keepdims=True))
    norm_ref[...] = norm
    clip_level = 0.5 * (4 * D * D + 2 * D * FF + 4 * D) ** 0.5
    factor = jnp.minimum(1.0, clip_level / norm)
    nn_ref[...], nnf_ref[...], nns_ref[...] = adam_update(
        np_ref[...], grads * factor, nm_ref[...], nv_ref[...], 0.0, NORM_RATE)

    def block(b):
        return gs_ref[pl.ds(pl.multiple_of(b * rows, 16), rows), :].astype(F32) * factor

    def step(b, _):
        slot = slot_ref[b]
        nw_ref[b], _, _ = adam_update(w_ref[b], block(b), mom_ref[slot, 0].astype(F32), mom_ref[slot, 1].astype(F32),
                                      WEIGHT_DECAY, LEARN_RATE)
        return 0
    lax.fori_loop(0, blocks, step, 0)
    for s in range(m_ref.shape[0]):
        owned = jnp.int32(-1)
        for b in range(blocks):
            owned = jnp.where(slot_ref[b] == dev_ref[0] * m_ref.shape[0] + s, b, owned)
        _, first, second = adam_update(0.0, block(jnp.maximum(owned, 0)), m_ref[s], v_ref[s], 0.0, LEARN_RATE)
        nf_ref[s] = jnp.where(owned >= 0, first, m_ref[s])
        ns_ref[s] = jnp.where(owned >= 0, second, v_ref[s])


def update_call(owner_slot, tot, gs, weights, first, second, moments, norm_params, norm_first, norm_second):
    sd = jax.ShapeDtypeStruct
    small = sd((4, D), F32)
    device = lax.axis_index("dp").reshape(1)
    return pl.pallas_call(
        update_kernel,
        out_shape=(sd((1, 1), F32), sd(weights.shape, F32), sd(first.shape, F32), sd(first.shape, F32), small, small, small),
        in_specs=[SMEM] * 2 + [VM] * 9,
        out_specs=(VM,) * 7,
        compiler_params=pltpu.CompilerParams(vmem_limit_bytes=32 << 20),
        name="clipped_update",
    )(owner_slot, device, tot, gs, weights, first, second, moments, norm_params, norm_first, norm_second)


def adam_update(current, gradient, first_moment, second_moment, decay_rate, step_rate):
    first_new = BETA_ONE * first_moment + (1.0 - BETA_ONE) * gradient
    second_new = BETA_TWO * second_moment + (1.0 - BETA_TWO) * gradient * gradient
    first_fix = 1.0 - BETA_ONE**STEP
    second_fix = 1.0 - BETA_TWO**STEP
    direction = first_new / first_fix / (jnp.sqrt(second_new / second_fix) + ADAM_EPS)
    return (current - step_rate * (direction + decay_rate * current), first_new, second_new)


def pad_frames(rows):
    split = rows.reshape(-1, PATCHES, rows.shape[-1])
    return jnp.pad(split, ((0, 0), (0, FROWS - PATCHES), (0, 0))).reshape(-1, rows.shape[-1])


def drop_pads(rows):
    return rows.reshape(-1, FROWS, rows.shape[-1])[:, :PATCHES].reshape(1, -1, rows.shape[-1])


def shards(tokens, cotangent, segment_ids, padding, pattern, owner_slot, weights, first_moments, second_moments,
           norm_params, norm_first, norm_second):
    groups = lax.axis_size("mp")
    me = lax.axis_index("mp")
    frames_own = FRAMES // groups
    moments = lax.all_gather(jnp.stack([first_moments, second_moments], axis=1).astype(BF16), "dp", axis=0, tiled=True)
    x = pad_frames(tokens[0])
    ct = pad_frames(cotangent[0])
    keep = 1.0 - lax.dynamic_slice_in_dim(padding, me * frames_own, frames_own, 1).astype(F32)
    h1, wq, wk, wv, own_shared = start_call(x, norm_params, weights)
    shared = lax.all_gather(own_shared, "mp", axis=0)
    o, ot, qa, ka, va, kt = attn_fwd(segment_ids, padding, pattern, h1, wq, wk, wv)
    result, dx2, do, late, nb = middle_call(o, x, ct, keep, shared, norm_params)
    late = lax.psum_scatter(late, "mp", scatter_dimension=0, tiled=False)
    dh, early = attn_bwd(segment_ids, padding, pattern, qa, ka, va, kt, ot, do, h1, wq, wk, wv)
    grad_in, gs, tot = reduce_call(lax.axis_size("dp"), dh, early, late, x, dx2, norm_params, nb)
    grad_norm, new_weights, new_first, new_second, new_norm, new_norm_first, new_norm_second = update_call(
        owner_slot, tot, gs, weights, first_moments, second_moments, moments, norm_params, norm_first, norm_second)
    return (drop_pads(result), drop_pads(grad_in), grad_norm[0, 0], new_weights, new_first, new_second,
            new_norm, new_norm_first, new_norm_second)


def solution(mesh):
    rows, blocks, slots = P("dp", "mp", None), P(None, "mp", None), P("dp", "mp", None)
    return jax.shard_map(
        shards,
        mesh=mesh,
        in_specs=(rows, rows, P("dp", None), P("dp", None), P(), P(), blocks, slots, slots, P(), P(), P()),
        out_specs=(rows, rows, P(), blocks, slots, slots, P(), P(), P()),
        check_vma=False,
    )
```

```python
import functools
import math

import jax
import jax.numpy as jnp
from jax import lax
from jax.experimental import pallas as pl
from jax.experimental.pallas import tpu as pltpu
from jax.sharding import PartitionSpec as P

FF = 1536
STEP = 10
NORM_EPS = 1e-05
BETA_ONE = 0.9
BETA_TWO = 0.95
ADAM_EPS = 1e-08
LEARN_RATE = 0.15
NORM_RATE = 0.6
WEIGHT_DECAY = 0.05

D = 384
HEAD_DIM = 24
FRAMES = 16
PATCHES = 196
FROWS = 208
FLANES = 256
HW = 32
HEADS_LOCAL = 4
WIDE = HEADS_LOCAL * HW
MASKED = -1e30
QSCALE = math.log2(math.e) / math.sqrt(HEAD_DIM)
F32 = jnp.float32
BF16 = jnp.bfloat16
NT = (((1,), (1,)), ((), ()))
TN = (((0,), (0,)), ((), ()))
HEADS = range(HEADS_LOCAL)


def dot(a, b):
    return jnp.dot(a, b, preferred_element_type=F32)


def dot_nt(a, b):
    return lax.dot_general(a, b, NT, preferred_element_type=F32)


def dot_tn(a, b):
    return lax.dot_general(a, b, TN, preferred_element_type=F32)


def frame_rows(f):
    return pl.ds(pl.multiple_of(f * FROWS, 16), FROWS)


def frame_lanes(f, size=FLANES):
    return pl.ds(pl.multiple_of(f * FLANES, 128), size)


def head_rows(h):
    return slice(HW * h, HW * (h + 1))


def seg_start(seg_ref, i, start):
    return jnp.where(seg_ref[0, i] == seg_ref[0, jnp.maximum(i - 1, 0)], start, i)


def fwd_kernel(seg_ref, pad_ref, pat_ref, h_ref, wq_ref, wk_ref, wv_ref,
               o_hbm, ot_hbm, qa_hbm, ka_hbm, va_hbm, kt_hbm,
               o_ref, ot_ref, qa_ref, ka_ref, va_ref, kt_ref, vt_s, qe_s, m_s, acc_s, out_sem):
    col = lax.broadcasted_iota(jnp.int32, (FROWS, WIDE), 1) % HW
    row = lax.broadcasted_iota(jnp.int32, (FROWS, WIDE), 0)
    ones = jnp.where((col == 24) | (col == 25), 1.0, 0.0)
    kadd = ones + jnp.where((col == 26) & (row >= PATCHES), MASKED, 0.0)
    trow = lax.broadcasted_iota(jnp.int32, (WIDE, FROWS), 0) % HW
    vtadd = jnp.where(trow == 24, 1.0, 0.0)
    qadd = jnp.where(trow == 26, 1.0, 0.0)
    zpad = jnp.zeros((WIDE, FLANES - FROWS), BF16)
    r32 = lax.broadcasted_iota(jnp.int32, (HW, FLANES), 0)
    qe_s[...] = jnp.zeros(qe_s.shape, BF16)

    def project(f):
        hf = h_ref[frame_rows(f), :]
        qt = (dot_nt(wq_ref[...], hf) * QSCALE + qadd).astype(BF16)
        kr = (dot_nt(hf, wk_ref[...]) + kadd).astype(BF16)
        vr = (dot_nt(hf, wv_ref[...]) + ones).astype(BF16)
        kt = dot_nt(wk_ref[...], hf).astype(BF16)
        vt = (dot_nt(wv_ref[...], hf) + vtadd).astype(BF16)
        qt = jnp.concatenate([qt, zpad], axis=1)
        for h in HEADS:
            qe_s[f % 2, h, head_rows(h), :] = qt[head_rows(h)]
        ka_ref[frame_rows(f), :] = kr
        va_ref[frame_rows(f), :] = vr
        kt_ref[:, frame_lanes(f, FROWS)] = kt
        vt_s[:, frame_lanes(f, FROWS)] = vt

    def scores(i, j):
        kj = ka_ref[frame_rows(j), :]
        return [dot(kj, qe_s[i % 2, h]) for h in HEADS]

    def gathered(j, ps):
        return [dot(vt_s[head_rows(h), frame_lanes(j, FROWS)], ps[h]) for h in HEADS]

    def finalize(i):
        outs, augs = [], []
        for h in HEADS:
            a = acc_s[i % 2, h]
            l = a[24:25, :]
            outs.append(jnp.where(r32 < HEAD_DIM, a / l, 0.0))
            lse = -(m_s[i % 2, h] + jnp.log2(l))
            hi = lse.astype(BF16).astype(F32)
            aug = jnp.where(r32 == 24, hi, jnp.where(r32 == 25, lse - hi, 0.0))
            augs.append(qe_s[i % 2, h, head_rows(h), :].astype(F32) + aug)
        ot = jnp.concatenate(outs, axis=0)
        ot_ref[:, frame_lanes(i)] = ot.astype(BF16)
        qa_ref[:, frame_lanes(i)] = jnp.concatenate(augs, axis=0).astype(BF16)
        o_ref[frame_rows(i), :] = ot.T[:FROWS, :].astype(BF16)

    by_rows = [(o_ref, o_hbm, 0), (ka_ref, ka_hbm, 1), (va_ref, va_hbm, 2)]
    by_lanes = [(ot_ref, ot_hbm, 3), (qa_ref, qa_hbm, 4), (kt_ref, kt_hbm, 5)]

    def keep(f):
        for src, dst, n in by_rows:
            pltpu.make_async_copy(src.at[frame_rows(f), :], dst.at[frame_rows(f), :], out_sem.at[n]).start()
        for src, dst, n in by_lanes:
            pltpu.make_async_copy(src.at[:, frame_lanes(f)], dst.at[:, frame_lanes(f)], out_sem.at[n]).start()

    project(0)

    def queries(i, start):
        start = seg_start(seg_ref, i, start)
        finalize(jnp.maximum(i - 1, 0))
        ss = scores(i, i)
        mn = [jnp.max(ss[h], axis=0, keepdims=True) for h in HEADS]
        ps = [jnp.exp2(ss[h] - mn[h]).astype(BF16) for h in HEADS]
        pv = gathered(i, ps)
        for h in HEADS:
            acc_s[i % 2, h] = pv[h]
            m_s[i % 2, h] = mn[h]
        project(jnp.minimum(i + 1, FRAMES - 1))

        def keys(j, _):
            @pl.when((pat_ref[i, j] == 1) & (pad_ref[0, j] == 0))
            def _():
                ss = scores(i, j)
                mo = [m_s[i % 2, h] for h in HEADS]
                mn = [jnp.maximum(mo[h], jnp.max(ss[h], axis=0, keepdims=True)) for h in HEADS]
                ps = [jnp.exp2(ss[h] - mn[h]).astype(BF16) for h in HEADS]
                pv = gathered(j, ps)
                for h in HEADS:
                    acc_s[i % 2, h] = acc_s[i % 2, h] * jnp.exp2(mo[h] - mn[h]) + pv[h]
                    m_s[i % 2, h] = mn[h]
            return 0
        lax.fori_loop(start, i, keys, 0)

        @pl.when(i > 0)
        def _():
            keep(i - 1)
        return start
    lax.fori_loop(0, FRAMES, queries, 0)
    finalize(FRAMES - 1)
    keep(FRAMES - 1)
    for src, dst, n in by_rows + by_lanes:
        pltpu.make_async_copy(src, dst, out_sem.at[n]).wait()


SMEM = pl.BlockSpec(memory_space=pltpu.SMEM)
HBM = pl.BlockSpec(memory_space=pltpu.HBM)


def in_hbm(value):
    return pltpu.with_memory_space_constraint(value, pltpu.HBM)
VM = pl.BlockSpec(memory_space=pltpu.VMEM)


def attn_fwd(seg, pad, pat, h, wqt, wkt, wvt):
    sd = jax.ShapeDtypeStruct
    V = pltpu.VMEM
    rows, lanes = sd((FRAMES * FROWS, WIDE), BF16), sd((WIDE, FRAMES * FLANES), BF16)
    return pl.pallas_call(
        fwd_kernel,
        out_shape=tuple(pltpu.HBM(a.shape, BF16) for a in (rows, lanes, lanes, rows, rows, lanes)),
        in_specs=[SMEM] * 3 + [VM] * 4,
        out_specs=(HBM,) * 6,
        scratch_shapes=[V(a.shape, BF16) for a in (rows, lanes, lanes, rows, rows, lanes)] + [V((WIDE, FRAMES * FLANES), BF16), V((2, HEADS_LOCAL, WIDE, FLANES), BF16),
                        V((2, HEADS_LOCAL, 1, FLANES), F32), V((2, HEADS_LOCAL, HW, FLANES), F32),
                        pltpu.SemaphoreType.DMA((6,))],
        compiler_params=pltpu.CompilerParams(vmem_limit_bytes=18 << 20),
        cost_estimate=pl.CostEstimate(flops=int(3e10), bytes_accessed=8 << 20, transcendentals=0),
        name="attend_forward",
    )(seg, pad, pat, h, wqt, wkt, wvt)


def bwd_kernel(seg_ref, pad_ref, pat_ref, qa_ref, ka_ref, va_ref, kt_ref, ot_ref, do_ref, h_ref, wq_ref, wk_ref, wv_ref,
               dh_ref, early_ref, qe_s, oe_s, qr_s, or_s, dq_s, dk_s, dv_s, dw_s, turn_s, blk_s, start_s):
    scale = HEAD_DIM ** -0.5
    for s in (qe_s, oe_s, qr_s, or_s):
        s[...] = jnp.zeros(s.shape, BF16)
    dk_s[...] = jnp.zeros(dk_s.shape, F32)
    dv_s[...] = jnp.zeros(dv_s.shape, F32)
    dq_s[...] = jnp.zeros(dq_s.shape, F32)
    dw_s[...] = jnp.zeros(dw_s.shape, F32)
    qrow = lax.broadcasted_iota(jnp.int32, (WIDE, FLANES), 0) % HW
    qcol = lax.broadcasted_iota(jnp.int32, (FROWS, WIDE), 1)
    r32 = lax.broadcasted_iota(jnp.int32, (HW, FLANES), 0)
    zpad = jnp.zeros((WIDE, FLANES - FROWS), F32)

    def starts(i, start):
        start_s[i] = seg_start(seg_ref, i, start)
        return start_s[i]
    lax.fori_loop(0, FRAMES, starts, 0)

    def prepare(i):
        t = i % 2
        qt = qa_ref[:, frame_lanes(i)]
        dor = do_ref[frame_rows(i), :].astype(F32)
        dot_ = jnp.concatenate([dor.T, zpad], axis=1)
        prod = dot_ * ot_ref[:, frame_lanes(i)].astype(F32)
        qrows = qt.astype(F32).T[:FROWS, :]
        for h in HEADS:
            d = -jnp.sum(prod[head_rows(h)], axis=0, keepdims=True)
            hi = d.astype(BF16).astype(F32)
            aug = jnp.where(r32 == 24, hi, jnp.where(r32 == 25, d - hi, 0.0))
            qe_s[t, h, head_rows(h), :] = qt[head_rows(h)]
            oe_s[t, h, head_rows(h), :] = (dot_[head_rows(h)] + aug).astype(BF16)
            mine = ((qcol // HW) == h) & (qcol % HW < HEAD_DIM)
            qr_s[t, h * FLANES:h * FLANES + FROWS, :] = jnp.where(mine, qrows, 0.0).astype(BF16)
            or_s[t, h * FLANES:h * FLANES + FROWS, :] = jnp.where(mine, dor, 0.0).astype(BF16)

    def pair(i, j):
        t = i % 2
        kj = ka_ref[frame_rows(j), :]
        vj = va_ref[frame_rows(j), :]
        ss = [dot(kj, qe_s[t, h]) for h in HEADS]
        dps = [dot(vj, oe_s[t, h]) for h in HEADS]
        ps = [jnp.exp2(ss[h]) for h in HEADS]
        ds = [(ps[h] * dps[h]).astype(BF16) for h in HEADS]
        pb = [ps[h].astype(BF16) for h in HEADS]
        dq = [dot(kt_ref[head_rows(h), frame_lanes(j, FROWS)], ds[h]) for h in HEADS]
        dv = dot(jnp.concatenate(pb, axis=1), or_s[t])
        dk = dot(jnp.concatenate(ds, axis=1), qr_s[t])
        dv_s[frame_rows(j), :] += dv
        dk_s[frame_rows(j), :] += dk
        return jnp.concatenate(dq, axis=0)

    def finish(f):
        dqt = jnp.where(qrow < HEAD_DIM, dq_s[f % 2] * scale, 0.0).astype(BF16)[:, :FROWS]
        dk = (dk_s[frame_rows(f), :] * math.log(2.0)).astype(BF16)
        dv = dv_s[frame_rows(f), :].astype(BF16)
        hf = h_ref[frame_rows(f), :]
        dh_ref[frame_rows(f), :] = (dot_tn(dqt, wq_ref[...]) + dot(dk, wk_ref[...]) + dot(dv, wv_ref[...])).astype(BF16)
        return dot(dqt, hf), dot_tn(dk, hf), dot_tn(dv, hf)

    prepare(FRAMES - 1)

    def queries(n, _):
        i = FRAMES - 1 - n
        above = jnp.minimum(i + 1, FRAMES - 1)
        dw = finish(above)
        dq_s[i % 2] = pair(i, i)
        for b in range(3):
            dw_s[b] += jnp.where(n > 0, dw[b], 0.0)
        prepare(jnp.maximum(i - 1, 0))

        def keys(j, _):
            @pl.when((pat_ref[i, j] == 1) & (pad_ref[0, j] == 0))
            def _():
                dq_s[i % 2] += pair(i, j)
            return 0
        lax.fori_loop(start_s[i], i, keys, 0)
        return 0
    lax.fori_loop(0, FRAMES, queries, 0)
    dw = finish(0)
    for b in range(3):
        turned = (dw_s[b] + dw[b]).T
        turn_s[:, 0:96] = jnp.concatenate([turned[:, HW * h:HW * h + HEAD_DIM] for h in HEADS], axis=1)
        line = [turn_s[pl.ds(k, 96, stride=4), :][:, 0:96] for k in range(4)]
        blk_s[pl.ds(0, 96, stride=3), :] = jnp.concatenate([line[0], line[1][:, :32]], axis=1)
        blk_s[pl.ds(1, 96, stride=3), :] = jnp.concatenate([line[1][:, 32:], line[2][:, :64]], axis=1)
        blk_s[pl.ds(2, 96, stride=3), :] = jnp.concatenate([line[2][:, 64:], line[3]], axis=1)
        early_ref[288 * b:288 * (b + 1), :] = blk_s[...].astype(BF16)


def attn_bwd(seg, pad, pat, qa, ka, va, kt, ot, do, h, wqt, wkt, wvt):
    sd = jax.ShapeDtypeStruct
    V = pltpu.VMEM
    return pl.pallas_call(
        bwd_kernel,
        out_shape=(sd((FRAMES * FROWS, D), BF16), sd((3 * 288, 128), BF16)),
        in_specs=[SMEM] * 3 + [VM] * 10,
        out_specs=(VM,) * 2,
        scratch_shapes=[V((2, HEADS_LOCAL, WIDE, FLANES), BF16), V((2, HEADS_LOCAL, WIDE, FLANES), BF16),
                        V((2, HEADS_LOCAL * FLANES, WIDE), BF16), V((2, HEADS_LOCAL * FLANES, WIDE), BF16),
                        V((2, WIDE, FLANES), F32), V((FRAMES * FROWS, WIDE), F32), V((FRAMES * FROWS, WIDE), F32),
                        V((3, WIDE, D), F32), V((D, 128), F32), V((288, 128), F32), pltpu.SMEM((FRAMES,), jnp.int32)],
        compiler_params=pltpu.CompilerParams(vmem_limit_bytes=26 << 20),
        cost_estimate=pl.CostEstimate(flops=int(5e10), bytes_accessed=12 << 20, transcendentals=0),
        name="attend_backward",
    )(seg, pad, pat, qa, ka, va, kt, ot, do, h, wqt, wkt, wvt)


MESH = pl.DeviceIdType.MESH
OWN_ROWS = 4 * FROWS


def place(d, m):
    return {"dp": d, "mp": m}


def remote(src, dst, send_sem, recv_sem, device):
    return pltpu.make_async_remote_copy(
        src_ref=src, dst_ref=dst, send_sem=send_sem, recv_sem=recv_sem, device_id=device, device_id_type=MESH
    )


def local(src, dst, sem):
    return pltpu.make_async_copy(src, dst, sem)


def greet(devices):
    barrier = pltpu.get_barrier_semaphore()
    for device in devices:
        pl.semaphore_signal(barrier, inc=1, device_id=device, device_id_type=MESH)
    pl.semaphore_wait(barrier, len(devices))


def group_peers():
    me = lax.axis_index("mp")
    return me, me ^ 1, me ^ 2, me ^ 3


def frame_part(device, c):
    return pl.ds(pl.multiple_of(device * OWN_ROWS + c * FROWS, 16), FROWS)


def normalised(v):
    centred = v - jnp.mean(v, axis=-1, keepdims=True)
    inv = lax.rsqrt(jnp.mean(centred * centred, axis=-1, keepdims=True) + NORM_EPS)
    return centred * inv, inv


def norm_pull(dy, hat, inv, gain):
    dg = dy * gain
    lead = jnp.mean(dg, axis=-1, keepdims=True)
    along = jnp.mean(dg * hat, axis=-1, keepdims=True)
    return inv * (dg - lead - hat * along)


def col_sum(v):
    return jnp.sum(v, axis=0, keepdims=True)


def load_frame(ref, c):
    base = c * PATCHES // 16 * 16
    rows = ref[base:base + FROWS, :].astype(F32)
    shift = c * PATCHES - base
    return pltpu.roll(rows, FROWS - shift, 0) if shift else rows


def live_rows():
    return lax.broadcasted_iota(jnp.int32, (FROWS, 1), 0) < PATCHES


def dp_peers(count):
    d = lax.axis_index("dp")
    side, line = d % 2, d // 2
    return side, line, {"dp": d ^ 1}, [lax.rem(line + n, count) for n in range(count)]


def start_kernel(count, x_hbm, np_ref, w_hbm, m_hbm, v_hbm, h_ref, wq_ref, wk_ref, wv_ref, ws_ref, ma_ref, mb_ref,
                 x_ref, w_ref, m_ref, v_ref, mo_s, w_s, load_x, load_w, keep_m,
                 send_x, recv_x, send_p, recv_p, send_f, recv_f, send_t, recv_t, send_l, recv_l):
    me, near, far, _ = group_peers()
    side, line, twin, around = dp_peers(count)
    frames = range(OWN_ROWS // FROWS)
    cuts = [0, 208, 400, 592, 784]
    loads = [local(x_hbm.at[a:b, :], x_ref.at[a:b, :], load_x.at[c]) for c, (a, b) in enumerate(zip(cuts, cuts[1:]))]
    others = [local(m_hbm, m_ref, load_w.at[0]), local(v_hbm, v_ref, load_w.at[1]), local(w_hbm, w_ref, load_w.at[2])]
    for copy in loads + others:
        copy.start()
    greet([{"mp": near}, {"mp": far}, twin] + [{"dp": q * 2 + side} for q in around[1:]])
    live = live_rows()
    to_far, to_near, moments = [], [], []
    for c in frames:
        loads[c].wait()
        hat, _ = normalised(load_frame(x_ref, c))
        h_ref[frame_part(me, c), :] = jnp.where(live, hat * np_ref[0:1, :] + np_ref[1:2, :], 0.0).astype(BF16)
        rows = h_ref.at[frame_part(me, c), :]
        to_far.append(remote(rows, rows, send_x.at[c], recv_x.at[c], {"mp": far}))
        to_near.append(remote(rows, rows, send_p.at[c], recv_p.at[c], {"mp": near}))
        to_far[c].start()
        to_near[c].start()

    slots, rows = m_ref.shape[0], m_ref.shape[1]
    others[0].wait()
    others[1].wait()
    for r in range(2 * slots):
        mo_s[r // slots, pl.ds((r % slots) * rows, rows), :] = (v_ref if r % 2 else m_ref)[r // 2].astype(BF16)
    first, second = ma_ref.at[side, line], mb_ref.at[side]
    kept = [local(mo_s.at[0], first, keep_m.at[0]), local(mo_s.at[1], second, keep_m.at[1])]
    for n, q in enumerate(around[1:]):
        moments.append(remote(mo_s.at[0], first, send_l.at[n], recv_l.at[n], {"dp": q * 2 + side}))
    moments.append(remote(mo_s.at[0], first, send_t.at[0], recv_t.at[0], twin))
    moments.append(remote(mo_s.at[1], second, send_t.at[1], recv_t.at[1], twin))
    for copy in moments + kept:
        copy.start()

    def incoming(device, sends, recvs, c):
        rows = h_ref.at[frame_part(device, c), :]
        return remote(rows, rows, sends.at[c], recvs.at[c], {"mp": near})

    def forward(c):
        incoming(far, send_x, recv_x, c).wait_recv()
        copy = incoming(far, send_f, recv_f, c)
        copy.start()
        return copy

    others[2].wait()
    for b, out in enumerate((wq_ref, wk_ref, wv_ref)):
        a = [w_ref[b, pl.ds(k, 96, stride=3), :] for k in range(3)]
        lines = [a[0][:, :96], jnp.concatenate([a[0][:, 96:], a[1][:, :64]], axis=1),
                 jnp.concatenate([a[1][:, 64:], a[2][:, :32]], axis=1), a[2][:, 32:]]
        gap = jnp.zeros((96, HW - HEAD_DIM), F32)
        for k in range(4):
            parts = []
            for h in HEADS:
                parts += [lines[k][:, HEAD_DIM * h:HEAD_DIM * (h + 1)], gap]
            w_s[pl.ds(k, 96, stride=4), :] = jnp.concatenate(parts, axis=1)
        out[...] = w_s[...].T.astype(BF16)
    copies = [forward(0)]
    for b in range(3, w_ref.shape[0]):
        for k in range(3):
            lanes = slice(128 * k, 128 * (k + 1))
            part = w_ref[b, pl.ds(k, 96, stride=3), :]
            if b == 3:
                gap = jnp.zeros((HW - HEAD_DIM, 128), F32)
                parts = []
                for h in HEADS:
                    parts += [part[HEAD_DIM * h:HEAD_DIM * (h + 1)], gap]
                ws_ref[2 * D:2 * D + WIDE, lanes] = jnp.concatenate(parts, axis=0).astype(BF16)
            else:
                ws_ref[96 * (b - 4):96 * (b - 3), lanes] = part.astype(BF16)
    for c in frames[1:]:
        copies.append(forward(c))
    for c in frames:
        incoming(near, send_p, recv_p, c).wait_recv()
        incoming(near ^ 2, send_f, recv_f, c).wait_recv()
    for n in range(1, count):
        part = ma_ref.at[side, around[count - n]]
        remote(part, part, send_l.at[n - 1], recv_l.at[n - 1], twin).wait_recv()
    part = ma_ref.at[1 - side, line]
    remote(part, part, send_t.at[0], recv_t.at[0], twin).wait_recv()
    part = mb_ref.at[1 - side]
    remote(part, part, send_t.at[1], recv_t.at[1], twin).wait_recv()
    for copy in kept:
        copy.wait()
    for copy in to_far + to_near + copies + moments:
        copy.wait_send()


def start_call(dp, x, norm_params, weights, first_moments, second_moments):
    sd, V, S = jax.ShapeDtypeStruct, pltpu.VMEM, pltpu.SemaphoreType.DMA
    blocks, count = weights.shape[0], dp // 2
    half = first_moments.shape[0] * first_moments.shape[1]
    turned = sd((WIDE, D), BF16)
    return pl.pallas_call(
        functools.partial(start_kernel, count),
        out_shape=(sd((FRAMES * FROWS, D), BF16), turned, turned, turned, sd((WIDE + 96 * (blocks - 4), D), BF16),
                   pltpu.HBM((2, count, half, 128), BF16), pltpu.HBM((2, half, 128), BF16)),
        in_specs=[HBM, VM, HBM, HBM, HBM],
        out_specs=(VM,) * 5 + (HBM,) * 2,
        scratch_shapes=[V(x.shape, BF16), V(weights.shape, F32), V(first_moments.shape, F32), V(first_moments.shape, F32),
                        V((2, half, 128), BF16), V((D, WIDE), F32), S((4,)), S((3,)), S((2,))] + [S((4,))] * 6 + [S((2,))] * 2 + [S((count,))] * 2,
        compiler_params=pltpu.CompilerParams(vmem_limit_bytes=16 << 20, collective_id=1, has_side_effects=True),
        name="norm_and_gather",
    )(in_hbm(x), norm_params, in_hbm(weights), in_hbm(first_moments), in_hbm(second_moments))


def gelu_parts(u):
    lead = math.sqrt(2.0 / math.pi)
    bend = lead * 0.044715
    square = u * u
    half = 0.5 + 0.5 * jnp.tanh(u * (lead + bend * square))
    slope = half + 2.0 * u * (half - half * half) * (lead + 3.0 * bend * square)
    return u * half, slope


def middle_kernel(count, o_ref, x_hbm, ct_hbm, keep_ref, w0_ref, w1_ref, w2_ref, w3_ref, np_ref, ma_ref, mb_ref,
                  out_ref, dx2_ref, do_ref, l0_ref, l1_ref, l2_ref, l3_ref, nb_ref, mom_ref,
                  ob_s, dob_s, g_s, a_s, du_s, da_s, h2_s, dxa_s, blk_s, res_s, ut_s, wot_s,
                  x_ref, ct_ref, o_s, load_s, keep_s,
                  send_o, recv_o, send_d, recv_d, send_t, recv_t, send_l, recv_l, send_f, recv_f):
    me, near, far, across = group_peers()
    side, line, twin, around = dp_peers(count)
    peers = (far, across, near)
    mine = pl.ds(pl.multiple_of(me * OWN_ROWS, 16), OWN_ROWS)
    loads = [local(ct_hbm, ct_ref, load_s.at[0]), local(x_hbm, x_ref, load_s.at[1]), local(o_ref.at[mine, :], o_s, load_s.at[2])]
    kept = [local(ma_ref.at[side], mom_ref.at[0, side], keep_s.at[0]),
            local(ma_ref.at[1 - side, line], mom_ref.at[0, 1 - side, line], keep_s.at[1]),
            local(mb_ref.at[side], mom_ref.at[1, side, line], keep_s.at[2]),
            local(mb_ref.at[1 - side], mom_ref.at[1, 1 - side, line], keep_s.at[3])]
    for copy in loads + kept:
        copy.start()
    greet([{"mp": p} for p in peers] + [twin] + [{"dp": q * 2 + side} for q in around[1:]])
    frames = range(OWN_ROWS // FROWS)
    live = live_rows()
    shards_w = (w0_ref, w1_ref, w2_ref, w3_ref)
    late = (l0_ref, l1_ref, l2_ref, l3_ref)
    places = range(len(shards_w))
    outgoing = []
    for c in frames:
        for n, p in enumerate(peers):
            outgoing.append(remote(o_ref.at[frame_part(p, c), :], ob_s.at[n, pl.ds(c * FROWS, FROWS), :],
                                   send_o.at[n, c], recv_o.at[n, c], {"mp": p}))
            outgoing[-1].start()
    moments = []
    for n, q in enumerate(around[1:]):
        own_half = mb_ref.at[side]
        moments.append(remote(own_half, mom_ref.at[1, side, line], send_l.at[n], recv_l.at[n], {"dp": q * 2 + side}))
        moments.append(remote(ma_ref.at[side, q], mom_ref.at[0, side, q], send_t.at[q], recv_t.at[q], twin))
    for copy in moments:
        copy.start()

    def pass_moments(n):
        q = around[count - n]
        part = mom_ref.at[1, side, q]
        remote(part, part, send_l.at[n - 1], recv_l.at[n - 1], twin).wait_recv()
        moments.append(remote(part, part, send_f.at[q], recv_f.at[q], twin))
        moments[-1].start()

    def w_up(m):
        return shards_w[m][0:D, :]

    def w_down(m):
        return shards_w[m][D:2 * D, :]

    def w_o(m):
        return shards_w[m][2 * D:2 * D + WIDE, :]

    def cols(m):
        return slice(m * D, (m + 1) * D)

    loads[0].wait()
    for c in frames:
        rows = slice(c * FROWS, (c + 1) * FROWS)
        g_s[rows, :] = jnp.where(live, load_frame(ct_ref, c) * keep_ref[0, c], 0.0).astype(BF16)
    for m in places:
        da_s[:, cols(m)] = dot_nt(g_s[...], w_down(m))
    for m in places:
        ut_s[cols(m), :] = w_up(m).astype(F32).T.astype(BF16)
        wot_s[:, m * WIDE:(m + 1) * WIDE] = w_o(m).astype(F32).T.astype(BF16)
    loads[1].wait()
    loads[2].wait()
    nb_ref[...] = jnp.zeros(nb_ref.shape, F32)
    down = jnp.concatenate([w_down(m) for m in places], axis=0)
    out_w = jnp.concatenate([w_o(m) for m in places], axis=0)
    sent = []
    for pair in range(len(frames) // 2):
        both = (2 * pair, 2 * pair + 1)
        rows = slice(2 * pair * FROWS, 2 * (pair + 1) * FROWS)
        for c in both:
            for n, p in enumerate(peers):
                part = ob_s.at[n, pl.ds(c * FROWS, FROWS), :]
                remote(part, part, send_o.at[n, c], recv_o.at[n, c], {"mp": p}).wait_recv()
        own_rows = pl.ds(pl.multiple_of(me * OWN_ROWS + 2 * pair * FROWS, 16), 2 * FROWS)
        heads = jnp.concatenate([o_s[rows, :]] + [ob_s[n, rows, :] for n in range(len(peers))], axis=1)
        x2 = jnp.concatenate([load_frame(x_ref, c) for c in both], axis=0) + dot(heads, out_w)
        x2 = jnp.where(jnp.concatenate([live, live], axis=0), x2, 0.0)
        hat, inv = normalised(x2)
        h2 = (hat * np_ref[2:3, :] + np_ref[3:4, :]).astype(BF16)
        h2_s[rows, :] = h2
        for m in places:
            value, slope = gelu_parts(dot(h2, w_up(m)))
            a_s[rows, cols(m)] = value.astype(BF16)
            du_s[rows, cols(m)] = (da_s[rows, cols(m)] * slope).astype(BF16)
        result = x2 + dot(a_s[rows, :], down)
        for k, c in enumerate(both):
            res_s[pl.ds(c * PATCHES, FROWS), :] = result[k * FROWS:(k + 1) * FROWS]
        dh2 = dot(du_s[rows, :], ut_s[...])
        nb_ref[0:1, :] += col_sum(dh2 * hat)
        nb_ref[1:2, :] += col_sum(dh2)
        dx2 = g_s[rows, :].astype(F32) + norm_pull(dh2, hat, inv, np_ref[2:3, :])
        dx2_ref[rows, :] = dx2
        dxa = dx2.astype(BF16)
        dxa_s[rows, :] = dxa
        d_heads = dot(dxa, wot_s[...]).astype(BF16)
        for n in range(len(peers)):
            dob_s[n, rows, :] = d_heads[:, (n + 1) * WIDE:(n + 2) * WIDE]
        for c in both:
            for n, p in enumerate(peers):
                sent.append(remote(dob_s.at[n, pl.ds(c * FROWS, FROWS), :], do_ref.at[frame_part(me, c), :],
                                   send_d.at[n, c], recv_d.at[n, c], {"mp": p}))
                sent[-1].start()
        do_ref[own_rows, :] = d_heads[:, 0:WIDE]
        for c in both:
            if 0 < c < count:
                pass_moments(c)
    for n in range(len(frames), count):
        pass_moments(n)
    out_ref[...] = res_s[0:out_ref.shape[0], :].astype(BF16)

    def as_block(shard, first, value):
        size = value.shape[0]
        for k in range(3):
            blk_s[pl.ds(k, size, stride=3), :] = value[:, 128 * k:128 * (k + 1)]
        late[shard][first * 288:first * 288 + 3 * size, :] = blk_s[0:3 * size, :].astype(BF16)

    def drop_gaps(value):
        return jnp.concatenate([value[HW * h:HW * h + HEAD_DIM] for h in HEADS], axis=0)

    dw1 = dot_tn(h2_s[...], du_s[...])
    dw2 = dot_tn(g_s[...], a_s[...])
    for m in places:
        as_block(m, 1, dw1[:, cols(m)])
        as_block(m, 5, dw2[:, cols(m)].T)
        o_m = o_s[...] if m == 0 else ob_s[m - 1]
        as_block(m, 0, drop_gaps(dot_tn(o_m, dxa_s[...])))
    for c in frames:
        for n, p in enumerate(peers):
            part = do_ref.at[frame_part(p, c), :]
            remote(part, part, send_d.at[n, c], recv_d.at[n, c], {"mp": p}).wait_recv()
    for q in around[1:]:
        for half, sends, recvs in ((0, send_t, recv_t), (1, send_f, recv_f)):
            part = mom_ref.at[half, 1 - side, q]
            remote(part, part, sends.at[q], recvs.at[q], twin).wait_recv()
    for copy in kept:
        copy.wait()
    for copy in outgoing + sent + moments:
        copy.wait_send()


def middle_call(dp, o, x, ct, keep, w, norm_params, ma, mb):
    sd = jax.ShapeDtypeStruct
    V, S = pltpu.VMEM, pltpu.SemaphoreType.DMA
    count = dp // 2
    late = sd((9 * 288, 128), BF16)
    return pl.pallas_call(
        functools.partial(middle_kernel, count),
        out_shape=(sd(x.shape, BF16), sd((OWN_ROWS, D), F32), sd((FRAMES * FROWS, WIDE), BF16),
                   late, late, late, late, sd((2, D), F32), pltpu.HBM((2,) + ma.shape, BF16)),
        in_specs=[HBM, HBM, HBM, SMEM] + [VM] * 5 + [HBM] * 2,
        out_specs=(VM,) * 8 + (HBM,),
        scratch_shapes=[V((3, OWN_ROWS, WIDE), BF16), V((3, OWN_ROWS, WIDE), BF16), V((OWN_ROWS, D), BF16),
                        V((OWN_ROWS, FF), BF16), V((OWN_ROWS, FF), BF16), V((OWN_ROWS, FF), F32),
                        V((OWN_ROWS, D), BF16), V((OWN_ROWS, D), BF16), V((1152, 128), F32), V((OWN_ROWS, D), F32),
                        V((FF, D), BF16), V((D, 4 * WIDE), BF16),
                        V(x.shape, BF16), V(x.shape, BF16), V((OWN_ROWS, WIDE), BF16), S((3,)), S((4,)), S((3, 4)), S((3, 4)), S((3, 4)), S((3, 4))] + [S((count,))] * 6,
        compiler_params=pltpu.CompilerParams(vmem_limit_bytes=36 << 20, collective_id=2, has_side_effects=True),
        cost_estimate=pl.CostEstimate(flops=int(6e9), bytes_accessed=12 << 20, transcendentals=0),
        name="feed_forward",
    )(in_hbm(o), in_hbm(x), in_hbm(ct), keep, *w, norm_params, in_hbm(ma), in_hbm(mb))


def reduce_kernel(dp, piece, dh_ref, early_ref, l0_ref, l1_ref, l2_ref, l3_ref, x_ref, dx2_ref, np_ref, nb_ref,
                  gin_ref, gs_ref, tot_ref,
                  res_s, pb_s, xs_s, xb_s, g_s, yb_s, zs_s, zb_s, msg_s, mb_s, dm_s, db_s,
                  send_p, recv_p, send_x, recv_x, send_y, recv_y, send_z, recv_z,
                  send_a, recv_a, send_w, recv_w, send_m, recv_m, send_n, recv_n):
    me, near, far, across = group_peers()
    d = lax.axis_index("dp")
    count = dp // 2
    side, line = d % 2, d // 2
    twin = {"dp": d ^ 1}

    def on_line(n):
        return lax.rem(line + n, count)

    def line_device(q):
        return {"dp": q * 2 + side}

    frames = range(OWN_ROWS // FROWS)
    others = [{"mp": near}, {"mp": far}, {"mp": across}] + [{"dp": lax.rem(d + n, dp)} for n in range(1, dp)]
    greet(others)

    def own(c):
        return pl.ds(c * FROWS, FROWS)

    to_near = []
    for k, target in ((1, across), (0, near)):
        for c in frames:
            to_near.append(remote(dh_ref.at[frame_part(target, c), :], pb_s.at[k, own(c), :],
                                  send_p.at[k, c], recv_p.at[k, c], {"mp": near}))
            to_near[-1].start()

    total = early_ref.shape[0] + l0_ref.shape[0]
    g_s[0:early_ref.shape[0], :] = early_ref[...]
    g_s[early_ref.shape[0]:total, :] = (l0_ref[...].astype(F32) + l1_ref[...].astype(F32)
                                        + (l2_ref[...].astype(F32) + l3_ref[...].astype(F32))).astype(BF16)
    if g_s.shape[0] > total:
        g_s[total:, :] = jnp.zeros((g_s.shape[0] - total, 128), BF16)

    def at(s, q):
        return pl.ds(pl.multiple_of((s * count + q) * piece, 16), piece)

    to_twin = []
    for n in range(count):
        q = on_line(n + 1)
        to_twin.append(remote(g_s.at[at(1 - side, q), :], yb_s.at[q], send_y.at[q], recv_y.at[q], twin))
        to_twin[-1].start()

    to_far = []
    for c in frames:
        remote(pb_s.at[1, own(c), :], pb_s.at[1, own(c), :], send_p.at[1, c], recv_p.at[1, c], {"mp": near}).wait_recv()
        xs_s[own(c), :] = (dh_ref[frame_part(far, c), :].astype(F32) + pb_s[1, own(c), :].astype(F32)).astype(BF16)
        to_far.append(remote(xs_s.at[own(c), :], xb_s.at[own(c), :], send_x.at[c], recv_x.at[c], {"mp": far}))
        to_far[-1].start()

    to_line = []
    for n in range(count):
        q = on_line(n + 1)
        remote(yb_s.at[q], yb_s.at[q], send_y.at[q], recv_y.at[q], twin).wait_recv()
        zs_s[q] = (g_s[at(side, q), :].astype(F32) + yb_s[q].astype(F32)).astype(BF16)
        if n < count - 1:
            to_line.append(remote(zs_s.at[q], zb_s.at[line], send_z.at[q], recv_z.at[line], line_device(q)))
            to_line[-1].start()
    mine = zs_s[line].astype(F32)
    for n in range(1, count):
        q = on_line(n)
        remote(zb_s.at[q], zb_s.at[q], send_z.at[q], recv_z.at[q], line_device(q)).wait_recv()
        mine = mine + zb_s[q].astype(F32)
    mine = mine.astype(BF16)
    gs_ref[at(side, line), :] = mine
    whole = gs_ref.at[at(side, line), :]
    spread = []
    for n in range(1, count):
        q = on_line(n)
        spread.append(remote(whole, whole, send_a.at[q], recv_a.at[line], line_device(q)))
        spread[-1].start()
    passed = [remote(whole, whole, send_w.at[line], recv_w.at[line], twin)]
    passed[0].start()
    mine = mine.astype(F32)
    squares = jnp.sum(mine * mine, axis=0, keepdims=True)

    live = live_rows()
    gain, bias = jnp.zeros((1, D), F32), jnp.zeros((1, D), F32)
    for c in frames:
        remote(pb_s.at[0, own(c), :], pb_s.at[0, own(c), :], send_p.at[0, c], recv_p.at[0, c], {"mp": near}).wait_recv()
        remote(xb_s.at[own(c), :], xb_s.at[own(c), :], send_x.at[c], recv_x.at[c], {"mp": far}).wait_recv()
        dy = dh_ref[frame_part(me, c), :].astype(F32) + pb_s[0, own(c), :].astype(F32) + xb_s[own(c), :].astype(F32)
        dy = jnp.where(live, dy, 0.0)
        hat, inv = normalised(load_frame(x_ref, c))
        gain = gain + col_sum(dy * hat)
        bias = bias + col_sum(dy)
        res_s[pl.ds(c * PATCHES, FROWS), :] = dx2_ref[own(c), :] + norm_pull(dy, hat, inv, np_ref[0:1, :])
    gin_ref[...] = res_s[0:gin_ref.shape[0], :].astype(BF16)

    msg_s[...] = jnp.zeros(msg_s.shape, F32)
    msg_s[0:1, :] = gain
    msg_s[1:2, :] = bias
    msg_s[2:4, :] = nb_ref[...]
    msg_s[4:5, 0:128] = squares
    small = []
    for n, p in enumerate((near, far, across)):
        small.append(remote(msg_s, mb_s.at[n], send_m.at[n], recv_m.at[n], {"mp": p}))
        small[-1].start()

    def pass_on(n):
        q = on_line(n)
        piece_at = gs_ref.at[at(side, q), :]
        remote(piece_at, piece_at, send_a.at[q], recv_a.at[q], line_device(q)).wait_recv()
        passed.append(remote(piece_at, piece_at, send_w.at[q], recv_w.at[q], twin))
        passed[-1].start()

    pass_on(1)
    add = msg_s[...]
    for n, p in enumerate((near, far, across)):
        remote(mb_s.at[n], mb_s.at[n], send_m.at[n], recv_m.at[n], {"mp": p}).wait_recv()
        add = add + mb_s[n]
    dm_s[...] = add
    for n in range(1, dp):
        small.append(remote(dm_s, db_s.at[n], send_n.at[n], recv_n.at[n], {"dp": lax.rem(d + n, dp)}))
        small[-1].start()
    for n in range(2, count):
        pass_on(n)
    for n in range(1, dp):
        remote(db_s.at[n], db_s.at[n], send_n.at[n], recv_n.at[n], {"dp": lax.rem(d + dp - n, dp)}).wait_recv()
        add = add + db_s[n]
    tot_ref[...] = add
    for n in range(count):
        q = on_line(n)
        piece_at = gs_ref.at[at(1 - side, q), :]
        remote(piece_at, piece_at, send_w.at[q], recv_w.at[q], twin).wait_recv()
    for copy in to_near + to_twin + to_far + to_line + spread + passed + small:
        copy.wait_send()


def reduce_call(dp, dh, early, late, x, dx2, norm_params, nb):
    sd = jax.ShapeDtypeStruct
    V, S = pltpu.VMEM, pltpu.SemaphoreType.DMA
    rows = early.shape[0] + late[0].shape[0]
    count = dp // 2
    piece = -(-rows // (2 * count * 16)) * 16
    held = 2 * count * piece
    return pl.pallas_call(
        functools.partial(reduce_kernel, dp, piece),
        out_shape=(sd(x.shape, BF16), sd((held, 128), BF16), sd((8, D), F32)),
        in_specs=[VM] * 10,
        out_specs=(VM,) * 3,
        scratch_shapes=[V((OWN_ROWS, D), F32), V((2, OWN_ROWS, D), BF16), V((OWN_ROWS, D), BF16), V((OWN_ROWS, D), BF16), V((held, 128), BF16),
                        V((count, piece, 128), BF16), V((count, piece, 128), BF16), V((count, piece, 128), BF16),
                        V((8, D), F32), V((3, 8, D), F32), V((8, D), F32), V((dp, 8, D), F32),
                        S((2, 4)), S((2, 4)), S((4,)), S((4,)), S((count,)), S((count,)), S((count,)), S((count,)),
                        S((count,)), S((count,)), S((count,)), S((count,)), S((3,)), S((3,)), S((dp,)), S((dp,))],
        compiler_params=pltpu.CompilerParams(vmem_limit_bytes=22 << 20, collective_id=3, has_side_effects=True),
        name="reduce_gradients",
    )(dh, early, *late, x, dx2, norm_params, nb)


def update_kernel(slot_ref, dev_ref, res_ref, gin_ref, tot_ref, gs_ref, w_ref, m_ref, v_ref, mom_ref, np_ref, nm_ref, nv_ref,
                  out_ref, gout_ref, norm_ref, nw_ref, nf_ref, ns_ref, nn_ref, nnf_ref, nns_ref, sem_s):
    carried = [local(res_ref, out_ref, sem_s.at[0]), local(gin_ref, gout_ref, sem_s.at[1])]
    for copy in carried:
        copy.start()
    blocks, rows, _ = w_ref.shape
    slots = m_ref.shape[0]
    tot = tot_ref[...]
    grads = tot[0:4, :]
    norm = jnp.sqrt(jnp.sum(grads * grads, keepdims=True) + jnp.sum(tot[4:5, 0:128], keepdims=True))
    norm_ref[...] = norm
    clip_level = 0.5 * (4 * D * D + 2 * D * FF + 4 * D) ** 0.5
    factor = jnp.minimum(1.0, clip_level / norm)
    nn_ref[...], nnf_ref[...], nns_ref[...] = adam_update(
        np_ref[...], grads * factor, nm_ref[...], nv_ref[...], 0.0, NORM_RATE)

    def block(b):
        return gs_ref[pl.ds(pl.multiple_of(b * rows, 16), rows), :].astype(F32) * factor

    def step(b, _):
        holder, first = slot_ref[b] // slots, slot_ref[b] % slots * 2
        old = [mom_ref[r // slots, holder % 2, holder // 2, pl.ds(pl.multiple_of(r % slots * rows, 16), rows), :].astype(F32)
               for r in (first, first + 1)]
        nw_ref[b], _, _ = adam_update(w_ref[b], block(b), old[0], old[1], WEIGHT_DECAY, LEARN_RATE)
        return 0
    lax.fori_loop(0, blocks, step, 0)
    for s in range(slots):
        owned = jnp.int32(-1)
        for b in range(blocks):
            owned = jnp.where(slot_ref[b] == dev_ref[0] * slots + s, b, owned)
        _, first, second = adam_update(0.0, block(jnp.maximum(owned, 0)), m_ref[s], v_ref[s], 0.0, LEARN_RATE)
        nf_ref[s] = jnp.where(owned >= 0, first, m_ref[s])
        ns_ref[s] = jnp.where(owned >= 0, second, v_ref[s])
    for copy in carried:
        copy.wait()


def update_call(owner_slot, result, grad_in, tot, gs, weights, first, second, moments, norm_params, norm_first, norm_second):
    sd = jax.ShapeDtypeStruct
    small = sd((4, D), F32)
    device = lax.axis_index("dp").reshape(1)
    return pl.pallas_call(
        update_kernel,
        out_shape=(pltpu.HBM(result.shape, BF16), pltpu.HBM(result.shape, BF16), sd((1, 1), F32), sd(weights.shape, F32), sd(first.shape, F32), sd(first.shape, F32), small, small, small),
        in_specs=[SMEM] * 2 + [VM] * 11,
        out_specs=(HBM,) * 2 + (VM,) * 7,
        scratch_shapes=[pltpu.SemaphoreType.DMA((2,))],
        compiler_params=pltpu.CompilerParams(vmem_limit_bytes=16 << 20),
        name="clipped_update",
    )(owner_slot, device, result, grad_in, tot, gs, weights, first, second, moments, norm_params, norm_first, norm_second)


def adam_update(current, gradient, first_moment, second_moment, decay_rate, step_rate):
    first_new = BETA_ONE * first_moment + (1.0 - BETA_ONE) * gradient
    second_new = BETA_TWO * second_moment + (1.0 - BETA_TWO) * gradient * gradient
    first_fix = 1.0 - BETA_ONE**STEP
    second_fix = 1.0 - BETA_TWO**STEP
    direction = first_new / first_fix / (jnp.sqrt(second_new / second_fix) + ADAM_EPS)
    return (current - step_rate * (direction + decay_rate * current), first_new, second_new)


def from_peers(value):
    count = lax.axis_size("mp")
    return [value] + [lax.ppermute(value, "mp", [(i, i ^ n) for i in range(count)]) for n in (2, 3, 1)]


def shards(tokens, cotangent, segment_ids, padding, pattern, owner_slot, weights, first_moments, second_moments,
           norm_params, norm_first, norm_second):
    groups = lax.axis_size("mp")
    me = lax.axis_index("mp")
    frames_own = FRAMES // groups
    dp = lax.axis_size("dp")
    x, ct = tokens[0], cotangent[0]
    keep = 1.0 - lax.dynamic_slice_in_dim(padding, me * frames_own, frames_own, 1).astype(F32)
    h1, wq, wk, wv, own_shared, ma, mb = start_call(dp, x, norm_params, weights, first_moments, second_moments)
    shared = from_peers(own_shared)
    o, ot, qa, ka, va, kt = attn_fwd(segment_ids, padding, pattern, h1, wq, wk, wv)
    result, dx2, do, *late, nb, moments = middle_call(dp, o, x, ct, keep, shared, norm_params, ma, mb)
    count = lax.axis_size("mp")
    late = late[:1] + [lax.ppermute(late[n], "mp", [(i, i ^ p) for i in range(count)]) for n, p in ((1, 2), (2, 3), (3, 1))]
    dh, early = attn_bwd(segment_ids, padding, pattern, qa, ka, va, kt, ot, do, h1, wq, wk, wv)
    grad_in, gs, tot = reduce_call(dp, dh, early, late, x, dx2, norm_params, nb)
    result, grad_in, grad_norm, new_weights, new_first, new_second, new_norm, new_norm_first, new_norm_second = update_call(
        owner_slot, result, grad_in, tot, gs, weights, first_moments, second_moments, moments, norm_params, norm_first, norm_second)
    return (result[None], grad_in[None], grad_norm[0, 0], new_weights, new_first, new_second,
            new_norm, new_norm_first, new_norm_second)


def solution(mesh):
    rows, blocks, slots = P("dp", "mp", None), P(None, "mp", None), P("dp", "mp", None)
    return jax.shard_map(
        shards,
        mesh=mesh,
        in_specs=(rows, rows, P("dp", None), P("dp", None), P(), P(), blocks, slots, slots, P(), P(), P()),
        out_specs=(rows, rows, P(), blocks, slots, slots, P(), P(), P()),
        check_vma=False,
    )
```

```python
import functools
import math

import jax
import jax.numpy as jnp
from jax import lax
from jax.experimental import pallas as pl
from jax.experimental.pallas import tpu as pltpu
from jax.sharding import PartitionSpec as P

FF = 1536
STEP = 10
NORM_EPS = 1e-05
BETA_ONE = 0.9
BETA_TWO = 0.95
ADAM_EPS = 1e-08
LEARN_RATE = 0.15
NORM_RATE = 0.6
WEIGHT_DECAY = 0.05

D = 384
HEAD_DIM = 24
FRAMES = 16
PATCHES = 196
FROWS = 208
FLANES = 256
HW = 32
HEADS_LOCAL = 4
WIDE = HEADS_LOCAL * HW
MASKED = -1e30
QSCALE = math.log2(math.e) / math.sqrt(HEAD_DIM)
F32 = jnp.float32
BF16 = jnp.bfloat16
NT = (((1,), (1,)), ((), ()))
TN = (((0,), (0,)), ((), ()))
HEADS = range(HEADS_LOCAL)
UNROLL = 4
TOGETHER = 4


def dot(a, b):
    return jnp.dot(a, b, preferred_element_type=F32)


def dot_nt(a, b):
    return lax.dot_general(a, b, NT, preferred_element_type=F32)


def dot_tn(a, b):
    return lax.dot_general(a, b, TN, preferred_element_type=F32)


def frame_rows(f):
    return pl.ds(pl.multiple_of(f * FROWS, 16), FROWS)


def frame_lanes(f, size=FLANES):
    return pl.ds(pl.multiple_of(f * FLANES, 128), size)


def head_rows(h):
    return slice(HW * h, HW * (h + 1))


def head_lanes(h):
    return slice(FLANES * h, FLANES * (h + 1))


def list_pairs(seg_ref, pad_ref, pat_ref, pairs_s):
    def rows(i, carry):
        start, count = carry
        start = jnp.where(seg_ref[0, i] == seg_ref[0, jnp.maximum(i - 1, 0)], start, i)

        def cols(j, count):
            pairs_s[count] = i * 32 + j
            return count + jnp.where((pat_ref[i, j] == 1) & (pad_ref[0, j] == 0), 1, 0)
        return start, lax.fori_loop(start, i, cols, count)
    _, count = lax.fori_loop(0, FRAMES, rows, (jnp.int32(0), jnp.int32(0)))
    for n in range(UNROLL):
        pairs_s[count + n] = FRAMES * 33
    return count


def each_pair(pairs_s, count, work):
    def step(n, _):
        codes = [pairs_s[n * UNROLL + u] for u in range(UNROLL)]
        work([(code // 32, code % 32) for code in codes])
        return 0
    lax.fori_loop(0, (count + UNROLL - 1) // UNROLL, step, 0)


def inside(f):
    return jnp.minimum(f, FRAMES - 1)


def split_rows(value, r32):
    high = value.astype(BF16).astype(F32)
    return jnp.where(r32 == 24, high, jnp.where(r32 == 25, value - high, 0.0))


def fwd_kernel(seg_ref, pad_ref, pat_ref, h_ref, wq_ref, wk_ref, wv_ref,
               o_hbm, ot_hbm, qa_hbm, ka_hbm, va_hbm, kt_hbm,
               o_ref, ot_ref, qa_ref, ka_ref, va_ref, kt_ref, vt_s, qe_s, m_s, acc_s, bad_s, w_s, pairs_s, out_sem):
    col = lax.broadcasted_iota(jnp.int32, (FROWS, WIDE), 1) % HW
    row = lax.broadcasted_iota(jnp.int32, (FROWS, WIDE), 0)
    ones = jnp.where((col == 24) | (col == 25), 1.0, 0.0)
    kadd = ones + jnp.where((col == 26) & (row >= PATCHES), MASKED, 0.0)
    trow = lax.broadcasted_iota(jnp.int32, (WIDE, FROWS), 0) % HW
    vtadd = jnp.where(trow == 24, 1.0, 0.0)
    zpad = jnp.zeros((WIDE, FLANES - FROWS), F32)
    r32 = lax.broadcasted_iota(jnp.int32, (HW, FLANES), 0)
    by_rows = [(o_ref, o_hbm, 0), (ka_ref, ka_hbm, 1), (va_ref, va_hbm, 2)]
    by_lanes = [(ot_ref, ot_hbm, 3), (qa_ref, qa_hbm, 4), (kt_ref, kt_hbm, 5)]
    qe_s[...] = jnp.zeros(qe_s.shape, BF16)
    for b, w_ref in enumerate((wq_ref, wk_ref, wv_ref)):
        w_s[b * WIDE:(b + 1) * WIDE, :] = w_ref[...]
    count = list_pairs(seg_ref, pad_ref, pat_ref, pairs_s)

    def keep(f):
        for src, dst, n in by_rows:
            pltpu.make_async_copy(src.at[frame_rows(f), :], dst.at[frame_rows(f), :], out_sem.at[n]).start()
        for src, dst, n in by_lanes:
            pltpu.make_async_copy(src.at[:, frame_lanes(f)], dst.at[:, frame_lanes(f)], out_sem.at[n]).start()

    def scores(i, j):
        s = dot(ka_ref[frame_rows(inside(j)), :], qe_s[inside(i)])
        return [s[:, head_lanes(h)] for h in HEADS]

    def gathered(j, ps):
        return [dot(vt_s[head_rows(h), frame_lanes(inside(j), FROWS)], ps[h]) for h in HEADS]

    def attend(exact):
        def project(f):
            hf = h_ref[frame_rows(f), :]
            turned = dot_nt(w_s[...], hf)
            qt = jnp.concatenate([turned[0:WIDE] * QSCALE, zpad], axis=1)
            kt = turned[WIDE:2 * WIDE]
            vt = (turned[2 * WIDE:3 * WIDE] + vtadd).astype(BF16)
            lined = dot_nt(hf, w_s[WIDE:3 * WIDE, :])
            kr = (lined[:, 0:WIDE] + kadd).astype(BF16)
            vr = (lined[:, WIDE:2 * WIDE] + ones).astype(BF16)
            own = qt * jnp.concatenate([kt, zpad], axis=1)
            for h in HEADS:
                if exact:
                    start = jnp.zeros((1, FLANES), F32)
                else:
                    start = jnp.sum(own[head_rows(h)], axis=0, keepdims=True)
                m_s[f, h] = start
                aug = jnp.where(r32 == 26, 1.0, split_rows(-start, r32))
                qe_s[f, head_rows(h), head_lanes(h)] = (qt[head_rows(h)] + aug).astype(BF16)
            ka_ref[frame_rows(f), :] = kr
            va_ref[frame_rows(f), :] = vr
            kt_ref[:, frame_lanes(f, FROWS)] = kt.astype(BF16)
            vt_s[:, frame_lanes(f, FROWS)] = vt

        def finalize(i):
            outs, augs = [], []
            for h in HEADS:
                a = acc_s[i, h]
                l = a[24:25, :]
                bad_s[...] = jnp.maximum(bad_s[...], jnp.where(l < 1e30, 0.0, 1.0))
                outs.append(jnp.where(r32 < HEAD_DIM, a / l, 0.0))
                lse = m_s[i, h] + jnp.log2(l)
                q = qe_s[i, head_rows(h), head_lanes(h)].astype(F32)
                augs.append(jnp.where((r32 == 24) | (r32 == 25), split_rows(-lse, r32), q))
            ot = jnp.concatenate(outs, axis=0)
            ot_ref[:, frame_lanes(i)] = ot.astype(BF16)
            qa_ref[:, frame_lanes(i)] = jnp.concatenate(augs, axis=0).astype(BF16)
            o_ref[frame_rows(i), :] = ot.T[:FROWS, :].astype(BF16)

        def attend_pairs(pairs, first):
            ss = [scores(i, j) for i, j in pairs]
            if exact:
                old = [None if first else [m_s[i, h] for h in HEADS] for i, _ in pairs]
                for n, (i, j) in enumerate(pairs):
                    if not first:
                        old[n] = [m_s[i, h] for h in HEADS]
                    top = [jnp.max(ss[n][h], axis=0, keepdims=True) for h in HEADS]
                    if not first:
                        top = [jnp.maximum(old[n][h], top[h]) for h in HEADS]
                    pv = gathered(j, [jnp.exp2(ss[n][h] - top[h]).astype(BF16) for h in HEADS])
                    for h in HEADS:
                        acc_s[i, h] = pv[h] if first else acc_s[i, h] * jnp.exp2(old[n][h] - top[h]) + pv[h]
                        m_s[i, h] = top[h]
                return
            ps = [[jnp.exp2(s[h]).astype(BF16) for h in HEADS] for s in ss]
            pvs = [gathered(j, p) for (_, j), p in zip(pairs, ps)]
            for (i, _), pv in zip(pairs, pvs):
                for h in HEADS:
                    acc_s[i, h] = pv[h] if first else acc_s[i, h] + pv[h]

        bad_s[...] = jnp.zeros(bad_s.shape, F32)
        for k in range(TOGETHER):
            project(k)

        def diagonal(n, _):
            attend_pairs([(n * TOGETHER + k,) * 2 for k in range(TOGETHER)], True)
            for k in range(TOGETHER):
                project(jnp.minimum((n + 1) * TOGETHER, FRAMES - TOGETHER) + k)
            return 0
        lax.fori_loop(0, FRAMES // TOGETHER, diagonal, 0)
        each_pair(pairs_s, count, lambda pairs: attend_pairs(pairs, False))

        def close(n, _):
            for k in range(TOGETHER):
                finalize(n * TOGETHER + k)
            for k in range(TOGETHER):
                keep(n * TOGETHER + k)
            return 0
        lax.fori_loop(0, FRAMES // TOGETHER, close, 0)
        for src, dst, n in by_rows + by_lanes:
            pltpu.make_async_copy(src, dst, out_sem.at[n]).wait()

    attend(False)

    @pl.when(jnp.max(bad_s[...]) > 0.0)
    def _():
        attend(True)


SMEM = pl.BlockSpec(memory_space=pltpu.SMEM)
HBM = pl.BlockSpec(memory_space=pltpu.HBM)


def in_hbm(value):
    return pltpu.with_memory_space_constraint(value, pltpu.HBM)
VM = pl.BlockSpec(memory_space=pltpu.VMEM)


def attn_fwd(seg, pad, pat, h, wqt, wkt, wvt):
    sd = jax.ShapeDtypeStruct
    V = pltpu.VMEM
    rows, lanes = sd((FRAMES * FROWS, WIDE), BF16), sd((WIDE, FRAMES * FLANES), BF16)
    return pl.pallas_call(
        fwd_kernel,
        out_shape=tuple(pltpu.HBM(a.shape, BF16) for a in (rows, lanes, lanes, rows, rows, lanes)),
        in_specs=[SMEM] * 3 + [VM] * 4,
        out_specs=(HBM,) * 6,
        scratch_shapes=[V(a.shape, BF16) for a in (rows, lanes, lanes, rows, rows, lanes)] + [V((WIDE, FRAMES * FLANES), BF16), V((FRAMES, WIDE, HEADS_LOCAL * FLANES), BF16),
                        V((FRAMES + 1, HEADS_LOCAL, 1, FLANES), F32), V((FRAMES + 1, HEADS_LOCAL, HW, FLANES), F32),
                        V((1, FLANES), F32), V((3 * WIDE, D), BF16), pltpu.SMEM((128 + UNROLL,), jnp.int32), pltpu.SemaphoreType.DMA((6,))],
        compiler_params=pltpu.CompilerParams(vmem_limit_bytes=30 << 20),
        cost_estimate=pl.CostEstimate(flops=int(3e10), bytes_accessed=8 << 20, transcendentals=0),
        name="attend_forward",
    )(seg, pad, pat, h, wqt, wkt, wvt)


def bwd_kernel(seg_ref, pad_ref, pat_ref, qa_ref, ka_ref, va_ref, kt_ref, ot_ref, do_ref, h_ref, wq_ref, wk_ref, wv_ref,
               dh_ref, early_ref, qe_s, oe_s, dq_s, dk_s, dv_s, dw_s, w_s, turn_s, blk_s, pairs_s):
    scale = HEAD_DIM ** -0.5
    for s in (qe_s, oe_s):
        s[...] = jnp.zeros(s.shape, BF16)
    count = list_pairs(seg_ref, pad_ref, pat_ref, pairs_s)
    dw_s[...] = jnp.zeros(dw_s.shape, F32)
    for b, w_ref in enumerate((wq_ref, wk_ref, wv_ref)):
        w_s[b * WIDE:(b + 1) * WIDE, :] = w_ref[...]
    real = lax.broadcasted_iota(jnp.int32, (WIDE, FROWS), 0) % HW < HEAD_DIM
    r32 = lax.broadcasted_iota(jnp.int32, (HW, FLANES), 0)
    zpad = jnp.zeros((WIDE, FLANES - FROWS), F32)

    def prepare(i):
        t = i
        qt = qa_ref[:, frame_lanes(i)]
        dot_ = jnp.concatenate([do_ref[frame_rows(i), :].astype(F32).T, zpad], axis=1)
        prod = dot_ * ot_ref[:, frame_lanes(i)].astype(F32)
        for h in HEADS:
            d = -jnp.sum(prod[head_rows(h)], axis=0, keepdims=True)
            qe_s[t, head_rows(h), head_lanes(h)] = qt[head_rows(h)]
            oe_s[t, head_rows(h), head_lanes(h)] = (dot_[head_rows(h)] + split_rows(d, r32)).astype(BF16)

    def scores(i, j):
        t, u = inside(i), inside(j)
        s, dp = dot(ka_ref[frame_rows(u), :], qe_s[t]), dot(va_ref[frame_rows(u), :], oe_s[t])
        ps = [jnp.exp2(s[:, head_lanes(h)]) for h in HEADS]
        return [p.astype(BF16) for p in ps], [(ps[h] * dp[:, head_lanes(h)]).astype(BF16) for h in HEADS]

    def products(i, j, pb, ds):
        t, u = inside(i), inside(j)
        dq = [dot(kt_ref[head_rows(h), frame_lanes(u, FROWS)], ds[h]) for h in HEADS]
        dv = [dot_nt(oe_s[t, head_rows(h), head_lanes(h)], pb[h]) for h in HEADS]
        dk = [dot_nt(qe_s[t, head_rows(h), head_lanes(h)], ds[h]) for h in HEADS]
        return [jnp.concatenate(value, axis=0) for value in (dq, dk, dv)]

    def attend_pairs(pairs, first):
        made = [scores(i, j) for i, j in pairs]
        values = [products(i, j, pb, ds) for (i, j), (pb, ds) in zip(pairs, made)]
        for (i, j), value in zip(pairs, values):
            for ref, at, part in ((dq_s, frame_lanes(i), 0), (dk_s, frame_lanes(j, FROWS), 1), (dv_s, frame_lanes(j, FROWS), 2)):
                ref[:, at] = value[part] if first else ref[:, at] + value[part]

    def finish(f):
        parts = (dq_s[:, frame_lanes(f, FROWS)] * scale, dk_s[:, frame_lanes(f, FROWS)] * math.log(2.0), dv_s[:, frame_lanes(f, FROWS)])
        grads = jnp.concatenate([jnp.where(real, part, 0.0).astype(BF16) for part in parts], axis=0)
        dh_ref[frame_rows(f), :] = dot_tn(grads, w_s[...]).astype(BF16)
        return dot(grads, h_ref[frame_rows(f), :])

    for k in range(TOGETHER):
        prepare(k)

    def diagonal(n, _):
        attend_pairs([(n * TOGETHER + k,) * 2 for k in range(TOGETHER)], True)
        for k in range(TOGETHER):
            prepare(jnp.minimum((n + 1) * TOGETHER, FRAMES - TOGETHER) + k)
        return 0
    lax.fori_loop(0, FRAMES // TOGETHER, diagonal, 0)
    each_pair(pairs_s, count, lambda pairs: attend_pairs(pairs, False))

    def close(n, _):
        dw = [finish(n * TOGETHER + k) for k in range(TOGETHER)]
        dw_s[...] += functools.reduce(jnp.add, dw)
        return 0
    lax.fori_loop(0, FRAMES // TOGETHER, close, 0)
    for b in range(3):
        turned = dw_s[b * WIDE:(b + 1) * WIDE, :].T
        turn_s[:, 0:96] = jnp.concatenate([turned[:, HW * h:HW * h + HEAD_DIM] for h in HEADS], axis=1)
        line = [turn_s[pl.ds(k, 96, stride=4), :][:, 0:96] for k in range(4)]
        blk_s[pl.ds(0, 96, stride=3), :] = jnp.concatenate([line[0], line[1][:, :32]], axis=1)
        blk_s[pl.ds(1, 96, stride=3), :] = jnp.concatenate([line[1][:, 32:], line[2][:, :64]], axis=1)
        blk_s[pl.ds(2, 96, stride=3), :] = jnp.concatenate([line[2][:, 64:], line[3]], axis=1)
        early_ref[288 * b:288 * (b + 1), :] = blk_s[...].astype(BF16)


def attn_bwd(seg, pad, pat, qa, ka, va, kt, ot, do, h, wqt, wkt, wvt):
    sd = jax.ShapeDtypeStruct
    V = pltpu.VMEM
    return pl.pallas_call(
        bwd_kernel,
        out_shape=(sd((FRAMES * FROWS, D), BF16), sd((3 * 288, 128), BF16)),
        in_specs=[SMEM] * 3 + [VM] * 10,
        out_specs=(VM,) * 2,
        scratch_shapes=[V((FRAMES, WIDE, HEADS_LOCAL * FLANES), BF16), V((FRAMES, WIDE, HEADS_LOCAL * FLANES), BF16)]
        + [V((WIDE, (FRAMES + 1) * FLANES), F32)] * 3
        + [V((3 * WIDE, D), F32), V((3 * WIDE, D), BF16), V((D, 128), F32), V((288, 128), F32),
           pltpu.SMEM((128 + UNROLL,), jnp.int32)],
        compiler_params=pltpu.CompilerParams(vmem_limit_bytes=42 << 20),
        cost_estimate=pl.CostEstimate(flops=int(5e10), bytes_accessed=12 << 20, transcendentals=0),
        name="attend_backward",
    )(seg, pad, pat, qa, ka, va, kt, ot, do, h, wqt, wkt, wvt)


MESH = pl.DeviceIdType.MESH
OWN_ROWS = 4 * FROWS


def place(d, m):
    return {"dp": d, "mp": m}


def remote(src, dst, send_sem, recv_sem, device):
    return pltpu.make_async_remote_copy(
        src_ref=src, dst_ref=dst, send_sem=send_sem, recv_sem=recv_sem, device_id=device, device_id_type=MESH
    )


def local(src, dst, sem):
    return pltpu.make_async_copy(src, dst, sem)


def greet(devices):
    barrier = pltpu.get_barrier_semaphore()
    for device in devices:
        pl.semaphore_signal(barrier, inc=1, device_id=device, device_id_type=MESH)
    pl.semaphore_wait(barrier, len(devices))


def group_peers():
    me = lax.axis_index("mp")
    return me, me ^ 1, me ^ 2, me ^ 3


def frame_part(device, c):
    return pl.ds(pl.multiple_of(device * OWN_ROWS + c * FROWS, 16), FROWS)


def normalised(v):
    centred = v - jnp.mean(v, axis=-1, keepdims=True)
    inv = lax.rsqrt(jnp.mean(centred * centred, axis=-1, keepdims=True) + NORM_EPS)
    return centred * inv, inv


def norm_pull(dy, hat, inv, gain):
    dg = dy * gain
    lead = jnp.mean(dg, axis=-1, keepdims=True)
    along = jnp.mean(dg * hat, axis=-1, keepdims=True)
    return inv * (dg - lead - hat * along)


def col_sum(v):
    return jnp.sum(v, axis=0, keepdims=True)


def load_frame(ref, c):
    base = c * PATCHES // 16 * 16
    rows = ref[base:base + FROWS, :].astype(F32)
    shift = c * PATCHES - base
    return pltpu.roll(rows, FROWS - shift, 0) if shift else rows


def live_rows():
    return lax.broadcasted_iota(jnp.int32, (FROWS, 1), 0) < PATCHES


def dp_peers(count):
    d = lax.axis_index("dp")
    side, line = d % 2, d // 2
    return side, line, {"dp": d ^ 1}, [lax.rem(line + n, count) for n in range(count)]


def start_kernel(count, x_hbm, np_ref, w_hbm, m_hbm, v_hbm, h_ref, wq_ref, wk_ref, wv_ref, ws_ref, ma_ref, mb_ref,
                 x_ref, w_ref, m_ref, v_ref, mo_s, w_s, load_x, load_w, keep_m,
                 send_x, recv_x, send_p, recv_p, send_f, recv_f, send_t, recv_t, send_l, recv_l):
    me, near, far, _ = group_peers()
    side, line, twin, around = dp_peers(count)
    frames = range(OWN_ROWS // FROWS)
    cuts = [0, 208, 400, 592, 784]
    loads = [local(x_hbm.at[a:b, :], x_ref.at[a:b, :], load_x.at[c]) for c, (a, b) in enumerate(zip(cuts, cuts[1:]))]
    others = [local(m_hbm, m_ref, load_w.at[0]), local(v_hbm, v_ref, load_w.at[1]), local(w_hbm, w_ref, load_w.at[2])]
    for copy in loads + others:
        copy.start()
    greet([{"mp": near}, {"mp": far}, twin] + [{"dp": q * 2 + side} for q in around[1:]])
    live = live_rows()
    to_far, to_near, moments = [], [], []
    for c in frames:
        loads[c].wait()
        hat, _ = normalised(load_frame(x_ref, c))
        h_ref[frame_part(me, c), :] = jnp.where(live, hat * np_ref[0:1, :] + np_ref[1:2, :], 0.0).astype(BF16)
        rows = h_ref.at[frame_part(me, c), :]
        to_far.append(remote(rows, rows, send_x.at[c], recv_x.at[c], {"mp": far}))
        to_near.append(remote(rows, rows, send_p.at[c], recv_p.at[c], {"mp": near}))
        to_far[c].start()
        to_near[c].start()

    slots, rows = m_ref.shape[0], m_ref.shape[1]
    others[0].wait()
    others[1].wait()
    for r in range(2 * slots):
        mo_s[r // slots, pl.ds((r % slots) * rows, rows), :] = (v_ref if r % 2 else m_ref)[r // 2].astype(BF16)
    first, second = ma_ref.at[side, line], mb_ref.at[side]
    kept = [local(mo_s.at[0], first, keep_m.at[0]), local(mo_s.at[1], second, keep_m.at[1])]
    for n, q in enumerate(around[1:]):
        moments.append(remote(mo_s.at[0], first, send_l.at[n], recv_l.at[n], {"dp": q * 2 + side}))
    moments.append(remote(mo_s.at[0], first, send_t.at[0], recv_t.at[0], twin))
    moments.append(remote(mo_s.at[1], second, send_t.at[1], recv_t.at[1], twin))
    for copy in moments + kept:
        copy.start()

    def incoming(device, sends, recvs, c):
        rows = h_ref.at[frame_part(device, c), :]
        return remote(rows, rows, sends.at[c], recvs.at[c], {"mp": near})

    def forward(c):
        incoming(far, send_x, recv_x, c).wait_recv()
        copy = incoming(far, send_f, recv_f, c)
        copy.start()
        return copy

    others[2].wait()
    for b, out in enumerate((wq_ref, wk_ref, wv_ref)):
        a = [w_ref[b, pl.ds(k, 96, stride=3), :] for k in range(3)]
        lines = [a[0][:, :96], jnp.concatenate([a[0][:, 96:], a[1][:, :64]], axis=1),
                 jnp.concatenate([a[1][:, 64:], a[2][:, :32]], axis=1), a[2][:, 32:]]
        gap = jnp.zeros((96, HW - HEAD_DIM), F32)
        for k in range(4):
            parts = []
            for h in HEADS:
                parts += [lines[k][:, HEAD_DIM * h:HEAD_DIM * (h + 1)], gap]
            w_s[pl.ds(k, 96, stride=4), :] = jnp.concatenate(parts, axis=1)
        out[...] = w_s[...].T.astype(BF16)
    copies = [forward(0)]
    for b in range(3, w_ref.shape[0]):
        for k in range(3):
            lanes = slice(128 * k, 128 * (k + 1))
            part = w_ref[b, pl.ds(k, 96, stride=3), :]
            if b == 3:
                gap = jnp.zeros((HW - HEAD_DIM, 128), F32)
                parts = []
                for h in HEADS:
                    parts += [part[HEAD_DIM * h:HEAD_DIM * (h + 1)], gap]
                ws_ref[2 * D:2 * D + WIDE, lanes] = jnp.concatenate(parts, axis=0).astype(BF16)
            else:
                ws_ref[96 * (b - 4):96 * (b - 3), lanes] = part.astype(BF16)
    for c in frames[1:]:
        copies.append(forward(c))
    for c in frames:
        incoming(near, send_p, recv_p, c).wait_recv()
        incoming(near ^ 2, send_f, recv_f, c).wait_recv()
    for n in range(1, count):
        part = ma_ref.at[side, around[count - n]]
        remote(part, part, send_l.at[n - 1], recv_l.at[n - 1], twin).wait_recv()
    part = ma_ref.at[1 - side, line]
    remote(part, part, send_t.at[0], recv_t.at[0], twin).wait_recv()
    part = mb_ref.at[1 - side]
    remote(part, part, send_t.at[1], recv_t.at[1], twin).wait_recv()
    for copy in kept:
        copy.wait()
    for copy in to_far + to_near + copies + moments:
        copy.wait_send()


def start_call(dp, x, norm_params, weights, first_moments, second_moments):
    sd, V, S = jax.ShapeDtypeStruct, pltpu.VMEM, pltpu.SemaphoreType.DMA
    blocks, count = weights.shape[0], dp // 2
    half = first_moments.shape[0] * first_moments.shape[1]
    turned = sd((WIDE, D), BF16)
    return pl.pallas_call(
        functools.partial(start_kernel, count),
        out_shape=(sd((FRAMES * FROWS, D), BF16), turned, turned, turned, sd((WIDE + 96 * (blocks - 4), D), BF16),
                   pltpu.HBM((2, count, half, 128), BF16), pltpu.HBM((2, half, 128), BF16)),
        in_specs=[HBM, VM, HBM, HBM, HBM],
        out_specs=(VM,) * 5 + (HBM,) * 2,
        scratch_shapes=[V(x.shape, BF16), V(weights.shape, F32), V(first_moments.shape, F32), V(first_moments.shape, F32),
                        V((2, half, 128), BF16), V((D, WIDE), F32), S((4,)), S((3,)), S((2,))] + [S((4,))] * 6 + [S((2,))] * 2 + [S((count,))] * 2,
        compiler_params=pltpu.CompilerParams(vmem_limit_bytes=16 << 20, collective_id=1, has_side_effects=True),
        name="norm_and_gather",
    )(in_hbm(x), norm_params, in_hbm(weights), in_hbm(first_moments), in_hbm(second_moments))


def gelu_parts(u):
    lead = math.sqrt(2.0 / math.pi)
    bend = lead * 0.044715
    square = u * u
    half = 0.5 + 0.5 * jnp.tanh(u * (lead + bend * square))
    slope = half + 2.0 * u * (half - half * half) * (lead + 3.0 * bend * square)
    return u * half, slope


def middle_kernel(count, o_ref, x_hbm, ct_hbm, keep_ref, w0_ref, w1_ref, w3_ref, np_ref, ma_ref, mb_ref,
                  out_ref, dx2_ref, do_ref, l0_ref, l1_ref, l2_ref, l3_ref, nb_ref, mom_ref,
                  ob_s, dob_s, g_s, a_s, du_s, da_s, h2_s, dxa_s, blk_s, res_s, ut_s, wot_s,
                  x_ref, ct_ref, o_s, w2_ref, load_s, send_w, recv_w,
                  send_o, recv_o, send_d, recv_d, send_t, recv_t, send_l, recv_l, send_f, recv_f):
    me, near, far, across = group_peers()
    side, line, twin, around = dp_peers(count)
    peers = (far, across, near)
    mine = pl.ds(pl.multiple_of(me * OWN_ROWS, 16), OWN_ROWS)
    loads = [local(ct_hbm, ct_ref, load_s.at[0]), local(x_hbm, x_ref, load_s.at[1]), local(o_ref.at[mine, :], o_s, load_s.at[2])]
    for copy in loads:
        copy.start()
    greet([{"mp": p} for p in peers] + [twin] + [{"dp": q * 2 + side} for q in around[1:]])
    frames = range(OWN_ROWS // FROWS)
    live = live_rows()
    shards_w = (w0_ref, w1_ref, w2_ref, w3_ref)
    late = (l0_ref, l1_ref, l2_ref, l3_ref)
    places = range(len(shards_w))
    outgoing = []
    for c in frames:
        for n, p in enumerate(peers):
            outgoing.append(remote(o_ref.at[frame_part(p, c), :], ob_s.at[n, pl.ds(c * FROWS, FROWS), :],
                                   send_o.at[n, c], recv_o.at[n, c], {"mp": p}))
            outgoing[-1].start()
    weights = remote(w1_ref, w2_ref, send_w.at[0], recv_w.at[0], {"mp": near})
    weights.start()
    moments = []
    for n, q in enumerate(around[1:]):
        own_half = mb_ref.at[side]
        moments.append(remote(own_half, mom_ref.at[1, side, line], send_l.at[n], recv_l.at[n], {"dp": q * 2 + side}))
        moments.append(remote(ma_ref.at[side, q], mom_ref.at[0, side, q], send_t.at[q], recv_t.at[q], twin))
    for copy in moments:
        copy.start()

    def pass_moments(n):
        q = around[count - n]
        part = mom_ref.at[1, side, q]
        remote(part, part, send_l.at[n - 1], recv_l.at[n - 1], twin).wait_recv()
        moments.append(remote(part, part, send_f.at[q], recv_f.at[q], twin))
        moments[-1].start()

    def w_up(m):
        return shards_w[m][0:D, :]

    def w_down(m):
        return shards_w[m][D:2 * D, :]

    def w_o(m):
        return shards_w[m][2 * D:2 * D + WIDE, :]

    def cols(m):
        return slice(m * D, (m + 1) * D)

    loads[0].wait()
    for c in frames:
        rows = slice(c * FROWS, (c + 1) * FROWS)
        g_s[rows, :] = jnp.where(live, load_frame(ct_ref, c) * keep_ref[0, c], 0.0).astype(BF16)
    for m in (0, 1, 3, 2):
        if m == 2:
            weights.wait_recv()
        da_s[:, cols(m)] = dot_nt(g_s[...], w_down(m))
        ut_s[cols(m), :] = w_up(m).astype(F32).T.astype(BF16)
        wot_s[:, m * WIDE:(m + 1) * WIDE] = w_o(m).astype(F32).T.astype(BF16)
    loads[1].wait()
    loads[2].wait()
    nb_ref[...] = jnp.zeros(nb_ref.shape, F32)
    down = jnp.concatenate([w_down(m) for m in places], axis=0)
    out_w = jnp.concatenate([w_o(m) for m in places], axis=0)
    sent = []
    for pair in range(len(frames) // 2):
        both = (2 * pair, 2 * pair + 1)
        rows = slice(2 * pair * FROWS, 2 * (pair + 1) * FROWS)
        for c in both:
            for n, p in enumerate(peers):
                part = ob_s.at[n, pl.ds(c * FROWS, FROWS), :]
                remote(part, part, send_o.at[n, c], recv_o.at[n, c], {"mp": p}).wait_recv()
        own_rows = pl.ds(pl.multiple_of(me * OWN_ROWS + 2 * pair * FROWS, 16), 2 * FROWS)
        heads = jnp.concatenate([o_s[rows, :]] + [ob_s[n, rows, :] for n in range(len(peers))], axis=1)
        x2 = jnp.concatenate([load_frame(x_ref, c) for c in both], axis=0) + dot(heads, out_w)
        x2 = jnp.where(jnp.concatenate([live, live], axis=0), x2, 0.0)
        hat, inv = normalised(x2)
        h2 = (hat * np_ref[2:3, :] + np_ref[3:4, :]).astype(BF16)
        h2_s[rows, :] = h2
        for m in places:
            value, slope = gelu_parts(dot(h2, w_up(m)))
            a_s[rows, cols(m)] = value.astype(BF16)
            du_s[rows, cols(m)] = (da_s[rows, cols(m)] * slope).astype(BF16)
        result = x2 + dot(a_s[rows, :], down)
        for k, c in enumerate(both):
            res_s[pl.ds(c * PATCHES, FROWS), :] = result[k * FROWS:(k + 1) * FROWS]
        dh2 = dot(du_s[rows, :], ut_s[...])
        nb_ref[0:1, :] += col_sum(dh2 * hat)
        nb_ref[1:2, :] += col_sum(dh2)
        dx2 = g_s[rows, :].astype(F32) + norm_pull(dh2, hat, inv, np_ref[2:3, :])
        dx2_ref[rows, :] = dx2
        dxa = dx2.astype(BF16)
        dxa_s[rows, :] = dxa
        d_heads = dot(dxa, wot_s[...]).astype(BF16)
        for n in range(len(peers)):
            dob_s[n, rows, :] = d_heads[:, (n + 1) * WIDE:(n + 2) * WIDE]
        for c in both:
            for n, p in enumerate(peers):
                sent.append(remote(dob_s.at[n, pl.ds(c * FROWS, FROWS), :], do_ref.at[frame_part(me, c), :],
                                   send_d.at[n, c], recv_d.at[n, c], {"mp": p}))
                sent[-1].start()
        do_ref[own_rows, :] = d_heads[:, 0:WIDE]
        for c in both:
            if 0 < c < count:
                pass_moments(c)
    for n in range(len(frames), count):
        pass_moments(n)
    out_ref[...] = res_s[0:out_ref.shape[0], :].astype(BF16)

    def as_block(shard, first, value):
        size = value.shape[0]
        for k in range(3):
            blk_s[pl.ds(k, size, stride=3), :] = value[:, 128 * k:128 * (k + 1)]
        late[shard][first * 288:first * 288 + 3 * size, :] = blk_s[0:3 * size, :].astype(BF16)

    def drop_gaps(value):
        return jnp.concatenate([value[HW * h:HW * h + HEAD_DIM] for h in HEADS], axis=0)

    dw1 = dot_tn(h2_s[...], du_s[...])
    dw2 = dot_tn(g_s[...], a_s[...])
    for m in places:
        as_block(m, 1, dw1[:, cols(m)])
        as_block(m, 5, dw2[:, cols(m)].T)
        o_m = o_s[...] if m == 0 else ob_s[m - 1]
        as_block(m, 0, drop_gaps(dot_tn(o_m, dxa_s[...])))
    for c in frames:
        for n, p in enumerate(peers):
            part = do_ref.at[frame_part(p, c), :]
            remote(part, part, send_d.at[n, c], recv_d.at[n, c], {"mp": p}).wait_recv()
    for q in around[1:]:
        for half, sends, recvs in ((0, send_t, recv_t), (1, send_f, recv_f)):
            part = mom_ref.at[half, 1 - side, q]
            remote(part, part, sends.at[q], recvs.at[q], twin).wait_recv()
    for copy in outgoing + sent + moments + [weights]:
        copy.wait_send()


def middle_call(dp, o, x, ct, keep, w, norm_params, ma, mb):
    sd = jax.ShapeDtypeStruct
    V, S = pltpu.VMEM, pltpu.SemaphoreType.DMA
    count = dp // 2
    late = sd((9 * 288, 128), BF16)
    return pl.pallas_call(
        functools.partial(middle_kernel, count),
        out_shape=(sd(x.shape, BF16), sd((OWN_ROWS, D), F32), sd((FRAMES * FROWS, WIDE), BF16),
                   late, late, late, late, sd((2, D), F32), pltpu.HBM((2,) + ma.shape, BF16)),
        in_specs=[HBM, HBM, HBM, SMEM] + [VM] * 4 + [HBM] * 2,
        out_specs=(VM,) * 8 + (HBM,),
        scratch_shapes=[V((3, OWN_ROWS, WIDE), BF16), V((3, OWN_ROWS, WIDE), BF16), V((OWN_ROWS, D), BF16),
                        V((OWN_ROWS, FF), BF16), V((OWN_ROWS, FF), BF16), V((OWN_ROWS, FF), F32),
                        V((OWN_ROWS, D), BF16), V((OWN_ROWS, D), BF16), V((1152, 128), F32), V((OWN_ROWS, D), F32),
                        V((FF, D), BF16), V((D, 4 * WIDE), BF16),
                        V(x.shape, BF16), V(x.shape, BF16), V((OWN_ROWS, WIDE), BF16), V(w[0].shape, BF16), S((3,)), S((1,)), S((1,)), S((3, 4)), S((3, 4)), S((3, 4)), S((3, 4))] + [S((count,))] * 6,
        compiler_params=pltpu.CompilerParams(vmem_limit_bytes=36 << 20, collective_id=2, has_side_effects=True),
        cost_estimate=pl.CostEstimate(flops=int(6e9), bytes_accessed=12 << 20, transcendentals=0),
        name="feed_forward",
    )(in_hbm(o), in_hbm(x), in_hbm(ct), keep, *w, norm_params, in_hbm(ma), in_hbm(mb))


def reduce_kernel(dp, piece, dh_ref, early_ref, l0_ref, l1_ref, l2_ref, l3_ref, x_ref, dx2_ref, np_ref, nb_ref,
                  gin_ref, gs_ref, tot_ref,
                  res_s, pb_s, xs_s, xb_s, g_s, yb_s, zs_s, zb_s, msg_s, mb_s, dm_s, db_s,
                  send_p, recv_p, send_x, recv_x, send_y, recv_y, send_z, recv_z,
                  send_a, recv_a, send_w, recv_w, send_m, recv_m, send_n, recv_n):
    me, near, far, across = group_peers()
    d = lax.axis_index("dp")
    count = dp // 2
    side, line = d % 2, d // 2
    twin = {"dp": d ^ 1}

    def on_line(n):
        return lax.rem(line + n, count)

    def line_device(q):
        return {"dp": q * 2 + side}

    frames = range(OWN_ROWS // FROWS)
    others = [{"mp": near}, {"mp": far}, {"mp": across}] + [{"dp": lax.rem(d + n, dp)} for n in range(1, dp)]
    greet(others)

    def own(c):
        return pl.ds(c * FROWS, FROWS)

    to_near = []
    for k, target in ((1, across), (0, near)):
        for c in frames:
            to_near.append(remote(dh_ref.at[frame_part(target, c), :], pb_s.at[k, own(c), :],
                                  send_p.at[k, c], recv_p.at[k, c], {"mp": near}))
            to_near[-1].start()

    total = early_ref.shape[0] + l0_ref.shape[0]
    g_s[0:early_ref.shape[0], :] = early_ref[...]
    g_s[early_ref.shape[0]:total, :] = (l0_ref[...].astype(F32) + l1_ref[...].astype(F32)
                                        + (l2_ref[...].astype(F32) + l3_ref[...].astype(F32))).astype(BF16)
    if g_s.shape[0] > total:
        g_s[total:, :] = jnp.zeros((g_s.shape[0] - total, 128), BF16)

    def at(s, q):
        return pl.ds(pl.multiple_of((s * count + q) * piece, 16), piece)

    to_twin = []
    for n in range(count):
        q = on_line(n + 1)
        to_twin.append(remote(g_s.at[at(1 - side, q), :], yb_s.at[q], send_y.at[q], recv_y.at[q], twin))
        to_twin[-1].start()

    to_far = []
    for c in frames:
        remote(pb_s.at[1, own(c), :], pb_s.at[1, own(c), :], send_p.at[1, c], recv_p.at[1, c], {"mp": near}).wait_recv()
        xs_s[own(c), :] = (dh_ref[frame_part(far, c), :].astype(F32) + pb_s[1, own(c), :].astype(F32)).astype(BF16)
        to_far.append(remote(xs_s.at[own(c), :], xb_s.at[own(c), :], send_x.at[c], recv_x.at[c], {"mp": far}))
        to_far[-1].start()

    to_line = []
    for n in range(count):
        q = on_line(n + 1)
        remote(yb_s.at[q], yb_s.at[q], send_y.at[q], recv_y.at[q], twin).wait_recv()
        zs_s[q] = (g_s[at(side, q), :].astype(F32) + yb_s[q].astype(F32)).astype(BF16)
        if n < count - 1:
            to_line.append(remote(zs_s.at[q], zb_s.at[line], send_z.at[q], recv_z.at[line], line_device(q)))
            to_line[-1].start()
    mine = zs_s[line].astype(F32)
    for n in range(1, count):
        q = on_line(n)
        remote(zb_s.at[q], zb_s.at[q], send_z.at[q], recv_z.at[q], line_device(q)).wait_recv()
        mine = mine + zb_s[q].astype(F32)
    mine = mine.astype(BF16)
    gs_ref[at(side, line), :] = mine
    whole = gs_ref.at[at(side, line), :]
    spread = []
    for n in range(1, count):
        q = on_line(n)
        spread.append(remote(whole, whole, send_a.at[q], recv_a.at[line], line_device(q)))
        spread[-1].start()
    passed = [remote(whole, whole, send_w.at[line], recv_w.at[line], twin)]
    passed[0].start()
    mine = mine.astype(F32)
    squares = jnp.sum(mine * mine, axis=0, keepdims=True)

    live = live_rows()
    gain, bias = jnp.zeros((1, D), F32), jnp.zeros((1, D), F32)
    for c in frames:
        remote(pb_s.at[0, own(c), :], pb_s.at[0, own(c), :], send_p.at[0, c], recv_p.at[0, c], {"mp": near}).wait_recv()
        remote(xb_s.at[own(c), :], xb_s.at[own(c), :], send_x.at[c], recv_x.at[c], {"mp": far}).wait_recv()
        dy = dh_ref[frame_part(me, c), :].astype(F32) + pb_s[0, own(c), :].astype(F32) + xb_s[own(c), :].astype(F32)
        dy = jnp.where(live, dy, 0.0)
        hat, inv = normalised(load_frame(x_ref, c))
        gain = gain + col_sum(dy * hat)
        bias = bias + col_sum(dy)
        res_s[pl.ds(c * PATCHES, FROWS), :] = dx2_ref[own(c), :] + norm_pull(dy, hat, inv, np_ref[0:1, :])
    gin_ref[...] = res_s[0:gin_ref.shape[0], :].astype(BF16)

    msg_s[...] = jnp.zeros(msg_s.shape, F32)
    msg_s[0:1, :] = gain
    msg_s[1:2, :] = bias
    msg_s[2:4, :] = nb_ref[...]
    msg_s[4:5, 0:128] = squares
    small = []
    for n, p in enumerate((near, far, across)):
        small.append(remote(msg_s, mb_s.at[n], send_m.at[n], recv_m.at[n], {"mp": p}))
        small[-1].start()

    def pass_on(n):
        q = on_line(n)
        piece_at = gs_ref.at[at(side, q), :]
        remote(piece_at, piece_at, send_a.at[q], recv_a.at[q], line_device(q)).wait_recv()
        passed.append(remote(piece_at, piece_at, send_w.at[q], recv_w.at[q], twin))
        passed[-1].start()

    pass_on(1)
    add = msg_s[...]
    for n, p in enumerate((near, far, across)):
        remote(mb_s.at[n], mb_s.at[n], send_m.at[n], recv_m.at[n], {"mp": p}).wait_recv()
        add = add + mb_s[n]
    dm_s[...] = add
    for n in range(1, dp):
        small.append(remote(dm_s, db_s.at[n], send_n.at[n], recv_n.at[n], {"dp": lax.rem(d + n, dp)}))
        small[-1].start()
    for n in range(2, count):
        pass_on(n)
    for n in range(1, dp):
        remote(db_s.at[n], db_s.at[n], send_n.at[n], recv_n.at[n], {"dp": lax.rem(d + dp - n, dp)}).wait_recv()
        add = add + db_s[n]
    tot_ref[...] = add
    for n in range(count):
        q = on_line(n)
        piece_at = gs_ref.at[at(1 - side, q), :]
        remote(piece_at, piece_at, send_w.at[q], recv_w.at[q], twin).wait_recv()
    for copy in to_near + to_twin + to_far + to_line + spread + passed + small:
        copy.wait_send()


def reduce_call(dp, dh, early, late, x, dx2, norm_params, nb):
    sd = jax.ShapeDtypeStruct
    V, S = pltpu.VMEM, pltpu.SemaphoreType.DMA
    rows = early.shape[0] + late[0].shape[0]
    count = dp // 2
    piece = -(-rows // (2 * count * 16)) * 16
    held = 2 * count * piece
    return pl.pallas_call(
        functools.partial(reduce_kernel, dp, piece),
        out_shape=(sd(x.shape, BF16), sd((held, 128), BF16), sd((8, D), F32)),
        in_specs=[VM] * 10,
        out_specs=(VM,) * 3,
        scratch_shapes=[V((OWN_ROWS, D), F32), V((2, OWN_ROWS, D), BF16), V((OWN_ROWS, D), BF16), V((OWN_ROWS, D), BF16), V((held, 128), BF16),
                        V((count, piece, 128), BF16), V((count, piece, 128), BF16), V((count, piece, 128), BF16),
                        V((8, D), F32), V((3, 8, D), F32), V((8, D), F32), V((dp, 8, D), F32),
                        S((2, 4)), S((2, 4)), S((4,)), S((4,)), S((count,)), S((count,)), S((count,)), S((count,)),
                        S((count,)), S((count,)), S((count,)), S((count,)), S((3,)), S((3,)), S((dp,)), S((dp,))],
        compiler_params=pltpu.CompilerParams(vmem_limit_bytes=22 << 20, collective_id=3, has_side_effects=True),
        name="reduce_gradients",
    )(dh, early, *late, x, dx2, norm_params, nb)


def update_kernel(slot_ref, dev_ref, res_ref, gin_ref, tot_ref, gs_ref, w_ref, m_ref, v_ref, ma_ref, mb_ref, mom_ref, np_ref, nm_ref, nv_ref,
                  out_ref, gout_ref, norm_ref, nw_ref, nf_ref, ns_ref, nn_ref, nnf_ref, nns_ref, sem_s):
    carried = [local(res_ref, out_ref, sem_s.at[0]), local(gin_ref, gout_ref, sem_s.at[1])]
    for copy in carried:
        copy.start()
    blocks, rows, _ = w_ref.shape
    slots = m_ref.shape[0]
    tot = tot_ref[...]
    grads = tot[0:4, :]
    norm = jnp.sqrt(jnp.sum(grads * grads, keepdims=True) + jnp.sum(tot[4:5, 0:128], keepdims=True))
    norm_ref[...] = norm
    clip_level = 0.5 * (4 * D * D + 2 * D * FF + 4 * D) ** 0.5
    factor = jnp.minimum(1.0, clip_level / norm)
    nn_ref[...], nnf_ref[...], nns_ref[...] = adam_update(
        np_ref[...], grads * factor, nm_ref[...], nv_ref[...], 0.0, NORM_RATE)

    def block(b):
        return gs_ref[pl.ds(pl.multiple_of(b * rows, 16), rows), :].astype(F32) * factor

    def step(b, _):
        holder, first = slot_ref[b] // slots, slot_ref[b] % slots * 2
        side, line = holder % 2, holder // 2
        on_side, on_line = side == dev_ref[0] % 2, line == dev_ref[0] // 2

        def moment(r):
            at = pl.ds(pl.multiple_of(r % slots * rows, 16), rows)
            late = mom_ref[r // slots, side, line, at, :]
            lead = jnp.where(on_side | on_line, ma_ref[side, line, at, :], late)
            rest = jnp.where(on_line, mb_ref[side, at, :], late)
            return jnp.where(r < slots, lead, rest).astype(F32)

        old = [moment(first), moment(first + 1)]
        nw_ref[b], _, _ = adam_update(w_ref[b], block(b), old[0], old[1], WEIGHT_DECAY, LEARN_RATE)
        return 0
    lax.fori_loop(0, blocks, step, 0)
    for s in range(slots):
        owned = jnp.int32(-1)
        for b in range(blocks):
            owned = jnp.where(slot_ref[b] == dev_ref[0] * slots + s, b, owned)
        _, first, second = adam_update(0.0, block(jnp.maximum(owned, 0)), m_ref[s], v_ref[s], 0.0, LEARN_RATE)
        nf_ref[s] = jnp.where(owned >= 0, first, m_ref[s])
        ns_ref[s] = jnp.where(owned >= 0, second, v_ref[s])
    for copy in carried:
        copy.wait()


def update_call(owner_slot, result, grad_in, tot, gs, weights, first, second, ma, mb, moments, norm_params, norm_first, norm_second):
    sd = jax.ShapeDtypeStruct
    small = sd((4, D), F32)
    device = lax.axis_index("dp").reshape(1)
    return pl.pallas_call(
        update_kernel,
        out_shape=(pltpu.HBM(result.shape, BF16), pltpu.HBM(result.shape, BF16), sd((1, 1), F32), sd(weights.shape, F32), sd(first.shape, F32), sd(first.shape, F32), small, small, small),
        in_specs=[SMEM] * 2 + [VM] * 13,
        out_specs=(HBM,) * 2 + (VM,) * 7,
        scratch_shapes=[pltpu.SemaphoreType.DMA((2,))],
        compiler_params=pltpu.CompilerParams(vmem_limit_bytes=16 << 20),
        name="clipped_update",
    )(owner_slot, device, result, grad_in, tot, gs, weights, first, second, ma, mb, moments, norm_params, norm_first, norm_second)


def adam_update(current, gradient, first_moment, second_moment, decay_rate, step_rate):
    first_new = BETA_ONE * first_moment + (1.0 - BETA_ONE) * gradient
    second_new = BETA_TWO * second_moment + (1.0 - BETA_TWO) * gradient * gradient
    first_fix = 1.0 - BETA_ONE**STEP
    second_fix = 1.0 - BETA_TWO**STEP
    direction = first_new / first_fix / (jnp.sqrt(second_new / second_fix) + ADAM_EPS)
    return (current - step_rate * (direction + decay_rate * current), first_new, second_new)


def from_peer(value, distance):
    return lax.ppermute(value, "mp", [(i, i ^ distance) for i in range(lax.axis_size("mp"))])


def shards(tokens, cotangent, segment_ids, padding, pattern, owner_slot, weights, first_moments, second_moments,
           norm_params, norm_first, norm_second):
    groups = lax.axis_size("mp")
    me = lax.axis_index("mp")
    frames_own = FRAMES // groups
    dp = lax.axis_size("dp")
    x, ct = tokens[0], cotangent[0]
    keep = 1.0 - lax.dynamic_slice_in_dim(padding, me * frames_own, frames_own, 1).astype(F32)
    h1, wq, wk, wv, own_shared, ma, mb = start_call(dp, x, norm_params, weights, first_moments, second_moments)
    shared = [own_shared, from_peer(own_shared, 2), from_peer(own_shared, 1)]
    o, ot, qa, ka, va, kt = attn_fwd(segment_ids, padding, pattern, h1, wq, wk, wv)
    result, dx2, do, *late, nb, moments = middle_call(dp, o, x, ct, keep, shared, norm_params, ma, mb)
    late = [late[0], from_peer(late[1], 2), from_peer(late[2], 3), from_peer(late[3], 1)]
    dh, early = attn_bwd(segment_ids, padding, pattern, qa, ka, va, kt, ot, do, h1, wq, wk, wv)
    grad_in, gs, tot = reduce_call(dp, dh, early, late, x, dx2, norm_params, nb)
    result, grad_in, grad_norm, new_weights, new_first, new_second, new_norm, new_norm_first, new_norm_second = update_call(
        owner_slot, result, grad_in, tot, gs, weights, first_moments, second_moments, ma, mb, moments, norm_params, norm_first, norm_second)
    return (result[None], grad_in[None], grad_norm[0, 0], new_weights, new_first, new_second,
            new_norm, new_norm_first, new_norm_second)


def solution(mesh):
    rows, blocks, slots = P("dp", "mp", None), P(None, "mp", None), P("dp", "mp", None)
    return jax.shard_map(
        shards,
        mesh=mesh,
        in_specs=(rows, rows, P("dp", None), P("dp", None), P(), P(), blocks, slots, slots, P(), P(), P()),
        out_specs=(rows, rows, P(), blocks, slots, slots, P(), P(), P()),
        check_vma=False,
    )
```

```python
import functools
import math

import jax
import jax.numpy as jnp
from jax import lax
from jax.experimental import pallas as pl
from jax.experimental.pallas import tpu as pltpu
from jax.sharding import PartitionSpec as P

FF = 1536
STEP = 10
NORM_EPS = 1e-05
BETA_ONE = 0.9
BETA_TWO = 0.95
ADAM_EPS = 1e-08
LEARN_RATE = 0.15
NORM_RATE = 0.6
WEIGHT_DECAY = 0.05

D = 384
HEAD_DIM = 24
FRAMES = 16
PATCHES = 196
FROWS = 208
FLANES = 256
HW = 32
HEADS_LOCAL = 4
WIDE = HEADS_LOCAL * HW
MASKED = -1e30
QSCALE = math.log2(math.e) / math.sqrt(HEAD_DIM)
F32 = jnp.float32
BF16 = jnp.bfloat16
NT = (((1,), (1,)), ((), ()))
TN = (((0,), (0,)), ((), ()))
HEADS = range(HEADS_LOCAL)
UNROLL = 4
TOGETHER = 4


def dot(a, b):
    return jnp.dot(a, b, preferred_element_type=F32)


def dot_nt(a, b):
    return lax.dot_general(a, b, NT, preferred_element_type=F32)


def dot_tn(a, b):
    return lax.dot_general(a, b, TN, preferred_element_type=F32)


def frame_rows(f):
    return pl.ds(pl.multiple_of(f * FROWS, 16), FROWS)


def frame_lanes(f, size=FLANES):
    return pl.ds(pl.multiple_of(f * FLANES, 128), size)


def head_rows(h):
    return slice(HW * h, HW * (h + 1))


def head_lanes(h):
    return slice(FLANES * h, FLANES * (h + 1))


def list_pairs(seg_ref, pad_ref, pat_ref, pairs_s):
    def rows(i, carry):
        start, count = carry
        start = jnp.where(seg_ref[0, i] == seg_ref[0, jnp.maximum(i - 1, 0)], start, i)

        def cols(j, count):
            pairs_s[count] = i * 32 + j
            return count + jnp.where((pat_ref[i, j] == 1) & (pad_ref[0, j] == 0), 1, 0)
        return start, lax.fori_loop(start, i, cols, count)
    _, count = lax.fori_loop(0, FRAMES, rows, (jnp.int32(0), jnp.int32(0)))
    for n in range(UNROLL):
        pairs_s[count + n] = FRAMES * 33
    return count


def each_pair(pairs_s, count, work):
    def step(n, _):
        codes = [pairs_s[n * UNROLL + u] for u in range(UNROLL)]
        work([(code // 32, code % 32) for code in codes])
        return 0
    lax.fori_loop(0, (count + UNROLL - 1) // UNROLL, step, 0)


def inside(f):
    return jnp.minimum(f, FRAMES - 1)


def split_rows(value, r32):
    high = value.astype(BF16).astype(F32)
    return jnp.where(r32 == 24, high, jnp.where(r32 == 25, value - high, 0.0))


def fwd_kernel(seg_ref, pad_ref, pat_ref, qt_ref, ka_ref, va_ref, kt_ref, vt_ref,
               o_hbm, ot_hbm, qa_hbm, ka_hbm, va_hbm, kt_hbm,
               o_ref, ot_ref, qa_ref, qe_s, m_s, acc_s, bad_s, pairs_s, out_sem):
    zpad = jnp.zeros((WIDE, FLANES - FROWS), F32)
    r32 = lax.broadcasted_iota(jnp.int32, (HW, FLANES), 0)
    by_rows = [(o_ref, o_hbm, 0)]
    by_lanes = [(ot_ref, ot_hbm, 1), (qa_ref, qa_hbm, 2)]
    saved = [pltpu.make_async_copy(src, dst, out_sem.at[n])
             for n, (src, dst) in enumerate(((ka_ref, ka_hbm), (va_ref, va_hbm), (kt_ref, kt_hbm)), 3)]
    for copy in saved:
        copy.start()
    qe_s[...] = jnp.zeros(qe_s.shape, BF16)
    count = list_pairs(seg_ref, pad_ref, pat_ref, pairs_s)

    def keep(f):
        for src, dst, n in by_rows:
            pltpu.make_async_copy(src.at[frame_rows(f), :], dst.at[frame_rows(f), :], out_sem.at[n]).start()
        for src, dst, n in by_lanes:
            pltpu.make_async_copy(src.at[:, frame_lanes(f)], dst.at[:, frame_lanes(f)], out_sem.at[n]).start()

    def scores(i, j):
        s = dot(ka_ref[frame_rows(inside(j)), :], qe_s[inside(i)])
        return [s[:, head_lanes(h)] for h in HEADS]

    def gathered(j, ps):
        return [dot(vt_ref[head_rows(h), frame_lanes(inside(j), FROWS)], ps[h]) for h in HEADS]

    def attend(exact):
        def prepare(f):
            qt = qt_ref[:, frame_lanes(f)].astype(F32)
            own = qt * jnp.concatenate([kt_ref[:, frame_lanes(f, FROWS)].astype(F32), zpad], axis=1)
            for h in HEADS:
                if exact:
                    start = jnp.zeros((1, FLANES), F32)
                else:
                    start = jnp.sum(own[head_rows(h)], axis=0, keepdims=True)
                    m_s[f, h] = start
                aug = jnp.where(r32 == 26, 1.0, split_rows(-start, r32))
                qe_s[f, head_rows(h), head_lanes(h)] = (qt[head_rows(h)] + aug).astype(BF16)

        def finalize(i):
            outs, augs = [], []
            for h in HEADS:
                a = acc_s[i, h]
                l = a[24:25, :]
                bad_s[...] = jnp.maximum(bad_s[...], jnp.where(l < 1e30, 0.0, 1.0))
                outs.append(jnp.where(r32 < HEAD_DIM, a * (1.0 / l), 0.0))
                lse = m_s[i, h] + jnp.log2(l)
                q = qe_s[i, head_rows(h), head_lanes(h)].astype(F32)
                augs.append(jnp.where((r32 == 24) | (r32 == 25), split_rows(-lse, r32), q))
            ot = jnp.concatenate(outs, axis=0)
            ot_ref[:, frame_lanes(i)] = ot.astype(BF16)
            qa_ref[:, frame_lanes(i)] = jnp.concatenate(augs, axis=0).astype(BF16)
            o_ref[frame_rows(i), :] = ot.T[:FROWS, :].astype(BF16)

        def attend_pairs(pairs, first):
            ss = [scores(i, j) for i, j in pairs]
            if exact:
                old = [None if first else [m_s[i, h] for h in HEADS] for i, _ in pairs]
                for n, (i, j) in enumerate(pairs):
                    if not first:
                        old[n] = [m_s[i, h] for h in HEADS]
                    top = [jnp.max(ss[n][h], axis=0, keepdims=True) for h in HEADS]
                    if not first:
                        top = [jnp.maximum(old[n][h], top[h]) for h in HEADS]
                    pv = gathered(j, [jnp.exp2(ss[n][h] - top[h]).astype(BF16) for h in HEADS])
                    for h in HEADS:
                        acc_s[i, h] = pv[h] if first else acc_s[i, h] * jnp.exp2(old[n][h] - top[h]) + pv[h]
                        m_s[i, h] = top[h]
                return
            ps = [[jnp.exp2(s[h]).astype(BF16) for h in HEADS] for s in ss]
            pvs = [gathered(j, p) for (_, j), p in zip(pairs, ps)]
            for (i, _), pv in zip(pairs, pvs):
                for h in HEADS:
                    acc_s[i, h] = pv[h] if first else acc_s[i, h] + pv[h]

        bad_s[...] = jnp.zeros(bad_s.shape, F32)
        for k in range(TOGETHER):
            prepare(k)

        def diagonal(n, _):
            attend_pairs([(n * TOGETHER + k,) * 2 for k in range(TOGETHER)], True)
            for k in range(TOGETHER):
                prepare(jnp.minimum((n + 1) * TOGETHER, FRAMES - TOGETHER) + k)
            return 0
        lax.fori_loop(0, FRAMES // TOGETHER, diagonal, 0)
        each_pair(pairs_s, count, lambda pairs: attend_pairs(pairs, False))

        def close(n, _):
            for k in range(TOGETHER):
                finalize(n * TOGETHER + k)
            for k in range(TOGETHER):
                keep(n * TOGETHER + k)
            return 0
        lax.fori_loop(0, FRAMES // TOGETHER, close, 0)
        for src, dst, n in by_rows + by_lanes:
            pltpu.make_async_copy(src, dst, out_sem.at[n]).wait()

    attend(False)

    @pl.when(jnp.max(bad_s[...]) > 0.0)
    def _():
        attend(True)
    for copy in saved:
        copy.wait()


SMEM = pl.BlockSpec(memory_space=pltpu.SMEM)
HBM = pl.BlockSpec(memory_space=pltpu.HBM)


def in_hbm(value):
    return pltpu.with_memory_space_constraint(value, pltpu.HBM)
VM = pl.BlockSpec(memory_space=pltpu.VMEM)


def attn_fwd(seg, pad, pat, qt, ka, va, kt, vt):
    V = pltpu.VMEM
    rows, lanes = (FRAMES * FROWS, WIDE), (WIDE, FRAMES * FLANES)
    return pl.pallas_call(
        fwd_kernel,
        out_shape=tuple(pltpu.HBM(shape, BF16) for shape in (rows, lanes, lanes, rows, rows, lanes)),
        in_specs=[SMEM] * 3 + [VM] * 5,
        out_specs=(HBM,) * 6,
        scratch_shapes=[V(rows, BF16), V(lanes, BF16), V(lanes, BF16), V((FRAMES, WIDE, HEADS_LOCAL * FLANES), BF16),
                        V((FRAMES + 1, HEADS_LOCAL, 1, FLANES), F32), V((FRAMES + 1, HEADS_LOCAL, HW, FLANES), F32),
                        V((1, FLANES), F32), pltpu.SMEM((128 + UNROLL,), jnp.int32), pltpu.SemaphoreType.DMA((6,))],
        compiler_params=pltpu.CompilerParams(vmem_limit_bytes=26 << 20),
        cost_estimate=pl.CostEstimate(flops=int(2.5e10), bytes_accessed=8 << 20, transcendentals=0),
        name="attend_forward",
    )(seg, pad, pat, qt, ka, va, kt, vt)


def bwd_kernel(seg_ref, pad_ref, pat_ref, qa_ref, ka_ref, va_ref, kt_ref, ot_ref, do_ref, h_ref, w_ref,
               dh_ref, early_ref, qe_s, oe_s, dq_s, dk_s, dv_s, dw_s, turn_s, blk_s, pairs_s):
    scale = HEAD_DIM ** -0.5
    for s in (qe_s, oe_s):
        s[...] = jnp.zeros(s.shape, BF16)
    count = list_pairs(seg_ref, pad_ref, pat_ref, pairs_s)
    dw_s[...] = jnp.zeros(dw_s.shape, F32)
    real = lax.broadcasted_iota(jnp.int32, (WIDE, FROWS), 0) % HW < HEAD_DIM
    r32 = lax.broadcasted_iota(jnp.int32, (HW, FLANES), 0)
    zpad = jnp.zeros((WIDE, FLANES - FROWS), F32)

    def prepare(i):
        t = i
        qt = qa_ref[:, frame_lanes(i)]
        dot_ = jnp.concatenate([do_ref[frame_rows(i), :].astype(F32).T, zpad], axis=1)
        prod = dot_ * ot_ref[:, frame_lanes(i)].astype(F32)
        for h in HEADS:
            d = -jnp.sum(prod[head_rows(h)], axis=0, keepdims=True)
            qe_s[t, head_rows(h), head_lanes(h)] = qt[head_rows(h)]
            oe_s[t, head_rows(h), head_lanes(h)] = (dot_[head_rows(h)] + split_rows(d, r32)).astype(BF16)

    def scores(i, j):
        t, u = inside(i), inside(j)
        s, dp = dot(ka_ref[frame_rows(u), :], qe_s[t]), dot(va_ref[frame_rows(u), :], oe_s[t])
        ps = [jnp.exp2(s[:, head_lanes(h)]) for h in HEADS]
        return [p.astype(BF16) for p in ps], [(ps[h] * dp[:, head_lanes(h)]).astype(BF16) for h in HEADS]

    def products(i, j, pb, ds):
        t, u = inside(i), inside(j)
        dq = [dot(kt_ref[head_rows(h), frame_lanes(u, FROWS)], ds[h]) for h in HEADS]
        dv = [dot_nt(oe_s[t, head_rows(h), head_lanes(h)], pb[h]) for h in HEADS]
        dk = [dot_nt(qe_s[t, head_rows(h), head_lanes(h)], ds[h]) for h in HEADS]
        return [jnp.concatenate(value, axis=0) for value in (dq, dk, dv)]

    def attend_pairs(pairs, first):
        made = [scores(i, j) for i, j in pairs]
        values = [products(i, j, pb, ds) for (i, j), (pb, ds) in zip(pairs, made)]
        for (i, j), value in zip(pairs, values):
            for ref, at, part in ((dq_s, frame_lanes(i), 0), (dk_s, frame_lanes(j, FROWS), 1), (dv_s, frame_lanes(j, FROWS), 2)):
                ref[:, at] = value[part] if first else ref[:, at] + value[part]

    def finish(f):
        parts = (dq_s[:, frame_lanes(f, FROWS)] * scale, dk_s[:, frame_lanes(f, FROWS)] * math.log(2.0), dv_s[:, frame_lanes(f, FROWS)])
        grads = jnp.concatenate([jnp.where(real, part, 0.0).astype(BF16) for part in parts], axis=0)
        dh_ref[frame_rows(f), :] = dot_tn(grads, w_ref[...]).astype(BF16)
        return dot(grads, h_ref[frame_rows(f), :])

    for k in range(TOGETHER):
        prepare(k)

    def diagonal(n, _):
        attend_pairs([(n * TOGETHER + k,) * 2 for k in range(TOGETHER)], True)
        for k in range(TOGETHER):
            prepare(jnp.minimum((n + 1) * TOGETHER, FRAMES - TOGETHER) + k)
        return 0
    lax.fori_loop(0, FRAMES // TOGETHER, diagonal, 0)
    each_pair(pairs_s, count, lambda pairs: attend_pairs(pairs, False))

    def close(n, _):
        dw = [finish(n * TOGETHER + k) for k in range(TOGETHER)]
        dw_s[...] += functools.reduce(jnp.add, dw)
        return 0
    lax.fori_loop(0, FRAMES // TOGETHER, close, 0)
    for b in range(3):
        turned = dw_s[b * WIDE:(b + 1) * WIDE, :].T
        turn_s[:, 0:96] = jnp.concatenate([turned[:, HW * h:HW * h + HEAD_DIM] for h in HEADS], axis=1)
        line = [turn_s[pl.ds(k, 96, stride=4), :][:, 0:96] for k in range(4)]
        blk_s[pl.ds(0, 96, stride=3), :] = jnp.concatenate([line[0], line[1][:, :32]], axis=1)
        blk_s[pl.ds(1, 96, stride=3), :] = jnp.concatenate([line[1][:, 32:], line[2][:, :64]], axis=1)
        blk_s[pl.ds(2, 96, stride=3), :] = jnp.concatenate([line[2][:, 64:], line[3]], axis=1)
        early_ref[288 * b:288 * (b + 1), :] = blk_s[...].astype(BF16)


def attn_bwd(seg, pad, pat, qa, ka, va, kt, ot, do, h, w):
    sd = jax.ShapeDtypeStruct
    V = pltpu.VMEM
    return pl.pallas_call(
        bwd_kernel,
        out_shape=(sd((FRAMES * FROWS, D), BF16), sd((3 * 288, 128), BF16)),
        in_specs=[SMEM] * 3 + [VM] * 8,
        out_specs=(VM,) * 2,
        scratch_shapes=[V((FRAMES, WIDE, HEADS_LOCAL * FLANES), BF16), V((FRAMES, WIDE, HEADS_LOCAL * FLANES), BF16)]
        + [V((WIDE, (FRAMES + 1) * FLANES), F32)] * 3
        + [V((3 * WIDE, D), F32), V((D, 128), F32), V((288, 128), F32),
           pltpu.SMEM((128 + UNROLL,), jnp.int32)],
        compiler_params=pltpu.CompilerParams(vmem_limit_bytes=42 << 20),
        cost_estimate=pl.CostEstimate(flops=int(5e10), bytes_accessed=12 << 20, transcendentals=0),
        name="attend_backward",
    )(seg, pad, pat, qa, ka, va, kt, ot, do, h, w)


MESH = pl.DeviceIdType.MESH
OWN_ROWS = 4 * FROWS


def place(d, m):
    return {"dp": d, "mp": m}


def remote(src, dst, send_sem, recv_sem, device):
    return pltpu.make_async_remote_copy(
        src_ref=src, dst_ref=dst, send_sem=send_sem, recv_sem=recv_sem, device_id=device, device_id_type=MESH
    )


def local(src, dst, sem):
    return pltpu.make_async_copy(src, dst, sem)


def greet(devices):
    barrier = pltpu.get_barrier_semaphore()
    for device in devices:
        pl.semaphore_signal(barrier, inc=1, device_id=device, device_id_type=MESH)
    return len(devices)


def met(count):
    pl.semaphore_wait(pltpu.get_barrier_semaphore(), count)


def group_peers():
    me = lax.axis_index("mp")
    return me, me ^ 1, me ^ 2, me ^ 3


def frame_part(device, c):
    return pl.ds(pl.multiple_of(device * OWN_ROWS + c * FROWS, 16), FROWS)


def normalised(v):
    centred = v - jnp.mean(v, axis=-1, keepdims=True)
    inv = lax.rsqrt(jnp.mean(centred * centred, axis=-1, keepdims=True) + NORM_EPS)
    return centred * inv, inv


def norm_pull(dy, hat, inv, gain):
    dg = dy * gain
    lead = jnp.mean(dg, axis=-1, keepdims=True)
    along = jnp.mean(dg * hat, axis=-1, keepdims=True)
    return inv * (dg - lead - hat * along)


def col_sum(v):
    return jnp.sum(v, axis=0, keepdims=True)


def load_frame(ref, c):
    base = c * PATCHES // 16 * 16
    rows = ref[base:base + FROWS, :].astype(F32)
    shift = c * PATCHES - base
    return pltpu.roll(rows, FROWS - shift, 0) if shift else rows


def live_rows():
    return lax.broadcasted_iota(jnp.int32, (FROWS, 1), 0) < PATCHES


def dp_peers(count):
    d = lax.axis_index("dp")
    side, line = d % 2, d // 2
    return side, line, {"dp": d ^ 1}, [lax.rem(line + n, count) for n in range(count)]


def start_kernel(count, x_hbm, np_hbm, w_hbm, m_hbm, v_hbm,
                 h_ref, qt_ref, ka_ref, va_ref, kt_ref, vt_ref, wa_ref, ws_ref, ma_ref, mb_ref,
                 x_ref, np_ref, w_ref, m_ref, v_ref, mo_s, w_s, load_x, load_w, keep_m,
                 send_x, recv_x, send_p, recv_p, send_f, recv_f, send_t, recv_t, send_l, recv_l):
    me, near, far, _ = group_peers()
    side, line, twin, around = dp_peers(count)
    frames = range(OWN_ROWS // FROWS)
    cuts = [0, 208, 400, 592, 784]
    loads = [local(x_hbm.at[a:b, :], x_ref.at[a:b, :], load_x.at[c]) for c, (a, b) in enumerate(zip(cuts, cuts[1:]))]
    others = [local(m_hbm, m_ref, load_w.at[0]), local(v_hbm, v_ref, load_w.at[1]), local(w_hbm, w_ref, load_w.at[2])]
    gains = local(np_hbm, np_ref, load_w.at[3])
    greeted = greet([{"mp": near}, {"mp": far}, twin] + [{"dp": q * 2 + side} for q in around[1:]])
    for copy in [gains] + loads + others:
        copy.start()
    live = live_rows()
    to_far, to_near, moments = [], [], []
    gains.wait()
    for c in frames:
        loads[c].wait()
        hat, _ = normalised(load_frame(x_ref, c))
        h_ref[frame_part(me, c), :] = jnp.where(live, hat * np_ref[0:1, :] + np_ref[1:2, :], 0.0).astype(BF16)
        rows = h_ref.at[frame_part(me, c), :]
        to_far.append(remote(rows, rows, send_x.at[c], recv_x.at[c], {"mp": far}))
        to_near.append(remote(rows, rows, send_p.at[c], recv_p.at[c], {"mp": near}))
        if c == 0:
            met(greeted)
        to_far[c].start()
        to_near[c].start()

    slots, rows = m_ref.shape[0], m_ref.shape[1]
    others[0].wait()
    others[1].wait()
    for r in range(2 * slots):
        mo_s[r // slots, pl.ds((r % slots) * rows, rows), :] = (v_ref if r % 2 else m_ref)[r // 2].astype(BF16)
    first, second = ma_ref.at[side, line], mb_ref.at[side]
    kept = [local(mo_s.at[0], first, keep_m.at[0]), local(mo_s.at[1], second, keep_m.at[1])]
    for n, q in enumerate(around[1:]):
        moments.append(remote(mo_s.at[0], first, send_l.at[n], recv_l.at[n], {"dp": q * 2 + side}))
    moments.append(remote(mo_s.at[0], first, send_t.at[0], recv_t.at[0], twin))
    moments.append(remote(mo_s.at[1], second, send_t.at[1], recv_t.at[1], twin))
    for copy in moments + kept:
        copy.start()

    def incoming(device, sends, recvs, c):
        rows = h_ref.at[frame_part(device, c), :]
        return remote(rows, rows, sends.at[c], recvs.at[c], {"mp": near})

    def forward(c):
        incoming(far, send_x, recv_x, c).wait_recv()
        copy = incoming(far, send_f, recv_f, c)
        copy.start()
        return copy

    others[2].wait()
    for b in range(3):
        a = [w_ref[b, pl.ds(k, 96, stride=3), :] for k in range(3)]
        lines = [a[0][:, :96], jnp.concatenate([a[0][:, 96:], a[1][:, :64]], axis=1),
                 jnp.concatenate([a[1][:, 64:], a[2][:, :32]], axis=1), a[2][:, 32:]]
        gap = jnp.zeros((96, HW - HEAD_DIM), F32)
        for k in range(4):
            parts = []
            for h in HEADS:
                parts += [lines[k][:, HEAD_DIM * h:HEAD_DIM * (h + 1)], gap]
            w_s[pl.ds(k, 96, stride=4), :] = jnp.concatenate(parts, axis=1)
        wa_ref[b * WIDE:(b + 1) * WIDE, :] = w_s[...].T.astype(BF16)

    col = lax.broadcasted_iota(jnp.int32, (FROWS, WIDE), 1) % HW
    ones = jnp.where((col == 24) | (col == 25), 1.0, 0.0)
    kadd = ones + jnp.where((col == 26) & jnp.logical_not(live), MASKED, 0.0)
    vtadd = jnp.where(lax.broadcasted_iota(jnp.int32, (WIDE, FROWS), 0) % HW == 24, 1.0, 0.0)
    zpad = jnp.zeros((WIDE, FLANES - FROWS), BF16)

    def project(devices, c):
        made = []
        for device in devices:
            hf = h_ref[frame_part(device, c), :]
            made.append((dot_nt(wa_ref[...], hf), dot_nt(hf, wa_ref[WIDE:3 * WIDE, :])))
        for device, (turned, lined) in zip(devices, made):
            f = device * (OWN_ROWS // FROWS) + c
            qt_ref[:, frame_lanes(f)] = jnp.concatenate([(turned[0:WIDE] * QSCALE).astype(BF16), zpad], axis=1)
            kt_ref[:, frame_lanes(f, FROWS)] = turned[WIDE:2 * WIDE].astype(BF16)
            vt_ref[:, frame_lanes(f, FROWS)] = (turned[2 * WIDE:3 * WIDE] + vtadd).astype(BF16)
            ka_ref[frame_rows(f), :] = (lined[:, 0:WIDE] + kadd).astype(BF16)
            va_ref[frame_rows(f), :] = (lined[:, WIDE:2 * WIDE] + ones).astype(BF16)

    copies = [forward(0)]
    for c in frames:
        incoming(near, send_p, recv_p, c).wait_recv()
        project((me, near), c)
    copies.append(forward(1))
    for b in range(3, w_ref.shape[0]):
        for k in range(3):
            lanes = slice(128 * k, 128 * (k + 1))
            part = w_ref[b, pl.ds(k, 96, stride=3), :]
            if b == 3:
                gap = jnp.zeros((HW - HEAD_DIM, 128), F32)
                parts = []
                for h in HEADS:
                    parts += [part[HEAD_DIM * h:HEAD_DIM * (h + 1)], gap]
                ws_ref[2 * D:2 * D + WIDE, lanes] = jnp.concatenate(parts, axis=0).astype(BF16)
            else:
                ws_ref[96 * (b - 4):96 * (b - 3), lanes] = part.astype(BF16)
    for c in frames:
        incoming(near ^ 2, send_f, recv_f, c).wait_recv()
        project((far, near ^ 2), c)
        if c + 2 < len(frames):
            copies.append(forward(c + 2))
    for n in range(1, count):
        part = ma_ref.at[side, around[count - n]]
        remote(part, part, send_l.at[n - 1], recv_l.at[n - 1], twin).wait_recv()
    part = ma_ref.at[1 - side, line]
    remote(part, part, send_t.at[0], recv_t.at[0], twin).wait_recv()
    part = mb_ref.at[1 - side]
    remote(part, part, send_t.at[1], recv_t.at[1], twin).wait_recv()
    for copy in kept:
        copy.wait()
    for copy in to_far + to_near + copies + moments:
        copy.wait_send()


def start_call(dp, x, norm_params, weights, first_moments, second_moments):
    sd, V, S = jax.ShapeDtypeStruct, pltpu.VMEM, pltpu.SemaphoreType.DMA
    blocks, count = weights.shape[0], dp // 2
    half = first_moments.shape[0] * first_moments.shape[1]
    rows, lanes = sd((FRAMES * FROWS, WIDE), BF16), sd((WIDE, FRAMES * FLANES), BF16)
    return pl.pallas_call(
        functools.partial(start_kernel, count),
        out_shape=(sd((FRAMES * FROWS, D), BF16), lanes, rows, rows, lanes, lanes, sd((3 * WIDE, D), BF16),
                   sd((WIDE + 96 * (blocks - 4), D), BF16),
                   pltpu.HBM((2, count, half, 128), BF16), pltpu.HBM((2, half, 128), BF16)),
        in_specs=[HBM] * 5,
        out_specs=(VM,) * 8 + (HBM,) * 2,
        scratch_shapes=[V(x.shape, BF16), V(norm_params.shape, F32), V(weights.shape, F32), V(first_moments.shape, F32),
                        V(first_moments.shape, F32), V((2, half, 128), BF16), V((D, WIDE), F32),
                        S((4,)), S((4,)), S((2,))] + [S((4,))] * 6 + [S((2,))] * 2 + [S((count,))] * 2,
        compiler_params=pltpu.CompilerParams(vmem_limit_bytes=24 << 20, collective_id=1, has_side_effects=True),
        name="norm_and_gather",
    )(*[in_hbm(value) for value in (x, norm_params, weights, first_moments, second_moments)])


def gelu_parts(u):
    lead = math.sqrt(2.0 / math.pi)
    bend = lead * 0.044715
    square = u * u
    half = 0.5 + 0.5 * jnp.tanh(u * (lead + bend * square))
    slope = half + 2.0 * u * (half - half * half) * (lead + 3.0 * bend * square)
    return u * half, slope


def middle_kernel(count, o_ref, x_hbm, ct_hbm, pad_ref, w0_ref, w1_ref, w3_ref, np_hbm, ma_ref, mb_ref,
                  out_ref, dx2_ref, do_ref, l0_ref, l1_ref, l2_ref, l3_ref, nb_ref, mom_ref,
                  ob_s, dob_s, g_s, a_s, du_s, da_s, h2_s, dxa_s, blk_s, res_s, ut_s, wot_s,
                  x_ref, ct_ref, o_s, w2_ref, np_ref, load_s, send_w, recv_w,
                  send_o, recv_o, send_d, recv_d, send_t, recv_t, send_l, recv_l, send_f, recv_f):
    me, near, far, across = group_peers()
    side, line, twin, around = dp_peers(count)
    peers = (far, across, near)
    mine = pl.ds(pl.multiple_of(me * OWN_ROWS, 16), OWN_ROWS)
    loads = [local(ct_hbm, ct_ref, load_s.at[0]), local(x_hbm, x_ref, load_s.at[1]), local(o_ref.at[mine, :], o_s, load_s.at[2]), local(np_hbm, np_ref, load_s.at[3])]
    greeted = greet([{"mp": p} for p in peers] + [twin] + [{"dp": q * 2 + side} for q in around[1:]])
    for copy in loads:
        copy.start()
    frames = range(OWN_ROWS // FROWS)
    live = live_rows()
    shards_w = (w0_ref, w1_ref, w2_ref, w3_ref)
    late = (l0_ref, l1_ref, l2_ref, l3_ref)
    places = range(len(shards_w))
    loads[0].wait()
    for c in frames:
        rows = slice(c * FROWS, (c + 1) * FROWS)
        g_s[rows, :] = jnp.where(live, load_frame(ct_ref, c) * (1 - pad_ref[0, me * len(frames) + c]).astype(F32), 0.0).astype(BF16)
    met(greeted)
    outgoing = []
    for c in frames:
        for n, p in enumerate(peers):
            outgoing.append(remote(o_ref.at[frame_part(p, c), :], ob_s.at[n, pl.ds(c * FROWS, FROWS), :],
                                   send_o.at[n, c], recv_o.at[n, c], {"mp": p}))
            outgoing[-1].start()
    weights = remote(w1_ref, w2_ref, send_w.at[0], recv_w.at[0], {"mp": near})
    weights.start()
    moments = []
    for n, q in enumerate(around[1:]):
        own_half = mb_ref.at[side]
        moments.append(remote(own_half, mom_ref.at[1, side, line], send_l.at[n], recv_l.at[n], {"dp": q * 2 + side}))
        moments.append(remote(ma_ref.at[side, q], mom_ref.at[0, side, q], send_t.at[q], recv_t.at[q], twin))
    for copy in moments:
        copy.start()

    def pass_moments(n):
        q = around[count - n]
        part = mom_ref.at[1, side, q]
        remote(part, part, send_l.at[n - 1], recv_l.at[n - 1], twin).wait_recv()
        moments.append(remote(part, part, send_f.at[q], recv_f.at[q], twin))
        moments[-1].start()

    def w_up(m):
        return shards_w[m][0:D, :]

    def w_down(m):
        return shards_w[m][D:2 * D, :]

    def w_o(m):
        return shards_w[m][2 * D:2 * D + WIDE, :]

    def cols(m):
        return slice(m * D, (m + 1) * D)

    for m in (0, 1, 3, 2):
        if m == 2:
            weights.wait_recv()
        da_s[:, cols(m)] = dot_nt(g_s[...], w_down(m))
        ut_s[cols(m), :] = w_up(m).astype(F32).T.astype(BF16)
        wot_s[:, m * WIDE:(m + 1) * WIDE] = w_o(m).astype(F32).T.astype(BF16)
    for copy in loads[1:]:
        copy.wait()
    nb_ref[...] = jnp.zeros(nb_ref.shape, F32)
    down = jnp.concatenate([w_down(m) for m in places], axis=0)
    out_w = jnp.concatenate([w_o(m) for m in places], axis=0)
    sent = []
    for pair in range(len(frames) // 2):
        both = (2 * pair, 2 * pair + 1)
        rows = slice(2 * pair * FROWS, 2 * (pair + 1) * FROWS)
        for c in both:
            for n, p in enumerate(peers):
                part = ob_s.at[n, pl.ds(c * FROWS, FROWS), :]
                remote(part, part, send_o.at[n, c], recv_o.at[n, c], {"mp": p}).wait_recv()
        own_rows = pl.ds(pl.multiple_of(me * OWN_ROWS + 2 * pair * FROWS, 16), 2 * FROWS)
        heads = jnp.concatenate([o_s[rows, :]] + [ob_s[n, rows, :] for n in range(len(peers))], axis=1)
        x2 = jnp.concatenate([load_frame(x_ref, c) for c in both], axis=0) + dot(heads, out_w)
        x2 = jnp.where(jnp.concatenate([live, live], axis=0), x2, 0.0)
        hat, inv = normalised(x2)
        h2 = (hat * np_ref[2:3, :] + np_ref[3:4, :]).astype(BF16)
        h2_s[rows, :] = h2
        for m in places:
            value, slope = gelu_parts(dot(h2, w_up(m)))
            a_s[rows, cols(m)] = value.astype(BF16)
            du_s[rows, cols(m)] = (da_s[rows, cols(m)] * slope).astype(BF16)
        result = x2 + dot(a_s[rows, :], down)
        for k, c in enumerate(both):
            res_s[pl.ds(c * PATCHES, FROWS), :] = result[k * FROWS:(k + 1) * FROWS]
        dh2 = dot(du_s[rows, :], ut_s[...])
        nb_ref[0:1, :] += col_sum(dh2 * hat)
        nb_ref[1:2, :] += col_sum(dh2)
        dx2 = g_s[rows, :].astype(F32) + norm_pull(dh2, hat, inv, np_ref[2:3, :])
        dx2_ref[rows, :] = dx2
        dxa = dx2.astype(BF16)
        dxa_s[rows, :] = dxa
        d_heads = dot(dxa, wot_s[...]).astype(BF16)
        for n in range(len(peers)):
            dob_s[n, rows, :] = d_heads[:, (n + 1) * WIDE:(n + 2) * WIDE]
        for c in both:
            for n, p in enumerate(peers):
                sent.append(remote(dob_s.at[n, pl.ds(c * FROWS, FROWS), :], do_ref.at[frame_part(me, c), :],
                                   send_d.at[n, c], recv_d.at[n, c], {"mp": p}))
                sent[-1].start()
        do_ref[own_rows, :] = d_heads[:, 0:WIDE]
        for c in both:
            if 0 < c < count:
                pass_moments(c)
    for n in range(len(frames), count):
        pass_moments(n)
    out_ref[...] = res_s[0:out_ref.shape[0], :].astype(BF16)

    def as_block(shard, first, value):
        size = value.shape[0]
        for k in range(3):
            blk_s[pl.ds(k, size, stride=3), :] = value[:, 128 * k:128 * (k + 1)]
        late[shard][first * 288:first * 288 + 3 * size, :] = blk_s[0:3 * size, :].astype(BF16)

    def drop_gaps(value):
        return jnp.concatenate([value[HW * h:HW * h + HEAD_DIM] for h in HEADS], axis=0)

    dw1 = dot_tn(h2_s[...], du_s[...])
    dw2 = dot_tn(g_s[...], a_s[...])
    for m in places:
        as_block(m, 1, dw1[:, cols(m)])
        as_block(m, 5, dw2[:, cols(m)].T)
        o_m = o_s[...] if m == 0 else ob_s[m - 1]
        as_block(m, 0, drop_gaps(dot_tn(o_m, dxa_s[...])))
    for c in frames:
        for n, p in enumerate(peers):
            part = do_ref.at[frame_part(p, c), :]
            remote(part, part, send_d.at[n, c], recv_d.at[n, c], {"mp": p}).wait_recv()
    for q in around[1:]:
        for half, sends, recvs in ((0, send_t, recv_t), (1, send_f, recv_f)):
            part = mom_ref.at[half, 1 - side, q]
            remote(part, part, sends.at[q], recvs.at[q], twin).wait_recv()
    for copy in outgoing + sent + moments + [weights]:
        copy.wait_send()


def middle_call(dp, o, x, ct, padding, w, norm_params, ma, mb):
    sd = jax.ShapeDtypeStruct
    V, S = pltpu.VMEM, pltpu.SemaphoreType.DMA
    count = dp // 2
    late = sd((9 * 288, 128), BF16)
    return pl.pallas_call(
        functools.partial(middle_kernel, count),
        out_shape=(sd(x.shape, BF16), sd((OWN_ROWS, D), F32), sd((FRAMES * FROWS, WIDE), BF16),
                   late, late, late, late, sd((2, D), F32), pltpu.HBM((2,) + ma.shape, BF16)),
        in_specs=[HBM, HBM, HBM, SMEM] + [VM] * 3 + [HBM] * 3,
        out_specs=(VM,) * 8 + (HBM,),
        scratch_shapes=[V((3, OWN_ROWS, WIDE), BF16), V((3, OWN_ROWS, WIDE), BF16), V((OWN_ROWS, D), BF16),
                        V((OWN_ROWS, FF), BF16), V((OWN_ROWS, FF), BF16), V((OWN_ROWS, FF), F32),
                        V((OWN_ROWS, D), BF16), V((OWN_ROWS, D), BF16), V((1152, 128), F32), V((OWN_ROWS, D), F32),
                        V((FF, D), BF16), V((D, 4 * WIDE), BF16),
                        V(x.shape, BF16), V(x.shape, BF16), V((OWN_ROWS, WIDE), BF16), V(w[0].shape, BF16), V(norm_params.shape, F32), S((4,)), S((1,)), S((1,)), S((3, 4)), S((3, 4)), S((3, 4)), S((3, 4))] + [S((count,))] * 6,
        compiler_params=pltpu.CompilerParams(vmem_limit_bytes=36 << 20, collective_id=2, has_side_effects=True),
        cost_estimate=pl.CostEstimate(flops=int(6e9), bytes_accessed=12 << 20, transcendentals=0),
        name="feed_forward",
    )(in_hbm(o), in_hbm(x), in_hbm(ct), padding, *w, in_hbm(norm_params), in_hbm(ma), in_hbm(mb))


def reduce_kernel(dp, piece, dh_ref, early_ref, l0_ref, l1_ref, l2_ref, l3_ref, x_ref, dx2_ref, np_ref, nb_ref,
                  gin_ref, gs_ref, tot_ref,
                  res_s, pb_s, xs_s, xb_s, g_s, yb_s, zs_s, zb_s, msg_s, mb_s, dm_s, db_s,
                  send_p, recv_p, send_x, recv_x, send_y, recv_y, send_z, recv_z,
                  send_a, recv_a, send_w, recv_w, send_m, recv_m, send_n, recv_n):
    me, near, far, across = group_peers()
    d = lax.axis_index("dp")
    count = dp // 2
    side, line = d % 2, d // 2
    twin = {"dp": d ^ 1}

    order, top = [], count
    while top > 1:
        top //= 2
        order += range(top, 2 * top)
    turns = [line ^ n for n in order]
    cut = -(-piece // 32) * 16
    halves = [(0, cut), (cut, piece - cut)]

    def line_device(q):
        return {"dp": q * 2 + side}

    frames = range(OWN_ROWS // FROWS)
    greeted = greet([{"mp": near}, {"mp": far}, {"mp": across}] + [{"dp": d ^ n} for n in range(1, dp)])
    total = early_ref.shape[0] + l0_ref.shape[0]
    g_s[0:early_ref.shape[0], :] = early_ref[...]
    g_s[early_ref.shape[0]:total, :] = (l0_ref[...].astype(F32) + l1_ref[...].astype(F32)
                                        + (l2_ref[...].astype(F32) + l3_ref[...].astype(F32))).astype(BF16)
    if g_s.shape[0] > total:
        g_s[total:, :] = jnp.zeros((g_s.shape[0] - total, 128), BF16)
    met(greeted)

    def own(c):
        return pl.ds(c * FROWS, FROWS)

    to_near = []
    for k, target in ((1, across), (0, near)):
        for c in frames:
            to_near.append(remote(dh_ref.at[frame_part(target, c), :], pb_s.at[k, own(c), :],
                                  send_p.at[k, c], recv_p.at[k, c], {"mp": near}))
            to_near[-1].start()

    def at(s, q, k):
        return pl.ds(pl.multiple_of((s * count + q) * piece + halves[k][0], 16), halves[k][1])

    def part(ref, q, k):
        return ref.at[q, pl.ds(*halves[k]), :]

    to_twin = []
    for q in turns + [line]:
        for k in range(2):
            to_twin.append(remote(g_s.at[at(1 - side, q, k), :], part(yb_s, q, k), send_y.at[q, k], recv_y.at[q, k], twin))
            to_twin[-1].start()

    to_far = []
    for c in frames:
        remote(pb_s.at[1, own(c), :], pb_s.at[1, own(c), :], send_p.at[1, c], recv_p.at[1, c], {"mp": near}).wait_recv()
        xs_s[own(c), :] = (dh_ref[frame_part(far, c), :].astype(F32) + pb_s[1, own(c), :].astype(F32)).astype(BF16)
        to_far.append(remote(xs_s.at[own(c), :], xb_s.at[own(c), :], send_x.at[c], recv_x.at[c], {"mp": far}))
        to_far[-1].start()

    to_line = []
    for q in turns + [line]:
        for k in range(2):
            got = part(yb_s, q, k)
            remote(got, got, send_y.at[q, k], recv_y.at[q, k], twin).wait_recv()
            rows = pl.ds(*halves[k])
            zs_s[q, rows, :] = (g_s[at(side, q, k), :].astype(F32) + yb_s[q, rows, :].astype(F32)).astype(BF16)
            if q is not line:
                to_line.append(remote(part(zs_s, q, k), part(zb_s, line, k), send_z.at[q, k], recv_z.at[line, k], line_device(q)))
                to_line[-1].start()
    spread, passed = [], []
    squares = jnp.zeros((1, 128), F32)
    for k in range(2):
        rows = pl.ds(*halves[k])
        mine = zs_s[line, rows, :].astype(F32)
        for q in turns:
            got = part(zb_s, q, k)
            remote(got, got, send_z.at[q, k], recv_z.at[q, k], line_device(q)).wait_recv()
            mine = mine + zb_s[q, rows, :].astype(F32)
        mine = mine.astype(BF16)
        gs_ref[at(side, line, k), :] = mine
        whole = gs_ref.at[at(side, line, k), :]
        for q in turns:
            spread.append(remote(whole, whole, send_a.at[q, k], recv_a.at[line, k], line_device(q)))
        passed.append(remote(whole, whole, send_w.at[line, k], recv_w.at[line, k], twin))
        for copy in spread[-len(turns):] + passed[-1:]:
            copy.start()
        mine = mine.astype(F32)
        squares = squares + col_sum(mine * mine)

    live = live_rows()
    gain, bias = jnp.zeros((1, D), F32), jnp.zeros((1, D), F32)
    for c in frames:
        remote(pb_s.at[0, own(c), :], pb_s.at[0, own(c), :], send_p.at[0, c], recv_p.at[0, c], {"mp": near}).wait_recv()
        remote(xb_s.at[own(c), :], xb_s.at[own(c), :], send_x.at[c], recv_x.at[c], {"mp": far}).wait_recv()
        dy = dh_ref[frame_part(me, c), :].astype(F32) + pb_s[0, own(c), :].astype(F32) + xb_s[own(c), :].astype(F32)
        dy = jnp.where(live, dy, 0.0)
        hat, inv = normalised(load_frame(x_ref, c))
        gain = gain + col_sum(dy * hat)
        bias = bias + col_sum(dy)
        res_s[pl.ds(c * PATCHES, FROWS), :] = dx2_ref[own(c), :] + norm_pull(dy, hat, inv, np_ref[0:1, :])
    gin_ref[...] = res_s[0:gin_ref.shape[0], :].astype(BF16)

    msg_s[...] = jnp.zeros(msg_s.shape, F32)
    msg_s[0:1, :] = gain
    msg_s[1:2, :] = bias
    msg_s[2:4, :] = nb_ref[...]
    msg_s[4:5, 0:128] = squares
    small = []
    for n, p in enumerate((near, far, across)):
        small.append(remote(msg_s, mb_s.at[n], send_m.at[n], recv_m.at[n], {"mp": p}))
        small[-1].start()

    def pass_on(q, k):
        piece_at = gs_ref.at[at(side, q, k), :]
        remote(piece_at, piece_at, send_a.at[q, k], recv_a.at[q, k], line_device(q)).wait_recv()
        passed.append(remote(piece_at, piece_at, send_w.at[q, k], recv_w.at[q, k], twin))
        passed[-1].start()

    pass_on(turns[0], 0)
    add = msg_s[...]
    for n, p in enumerate((near, far, across)):
        remote(mb_s.at[n], mb_s.at[n], send_m.at[n], recv_m.at[n], {"mp": p}).wait_recv()
        add = add + mb_s[n]
    dm_s[...] = add
    for n in range(1, dp):
        small.append(remote(dm_s, db_s.at[n], send_n.at[n], recv_n.at[n], {"dp": d ^ n}))
        small[-1].start()
    for k in range(2):
        for q in turns[1 - k:]:
            pass_on(q, k)
    for n in range(1, dp):
        remote(db_s.at[n], db_s.at[n], send_n.at[n], recv_n.at[n], {"dp": d ^ n}).wait_recv()
        add = add + db_s[n]
    tot_ref[...] = add
    for k in range(2):
        for q in turns + [line]:
            piece_at = gs_ref.at[at(1 - side, q, k), :]
            remote(piece_at, piece_at, send_w.at[q, k], recv_w.at[q, k], twin).wait_recv()
    for copy in to_near + to_twin + to_far + to_line + spread + passed + small:
        copy.wait_send()


def reduce_call(dp, dh, early, late, x, dx2, norm_params, nb):
    sd = jax.ShapeDtypeStruct
    V, S = pltpu.VMEM, pltpu.SemaphoreType.DMA
    rows = early.shape[0] + late[0].shape[0]
    count = dp // 2
    piece = -(-rows // (2 * count * 16)) * 16
    held = 2 * count * piece
    return pl.pallas_call(
        functools.partial(reduce_kernel, dp, piece),
        out_shape=(sd(x.shape, BF16), sd((held, 128), BF16), sd((8, D), F32)),
        in_specs=[VM] * 10,
        out_specs=(VM,) * 3,
        scratch_shapes=[V((OWN_ROWS, D), F32), V((2, OWN_ROWS, D), BF16), V((OWN_ROWS, D), BF16), V((OWN_ROWS, D), BF16), V((held, 128), BF16),
                        V((count, piece, 128), BF16), V((count, piece, 128), BF16), V((count, piece, 128), BF16),
                        V((8, D), F32), V((3, 8, D), F32), V((8, D), F32), V((dp, 8, D), F32),
                        S((2, 4)), S((2, 4)), S((4,)), S((4,))] + [S((count, 2))] * 8 + [S((3,)), S((3,)), S((dp,)), S((dp,))],
        compiler_params=pltpu.CompilerParams(vmem_limit_bytes=22 << 20, collective_id=3, has_side_effects=True),
        name="reduce_gradients",
    )(dh, early, *late, x, dx2, norm_params, nb)


def update_kernel(slot_ref, dev_ref, res_ref, gin_ref, tot_ref, gs_ref, w_ref, m_ref, v_ref, ma_ref, mb_ref, mom_ref, np_ref, nm_ref, nv_ref,
                  out_ref, gout_ref, norm_ref, nw_ref, nf_ref, ns_ref, nn_ref, nnf_ref, nns_ref, sem_s):
    carried = [local(res_ref, out_ref, sem_s.at[0]), local(gin_ref, gout_ref, sem_s.at[1])]
    for copy in carried:
        copy.start()
    blocks, rows, _ = w_ref.shape
    slots = m_ref.shape[0]
    tot = tot_ref[...]
    grads = tot[0:4, :]
    norm = jnp.sqrt(jnp.sum(grads * grads, keepdims=True) + jnp.sum(tot[4:5, 0:128], keepdims=True))
    norm_ref[...] = norm
    clip_level = 0.5 * (4 * D * D + 2 * D * FF + 4 * D) ** 0.5
    factor = jnp.minimum(1.0, clip_level / norm)
    nn_ref[...], nnf_ref[...], nns_ref[...] = adam_update(
        np_ref[...], grads * factor, nm_ref[...], nv_ref[...], 0.0, NORM_RATE)

    def block(b):
        return gs_ref[pl.ds(pl.multiple_of(b * rows, 16), rows), :].astype(F32) * factor

    def step(b, _):
        holder, first = slot_ref[b] // slots, slot_ref[b] % slots * 2
        side, line = holder % 2, holder // 2
        on_side, on_line = side == dev_ref[0] % 2, line == dev_ref[0] // 2

        def moment(r):
            at = pl.ds(pl.multiple_of(r % slots * rows, 16), rows)
            late = mom_ref[r // slots, side, line, at, :]
            lead = jnp.where(on_side | on_line, ma_ref[side, line, at, :], late)
            rest = jnp.where(on_line, mb_ref[side, at, :], late)
            return jnp.where(r < slots, lead, rest).astype(F32)

        old = [moment(first), moment(first + 1)]
        nw_ref[b], _, _ = adam_update(w_ref[b], block(b), old[0], old[1], WEIGHT_DECAY, LEARN_RATE)
        return 0
    lax.fori_loop(0, blocks, step, 0)
    for s in range(slots):
        owned = jnp.int32(-1)
        for b in range(blocks):
            owned = jnp.where(slot_ref[b] == dev_ref[0] * slots + s, b, owned)
        _, first, second = adam_update(0.0, block(jnp.maximum(owned, 0)), m_ref[s], v_ref[s], 0.0, LEARN_RATE)
        nf_ref[s] = jnp.where(owned >= 0, first, m_ref[s])
        ns_ref[s] = jnp.where(owned >= 0, second, v_ref[s])
    for copy in carried:
        copy.wait()


def update_call(owner_slot, result, grad_in, tot, gs, weights, first, second, ma, mb, moments, norm_params, norm_first, norm_second):
    sd = jax.ShapeDtypeStruct
    small = sd((4, D), F32)
    device = lax.axis_index("dp").reshape(1)
    return pl.pallas_call(
        update_kernel,
        out_shape=(pltpu.HBM(result.shape, BF16), pltpu.HBM(result.shape, BF16), sd((1, 1), F32), sd(weights.shape, F32), sd(first.shape, F32), sd(first.shape, F32), small, small, small),
        in_specs=[SMEM] * 2 + [VM] * 13,
        out_specs=(HBM,) * 2 + (VM,) * 7,
        scratch_shapes=[pltpu.SemaphoreType.DMA((2,))],
        compiler_params=pltpu.CompilerParams(vmem_limit_bytes=16 << 20),
        name="clipped_update",
    )(owner_slot, device, result, grad_in, tot, gs, weights, first, second, ma, mb, moments, norm_params, norm_first, norm_second)


def adam_update(current, gradient, first_moment, second_moment, decay_rate, step_rate):
    first_new = BETA_ONE * first_moment + (1.0 - BETA_ONE) * gradient
    second_new = BETA_TWO * second_moment + (1.0 - BETA_TWO) * gradient * gradient
    first_fix = 1.0 / (1.0 - BETA_ONE**STEP)
    second_fix = 1.0 / (1.0 - BETA_TWO**STEP)
    direction = first_new * (step_rate * first_fix) / (jnp.sqrt(second_new * second_fix) + ADAM_EPS)
    return (current * (1.0 - step_rate * decay_rate) - direction, first_new, second_new)


def from_peer(value, distance):
    return lax.ppermute(value, "mp", [(i, i ^ distance) for i in range(lax.axis_size("mp"))])


def shards(tokens, cotangent, segment_ids, padding, pattern, owner_slot, weights, first_moments, second_moments,
           norm_params, norm_first, norm_second):
    dp = lax.axis_size("dp")
    x, ct = tokens[0], cotangent[0]
    h1, qt, ka, va, kt, vt, wa, own_shared, ma, mb = start_call(dp, x, norm_params, weights, first_moments, second_moments)
    shared = [own_shared, from_peer(own_shared, 2), from_peer(own_shared, 1)]
    o, ot, qa, ka, va, kt = attn_fwd(segment_ids, padding, pattern, qt, ka, va, kt, vt)
    result, dx2, do, *late, nb, moments = middle_call(dp, o, x, ct, padding, shared, norm_params, ma, mb)
    late = [late[0], from_peer(late[1], 2), from_peer(late[2], 3), from_peer(late[3], 1)]
    dh, early = attn_bwd(segment_ids, padding, pattern, qa, ka, va, kt, ot, do, h1, wa)
    grad_in, gs, tot = reduce_call(dp, dh, early, late, x, dx2, norm_params, nb)
    result, grad_in, grad_norm, new_weights, new_first, new_second, new_norm, new_norm_first, new_norm_second = update_call(
        owner_slot, result, grad_in, tot, gs, weights, first_moments, second_moments, ma, mb, moments, norm_params, norm_first, norm_second)
    return (result[None], grad_in[None], grad_norm[0, 0], new_weights, new_first, new_second,
            new_norm, new_norm_first, new_norm_second)


def solution(mesh):
    rows, blocks, slots = P("dp", "mp", None), P(None, "mp", None), P("dp", "mp", None)
    return jax.shard_map(
        shards,
        mesh=mesh,
        in_specs=(rows, rows, P("dp", None), P("dp", None), P(), P(), blocks, slots, slots, P(), P(), P()),
        out_specs=(rows, rows, P(), blocks, slots, slots, P(), P(), P()),
        check_vma=False,
    )
```

```python
import functools
import math

import jax
import jax.numpy as jnp
from jax import lax
from jax.experimental import pallas as pl
from jax.experimental.pallas import tpu as pltpu
from jax.sharding import PartitionSpec as P

FF = 1536
STEP = 10
NORM_EPS = 1e-05
BETA_ONE = 0.9
BETA_TWO = 0.95
ADAM_EPS = 1e-08
LEARN_RATE = 0.15
NORM_RATE = 0.6
WEIGHT_DECAY = 0.05

D = 384
HEAD_DIM = 24
FRAMES = 16
PATCHES = 196
FROWS = 208
FLANES = 256
HW = 32
HEADS_LOCAL = 4
WIDE = HEADS_LOCAL * HW
MASKED = -1e30
QSCALE = math.log2(math.e) / math.sqrt(HEAD_DIM)
F32 = jnp.float32
BF16 = jnp.bfloat16
NT = (((1,), (1,)), ((), ()))
TN = (((0,), (0,)), ((), ()))
HEADS = range(HEADS_LOCAL)
UNROLL = 6
TOGETHER = 4


def dot(a, b):
    return jnp.dot(a, b, preferred_element_type=F32)


def dot_nt(a, b):
    return lax.dot_general(a, b, NT, preferred_element_type=F32)


def dot_tn(a, b):
    return lax.dot_general(a, b, TN, preferred_element_type=F32)


def frame_rows(f):
    return pl.ds(pl.multiple_of(f * FROWS, 16), FROWS)


def frame_lanes(f, size=FLANES):
    return pl.ds(pl.multiple_of(f * FLANES, 128), size)


def head_rows(h):
    return slice(HW * h, HW * (h + 1))


def head_lanes(h):
    return slice(FLANES * h, FLANES * (h + 1))


def list_pairs(seg_ref, pad_ref, pat_ref, pairs_s):
    def rows(i, carry):
        start, count = carry
        start = jnp.where(seg_ref[0, i] == seg_ref[0, jnp.maximum(i - 1, 0)], start, i)

        def cols(j, count):
            pairs_s[count] = i * 32 + j
            return count + jnp.where((pat_ref[i, j] == 1) & (pad_ref[0, j] == 0), 1, 0)
        return start, lax.fori_loop(start, i, cols, count)
    _, count = lax.fori_loop(0, FRAMES, rows, (jnp.int32(0), jnp.int32(0)))
    for n in range(UNROLL):
        pairs_s[count + n] = FRAMES * 33
    return count


def each_pair(pairs_s, count, work):
    def step(first, size):
        def body(n, _):
            codes = [pairs_s[first + n * size + u] for u in range(size)]
            work([(code // 32, code % 32) for code in codes])
            return 0
        return body
    whole = count // UNROLL
    lax.fori_loop(0, whole, step(0, UNROLL), 0)
    lax.fori_loop(0, (count - whole * UNROLL + 1) // 2, step(whole * UNROLL, 2), 0)


def inside(f):
    return jnp.minimum(f, FRAMES - 1)


def split_rows(value, r32):
    high = value.astype(BF16).astype(F32)
    return jnp.where(r32 == 24, high, jnp.where(r32 == 25, value - high, 0.0))


def fwd_kernel(seg_ref, pad_ref, pat_ref, qt_ref, ka_ref, va_ref, kt_ref, vt_ref,
               o_hbm, ot_hbm, qa_hbm, ka_hbm, va_hbm, kt_hbm,
               o_ref, ot_ref, qa_ref, qe_s, m_s, acc_s, bad_s, pairs_s, out_sem):
    zpad = jnp.zeros((WIDE, FLANES - FROWS), F32)
    r32 = lax.broadcasted_iota(jnp.int32, (HW, FLANES), 0)
    by_rows = [(o_ref, o_hbm, 0)]
    by_lanes = [(ot_ref, ot_hbm, 1), (qa_ref, qa_hbm, 2)]
    saved = [pltpu.make_async_copy(src, dst, out_sem.at[n])
             for n, (src, dst) in enumerate(((ka_ref, ka_hbm), (va_ref, va_hbm), (kt_ref, kt_hbm)), 3)]
    for copy in saved:
        copy.start()
    qe_s[...] = jnp.zeros(qe_s.shape, BF16)
    count = list_pairs(seg_ref, pad_ref, pat_ref, pairs_s)

    def keep(f):
        for src, dst, n in by_rows:
            pltpu.make_async_copy(src.at[frame_rows(f), :], dst.at[frame_rows(f), :], out_sem.at[n]).start()
        for src, dst, n in by_lanes:
            pltpu.make_async_copy(src.at[:, frame_lanes(f)], dst.at[:, frame_lanes(f)], out_sem.at[n]).start()

    def scores(i, j):
        s = dot(ka_ref[frame_rows(inside(j)), :], qe_s[inside(i)])
        return [s[:, head_lanes(h)] for h in HEADS]

    def gathered(j, ps):
        return [dot(vt_ref[head_rows(h), frame_lanes(inside(j), FROWS)], ps[h]) for h in HEADS]

    def attend(exact):
        def prepare(f):
            qt = qt_ref[:, frame_lanes(f)].astype(F32)
            own = qt * jnp.concatenate([kt_ref[:, frame_lanes(f, FROWS)].astype(F32), zpad], axis=1)
            for h in HEADS:
                if exact:
                    start = jnp.zeros((1, FLANES), F32)
                else:
                    start = jnp.sum(own[head_rows(h)], axis=0, keepdims=True)
                    m_s[f, h] = start
                aug = jnp.where(r32 == 26, 1.0, split_rows(-start, r32))
                qe_s[f, head_rows(h), head_lanes(h)] = (qt[head_rows(h)] + aug).astype(BF16)

        def finalize(i):
            outs, augs = [], []
            for h in HEADS:
                a = acc_s[i, h]
                l = a[24:25, :]
                bad_s[...] = jnp.maximum(bad_s[...], jnp.where(l < 1e30, 0.0, 1.0))
                outs.append(jnp.where(r32 < HEAD_DIM, a * (1.0 / l), 0.0))
                lse = m_s[i, h] + jnp.log2(l)
                q = qe_s[i, head_rows(h), head_lanes(h)].astype(F32)
                augs.append(jnp.where((r32 == 24) | (r32 == 25), split_rows(-lse, r32), q))
            ot = jnp.concatenate(outs, axis=0)
            ot_ref[:, frame_lanes(i)] = ot.astype(BF16)
            qa_ref[:, frame_lanes(i)] = jnp.concatenate(augs, axis=0).astype(BF16)
            o_ref[frame_rows(i), :] = ot.T[:FROWS, :].astype(BF16)

        def attend_pairs(pairs, first):
            ss = [scores(i, j) for i, j in pairs]
            if exact:
                old = [None if first else [m_s[i, h] for h in HEADS] for i, _ in pairs]
                for n, (i, j) in enumerate(pairs):
                    if not first:
                        old[n] = [m_s[i, h] for h in HEADS]
                    top = [jnp.max(ss[n][h], axis=0, keepdims=True) for h in HEADS]
                    if not first:
                        top = [jnp.maximum(old[n][h], top[h]) for h in HEADS]
                    pv = gathered(j, [jnp.exp2(ss[n][h] - top[h]).astype(BF16) for h in HEADS])
                    for h in HEADS:
                        acc_s[i, h] = pv[h] if first else acc_s[i, h] * jnp.exp2(old[n][h] - top[h]) + pv[h]
                        m_s[i, h] = top[h]
                return
            ps = [[jnp.exp2(s[h]).astype(BF16) for h in HEADS] for s in ss]
            pvs = [gathered(j, p) for (_, j), p in zip(pairs, ps)]
            for (i, _), pv in zip(pairs, pvs):
                for h in HEADS:
                    acc_s[i, h] = pv[h] if first else acc_s[i, h] + pv[h]

        bad_s[...] = jnp.zeros(bad_s.shape, F32)
        for k in range(TOGETHER):
            prepare(k)

        def diagonal(n, _):
            attend_pairs([(n * TOGETHER + k,) * 2 for k in range(TOGETHER)], True)
            for k in range(TOGETHER):
                prepare(jnp.minimum((n + 1) * TOGETHER, FRAMES - TOGETHER) + k)
            return 0
        lax.fori_loop(0, FRAMES // TOGETHER, diagonal, 0)
        each_pair(pairs_s, count, lambda pairs: attend_pairs(pairs, False))

        def close(n, _):
            for k in range(TOGETHER):
                finalize(n * TOGETHER + k)
            for k in range(TOGETHER):
                keep(n * TOGETHER + k)
            return 0
        lax.fori_loop(0, FRAMES // TOGETHER, close, 0)
        for src, dst, n in by_rows + by_lanes:
            pltpu.make_async_copy(src, dst, out_sem.at[n]).wait()

    attend(False)

    @pl.when(jnp.max(bad_s[...]) > 0.0)
    def _():
        attend(True)
    for copy in saved:
        copy.wait()


SMEM = pl.BlockSpec(memory_space=pltpu.SMEM)
HBM = pl.BlockSpec(memory_space=pltpu.HBM)


def in_hbm(value):
    return pltpu.with_memory_space_constraint(value, pltpu.HBM)
VM = pl.BlockSpec(memory_space=pltpu.VMEM)


def attn_fwd(seg, pad, pat, qt, ka, va, kt, vt):
    V = pltpu.VMEM
    rows, lanes = (FRAMES * FROWS, WIDE), (WIDE, FRAMES * FLANES)
    return pl.pallas_call(
        fwd_kernel,
        out_shape=tuple(pltpu.HBM(shape, BF16) for shape in (rows, lanes, lanes, rows, rows, lanes)),
        in_specs=[SMEM] * 3 + [VM] * 5,
        out_specs=(HBM,) * 6,
        scratch_shapes=[V(rows, BF16), V(lanes, BF16), V(lanes, BF16), V((FRAMES, WIDE, HEADS_LOCAL * FLANES), BF16),
                        V((FRAMES + 1, HEADS_LOCAL, 1, FLANES), F32), V((FRAMES + 1, HEADS_LOCAL, HW, FLANES), F32),
                        V((1, FLANES), F32), pltpu.SMEM((128 + UNROLL,), jnp.int32), pltpu.SemaphoreType.DMA((6,))],
        compiler_params=pltpu.CompilerParams(vmem_limit_bytes=26 << 20),
        cost_estimate=pl.CostEstimate(flops=int(2.5e10), bytes_accessed=8 << 20, transcendentals=0),
        name="attend_forward",
    )(seg, pad, pat, qt, ka, va, kt, vt)


def bwd_kernel(seg_ref, pad_ref, pat_ref, qa_ref, ka_ref, va_ref, kt_ref, ot_ref, do_ref, h_ref, w_ref,
               dh_ref, early_ref, qe_s, oe_s, dq_s, dk_s, dv_s, dw_s, turn_s, blk_s, pairs_s):
    scale = HEAD_DIM ** -0.5
    for s in (qe_s, oe_s):
        s[...] = jnp.zeros(s.shape, BF16)
    count = list_pairs(seg_ref, pad_ref, pat_ref, pairs_s)
    dw_s[...] = jnp.zeros(dw_s.shape, F32)
    real = lax.broadcasted_iota(jnp.int32, (WIDE, FROWS), 0) % HW < HEAD_DIM
    r32 = lax.broadcasted_iota(jnp.int32, (HW, FLANES), 0)
    zpad = jnp.zeros((WIDE, FLANES - FROWS), F32)

    def prepare(i):
        t = i
        qt = qa_ref[:, frame_lanes(i)]
        dot_ = jnp.concatenate([do_ref[frame_rows(i), :].astype(F32).T, zpad], axis=1)
        prod = dot_ * ot_ref[:, frame_lanes(i)].astype(F32)
        for h in HEADS:
            d = -jnp.sum(prod[head_rows(h)], axis=0, keepdims=True)
            qe_s[t, head_rows(h), head_lanes(h)] = qt[head_rows(h)]
            oe_s[t, head_rows(h), head_lanes(h)] = (dot_[head_rows(h)] + split_rows(d, r32)).astype(BF16)

    def scores(i, j):
        t, u = inside(i), inside(j)
        s, dp = dot(ka_ref[frame_rows(u), :], qe_s[t]), dot(va_ref[frame_rows(u), :], oe_s[t])
        ps = [jnp.exp2(s[:, head_lanes(h)]) for h in HEADS]
        return [p.astype(BF16) for p in ps], [(ps[h] * dp[:, head_lanes(h)]).astype(BF16) for h in HEADS]

    def products(i, j, pb, ds):
        t, u = inside(i), inside(j)
        dq = [dot(kt_ref[head_rows(h), frame_lanes(u, FROWS)], ds[h]) for h in HEADS]
        dv = [dot_nt(oe_s[t, head_rows(h), head_lanes(h)], pb[h]) for h in HEADS]
        dk = [dot_nt(qe_s[t, head_rows(h), head_lanes(h)], ds[h]) for h in HEADS]
        return [jnp.concatenate(value, axis=0) for value in (dq, dk, dv)]

    def attend_pairs(pairs, first):
        made = [scores(i, j) for i, j in pairs]
        values = [products(i, j, pb, ds) for (i, j), (pb, ds) in zip(pairs, made)]
        for (i, j), value in zip(pairs, values):
            for ref, at, part in ((dq_s, frame_lanes(i), 0), (dk_s, frame_lanes(j, FROWS), 1), (dv_s, frame_lanes(j, FROWS), 2)):
                ref[:, at] = value[part] if first else ref[:, at] + value[part]

    def finish(f):
        parts = (dq_s[:, frame_lanes(f, FROWS)] * scale, dk_s[:, frame_lanes(f, FROWS)] * math.log(2.0), dv_s[:, frame_lanes(f, FROWS)])
        grads = jnp.concatenate([jnp.where(real, part, 0.0).astype(BF16) for part in parts], axis=0)
        dh_ref[frame_rows(f), :] = dot_tn(grads, w_ref[...]).astype(BF16)
        return dot(grads, h_ref[frame_rows(f), :])

    for k in range(TOGETHER):
        prepare(k)

    def diagonal(n, _):
        attend_pairs([(n * TOGETHER + k,) * 2 for k in range(TOGETHER)], True)
        for k in range(TOGETHER):
            prepare(jnp.minimum((n + 1) * TOGETHER, FRAMES - TOGETHER) + k)
        return 0
    lax.fori_loop(0, FRAMES // TOGETHER, diagonal, 0)
    each_pair(pairs_s, count, lambda pairs: attend_pairs(pairs, False))

    def close(n, _):
        dw = [finish(n * TOGETHER + k) for k in range(TOGETHER)]
        dw_s[...] += functools.reduce(jnp.add, dw)
        return 0
    lax.fori_loop(0, FRAMES // TOGETHER, close, 0)
    for b in range(3):
        turned = dw_s[b * WIDE:(b + 1) * WIDE, :].T
        turn_s[:, 0:96] = jnp.concatenate([turned[:, HW * h:HW * h + HEAD_DIM] for h in HEADS], axis=1)
        line = [turn_s[pl.ds(k, 96, stride=4), :][:, 0:96] for k in range(4)]
        blk_s[pl.ds(0, 96, stride=3), :] = jnp.concatenate([line[0], line[1][:, :32]], axis=1)
        blk_s[pl.ds(1, 96, stride=3), :] = jnp.concatenate([line[1][:, 32:], line[2][:, :64]], axis=1)
        blk_s[pl.ds(2, 96, stride=3), :] = jnp.concatenate([line[2][:, 64:], line[3]], axis=1)
        early_ref[288 * b:288 * (b + 1), :] = blk_s[...].astype(BF16)


def attn_bwd(seg, pad, pat, qa, ka, va, kt, ot, do, h, w):
    sd = jax.ShapeDtypeStruct
    V = pltpu.VMEM
    return pl.pallas_call(
        bwd_kernel,
        out_shape=(sd((FRAMES * FROWS, D), BF16), sd((3 * 288, 128), BF16)),
        in_specs=[SMEM] * 3 + [VM] * 8,
        out_specs=(VM,) * 2,
        scratch_shapes=[V((FRAMES, WIDE, HEADS_LOCAL * FLANES), BF16), V((FRAMES, WIDE, HEADS_LOCAL * FLANES), BF16)]
        + [V((WIDE, (FRAMES + 1) * FLANES), F32)] * 3
        + [V((3 * WIDE, D), F32), V((D, 128), F32), V((288, 128), F32),
           pltpu.SMEM((128 + UNROLL,), jnp.int32)],
        compiler_params=pltpu.CompilerParams(vmem_limit_bytes=42 << 20),
        cost_estimate=pl.CostEstimate(flops=int(5e10), bytes_accessed=12 << 20, transcendentals=0),
        name="attend_backward",
    )(seg, pad, pat, qa, ka, va, kt, ot, do, h, w)


MESH = pl.DeviceIdType.MESH
OWN_ROWS = 4 * FROWS


def place(d, m):
    return {"dp": d, "mp": m}


def remote(src, dst, send_sem, recv_sem, device):
    return pltpu.make_async_remote_copy(
        src_ref=src, dst_ref=dst, send_sem=send_sem, recv_sem=recv_sem, device_id=device, device_id_type=MESH
    )


def local(src, dst, sem):
    return pltpu.make_async_copy(src, dst, sem)


def greet(devices):
    barrier = pltpu.get_barrier_semaphore()
    for device in devices:
        pl.semaphore_signal(barrier, inc=1, device_id=device, device_id_type=MESH)
    return len(devices)


def met(count):
    pl.semaphore_wait(pltpu.get_barrier_semaphore(), count)


def group_peers():
    me = lax.axis_index("mp")
    return me, me ^ 1, me ^ 2, me ^ 3


def frame_part(device, c):
    return pl.ds(pl.multiple_of(device * OWN_ROWS + c * FROWS, 16), FROWS)


def normalised(v):
    centred = v - jnp.mean(v, axis=-1, keepdims=True)
    inv = lax.rsqrt(jnp.mean(centred * centred, axis=-1, keepdims=True) + NORM_EPS)
    return centred * inv, inv


def norm_pull(dy, hat, inv, gain):
    dg = dy * gain
    lead = jnp.mean(dg, axis=-1, keepdims=True)
    along = jnp.mean(dg * hat, axis=-1, keepdims=True)
    return inv * (dg - lead - hat * along)


def col_sum(v):
    return jnp.sum(v, axis=0, keepdims=True)


def load_frame(ref, c):
    base = c * PATCHES // 16 * 16
    rows = ref[base:base + FROWS, :].astype(F32)
    shift = c * PATCHES - base
    return pltpu.roll(rows, FROWS - shift, 0) if shift else rows


def live_rows():
    return lax.broadcasted_iota(jnp.int32, (FROWS, 1), 0) < PATCHES


def dp_peers(count):
    d = lax.axis_index("dp")
    side, line = d % 2, d // 2
    return side, line, {"dp": d ^ 1}, [lax.rem(line + n, count) for n in range(count)]


def start_kernel(count, x_hbm, np_hbm, w_hbm, m_hbm, v_hbm,
                 h_ref, qt_ref, ka_ref, va_ref, kt_ref, vt_ref, wa_ref, ws_ref, ma_ref, mb_ref,
                 x_ref, np_ref, w_ref, m_ref, v_ref, mo_s, w_s, load_x, load_w, keep_m,
                 send_x, recv_x, send_p, recv_p, send_f, recv_f, send_t, recv_t, send_l, recv_l):
    me, near, far, _ = group_peers()
    side, line, twin, around = dp_peers(count)
    frames = range(OWN_ROWS // FROWS)
    cuts = [0, 208, 400, 592, 784]
    loads = [local(x_hbm.at[a:b, :], x_ref.at[a:b, :], load_x.at[c]) for c, (a, b) in enumerate(zip(cuts, cuts[1:]))]
    others = [local(m_hbm, m_ref, load_w.at[0]), local(v_hbm, v_ref, load_w.at[1]), local(w_hbm, w_ref, load_w.at[2])]
    gains = local(np_hbm, np_ref, load_w.at[3])
    greeted = greet([{"mp": near}, {"mp": far}, twin] + [{"dp": q * 2 + side} for q in around[1:]])
    for copy in [gains] + loads + others:
        copy.start()
    live = live_rows()
    to_far, to_near, moments = [], [], []
    gains.wait()
    for c in frames:
        loads[c].wait()
        hat, _ = normalised(load_frame(x_ref, c))
        h_ref[frame_part(me, c), :] = jnp.where(live, hat * np_ref[0:1, :] + np_ref[1:2, :], 0.0).astype(BF16)
        rows = h_ref.at[frame_part(me, c), :]
        to_far.append(remote(rows, rows, send_x.at[c], recv_x.at[c], {"mp": far}))
        to_near.append(remote(rows, rows, send_p.at[c], recv_p.at[c], {"mp": near}))
        if c == 0:
            met(greeted)
        to_far[c].start()
        to_near[c].start()

    slots, rows = m_ref.shape[0], m_ref.shape[1]
    others[0].wait()
    others[1].wait()
    for r in range(2 * slots):
        mo_s[r // slots, pl.ds((r % slots) * rows, rows), :] = (v_ref if r % 2 else m_ref)[r // 2].astype(BF16)
    first, second = ma_ref.at[side, line], mb_ref.at[side]
    kept = [local(mo_s.at[0], first, keep_m.at[0]), local(mo_s.at[1], second, keep_m.at[1])]
    for n, q in enumerate(around[1:]):
        moments.append(remote(mo_s.at[0], first, send_l.at[n], recv_l.at[n], {"dp": q * 2 + side}))
    moments.append(remote(mo_s.at[0], first, send_t.at[0], recv_t.at[0], twin))
    moments.append(remote(mo_s.at[1], second, send_t.at[1], recv_t.at[1], twin))
    for copy in moments + kept:
        copy.start()

    def incoming(device, sends, recvs, c):
        rows = h_ref.at[frame_part(device, c), :]
        return remote(rows, rows, sends.at[c], recvs.at[c], {"mp": near})

    def forward(c):
        incoming(far, send_x, recv_x, c).wait_recv()
        copy = incoming(far, send_f, recv_f, c)
        copy.start()
        return copy

    others[2].wait()
    for b in range(3):
        a = [w_ref[b, pl.ds(k, 96, stride=3), :] for k in range(3)]
        lines = [a[0][:, :96], jnp.concatenate([a[0][:, 96:], a[1][:, :64]], axis=1),
                 jnp.concatenate([a[1][:, 64:], a[2][:, :32]], axis=1), a[2][:, 32:]]
        gap = jnp.zeros((96, HW - HEAD_DIM), F32)
        for k in range(4):
            parts = []
            for h in HEADS:
                parts += [lines[k][:, HEAD_DIM * h:HEAD_DIM * (h + 1)], gap]
            w_s[pl.ds(k, 96, stride=4), :] = jnp.concatenate(parts, axis=1)
        wa_ref[b * WIDE:(b + 1) * WIDE, :] = w_s[...].T.astype(BF16)

    col = lax.broadcasted_iota(jnp.int32, (FROWS, WIDE), 1) % HW
    ones = jnp.where((col == 24) | (col == 25), 1.0, 0.0)
    kadd = ones + jnp.where((col == 26) & jnp.logical_not(live), MASKED, 0.0)
    vtadd = jnp.where(lax.broadcasted_iota(jnp.int32, (WIDE, FROWS), 0) % HW == 24, 1.0, 0.0)
    zpad = jnp.zeros((WIDE, FLANES - FROWS), BF16)

    def project(devices, c):
        made = []
        for device in devices:
            hf = h_ref[frame_part(device, c), :]
            made.append((dot_nt(wa_ref[...], hf), dot_nt(hf, wa_ref[WIDE:3 * WIDE, :])))
        for device, (turned, lined) in zip(devices, made):
            f = device * (OWN_ROWS // FROWS) + c
            qt_ref[:, frame_lanes(f)] = jnp.concatenate([(turned[0:WIDE] * QSCALE).astype(BF16), zpad], axis=1)
            kt_ref[:, frame_lanes(f, FROWS)] = turned[WIDE:2 * WIDE].astype(BF16)
            vt_ref[:, frame_lanes(f, FROWS)] = (turned[2 * WIDE:3 * WIDE] + vtadd).astype(BF16)
            ka_ref[frame_rows(f), :] = (lined[:, 0:WIDE] + kadd).astype(BF16)
            va_ref[frame_rows(f), :] = (lined[:, WIDE:2 * WIDE] + ones).astype(BF16)

    copies = [forward(0)]
    for c in frames:
        incoming(near, send_p, recv_p, c).wait_recv()
        project((me, near), c)
    copies.append(forward(1))
    for b in range(3, w_ref.shape[0]):
        for k in range(3):
            lanes = slice(128 * k, 128 * (k + 1))
            part = w_ref[b, pl.ds(k, 96, stride=3), :]
            if b == 3:
                gap = jnp.zeros((HW - HEAD_DIM, 128), F32)
                parts = []
                for h in HEADS:
                    parts += [part[HEAD_DIM * h:HEAD_DIM * (h + 1)], gap]
                ws_ref[2 * D:2 * D + WIDE, lanes] = jnp.concatenate(parts, axis=0).astype(BF16)
            else:
                ws_ref[96 * (b - 4):96 * (b - 3), lanes] = part.astype(BF16)
    for c in frames:
        incoming(near ^ 2, send_f, recv_f, c).wait_recv()
        project((far, near ^ 2), c)
        if c + 2 < len(frames):
            copies.append(forward(c + 2))
    for n in range(1, count):
        part = ma_ref.at[side, around[count - n]]
        remote(part, part, send_l.at[n - 1], recv_l.at[n - 1], twin).wait_recv()
    part = ma_ref.at[1 - side, line]
    remote(part, part, send_t.at[0], recv_t.at[0], twin).wait_recv()
    part = mb_ref.at[1 - side]
    remote(part, part, send_t.at[1], recv_t.at[1], twin).wait_recv()
    for copy in kept:
        copy.wait()
    for copy in to_far + to_near + copies + moments:
        copy.wait_send()


def start_call(dp, x, norm_params, weights, first_moments, second_moments):
    sd, V, S = jax.ShapeDtypeStruct, pltpu.VMEM, pltpu.SemaphoreType.DMA
    blocks, count = weights.shape[0], dp // 2
    half = first_moments.shape[0] * first_moments.shape[1]
    rows, lanes = sd((FRAMES * FROWS, WIDE), BF16), sd((WIDE, FRAMES * FLANES), BF16)
    return pl.pallas_call(
        functools.partial(start_kernel, count),
        out_shape=(sd((FRAMES * FROWS, D), BF16), lanes, rows, rows, lanes, lanes, sd((3 * WIDE, D), BF16),
                   sd((WIDE + 96 * (blocks - 4), D), BF16),
                   pltpu.HBM((2, count, half, 128), BF16), pltpu.HBM((2, half, 128), BF16)),
        in_specs=[HBM] * 5,
        out_specs=(VM,) * 8 + (HBM,) * 2,
        scratch_shapes=[V(x.shape, BF16), V(norm_params.shape, F32), V(weights.shape, F32), V(first_moments.shape, F32),
                        V(first_moments.shape, F32), V((2, half, 128), BF16), V((D, WIDE), F32),
                        S((4,)), S((4,)), S((2,))] + [S((4,))] * 6 + [S((2,))] * 2 + [S((count,))] * 2,
        compiler_params=pltpu.CompilerParams(vmem_limit_bytes=24 << 20, collective_id=1, has_side_effects=True),
        name="norm_and_gather",
    )(*[in_hbm(value) for value in (x, norm_params, weights, first_moments, second_moments)])


def gelu_parts(u):
    lead = math.sqrt(2.0 / math.pi)
    bend = lead * 0.044715
    square = u * u
    half = 0.5 + 0.5 * jnp.tanh(u * (lead + bend * square))
    slope = half + 2.0 * u * (half - half * half) * (lead + 3.0 * bend * square)
    return u * half, slope


def middle_kernel(count, o_ref, x_hbm, ct_hbm, pad_ref, w0_ref, w1_ref, np_hbm, ma_ref, mb_ref,
                  out_ref, dx2_ref, do_ref, l0_ref, l1_ref, l2_ref, l3_ref, nb_ref, mom_ref,
                  ob_s, dob_s, g_s, a_s, du_s, da_s, h2_s, dxa_s, blk_s, res_s, ut_s, wot_s,
                  x_ref, ct_ref, o_s, w2_ref, w3_ref, np_ref, load_s, send_w, recv_w,
                  send_o, recv_o, send_d, recv_d, send_t, recv_t, send_l, recv_l, send_f, recv_f):
    me, near, far, across = group_peers()
    side, line, twin, around = dp_peers(count)
    peers = (far, across, near)
    mine = pl.ds(pl.multiple_of(me * OWN_ROWS, 16), OWN_ROWS)
    loads = [local(ct_hbm, ct_ref, load_s.at[0]), local(x_hbm, x_ref, load_s.at[1]), local(o_ref.at[mine, :], o_s, load_s.at[2]), local(np_hbm, np_ref, load_s.at[3])]
    greeted = greet([{"mp": p} for p in peers] + [twin] + [{"dp": q * 2 + side} for q in around[1:]])
    for copy in loads:
        copy.start()
    frames = range(OWN_ROWS // FROWS)
    live = live_rows()
    shards_w = (w0_ref, w1_ref, w2_ref, w3_ref)
    late = (l0_ref, l1_ref, l2_ref, l3_ref)
    places = range(len(shards_w))
    loads[0].wait()
    for c in frames:
        rows = slice(c * FROWS, (c + 1) * FROWS)
        g_s[rows, :] = jnp.where(live, load_frame(ct_ref, c) * (1 - pad_ref[0, me * len(frames) + c]).astype(F32), 0.0).astype(BF16)
    met(greeted)
    outgoing = []
    for c in frames:
        for n, p in enumerate(peers):
            outgoing.append(remote(o_ref.at[frame_part(p, c), :], ob_s.at[n, pl.ds(c * FROWS, FROWS), :],
                                   send_o.at[n, c], recv_o.at[n, c], {"mp": p}))
            outgoing[-1].start()
    weights = [remote(w0_ref, w3_ref, send_w.at[0], recv_w.at[0], {"mp": near}),
               remote(w1_ref, w2_ref, send_w.at[1], recv_w.at[1], {"mp": near})]
    for copy in weights:
        copy.start()
    moments = []
    for n, q in enumerate(around[1:]):
        own_half = mb_ref.at[side]
        moments.append(remote(own_half, mom_ref.at[1, side, line], send_l.at[n], recv_l.at[n], {"dp": q * 2 + side}))
        moments.append(remote(ma_ref.at[side, q], mom_ref.at[0, side, q], send_t.at[q], recv_t.at[q], twin))
    for copy in moments:
        copy.start()

    def pass_moments(n):
        q = around[count - n]
        part = mom_ref.at[1, side, q]
        remote(part, part, send_l.at[n - 1], recv_l.at[n - 1], twin).wait_recv()
        moments.append(remote(part, part, send_f.at[q], recv_f.at[q], twin))
        moments[-1].start()

    def w_up(m):
        return shards_w[m][0:D, :]

    def w_down(m):
        return shards_w[m][D:2 * D, :]

    def w_o(m):
        return shards_w[m][2 * D:2 * D + WIDE, :]

    def cols(m):
        return slice(m * D, (m + 1) * D)

    for m in (0, 1, 3, 2):
        if m > 1:
            weights[3 - m].wait_recv()
        da_s[:, cols(m)] = dot_nt(g_s[...], w_down(m))
        ut_s[cols(m), :] = w_up(m).astype(F32).T.astype(BF16)
        wot_s[:, m * WIDE:(m + 1) * WIDE] = w_o(m).astype(F32).T.astype(BF16)
    for copy in loads[1:]:
        copy.wait()
    nb_ref[...] = jnp.zeros(nb_ref.shape, F32)
    down = jnp.concatenate([w_down(m) for m in places], axis=0)
    out_w = jnp.concatenate([w_o(m) for m in places], axis=0)
    sent, left = [], list(range(1, count))
    for both in ((0,), (1, 2), (3,)):
        rows = slice(both[0] * FROWS, (both[-1] + 1) * FROWS)
        for c in both:
            for n, p in enumerate(peers):
                part = ob_s.at[n, pl.ds(c * FROWS, FROWS), :]
                remote(part, part, send_o.at[n, c], recv_o.at[n, c], {"mp": p}).wait_recv()
        own_rows = pl.ds(pl.multiple_of(me * OWN_ROWS + both[0] * FROWS, 16), len(both) * FROWS)
        heads = jnp.concatenate([o_s[rows, :]] + [ob_s[n, rows, :] for n in range(len(peers))], axis=1)
        x2 = jnp.concatenate([load_frame(x_ref, c) for c in both], axis=0) + dot(heads, out_w)
        x2 = jnp.where(jnp.concatenate([live] * len(both), axis=0), x2, 0.0)
        hat, inv = normalised(x2)
        h2 = (hat * np_ref[2:3, :] + np_ref[3:4, :]).astype(BF16)
        h2_s[rows, :] = h2
        for m in places:
            value, slope = gelu_parts(dot(h2, w_up(m)))
            a_s[rows, cols(m)] = value.astype(BF16)
            du_s[rows, cols(m)] = (da_s[rows, cols(m)] * slope).astype(BF16)
        if left and len(both) > 1:
            pass_moments(left.pop(0))
        result = x2 + dot(a_s[rows, :], down)
        for k, c in enumerate(both):
            res_s[pl.ds(c * PATCHES, FROWS), :] = result[k * FROWS:(k + 1) * FROWS]
        dh2 = dot(du_s[rows, :], ut_s[...])
        nb_ref[0:1, :] += col_sum(dh2 * hat)
        nb_ref[1:2, :] += col_sum(dh2)
        dx2 = g_s[rows, :].astype(F32) + norm_pull(dh2, hat, inv, np_ref[2:3, :])
        dx2_ref[rows, :] = dx2
        dxa = dx2.astype(BF16)
        dxa_s[rows, :] = dxa
        d_heads = dot(dxa, wot_s[...]).astype(BF16)
        for n in range(len(peers)):
            dob_s[n, rows, :] = d_heads[:, (n + 1) * WIDE:(n + 2) * WIDE]
        for c in both:
            for n, p in enumerate(peers):
                sent.append(remote(dob_s.at[n, pl.ds(c * FROWS, FROWS), :], do_ref.at[frame_part(me, c), :],
                                   send_d.at[n, c], recv_d.at[n, c], {"mp": p}))
                sent[-1].start()
        do_ref[own_rows, :] = d_heads[:, 0:WIDE]
        if left and both[-1] < 3:
            pass_moments(left.pop(0))
    while left:
        pass_moments(left.pop(0))
    out_ref[...] = res_s[0:out_ref.shape[0], :].astype(BF16)

    def as_block(shard, first, value):
        size = value.shape[0]
        for k in range(3):
            blk_s[pl.ds(k, size, stride=3), :] = value[:, 128 * k:128 * (k + 1)]
        late[shard][first * 288:first * 288 + 3 * size, :] = blk_s[0:3 * size, :].astype(BF16)

    def drop_gaps(value):
        return jnp.concatenate([value[HW * h:HW * h + HEAD_DIM] for h in HEADS], axis=0)

    dw1 = dot_tn(h2_s[...], du_s[...])
    dw2 = dot_tn(g_s[...], a_s[...])
    for m in places:
        as_block(m, 1, dw1[:, cols(m)])
        as_block(m, 5, dw2[:, cols(m)].T)
        o_m = o_s[...] if m == 0 else ob_s[m - 1]
        as_block(m, 0, drop_gaps(dot_tn(o_m, dxa_s[...])))
    for c in frames:
        for n, p in enumerate(peers):
            part = do_ref.at[frame_part(p, c), :]
            remote(part, part, send_d.at[n, c], recv_d.at[n, c], {"mp": p}).wait_recv()
    for q in around[1:]:
        for half, sends, recvs in ((0, send_t, recv_t), (1, send_f, recv_f)):
            part = mom_ref.at[half, 1 - side, q]
            remote(part, part, sends.at[q], recvs.at[q], twin).wait_recv()
    for copy in outgoing + sent + moments + weights:
        copy.wait_send()


def middle_call(dp, o, x, ct, padding, w, norm_params, ma, mb):
    sd = jax.ShapeDtypeStruct
    V, S = pltpu.VMEM, pltpu.SemaphoreType.DMA
    count = dp // 2
    late = sd((9 * 288, 128), BF16)
    return pl.pallas_call(
        functools.partial(middle_kernel, count),
        out_shape=(sd(x.shape, BF16), sd((OWN_ROWS, D), F32), sd((FRAMES * FROWS, WIDE), BF16),
                   late, late, late, late, sd((2, D), F32), pltpu.HBM((2,) + ma.shape, BF16)),
        in_specs=[HBM, HBM, HBM, SMEM] + [VM] * 2 + [HBM] * 3,
        out_specs=(VM,) * 8 + (HBM,),
        scratch_shapes=[V((3, OWN_ROWS, WIDE), BF16), V((3, OWN_ROWS, WIDE), BF16), V((OWN_ROWS, D), BF16),
                        V((OWN_ROWS, FF), BF16), V((OWN_ROWS, FF), BF16), V((OWN_ROWS, FF), F32),
                        V((OWN_ROWS, D), BF16), V((OWN_ROWS, D), BF16), V((1152, 128), F32), V((OWN_ROWS, D), F32),
                        V((FF, D), BF16), V((D, 4 * WIDE), BF16),
                        V(x.shape, BF16), V(x.shape, BF16), V((OWN_ROWS, WIDE), BF16), V(w[0].shape, BF16), V(w[0].shape, BF16), V(norm_params.shape, F32), S((4,)), S((2,)), S((2,)), S((3, 4)), S((3, 4)), S((3, 4)), S((3, 4))] + [S((count,))] * 6,
        compiler_params=pltpu.CompilerParams(vmem_limit_bytes=36 << 20, collective_id=2, has_side_effects=True),
        cost_estimate=pl.CostEstimate(flops=int(6e9), bytes_accessed=12 << 20, transcendentals=0),
        name="feed_forward",
    )(in_hbm(o), in_hbm(x), in_hbm(ct), padding, *w, in_hbm(norm_params), in_hbm(ma), in_hbm(mb))


def reduce_kernel(dp, piece, dh_ref, early_ref, l0_ref, l1_ref, l2_ref, l3_ref, x_ref, dx2_ref, np_ref, nb_ref,
                  gin_ref, gs_ref, tot_ref,
                  res_s, pb_s, xs_s, xb_s, g_s, yb_s, zs_s, zb_s, msg_s, mb_s, dm_s, db_s,
                  send_p, recv_p, send_x, recv_x, send_y, recv_y, send_z, recv_z,
                  send_a, recv_a, send_w, recv_w, send_m, recv_m, send_n, recv_n):
    me, near, far, across = group_peers()
    d = lax.axis_index("dp")
    count = dp // 2
    side, line = d % 2, d // 2
    twin = {"dp": d ^ 1}

    order, top = [], count
    while top > 1:
        top //= 2
        order += range(top, 2 * top)
    turns = [line ^ n for n in order]
    cut = -(-piece // 32) * 16
    halves = [(0, cut), (cut, piece - cut)]

    def line_device(q):
        return {"dp": q * 2 + side}

    frames = range(OWN_ROWS // FROWS)
    greeted = greet([{"mp": near}, {"mp": far}, {"mp": across}] + [{"dp": d ^ n} for n in range(1, dp)])
    total = early_ref.shape[0] + l0_ref.shape[0]
    g_s[0:early_ref.shape[0], :] = early_ref[...]
    g_s[early_ref.shape[0]:total, :] = (l0_ref[...].astype(F32) + l1_ref[...].astype(F32)
                                        + (l2_ref[...].astype(F32) + l3_ref[...].astype(F32))).astype(BF16)
    if g_s.shape[0] > total:
        g_s[total:, :] = jnp.zeros((g_s.shape[0] - total, 128), BF16)
    met(greeted)

    def own(c):
        return pl.ds(c * FROWS, FROWS)

    to_near = []
    for k, target in ((1, across), (0, near)):
        for c in frames:
            to_near.append(remote(dh_ref.at[frame_part(target, c), :], pb_s.at[k, own(c), :],
                                  send_p.at[k, c], recv_p.at[k, c], {"mp": near}))
            to_near[-1].start()

    def at(s, q, k):
        return pl.ds(pl.multiple_of((s * count + q) * piece + halves[k][0], 16), halves[k][1])

    def part(ref, q, k):
        return ref.at[q, pl.ds(*halves[k]), :]

    to_twin = []
    for q in turns + [line]:
        for k in range(2):
            to_twin.append(remote(g_s.at[at(1 - side, q, k), :], part(yb_s, q, k), send_y.at[q, k], recv_y.at[q, k], twin))
            to_twin[-1].start()

    to_far = []
    for c in frames:
        remote(pb_s.at[1, own(c), :], pb_s.at[1, own(c), :], send_p.at[1, c], recv_p.at[1, c], {"mp": near}).wait_recv()
        xs_s[own(c), :] = (dh_ref[frame_part(far, c), :].astype(F32) + pb_s[1, own(c), :].astype(F32)).astype(BF16)
        to_far.append(remote(xs_s.at[own(c), :], xb_s.at[own(c), :], send_x.at[c], recv_x.at[c], {"mp": far}))
        to_far[-1].start()

    to_line = []
    for q in turns + [line]:
        for k in range(2):
            got = part(yb_s, q, k)
            remote(got, got, send_y.at[q, k], recv_y.at[q, k], twin).wait_recv()
            rows = pl.ds(*halves[k])
            zs_s[q, rows, :] = (g_s[at(side, q, k), :].astype(F32) + yb_s[q, rows, :].astype(F32)).astype(BF16)
            if q is not line:
                to_line.append(remote(part(zs_s, q, k), part(zb_s, line, k), send_z.at[q, k], recv_z.at[line, k], line_device(q)))
                to_line[-1].start()
    spread, passed = [], []
    squares = jnp.zeros((1, 128), F32)
    for k in range(2):
        rows = pl.ds(*halves[k])
        mine = zs_s[line, rows, :].astype(F32)
        for q in turns:
            got = part(zb_s, q, k)
            remote(got, got, send_z.at[q, k], recv_z.at[q, k], line_device(q)).wait_recv()
            mine = mine + zb_s[q, rows, :].astype(F32)
        mine = mine.astype(BF16)
        gs_ref[at(side, line, k), :] = mine
        whole = gs_ref.at[at(side, line, k), :]
        for q in turns:
            spread.append(remote(whole, whole, send_a.at[q, k], recv_a.at[line, k], line_device(q)))
        passed.append(remote(whole, whole, send_w.at[line, k], recv_w.at[line, k], twin))
        for copy in spread[-len(turns):] + passed[-1:]:
            copy.start()
        mine = mine.astype(F32)
        squares = squares + col_sum(mine * mine)

    live = live_rows()
    gain, bias = jnp.zeros((1, D), F32), jnp.zeros((1, D), F32)
    for c in frames:
        remote(pb_s.at[0, own(c), :], pb_s.at[0, own(c), :], send_p.at[0, c], recv_p.at[0, c], {"mp": near}).wait_recv()
        remote(xb_s.at[own(c), :], xb_s.at[own(c), :], send_x.at[c], recv_x.at[c], {"mp": far}).wait_recv()
        dy = dh_ref[frame_part(me, c), :].astype(F32) + pb_s[0, own(c), :].astype(F32) + xb_s[own(c), :].astype(F32)
        dy = jnp.where(live, dy, 0.0)
        hat, inv = normalised(load_frame(x_ref, c))
        gain = gain + col_sum(dy * hat)
        bias = bias + col_sum(dy)
        res_s[pl.ds(c * PATCHES, FROWS), :] = dx2_ref[own(c), :] + norm_pull(dy, hat, inv, np_ref[0:1, :])
    gin_ref[...] = res_s[0:gin_ref.shape[0], :].astype(BF16)

    msg_s[...] = jnp.zeros(msg_s.shape, F32)
    msg_s[0:1, :] = gain
    msg_s[1:2, :] = bias
    msg_s[2:4, :] = nb_ref[...]
    msg_s[4:5, 0:128] = squares
    small = []
    for n, p in enumerate((near, far, across)):
        small.append(remote(msg_s, mb_s.at[n], send_m.at[n], recv_m.at[n], {"mp": p}))
        small[-1].start()

    def pass_on(q, k):
        piece_at = gs_ref.at[at(side, q, k), :]
        remote(piece_at, piece_at, send_a.at[q, k], recv_a.at[q, k], line_device(q)).wait_recv()
        passed.append(remote(piece_at, piece_at, send_w.at[q, k], recv_w.at[q, k], twin))
        passed[-1].start()

    pass_on(turns[0], 0)
    add = msg_s[...]
    for n, p in enumerate((near, far, across)):
        remote(mb_s.at[n], mb_s.at[n], send_m.at[n], recv_m.at[n], {"mp": p}).wait_recv()
        add = add + mb_s[n]
    dm_s[...] = add
    for n in range(1, dp):
        small.append(remote(dm_s, db_s.at[n], send_n.at[n], recv_n.at[n], {"dp": d ^ n}))
        small[-1].start()
    for k in range(2):
        for q in turns[1 - k:]:
            pass_on(q, k)
    for n in range(1, dp):
        remote(db_s.at[n], db_s.at[n], send_n.at[n], recv_n.at[n], {"dp": d ^ n}).wait_recv()
        add = add + db_s[n]
    tot_ref[...] = add
    for k in range(2):
        for q in turns + [line]:
            piece_at = gs_ref.at[at(1 - side, q, k), :]
            remote(piece_at, piece_at, send_w.at[q, k], recv_w.at[q, k], twin).wait_recv()
    for copy in to_near + to_twin + to_far + to_line + spread + passed + small:
        copy.wait_send()


def reduce_call(dp, dh, early, late, x, dx2, norm_params, nb):
    sd = jax.ShapeDtypeStruct
    V, S = pltpu.VMEM, pltpu.SemaphoreType.DMA
    rows = early.shape[0] + late[0].shape[0]
    count = dp // 2
    piece = -(-rows // (2 * count * 16)) * 16
    held = 2 * count * piece
    return pl.pallas_call(
        functools.partial(reduce_kernel, dp, piece),
        out_shape=(sd(x.shape, BF16), sd((held, 128), BF16), sd((8, D), F32)),
        in_specs=[VM] * 10,
        out_specs=(VM,) * 3,
        scratch_shapes=[V((OWN_ROWS, D), F32), V((2, OWN_ROWS, D), BF16), V((OWN_ROWS, D), BF16), V((OWN_ROWS, D), BF16), V((held, 128), BF16),
                        V((count, piece, 128), BF16), V((count, piece, 128), BF16), V((count, piece, 128), BF16),
                        V((8, D), F32), V((3, 8, D), F32), V((8, D), F32), V((dp, 8, D), F32),
                        S((2, 4)), S((2, 4)), S((4,)), S((4,))] + [S((count, 2))] * 8 + [S((3,)), S((3,)), S((dp,)), S((dp,))],
        compiler_params=pltpu.CompilerParams(vmem_limit_bytes=22 << 20, collective_id=3, has_side_effects=True),
        name="reduce_gradients",
    )(dh, early, *late, x, dx2, norm_params, nb)


def update_kernel(slot_ref, dev_ref, res_ref, gin_ref, tot_ref, gs_ref, w_ref, m_ref, v_ref, ma_ref, mb_ref, mom_ref, np_ref, nm_ref, nv_ref,
                  out_ref, gout_ref, norm_ref, nw_ref, nf_ref, ns_ref, nn_ref, nnf_ref, nns_ref, sem_s):
    carried = [local(res_ref, out_ref, sem_s.at[0]), local(gin_ref, gout_ref, sem_s.at[1])]
    for copy in carried:
        copy.start()
    blocks, rows, _ = w_ref.shape
    slots = m_ref.shape[0]
    tot = tot_ref[...]
    grads = tot[0:4, :]
    norm = jnp.sqrt(jnp.sum(grads * grads, keepdims=True) + jnp.sum(tot[4:5, 0:128], keepdims=True))
    norm_ref[...] = norm
    clip_level = 0.5 * (4 * D * D + 2 * D * FF + 4 * D) ** 0.5
    factor = jnp.minimum(1.0, clip_level / norm)
    nn_ref[...], nnf_ref[...], nns_ref[...] = adam_update(
        np_ref[...], grads * factor, nm_ref[...], nv_ref[...], 0.0, NORM_RATE)

    def block(b):
        return gs_ref[pl.ds(pl.multiple_of(b * rows, 16), rows), :].astype(F32) * factor

    def step(b, _):
        holder, first = slot_ref[b] // slots, slot_ref[b] % slots * 2
        side, line = holder % 2, holder // 2
        on_side, on_line = side == dev_ref[0] % 2, line == dev_ref[0] // 2

        def moment(r):
            at = pl.ds(pl.multiple_of(r % slots * rows, 16), rows)
            late = mom_ref[r // slots, side, line, at, :]
            lead = jnp.where(on_side | on_line, ma_ref[side, line, at, :], late)
            rest = jnp.where(on_line, mb_ref[side, at, :], late)
            return jnp.where(r < slots, lead, rest).astype(F32)

        old = [moment(first), moment(first + 1)]
        nw_ref[b], _, _ = adam_update(w_ref[b], block(b), old[0], old[1], WEIGHT_DECAY, LEARN_RATE)
        return 0
    lax.fori_loop(0, blocks, step, 0)
    for s in range(slots):
        owned = jnp.int32(-1)
        for b in range(blocks):
            owned = jnp.where(slot_ref[b] == dev_ref[0] * slots + s, b, owned)
        _, first, second = adam_update(0.0, block(jnp.maximum(owned, 0)), m_ref[s], v_ref[s], 0.0, LEARN_RATE)
        nf_ref[s] = jnp.where(owned >= 0, first, m_ref[s])
        ns_ref[s] = jnp.where(owned >= 0, second, v_ref[s])
    for copy in carried:
        copy.wait()


def update_call(owner_slot, result, grad_in, tot, gs, weights, first, second, ma, mb, moments, norm_params, norm_first, norm_second):
    sd = jax.ShapeDtypeStruct
    small = sd((4, D), F32)
    device = lax.axis_index("dp").reshape(1)
    return pl.pallas_call(
        update_kernel,
        out_shape=(pltpu.HBM(result.shape, BF16), pltpu.HBM(result.shape, BF16), sd((1, 1), F32), sd(weights.shape, F32), sd(first.shape, F32), sd(first.shape, F32), small, small, small),
        in_specs=[SMEM] * 2 + [VM] * 13,
        out_specs=(HBM,) * 2 + (VM,) * 7,
        scratch_shapes=[pltpu.SemaphoreType.DMA((2,))],
        compiler_params=pltpu.CompilerParams(vmem_limit_bytes=16 << 20),
        name="clipped_update",
    )(owner_slot, device, result, grad_in, tot, gs, weights, first, second, ma, mb, moments, norm_params, norm_first, norm_second)


def adam_update(current, gradient, first_moment, second_moment, decay_rate, step_rate):
    first_new = BETA_ONE * first_moment + (1.0 - BETA_ONE) * gradient
    second_new = BETA_TWO * second_moment + (1.0 - BETA_TWO) * gradient * gradient
    first_fix = 1.0 / (1.0 - BETA_ONE**STEP)
    second_fix = 1.0 / (1.0 - BETA_TWO**STEP)
    direction = first_new * (step_rate * first_fix) / (jnp.sqrt(second_new * second_fix) + ADAM_EPS)
    return (current * (1.0 - step_rate * decay_rate) - direction, first_new, second_new)


def from_peer(value, distance):
    return lax.ppermute(value, "mp", [(i, i ^ distance) for i in range(lax.axis_size("mp"))])


def shards(tokens, cotangent, segment_ids, padding, pattern, owner_slot, weights, first_moments, second_moments,
           norm_params, norm_first, norm_second):
    dp = lax.axis_size("dp")
    x, ct = tokens[0], cotangent[0]
    h1, qt, ka, va, kt, vt, wa, own_shared, ma, mb = start_call(dp, x, norm_params, weights, first_moments, second_moments)
    shared = [own_shared, from_peer(own_shared, 2)]
    o, ot, qa, ka, va, kt = attn_fwd(segment_ids, padding, pattern, qt, ka, va, kt, vt)
    result, dx2, do, *late, nb, moments = middle_call(dp, o, x, ct, padding, shared, norm_params, ma, mb)
    late = [late[0], from_peer(late[1], 2), from_peer(late[2], 3), from_peer(late[3], 1)]
    dh, early = attn_bwd(segment_ids, padding, pattern, qa, ka, va, kt, ot, do, h1, wa)
    grad_in, gs, tot = reduce_call(dp, dh, early, late, x, dx2, norm_params, nb)
    result, grad_in, grad_norm, new_weights, new_first, new_second, new_norm, new_norm_first, new_norm_second = update_call(
        owner_slot, result, grad_in, tot, gs, weights, first_moments, second_moments, ma, mb, moments, norm_params, norm_first, norm_second)
    return (result[None], grad_in[None], grad_norm[0, 0], new_weights, new_first, new_second,
            new_norm, new_norm_first, new_norm_second)


def solution(mesh):
    rows, blocks, slots = P("dp", "mp", None), P(None, "mp", None), P("dp", "mp", None)
    return jax.shard_map(
        shards,
        mesh=mesh,
        in_specs=(rows, rows, P("dp", None), P("dp", None), P(), P(), blocks, slots, slots, P(), P(), P()),
        out_specs=(rows, rows, P(), blocks, slots, slots, P(), P(), P()),
        check_vma=False,
    )
```

```python
import functools
import math

import jax
import jax.numpy as jnp
from jax import lax
from jax.experimental import pallas as pl
from jax.experimental.pallas import tpu as pltpu
from jax.sharding import PartitionSpec as P

FF = 1536
STEP = 10
NORM_EPS = 1e-05
BETA_ONE = 0.9
BETA_TWO = 0.95
ADAM_EPS = 1e-08
LEARN_RATE = 0.15
NORM_RATE = 0.6
WEIGHT_DECAY = 0.05

D = 384
HEAD_DIM = 24
FRAMES = 16
PATCHES = 196
FROWS = 208
FLANES = 256
HW = 32
HEADS_LOCAL = 4
WIDE = HEADS_LOCAL * HW
MASKED = -1e30
QSCALE = math.log2(math.e) / math.sqrt(HEAD_DIM)
F32 = jnp.float32
BF16 = jnp.bfloat16
NT = (((1,), (1,)), ((), ()))
TN = (((0,), (0,)), ((), ()))
HEADS = range(HEADS_LOCAL)
UNROLL = 6
TOGETHER = 4


def dot(a, b):
    return jnp.dot(a, b, preferred_element_type=F32)


def dot_nt(a, b):
    return lax.dot_general(a, b, NT, preferred_element_type=F32)


def dot_tn(a, b):
    return lax.dot_general(a, b, TN, preferred_element_type=F32)


def frame_rows(f):
    return pl.ds(pl.multiple_of(f * FROWS, 16), FROWS)


def frame_lanes(f, size=FLANES):
    return pl.ds(pl.multiple_of(f * FLANES, 128), size)


def head_rows(h):
    return slice(HW * h, HW * (h + 1))


def head_lanes(h):
    return slice(FLANES * h, FLANES * (h + 1))


def list_pairs(seg_ref, pad_ref, pat_ref, pairs_s):
    def rows(i, carry):
        start, count = carry
        start = jnp.where(seg_ref[0, i] == seg_ref[0, jnp.maximum(i - 1, 0)], start, i)

        def cols(j, count):
            pairs_s[count] = i * 32 + j
            return count + jnp.where((pat_ref[i, j] == 1) & (pad_ref[0, j] == 0), 1, 0)
        return start, lax.fori_loop(start, i, cols, count)
    _, count = lax.fori_loop(0, FRAMES, rows, (jnp.int32(0), jnp.int32(0)))
    for n in range(UNROLL):
        pairs_s[count + n] = FRAMES * 33
    return count


def each_pair(pairs_s, count, work):
    def step(first, size):
        def body(n, _):
            codes = [pairs_s[first + n * size + u] for u in range(size)]
            work([(code // 32, code % 32) for code in codes])
            return 0
        return body
    whole = count // UNROLL
    lax.fori_loop(0, whole, step(0, UNROLL), 0)
    lax.fori_loop(0, (count - whole * UNROLL + 1) // 2, step(whole * UNROLL, 2), 0)


def inside(f):
    return jnp.minimum(f, FRAMES - 1)


def split_rows(value, r32):
    high = value.astype(BF16).astype(F32)
    return jnp.where(r32 == 24, high, jnp.where(r32 == 25, value - high, 0.0))


def fwd_kernel(seg_ref, pad_ref, pat_ref, qt_ref, ka_ref, va_ref, kt_ref, vt_ref,
               o_hbm, ot_hbm, qa_hbm, ka_hbm, va_hbm, kt_hbm,
               o_ref, ot_ref, qa_ref, qe_s, m_s, acc_s, bad_s, pairs_s, out_sem):
    zpad = jnp.zeros((WIDE, FLANES - FROWS), F32)
    r32 = lax.broadcasted_iota(jnp.int32, (HW, FLANES), 0)
    by_rows = [(o_ref, o_hbm, 0)]
    by_lanes = [(ot_ref, ot_hbm, 1), (qa_ref, qa_hbm, 2)]
    saved = [pltpu.make_async_copy(src, dst, out_sem.at[n])
             for n, (src, dst) in enumerate(((ka_ref, ka_hbm), (va_ref, va_hbm), (kt_ref, kt_hbm)), 3)]
    for copy in saved:
        copy.start()
    qe_s[...] = jnp.zeros(qe_s.shape, BF16)
    count = list_pairs(seg_ref, pad_ref, pat_ref, pairs_s)

    def keep(f):
        for src, dst, n in by_rows:
            pltpu.make_async_copy(src.at[frame_rows(f), :], dst.at[frame_rows(f), :], out_sem.at[n]).start()
        for src, dst, n in by_lanes:
            pltpu.make_async_copy(src.at[:, frame_lanes(f)], dst.at[:, frame_lanes(f)], out_sem.at[n]).start()

    def scores(i, j):
        s = dot(ka_ref[frame_rows(inside(j)), :], qe_s[inside(i)])
        return [s[:, head_lanes(h)] for h in HEADS]

    def gathered(j, ps):
        return [dot(vt_ref[head_rows(h), frame_lanes(inside(j), FROWS)], ps[h]) for h in HEADS]

    def attend(exact):
        def prepare(f):
            qt = qt_ref[:, frame_lanes(f)].astype(F32)
            own = qt * jnp.concatenate([kt_ref[:, frame_lanes(f, FROWS)].astype(F32), zpad], axis=1)
            for h in HEADS:
                if exact:
                    start = jnp.zeros((1, FLANES), F32)
                else:
                    start = jnp.sum(own[head_rows(h)], axis=0, keepdims=True)
                    m_s[f, h] = start
                aug = jnp.where(r32 == 26, 1.0, split_rows(-start, r32))
                qe_s[f, head_rows(h), head_lanes(h)] = (qt[head_rows(h)] + aug).astype(BF16)

        def finalize(i):
            outs, augs = [], []
            for h in HEADS:
                a = acc_s[i, h]
                l = a[24:25, :]
                bad_s[...] = jnp.maximum(bad_s[...], jnp.where(l < 1e30, 0.0, 1.0))
                outs.append(jnp.where(r32 < HEAD_DIM, a * (1.0 / l), 0.0))
                lse = m_s[i, h] + jnp.log2(l)
                q = qe_s[i, head_rows(h), head_lanes(h)].astype(F32)
                augs.append(jnp.where((r32 == 24) | (r32 == 25), split_rows(-lse, r32), q))
            ot = jnp.concatenate(outs, axis=0)
            ot_ref[:, frame_lanes(i)] = ot.astype(BF16)
            qa_ref[:, frame_lanes(i)] = jnp.concatenate(augs, axis=0).astype(BF16)
            o_ref[frame_rows(i), :] = ot.T[:FROWS, :].astype(BF16)

        def attend_pairs(pairs, first):
            ss = [scores(i, j) for i, j in pairs]
            if exact:
                old = [None if first else [m_s[i, h] for h in HEADS] for i, _ in pairs]
                for n, (i, j) in enumerate(pairs):
                    if not first:
                        old[n] = [m_s[i, h] for h in HEADS]
                    top = [jnp.max(ss[n][h], axis=0, keepdims=True) for h in HEADS]
                    if not first:
                        top = [jnp.maximum(old[n][h], top[h]) for h in HEADS]
                    pv = gathered(j, [jnp.exp2(ss[n][h] - top[h]).astype(BF16) for h in HEADS])
                    for h in HEADS:
                        acc_s[i, h] = pv[h] if first else acc_s[i, h] * jnp.exp2(old[n][h] - top[h]) + pv[h]
                        m_s[i, h] = top[h]
                return
            ps = [[jnp.exp2(s[h]).astype(BF16) for h in HEADS] for s in ss]
            pvs = [gathered(j, p) for (_, j), p in zip(pairs, ps)]
            for (i, _), pv in zip(pairs, pvs):
                for h in HEADS:
                    acc_s[i, h] = pv[h] if first else acc_s[i, h] + pv[h]

        bad_s[...] = jnp.zeros(bad_s.shape, F32)
        for k in range(TOGETHER):
            prepare(k)

        def diagonal(n, _):
            attend_pairs([(n * TOGETHER + k,) * 2 for k in range(TOGETHER)], True)
            for k in range(TOGETHER):
                prepare(jnp.minimum((n + 1) * TOGETHER, FRAMES - TOGETHER) + k)
            return 0
        lax.fori_loop(0, FRAMES // TOGETHER, diagonal, 0)
        each_pair(pairs_s, count, lambda pairs: attend_pairs(pairs, False))

        def close(n, _):
            for k in range(TOGETHER):
                finalize(n * TOGETHER + k)
            for k in range(TOGETHER):
                keep(n * TOGETHER + k)
            return 0
        lax.fori_loop(0, FRAMES // TOGETHER, close, 0)
        for src, dst, n in by_rows + by_lanes:
            pltpu.make_async_copy(src, dst, out_sem.at[n]).wait()

    attend(False)

    @pl.when(jnp.max(bad_s[...]) > 0.0)
    def _():
        attend(True)
    for copy in saved:
        copy.wait()


SMEM = pl.BlockSpec(memory_space=pltpu.SMEM)
HBM = pl.BlockSpec(memory_space=pltpu.HBM)


def in_hbm(value):
    return pltpu.with_memory_space_constraint(value, pltpu.HBM)
VM = pl.BlockSpec(memory_space=pltpu.VMEM)


def attn_fwd(seg, pad, pat, qt, ka, va, kt, vt):
    V = pltpu.VMEM
    rows, lanes = (FRAMES * FROWS, WIDE), (WIDE, FRAMES * FLANES)
    return pl.pallas_call(
        fwd_kernel,
        out_shape=tuple(pltpu.HBM(shape, BF16) for shape in (rows, lanes, lanes, rows, rows, lanes)),
        in_specs=[SMEM] * 3 + [VM] * 5,
        out_specs=(HBM,) * 6,
        scratch_shapes=[V(rows, BF16), V(lanes, BF16), V(lanes, BF16), V((FRAMES, WIDE, HEADS_LOCAL * FLANES), BF16),
                        V((FRAMES + 1, HEADS_LOCAL, 1, FLANES), F32), V((FRAMES + 1, HEADS_LOCAL, HW, FLANES), F32),
                        V((1, FLANES), F32), pltpu.SMEM((128 + UNROLL,), jnp.int32), pltpu.SemaphoreType.DMA((6,))],
        compiler_params=pltpu.CompilerParams(vmem_limit_bytes=26 << 20),
        cost_estimate=pl.CostEstimate(flops=int(2.5e10), bytes_accessed=8 << 20, transcendentals=0),
        name="attend_forward",
    )(seg, pad, pat, qt, ka, va, kt, vt)


def bwd_kernel(seg_ref, pad_ref, pat_ref, qa_ref, ka_ref, va_ref, kt_ref, ot_ref, do_ref, h_ref, w_ref, res_ref,
               dh_ref, early_ref, res_hbm, qe_s, oe_s, dq_s, dk_s, dv_s, dw_s, turn_s, blk_s, pairs_s, res_sem):
    carried = pltpu.make_async_copy(res_ref, res_hbm, res_sem.at[0])
    carried.start()
    scale = HEAD_DIM ** -0.5
    for s in (qe_s, oe_s):
        s[...] = jnp.zeros(s.shape, BF16)
    count = list_pairs(seg_ref, pad_ref, pat_ref, pairs_s)
    dw_s[...] = jnp.zeros(dw_s.shape, F32)
    real = lax.broadcasted_iota(jnp.int32, (WIDE, FROWS), 0) % HW < HEAD_DIM
    r32 = lax.broadcasted_iota(jnp.int32, (HW, FLANES), 0)
    zpad = jnp.zeros((WIDE, FLANES - FROWS), F32)

    def prepare(i):
        t = i
        qt = qa_ref[:, frame_lanes(i)]
        dot_ = jnp.concatenate([do_ref[frame_rows(i), :].astype(F32).T, zpad], axis=1)
        prod = dot_ * ot_ref[:, frame_lanes(i)].astype(F32)
        for h in HEADS:
            d = -jnp.sum(prod[head_rows(h)], axis=0, keepdims=True)
            qe_s[t, head_rows(h), head_lanes(h)] = qt[head_rows(h)]
            oe_s[t, head_rows(h), head_lanes(h)] = (dot_[head_rows(h)] + split_rows(d, r32)).astype(BF16)

    def scores(i, j):
        t, u = inside(i), inside(j)
        s, dp = dot(ka_ref[frame_rows(u), :], qe_s[t]), dot(va_ref[frame_rows(u), :], oe_s[t])
        ps = [jnp.exp2(s[:, head_lanes(h)]) for h in HEADS]
        return [p.astype(BF16) for p in ps], [(ps[h] * dp[:, head_lanes(h)]).astype(BF16) for h in HEADS]

    def products(i, j, pb, ds):
        t, u = inside(i), inside(j)
        dq = [dot(kt_ref[head_rows(h), frame_lanes(u, FROWS)], ds[h]) for h in HEADS]
        dv = [dot_nt(oe_s[t, head_rows(h), head_lanes(h)], pb[h]) for h in HEADS]
        dk = [dot_nt(qe_s[t, head_rows(h), head_lanes(h)], ds[h]) for h in HEADS]
        return [jnp.concatenate(value, axis=0) for value in (dq, dk, dv)]

    def attend_pairs(pairs, first):
        made = [scores(i, j) for i, j in pairs]
        values = [products(i, j, pb, ds) for (i, j), (pb, ds) in zip(pairs, made)]
        for (i, j), value in zip(pairs, values):
            for ref, at, part in ((dq_s, frame_lanes(i), 0), (dk_s, frame_lanes(j, FROWS), 1), (dv_s, frame_lanes(j, FROWS), 2)):
                ref[:, at] = value[part] if first else ref[:, at] + value[part]

    def finish(f):
        parts = (dq_s[:, frame_lanes(f, FROWS)] * scale, dk_s[:, frame_lanes(f, FROWS)] * math.log(2.0), dv_s[:, frame_lanes(f, FROWS)])
        grads = jnp.concatenate([jnp.where(real, part, 0.0).astype(BF16) for part in parts], axis=0)
        dh_ref[frame_rows(f), :] = dot_tn(grads, w_ref[...]).astype(BF16)
        return dot(grads, h_ref[frame_rows(f), :])

    for k in range(TOGETHER):
        prepare(k)

    def diagonal(n, _):
        attend_pairs([(n * TOGETHER + k,) * 2 for k in range(TOGETHER)], True)
        for k in range(TOGETHER):
            prepare(jnp.minimum((n + 1) * TOGETHER, FRAMES - TOGETHER) + k)
        return 0
    lax.fori_loop(0, FRAMES // TOGETHER, diagonal, 0)
    each_pair(pairs_s, count, lambda pairs: attend_pairs(pairs, False))

    def close(n, _):
        dw = [finish(n * TOGETHER + k) for k in range(TOGETHER)]
        dw_s[...] += functools.reduce(jnp.add, dw)
        return 0
    lax.fori_loop(0, FRAMES // TOGETHER, close, 0)
    for b in range(3):
        turned = dw_s[b * WIDE:(b + 1) * WIDE, :].T
        turn_s[:, 0:96] = jnp.concatenate([turned[:, HW * h:HW * h + HEAD_DIM] for h in HEADS], axis=1)
        line = [turn_s[pl.ds(k, 96, stride=4), :][:, 0:96] for k in range(4)]
        blk_s[pl.ds(0, 96, stride=3), :] = jnp.concatenate([line[0], line[1][:, :32]], axis=1)
        blk_s[pl.ds(1, 96, stride=3), :] = jnp.concatenate([line[1][:, 32:], line[2][:, :64]], axis=1)
        blk_s[pl.ds(2, 96, stride=3), :] = jnp.concatenate([line[2][:, 64:], line[3]], axis=1)
        early_ref[288 * b:288 * (b + 1), :] = blk_s[...].astype(BF16)
    carried.wait()


def attn_bwd(seg, pad, pat, qa, ka, va, kt, ot, do, h, w, result):
    sd = jax.ShapeDtypeStruct
    V = pltpu.VMEM
    return pl.pallas_call(
        bwd_kernel,
        out_shape=(sd((FRAMES * FROWS, D), BF16), sd((3 * 288, 128), BF16), pltpu.HBM(result.shape, BF16)),
        in_specs=[SMEM] * 3 + [VM] * 9,
        out_specs=(VM,) * 2 + (HBM,),
        scratch_shapes=[V((FRAMES, WIDE, HEADS_LOCAL * FLANES), BF16), V((FRAMES, WIDE, HEADS_LOCAL * FLANES), BF16)]
        + [V((WIDE, (FRAMES + 1) * FLANES), F32)] * 3
        + [V((3 * WIDE, D), F32), V((D, 128), F32), V((288, 128), F32),
           pltpu.SMEM((128 + UNROLL,), jnp.int32), pltpu.SemaphoreType.DMA((1,))],
        compiler_params=pltpu.CompilerParams(vmem_limit_bytes=42 << 20),
        cost_estimate=pl.CostEstimate(flops=int(5e10), bytes_accessed=12 << 20, transcendentals=0),
        name="attend_backward",
    )(seg, pad, pat, qa, ka, va, kt, ot, do, h, w, result)


MESH = pl.DeviceIdType.MESH
OWN_ROWS = 4 * FROWS


def place(d, m):
    return {"dp": d, "mp": m}


def remote(src, dst, send_sem, recv_sem, device):
    return pltpu.make_async_remote_copy(
        src_ref=src, dst_ref=dst, send_sem=send_sem, recv_sem=recv_sem, device_id=device, device_id_type=MESH
    )


def local(src, dst, sem):
    return pltpu.make_async_copy(src, dst, sem)


def greet(devices):
    barrier = pltpu.get_barrier_semaphore()
    for device in devices:
        pl.semaphore_signal(barrier, inc=1, device_id=device, device_id_type=MESH)
    return len(devices)


def met(count):
    pl.semaphore_wait(pltpu.get_barrier_semaphore(), count)


def group_peers():
    me = lax.axis_index("mp")
    return me, me ^ 1, me ^ 2, me ^ 3


def frame_part(device, c):
    return pl.ds(pl.multiple_of(device * OWN_ROWS + c * FROWS, 16), FROWS)


def normalised(v):
    centred = v - jnp.mean(v, axis=-1, keepdims=True)
    inv = lax.rsqrt(jnp.mean(centred * centred, axis=-1, keepdims=True) + NORM_EPS)
    return centred * inv, inv


def norm_pull(dy, hat, inv, gain):
    dg = dy * gain
    lead = jnp.mean(dg, axis=-1, keepdims=True)
    along = jnp.mean(dg * hat, axis=-1, keepdims=True)
    return inv * (dg - lead - hat * along)


def col_sum(v):
    return jnp.sum(v, axis=0, keepdims=True)


def load_frame(ref, c):
    base = c * PATCHES // 16 * 16
    rows = ref[base:base + FROWS, :].astype(F32)
    shift = c * PATCHES - base
    return pltpu.roll(rows, FROWS - shift, 0) if shift else rows


def live_rows():
    return lax.broadcasted_iota(jnp.int32, (FROWS, 1), 0) < PATCHES


def dp_peers(count):
    d = lax.axis_index("dp")
    side, line = d % 2, d // 2
    return side, line, {"dp": d ^ 1}, [lax.rem(line + n, count) for n in range(count)]


def start_kernel(count, x_hbm, np_hbm, w_hbm, m_hbm, v_hbm,
                 h_ref, qt_ref, ka_ref, va_ref, kt_ref, vt_ref, wa_ref, ws_ref, ma_ref, mb_ref,
                 x_ref, np_ref, w_ref, m_ref, v_ref, mo_s, w_s, load_x, load_w, keep_m,
                 send_x, recv_x, send_p, recv_p, send_f, recv_f, send_t, recv_t, send_l, recv_l):
    me, near, far, _ = group_peers()
    side, line, twin, around = dp_peers(count)
    frames = range(OWN_ROWS // FROWS)
    cuts = [0, 208, 400, 592, 784]
    loads = [local(x_hbm.at[a:b, :], x_ref.at[a:b, :], load_x.at[c]) for c, (a, b) in enumerate(zip(cuts, cuts[1:]))]
    others = [local(m_hbm, m_ref, load_w.at[0]), local(v_hbm, v_ref, load_w.at[1]), local(w_hbm, w_ref, load_w.at[2])]
    gains = local(np_hbm, np_ref, load_w.at[3])
    greeted = greet([{"mp": near}, {"mp": far}, twin] + [{"dp": q * 2 + side} for q in around[1:]])
    for copy in [gains] + loads + others:
        copy.start()
    live = live_rows()
    to_far, to_near, moments = [], [], []
    gains.wait()
    for c in frames:
        loads[c].wait()
        hat, _ = normalised(load_frame(x_ref, c))
        h_ref[frame_part(me, c), :] = jnp.where(live, hat * np_ref[0:1, :] + np_ref[1:2, :], 0.0).astype(BF16)
        rows = h_ref.at[frame_part(me, c), :]
        to_far.append(remote(rows, rows, send_x.at[c], recv_x.at[c], {"mp": far}))
        to_near.append(remote(rows, rows, send_p.at[c], recv_p.at[c], {"mp": near}))
        if c == 0:
            met(greeted)
        to_far[c].start()
        to_near[c].start()

    slots, rows = m_ref.shape[0], m_ref.shape[1]
    others[0].wait()
    others[1].wait()
    for r in range(2 * slots):
        mo_s[r // slots, pl.ds((r % slots) * rows, rows), :] = (v_ref if r % 2 else m_ref)[r // 2].astype(BF16)
    first, second = ma_ref.at[side, line], mb_ref.at[side]
    kept = [local(mo_s.at[0], first, keep_m.at[0]), local(mo_s.at[1], second, keep_m.at[1])]
    for n, q in enumerate(around[1:]):
        moments.append(remote(mo_s.at[0], first, send_l.at[n], recv_l.at[n], {"dp": q * 2 + side}))
    moments.append(remote(mo_s.at[0], first, send_t.at[0], recv_t.at[0], twin))
    moments.append(remote(mo_s.at[1], second, send_t.at[1], recv_t.at[1], twin))
    for copy in moments + kept:
        copy.start()

    def incoming(device, sends, recvs, c):
        rows = h_ref.at[frame_part(device, c), :]
        return remote(rows, rows, sends.at[c], recvs.at[c], {"mp": near})

    def forward(c):
        incoming(far, send_x, recv_x, c).wait_recv()
        copy = incoming(far, send_f, recv_f, c)
        copy.start()
        return copy

    others[2].wait()
    for b in range(3):
        a = [w_ref[b, pl.ds(k, 96, stride=3), :] for k in range(3)]
        lines = [a[0][:, :96], jnp.concatenate([a[0][:, 96:], a[1][:, :64]], axis=1),
                 jnp.concatenate([a[1][:, 64:], a[2][:, :32]], axis=1), a[2][:, 32:]]
        gap = jnp.zeros((96, HW - HEAD_DIM), F32)
        for k in range(4):
            parts = []
            for h in HEADS:
                parts += [lines[k][:, HEAD_DIM * h:HEAD_DIM * (h + 1)], gap]
            w_s[pl.ds(k, 96, stride=4), :] = jnp.concatenate(parts, axis=1)
        wa_ref[b * WIDE:(b + 1) * WIDE, :] = w_s[...].T.astype(BF16)

    col = lax.broadcasted_iota(jnp.int32, (FROWS, WIDE), 1) % HW
    ones = jnp.where((col == 24) | (col == 25), 1.0, 0.0)
    kadd = ones + jnp.where((col == 26) & jnp.logical_not(live), MASKED, 0.0)
    vtadd = jnp.where(lax.broadcasted_iota(jnp.int32, (WIDE, FROWS), 0) % HW == 24, 1.0, 0.0)
    zpad = jnp.zeros((WIDE, FLANES - FROWS), BF16)

    def project(devices, c):
        made = []
        for device in devices:
            hf = h_ref[frame_part(device, c), :]
            made.append((dot_nt(wa_ref[...], hf), dot_nt(hf, wa_ref[WIDE:3 * WIDE, :])))
        for device, (turned, lined) in zip(devices, made):
            f = device * (OWN_ROWS // FROWS) + c
            qt_ref[:, frame_lanes(f)] = jnp.concatenate([(turned[0:WIDE] * QSCALE).astype(BF16), zpad], axis=1)
            kt_ref[:, frame_lanes(f, FROWS)] = turned[WIDE:2 * WIDE].astype(BF16)
            vt_ref[:, frame_lanes(f, FROWS)] = (turned[2 * WIDE:3 * WIDE] + vtadd).astype(BF16)
            ka_ref[frame_rows(f), :] = (lined[:, 0:WIDE] + kadd).astype(BF16)
            va_ref[frame_rows(f), :] = (lined[:, WIDE:2 * WIDE] + ones).astype(BF16)

    copies = [forward(0)]
    for c in frames:
        incoming(near, send_p, recv_p, c).wait_recv()
        project((me, near), c)
    copies.append(forward(1))
    for b in range(3, w_ref.shape[0]):
        for k in range(3):
            lanes = slice(128 * k, 128 * (k + 1))
            part = w_ref[b, pl.ds(k, 96, stride=3), :]
            if b == 3:
                gap = jnp.zeros((HW - HEAD_DIM, 128), F32)
                parts = []
                for h in HEADS:
                    parts += [part[HEAD_DIM * h:HEAD_DIM * (h + 1)], gap]
                ws_ref[2 * D:2 * D + WIDE, lanes] = jnp.concatenate(parts, axis=0).astype(BF16)
            else:
                ws_ref[96 * (b - 4):96 * (b - 3), lanes] = part.astype(BF16)
    for c in frames:
        incoming(near ^ 2, send_f, recv_f, c).wait_recv()
        project((far, near ^ 2), c)
        if c + 2 < len(frames):
            copies.append(forward(c + 2))
    for n in range(1, count):
        part = ma_ref.at[side, around[count - n]]
        remote(part, part, send_l.at[n - 1], recv_l.at[n - 1], twin).wait_recv()
    part = ma_ref.at[1 - side, line]
    remote(part, part, send_t.at[0], recv_t.at[0], twin).wait_recv()
    part = mb_ref.at[1 - side]
    remote(part, part, send_t.at[1], recv_t.at[1], twin).wait_recv()
    for copy in kept:
        copy.wait()
    for copy in to_far + to_near + copies + moments:
        copy.wait_send()


def start_call(dp, x, norm_params, weights, first_moments, second_moments):
    sd, V, S = jax.ShapeDtypeStruct, pltpu.VMEM, pltpu.SemaphoreType.DMA
    blocks, count = weights.shape[0], dp // 2
    half = first_moments.shape[0] * first_moments.shape[1]
    rows, lanes = sd((FRAMES * FROWS, WIDE), BF16), sd((WIDE, FRAMES * FLANES), BF16)
    return pl.pallas_call(
        functools.partial(start_kernel, count),
        out_shape=(sd((FRAMES * FROWS, D), BF16), lanes, rows, rows, lanes, lanes, sd((3 * WIDE, D), BF16),
                   sd((WIDE + 96 * (blocks - 4), D), BF16),
                   pltpu.HBM((2, count, half, 128), BF16), pltpu.HBM((2, half, 128), BF16)),
        in_specs=[HBM] * 5,
        out_specs=(VM,) * 8 + (HBM,) * 2,
        scratch_shapes=[V(x.shape, BF16), V(norm_params.shape, F32), V(weights.shape, F32), V(first_moments.shape, F32),
                        V(first_moments.shape, F32), V((2, half, 128), BF16), V((D, WIDE), F32),
                        S((4,)), S((4,)), S((2,))] + [S((4,))] * 6 + [S((2,))] * 2 + [S((count,))] * 2,
        compiler_params=pltpu.CompilerParams(vmem_limit_bytes=24 << 20, collective_id=1, has_side_effects=True),
        name="norm_and_gather",
    )(*[in_hbm(value) for value in (x, norm_params, weights, first_moments, second_moments)])


def gelu_parts(u):
    lead = math.sqrt(2.0 / math.pi)
    bend = lead * 0.044715
    square = u * u
    half = 0.5 + 0.5 * jnp.tanh(u * (lead + bend * square))
    slope = half + 2.0 * u * (half - half * half) * (lead + 3.0 * bend * square)
    return u * half, slope


def middle_kernel(count, o_ref, x_hbm, ct_hbm, pad_ref, w0_ref, w1_ref, np_hbm, ma_ref, mb_ref,
                  out_ref, dx2_ref, do_ref, l0_ref, l1_ref, l2_ref, l3_ref, nb_ref, mom_ref,
                  ob_s, dob_s, g_s, a_s, du_s, da_s, h2_s, dxa_s, blk_s, res_s, ut_s, wot_s,
                  x_ref, ct_ref, o_s, w2_ref, w3_ref, np_ref, load_s, send_w, recv_w,
                  send_o, recv_o, send_d, recv_d, send_t, recv_t, send_l, recv_l, send_f, recv_f):
    me, near, far, across = group_peers()
    side, line, twin, around = dp_peers(count)
    peers = (far, across, near)
    mine = pl.ds(pl.multiple_of(me * OWN_ROWS, 16), OWN_ROWS)
    loads = [local(ct_hbm, ct_ref, load_s.at[0]), local(x_hbm, x_ref, load_s.at[1]), local(o_ref.at[mine, :], o_s, load_s.at[2]), local(np_hbm, np_ref, load_s.at[3])]
    greeted = greet([{"mp": p} for p in peers] + [twin] + [{"dp": q * 2 + side} for q in around[1:]])
    for copy in loads:
        copy.start()
    frames = range(OWN_ROWS // FROWS)
    live = live_rows()
    shards_w = (w0_ref, w1_ref, w2_ref, w3_ref)
    late = (l0_ref, l1_ref, l2_ref, l3_ref)
    places = range(len(shards_w))
    loads[0].wait()
    for c in frames:
        rows = slice(c * FROWS, (c + 1) * FROWS)
        g_s[rows, :] = jnp.where(live, load_frame(ct_ref, c) * (1 - pad_ref[0, me * len(frames) + c]).astype(F32), 0.0).astype(BF16)
    met(greeted)
    outgoing = []
    for c in frames:
        for n, p in enumerate(peers):
            outgoing.append(remote(o_ref.at[frame_part(p, c), :], ob_s.at[n, pl.ds(c * FROWS, FROWS), :],
                                   send_o.at[n, c], recv_o.at[n, c], {"mp": p}))
            outgoing[-1].start()
    weights = [remote(w0_ref, w3_ref, send_w.at[0], recv_w.at[0], {"mp": near}),
               remote(w1_ref, w2_ref, send_w.at[1], recv_w.at[1], {"mp": near})]
    for copy in weights:
        copy.start()
    moments = []
    for n, q in enumerate(around[1:]):
        own_half = mb_ref.at[side]
        moments.append(remote(own_half, mom_ref.at[1, side, line], send_l.at[n], recv_l.at[n], {"dp": q * 2 + side}))
        moments.append(remote(ma_ref.at[side, q], mom_ref.at[0, side, q], send_t.at[q], recv_t.at[q], twin))
    for copy in moments:
        copy.start()

    def pass_moments(n):
        q = around[count - n]
        part = mom_ref.at[1, side, q]
        remote(part, part, send_l.at[n - 1], recv_l.at[n - 1], twin).wait_recv()
        moments.append(remote(part, part, send_f.at[q], recv_f.at[q], twin))
        moments[-1].start()

    def w_up(m):
        return shards_w[m][0:D, :]

    def w_down(m):
        return shards_w[m][D:2 * D, :]

    def w_o(m):
        return shards_w[m][2 * D:2 * D + WIDE, :]

    def cols(m):
        return slice(m * D, (m + 1) * D)

    for m in (0, 1, 3, 2):
        if m > 1:
            weights[3 - m].wait_recv()
        da_s[:, cols(m)] = dot_nt(g_s[...], w_down(m))
        ut_s[cols(m), :] = w_up(m).astype(F32).T.astype(BF16)
        wot_s[:, m * WIDE:(m + 1) * WIDE] = w_o(m).astype(F32).T.astype(BF16)
    for copy in loads[1:]:
        copy.wait()
    nb_ref[...] = jnp.zeros(nb_ref.shape, F32)
    down = jnp.concatenate([w_down(m) for m in places], axis=0)
    out_w = jnp.concatenate([w_o(m) for m in places], axis=0)
    sent, left = [], list(range(1, count))
    for both in ((0,), (1, 2), (3,)):
        rows = slice(both[0] * FROWS, (both[-1] + 1) * FROWS)
        for c in both:
            for n, p in enumerate(peers):
                part = ob_s.at[n, pl.ds(c * FROWS, FROWS), :]
                remote(part, part, send_o.at[n, c], recv_o.at[n, c], {"mp": p}).wait_recv()
        own_rows = pl.ds(pl.multiple_of(me * OWN_ROWS + both[0] * FROWS, 16), len(both) * FROWS)
        heads = jnp.concatenate([o_s[rows, :]] + [ob_s[n, rows, :] for n in range(len(peers))], axis=1)
        x2 = jnp.concatenate([load_frame(x_ref, c) for c in both], axis=0) + dot(heads, out_w)
        x2 = jnp.where(jnp.concatenate([live] * len(both), axis=0), x2, 0.0)
        hat, inv = normalised(x2)
        h2 = (hat * np_ref[2:3, :] + np_ref[3:4, :]).astype(BF16)
        h2_s[rows, :] = h2
        for m in places:
            value, slope = gelu_parts(dot(h2, w_up(m)))
            a_s[rows, cols(m)] = value.astype(BF16)
            du_s[rows, cols(m)] = (da_s[rows, cols(m)] * slope).astype(BF16)
        if left and len(both) > 1:
            pass_moments(left.pop(0))
        result = x2 + dot(a_s[rows, :], down)
        for k, c in enumerate(both):
            res_s[pl.ds(c * PATCHES, FROWS), :] = result[k * FROWS:(k + 1) * FROWS]
        dh2 = dot(du_s[rows, :], ut_s[...])
        nb_ref[0:1, :] += col_sum(dh2 * hat)
        nb_ref[1:2, :] += col_sum(dh2)
        dx2 = g_s[rows, :].astype(F32) + norm_pull(dh2, hat, inv, np_ref[2:3, :])
        dx2_ref[rows, :] = dx2
        dxa = dx2.astype(BF16)
        dxa_s[rows, :] = dxa
        d_heads = dot(dxa, wot_s[...]).astype(BF16)
        for n in range(len(peers)):
            dob_s[n, rows, :] = d_heads[:, (n + 1) * WIDE:(n + 2) * WIDE]
        for c in both:
            for n, p in enumerate(peers):
                sent.append(remote(dob_s.at[n, pl.ds(c * FROWS, FROWS), :], do_ref.at[frame_part(me, c), :],
                                   send_d.at[n, c], recv_d.at[n, c], {"mp": p}))
                sent[-1].start()
        do_ref[own_rows, :] = d_heads[:, 0:WIDE]
        if left and both[-1] < 3:
            pass_moments(left.pop(0))
    while left:
        pass_moments(left.pop(0))
    out_ref[...] = res_s[0:out_ref.shape[0], :].astype(BF16)

    def as_block(shard, first, value):
        size = value.shape[0]
        for k in range(3):
            blk_s[pl.ds(k, size, stride=3), :] = value[:, 128 * k:128 * (k + 1)]
        late[shard][first * 288:first * 288 + 3 * size, :] = blk_s[0:3 * size, :].astype(BF16)

    def drop_gaps(value):
        return jnp.concatenate([value[HW * h:HW * h + HEAD_DIM] for h in HEADS], axis=0)

    dw1 = dot_tn(h2_s[...], du_s[...])
    dw2 = dot_tn(g_s[...], a_s[...])
    for m in places:
        as_block(m, 1, dw1[:, cols(m)])
        as_block(m, 5, dw2[:, cols(m)].T)
        o_m = o_s[...] if m == 0 else ob_s[m - 1]
        as_block(m, 0, drop_gaps(dot_tn(o_m, dxa_s[...])))
    for c in frames:
        for n, p in enumerate(peers):
            part = do_ref.at[frame_part(p, c), :]
            remote(part, part, send_d.at[n, c], recv_d.at[n, c], {"mp": p}).wait_recv()
    for q in around[1:]:
        for half, sends, recvs in ((0, send_t, recv_t), (1, send_f, recv_f)):
            part = mom_ref.at[half, 1 - side, q]
            remote(part, part, sends.at[q], recvs.at[q], twin).wait_recv()
    for copy in outgoing + sent + moments + weights:
        copy.wait_send()


def middle_call(dp, o, x, ct, padding, w, norm_params, ma, mb):
    sd = jax.ShapeDtypeStruct
    V, S = pltpu.VMEM, pltpu.SemaphoreType.DMA
    count = dp // 2
    late = sd((9 * 288, 128), BF16)
    return pl.pallas_call(
        functools.partial(middle_kernel, count),
        out_shape=(sd(x.shape, BF16), sd((OWN_ROWS, D), F32), sd((FRAMES * FROWS, WIDE), BF16),
                   late, late, late, late, sd((2, D), F32), pltpu.HBM((2,) + ma.shape, BF16)),
        in_specs=[HBM, HBM, HBM, SMEM] + [VM] * 2 + [HBM] * 3,
        out_specs=(VM,) * 8 + (HBM,),
        scratch_shapes=[V((3, OWN_ROWS, WIDE), BF16), V((3, OWN_ROWS, WIDE), BF16), V((OWN_ROWS, D), BF16),
                        V((OWN_ROWS, FF), BF16), V((OWN_ROWS, FF), BF16), V((OWN_ROWS, FF), F32),
                        V((OWN_ROWS, D), BF16), V((OWN_ROWS, D), BF16), V((1152, 128), F32), V((OWN_ROWS, D), F32),
                        V((FF, D), BF16), V((D, 4 * WIDE), BF16),
                        V(x.shape, BF16), V(x.shape, BF16), V((OWN_ROWS, WIDE), BF16), V(w[0].shape, BF16), V(w[0].shape, BF16), V(norm_params.shape, F32), S((4,)), S((2,)), S((2,)), S((3, 4)), S((3, 4)), S((3, 4)), S((3, 4))] + [S((count,))] * 6,
        compiler_params=pltpu.CompilerParams(vmem_limit_bytes=36 << 20, collective_id=2, has_side_effects=True),
        cost_estimate=pl.CostEstimate(flops=int(6e9), bytes_accessed=12 << 20, transcendentals=0),
        name="feed_forward",
    )(in_hbm(o), in_hbm(x), in_hbm(ct), padding, *w, in_hbm(norm_params), in_hbm(ma), in_hbm(mb))


def reduce_kernel(dp, piece, dh_ref, early_ref, l0_ref, l1_ref, l2_ref, l3_ref, x_ref, dx2_ref, np_ref, nb_ref,
                  gin_ref, gs_ref, tot_ref,
                  res_s, pb_s, xs_s, xb_s, g_s, yb_s, zs_s, zb_s, msg_s, mb_s, dm_s, db_s,
                  send_p, recv_p, send_x, recv_x, send_y, recv_y, send_z, recv_z,
                  send_a, recv_a, send_w, recv_w, send_m, recv_m, send_n, recv_n):
    me, near, far, across = group_peers()
    d = lax.axis_index("dp")
    count = dp // 2
    side, line = d % 2, d // 2
    twin = {"dp": d ^ 1}

    order, top = [], count
    while top > 1:
        top //= 2
        order += range(top, 2 * top)
    turns = [line ^ n for n in order]
    cut = -(-piece // 32) * 16
    halves = [(0, cut), (cut, piece - cut)]

    def line_device(q):
        return {"dp": q * 2 + side}

    frames = range(OWN_ROWS // FROWS)
    greeted = greet([{"mp": near}, {"mp": far}, {"mp": across}] + [{"dp": d ^ n} for n in range(1, dp)])
    total = early_ref.shape[0] + l0_ref.shape[0]
    g_s[0:early_ref.shape[0], :] = early_ref[...]
    g_s[early_ref.shape[0]:total, :] = (l0_ref[...].astype(F32) + l1_ref[...].astype(F32)
                                        + (l2_ref[...].astype(F32) + l3_ref[...].astype(F32))).astype(BF16)
    if g_s.shape[0] > total:
        g_s[total:, :] = jnp.zeros((g_s.shape[0] - total, 128), BF16)
    met(greeted)

    def own(c):
        return pl.ds(c * FROWS, FROWS)

    to_near = []
    for k, target in ((1, across), (0, near)):
        for c in frames:
            to_near.append(remote(dh_ref.at[frame_part(target, c), :], pb_s.at[k, own(c), :],
                                  send_p.at[k, c], recv_p.at[k, c], {"mp": near}))
            to_near[-1].start()

    def at(s, q, k):
        return pl.ds(pl.multiple_of((s * count + q) * piece + halves[k][0], 16), halves[k][1])

    def part(ref, q, k):
        return ref.at[q, pl.ds(*halves[k]), :]

    to_twin = []
    for q in turns + [line]:
        for k in range(2):
            to_twin.append(remote(g_s.at[at(1 - side, q, k), :], part(yb_s, q, k), send_y.at[q, k], recv_y.at[q, k], twin))
            to_twin[-1].start()

    to_far = []
    for c in frames:
        remote(pb_s.at[1, own(c), :], pb_s.at[1, own(c), :], send_p.at[1, c], recv_p.at[1, c], {"mp": near}).wait_recv()
        xs_s[own(c), :] = (dh_ref[frame_part(far, c), :].astype(F32) + pb_s[1, own(c), :].astype(F32)).astype(BF16)
        to_far.append(remote(xs_s.at[own(c), :], xb_s.at[own(c), :], send_x.at[c], recv_x.at[c], {"mp": far}))
        to_far[-1].start()

    to_line = []
    for q in turns + [line]:
        for k in range(2):
            got = part(yb_s, q, k)
            remote(got, got, send_y.at[q, k], recv_y.at[q, k], twin).wait_recv()
            rows = pl.ds(*halves[k])
            zs_s[q, rows, :] = (g_s[at(side, q, k), :].astype(F32) + yb_s[q, rows, :].astype(F32)).astype(BF16)
            if q is not line:
                to_line.append(remote(part(zs_s, q, k), part(zb_s, line, k), send_z.at[q, k], recv_z.at[line, k], line_device(q)))
                to_line[-1].start()
    live = live_rows()
    norm_sums = [jnp.zeros((1, D), F32), jnp.zeros((1, D), F32)]

    def norm_frame(c):
        remote(pb_s.at[0, own(c), :], pb_s.at[0, own(c), :], send_p.at[0, c], recv_p.at[0, c], {"mp": near}).wait_recv()
        remote(xb_s.at[own(c), :], xb_s.at[own(c), :], send_x.at[c], recv_x.at[c], {"mp": far}).wait_recv()
        dy = dh_ref[frame_part(me, c), :].astype(F32) + pb_s[0, own(c), :].astype(F32) + xb_s[own(c), :].astype(F32)
        dy = jnp.where(live, dy, 0.0)
        hat, inv = normalised(load_frame(x_ref, c))
        norm_sums[0] = norm_sums[0] + col_sum(dy * hat)
        norm_sums[1] = norm_sums[1] + col_sum(dy)
        res_s[pl.ds(c * PATCHES, FROWS), :] = dx2_ref[own(c), :] + norm_pull(dy, hat, inv, np_ref[0:1, :])

    norm_frame(0)
    norm_frame(1)
    spread, passed = [], []
    squares = jnp.zeros((1, 128), F32)
    for k in range(2):
        rows = pl.ds(*halves[k])
        mine = zs_s[line, rows, :].astype(F32)
        for q in turns:
            got = part(zb_s, q, k)
            remote(got, got, send_z.at[q, k], recv_z.at[q, k], line_device(q)).wait_recv()
            mine = mine + zb_s[q, rows, :].astype(F32)
        mine = mine.astype(BF16)
        gs_ref[at(side, line, k), :] = mine
        whole = gs_ref.at[at(side, line, k), :]
        for q in turns:
            spread.append(remote(whole, whole, send_a.at[q, k], recv_a.at[line, k], line_device(q)))
        passed.append(remote(whole, whole, send_w.at[line, k], recv_w.at[line, k], twin))
        for copy in spread[-len(turns):] + passed[-1:]:
            copy.start()
        mine = mine.astype(F32)
        squares = squares + col_sum(mine * mine)
        norm_frame(2 + k)

    msg_s[...] = jnp.zeros(msg_s.shape, F32)
    msg_s[0:1, :] = norm_sums[0]
    msg_s[1:2, :] = norm_sums[1]
    msg_s[2:4, :] = nb_ref[...]
    msg_s[4:5, 0:128] = squares
    small = []
    for n, p in enumerate((near, far, across)):
        small.append(remote(msg_s, mb_s.at[n], send_m.at[n], recv_m.at[n], {"mp": p}))
        small[-1].start()

    def pass_on(q, k):
        piece_at = gs_ref.at[at(side, q, k), :]
        remote(piece_at, piece_at, send_a.at[q, k], recv_a.at[q, k], line_device(q)).wait_recv()
        passed.append(remote(piece_at, piece_at, send_w.at[q, k], recv_w.at[q, k], twin))
        passed[-1].start()

    pass_on(turns[0], 0)
    add = msg_s[...]
    for n, p in enumerate((near, far, across)):
        remote(mb_s.at[n], mb_s.at[n], send_m.at[n], recv_m.at[n], {"mp": p}).wait_recv()
        add = add + mb_s[n]
    dm_s[...] = add
    for n in range(1, dp):
        small.append(remote(dm_s, db_s.at[n], send_n.at[n], recv_n.at[n], {"dp": d ^ n}))
        small[-1].start()
    for k in range(2):
        for q in turns[1 - k:]:
            pass_on(q, k)
    gin_ref[...] = res_s[0:gin_ref.shape[0], :].astype(BF16)
    for n in range(1, dp):
        remote(db_s.at[n], db_s.at[n], send_n.at[n], recv_n.at[n], {"dp": d ^ n}).wait_recv()
        add = add + db_s[n]
    tot_ref[...] = add
    for k in range(2):
        for q in turns + [line]:
            piece_at = gs_ref.at[at(1 - side, q, k), :]
            remote(piece_at, piece_at, send_w.at[q, k], recv_w.at[q, k], twin).wait_recv()
    for copy in to_near + to_twin + to_far + to_line + spread + passed + small:
        copy.wait_send()


def reduce_call(dp, dh, early, late, x, dx2, norm_params, nb):
    sd = jax.ShapeDtypeStruct
    V, S = pltpu.VMEM, pltpu.SemaphoreType.DMA
    rows = early.shape[0] + late[0].shape[0]
    count = dp // 2
    piece = -(-rows // (2 * count * 16)) * 16
    held = 2 * count * piece
    return pl.pallas_call(
        functools.partial(reduce_kernel, dp, piece),
        out_shape=(sd(x.shape, BF16), sd((held, 128), BF16), sd((8, D), F32)),
        in_specs=[VM] * 10,
        out_specs=(VM,) * 3,
        scratch_shapes=[V((OWN_ROWS, D), F32), V((2, OWN_ROWS, D), BF16), V((OWN_ROWS, D), BF16), V((OWN_ROWS, D), BF16), V((held, 128), BF16),
                        V((count, piece, 128), BF16), V((count, piece, 128), BF16), V((count, piece, 128), BF16),
                        V((8, D), F32), V((3, 8, D), F32), V((8, D), F32), V((dp, 8, D), F32),
                        S((2, 4)), S((2, 4)), S((4,)), S((4,))] + [S((count, 2))] * 8 + [S((3,)), S((3,)), S((dp,)), S((dp,))],
        compiler_params=pltpu.CompilerParams(vmem_limit_bytes=22 << 20, collective_id=3, has_side_effects=True),
        name="reduce_gradients",
    )(dh, early, *late, x, dx2, norm_params, nb)


def update_kernel(slot_ref, dev_ref, gin_ref, tot_ref, gs_ref, w_ref, m_ref, v_ref, ma_ref, mb_ref, mom_ref, np_ref, nm_ref, nv_ref,
                  gout_ref, norm_ref, nw_hbm, nf_hbm, ns_hbm, nn_ref, nnf_ref, nns_ref, nw_ref, nf_ref, ns_ref, sem_s):
    carried = [local(gin_ref, gout_ref, sem_s.at[0])]
    for copy in carried:
        copy.start()
    blocks, rows, _ = w_ref.shape
    slots = m_ref.shape[0]
    tot = tot_ref[...]
    grads = tot[0:4, :]
    norm = jnp.sqrt(jnp.sum(grads * grads, keepdims=True) + jnp.sum(tot[4:5, 0:128], keepdims=True))
    norm_ref[...] = norm
    clip_level = 0.5 * (4 * D * D + 2 * D * FF + 4 * D) ** 0.5
    factor = jnp.minimum(1.0, clip_level / norm)
    nn_ref[...], nnf_ref[...], nns_ref[...] = adam_update(
        np_ref[...], grads * factor, nm_ref[...], nv_ref[...], 0.0, NORM_RATE)

    def block(b):
        return gs_ref[pl.ds(pl.multiple_of(b * rows, 16), rows), :].astype(F32) * factor

    for s in range(slots):
        owned = jnp.int32(-1)
        for b in range(blocks):
            owned = jnp.where(slot_ref[b] == dev_ref[0] * slots + s, b, owned)
        _, first, second = adam_update(0.0, block(jnp.maximum(owned, 0)), m_ref[s], v_ref[s], 0.0, LEARN_RATE)
        nf_ref[s] = jnp.where(owned >= 0, first, m_ref[s])
        ns_ref[s] = jnp.where(owned >= 0, second, v_ref[s])
    leaving = [local(nf_ref, nf_hbm, sem_s.at[2]), local(ns_ref, ns_hbm, sem_s.at[3])]
    for copy in leaving:
        copy.start()

    def step(b, _):
        holder, first = slot_ref[b] // slots, slot_ref[b] % slots * 2
        side, line = holder % 2, holder // 2
        on_side, on_line = side == dev_ref[0] % 2, line == dev_ref[0] // 2

        def moment(r):
            at = pl.ds(pl.multiple_of(r % slots * rows, 16), rows)
            late = mom_ref[r // slots, side, line, at, :]
            lead = jnp.where(on_side | on_line, ma_ref[side, line, at, :], late)
            rest = jnp.where(on_line, mb_ref[side, at, :], late)
            return jnp.where(r < slots, lead, rest).astype(F32)

        old = [moment(first), moment(first + 1)]
        nw_ref[b], _, _ = adam_update(w_ref[b], block(b), old[0], old[1], WEIGHT_DECAY, LEARN_RATE)
        local(nw_ref.at[b], nw_hbm.at[b], sem_s.at[4]).start()
        return 0
    lax.fori_loop(0, blocks, step, 0)
    for copy in carried + leaving + [local(nw_ref, nw_hbm, sem_s.at[4])]:
        copy.wait()


def update_call(owner_slot, grad_in, tot, gs, weights, first, second, ma, mb, moments, norm_params, norm_first, norm_second):
    sd = jax.ShapeDtypeStruct
    small = sd((4, D), F32)
    device = lax.axis_index("dp").reshape(1)
    return pl.pallas_call(
        update_kernel,
        out_shape=(pltpu.HBM(grad_in.shape, BF16), sd((1, 1), F32), pltpu.HBM(weights.shape, F32),
                   pltpu.HBM(first.shape, F32), pltpu.HBM(first.shape, F32), small, small, small),
        in_specs=[SMEM] * 2 + [VM] * 12,
        out_specs=(HBM, VM) + (HBM,) * 3 + (VM,) * 3,
        scratch_shapes=[pltpu.VMEM(weights.shape, F32), pltpu.VMEM(first.shape, F32), pltpu.VMEM(first.shape, F32),
                        pltpu.SemaphoreType.DMA((5,))],
        compiler_params=pltpu.CompilerParams(vmem_limit_bytes=16 << 20),
        name="clipped_update",
    )(owner_slot, device, grad_in, tot, gs, weights, first, second, ma, mb, moments, norm_params, norm_first, norm_second)


def adam_update(current, gradient, first_moment, second_moment, decay_rate, step_rate):
    first_new = BETA_ONE * first_moment + (1.0 - BETA_ONE) * gradient
    second_new = BETA_TWO * second_moment + (1.0 - BETA_TWO) * gradient * gradient
    first_fix = 1.0 / (1.0 - BETA_ONE**STEP)
    second_fix = 1.0 / (1.0 - BETA_TWO**STEP)
    direction = first_new * (step_rate * first_fix) / (jnp.sqrt(second_new * second_fix) + ADAM_EPS)
    return (current * (1.0 - step_rate * decay_rate) - direction, first_new, second_new)


def from_peer(value, distance):
    return lax.ppermute(value, "mp", [(i, i ^ distance) for i in range(lax.axis_size("mp"))])


def shards(tokens, cotangent, segment_ids, padding, pattern, owner_slot, weights, first_moments, second_moments,
           norm_params, norm_first, norm_second):
    dp = lax.axis_size("dp")
    x, ct = tokens[0], cotangent[0]
    h1, qt, ka, va, kt, vt, wa, own_shared, ma, mb = start_call(dp, x, norm_params, weights, first_moments, second_moments)
    shared = [own_shared, from_peer(own_shared, 2)]
    o, ot, qa, ka, va, kt = attn_fwd(segment_ids, padding, pattern, qt, ka, va, kt, vt)
    result, dx2, do, *late, nb, moments = middle_call(dp, o, x, ct, padding, shared, norm_params, ma, mb)
    late = [late[0], from_peer(late[1], 2), from_peer(late[2], 3), from_peer(late[3], 1)]
    dh, early, result = attn_bwd(segment_ids, padding, pattern, qa, ka, va, kt, ot, do, h1, wa, result)
    grad_in, gs, tot = reduce_call(dp, dh, early, late, x, dx2, norm_params, nb)
    grad_in, grad_norm, new_weights, new_first, new_second, new_norm, new_norm_first, new_norm_second = update_call(
        owner_slot, grad_in, tot, gs, weights, first_moments, second_moments, ma, mb, moments, norm_params, norm_first, norm_second)
    return (result[None], grad_in[None], grad_norm[0, 0], new_weights, new_first, new_second,
            new_norm, new_norm_first, new_norm_second)


def solution(mesh):
    rows, blocks, slots = P("dp", "mp", None), P(None, "mp", None), P("dp", "mp", None)
    return jax.shard_map(
        shards,
        mesh=mesh,
        in_specs=(rows, rows, P("dp", None), P("dp", None), P(), P(), blocks, slots, slots, P(), P(), P()),
        out_specs=(rows, rows, P(), blocks, slots, slots, P(), P(), P()),
        check_vma=False,
    )
```

```python
import functools
import math

import jax
import jax.numpy as jnp
from jax import lax
from jax.experimental import pallas as pl
from jax.experimental.pallas import tpu as pltpu
from jax.sharding import PartitionSpec as P

FF = 1536
STEP = 10
NORM_EPS = 1e-05
BETA_ONE = 0.9
BETA_TWO = 0.95
ADAM_EPS = 1e-08
LEARN_RATE = 0.15
NORM_RATE = 0.6
WEIGHT_DECAY = 0.05

D = 384
HEAD_DIM = 24
FRAMES = 16
PATCHES = 196
FROWS = 208
FLANES = 256
HW = 32
HEADS_LOCAL = 4
WIDE = HEADS_LOCAL * HW
MASKED = -1e30
QSCALE = math.log2(math.e) / math.sqrt(HEAD_DIM)
F32 = jnp.float32
BF16 = jnp.bfloat16
NT = (((1,), (1,)), ((), ()))
TN = (((0,), (0,)), ((), ()))
HEADS = range(HEADS_LOCAL)
UNROLL = 6
LISTED = 136
TOGETHER = 4


def dot(a, b):
    return jnp.dot(a, b, preferred_element_type=F32)


def dot_nt(a, b):
    return lax.dot_general(a, b, NT, preferred_element_type=F32)


def dot_tn(a, b):
    return lax.dot_general(a, b, TN, preferred_element_type=F32)


def frame_rows(f):
    return pl.ds(pl.multiple_of(f * FROWS, 16), FROWS)


def frame_lanes(f, size=FLANES):
    return pl.ds(pl.multiple_of(f * FLANES, 128), size)


def head_rows(h):
    return slice(HW * h, HW * (h + 1))


def head_lanes(h):
    return slice(FLANES * h, FLANES * (h + 1))


def list_pairs(seg_ref, pad_ref, pat_ref, pairs_s):
    def rows(i, carry):
        start, count = carry
        start = jnp.where(seg_ref[0, i] == seg_ref[0, jnp.maximum(i - 1, 0)], start, i)

        def cols(j, count):
            pairs_s[count] = i * 32 + j
            return count + jnp.where((pat_ref[i, j] == 1) & (pad_ref[0, j] == 0), 1, 0)
        return start, lax.fori_loop(start, i, cols, count)
    _, count = lax.fori_loop(0, FRAMES, rows, (jnp.int32(0), jnp.int32(0)))
    for n in range(UNROLL):
        pairs_s[count + n] = FRAMES * 33
    pairs_s[LISTED - 1] = count
    return count


def each_pair(pairs_s, count, work):
    def step(first, size):
        def body(n, _):
            codes = [pairs_s[first + n * size + u] for u in range(size)]
            work([(code // 32, code % 32) for code in codes])
            return 0
        return body
    whole = count // UNROLL
    lax.fori_loop(0, whole, step(0, UNROLL), 0)
    lax.fori_loop(0, (count - whole * UNROLL + 1) // 2, step(whole * UNROLL, 2), 0)


def inside(f):
    return jnp.minimum(f, FRAMES - 1)


def split_rows(value, r32):
    high = value.astype(BF16).astype(F32)
    return jnp.where(r32 == 24, high, jnp.where(r32 == 25, value - high, 0.0))


def fwd_kernel(seg_ref, pad_ref, pat_ref, qt_ref, ka_ref, va_ref, kt_ref, vt_ref,
               o_hbm, ot_hbm, qa_hbm, ka_hbm, va_hbm, kt_hbm, pairs_s,
               o_ref, ot_ref, qa_ref, qe_s, m_s, acc_s, bad_s, out_sem):
    zpad = jnp.zeros((WIDE, FLANES - FROWS), F32)
    r32 = lax.broadcasted_iota(jnp.int32, (HW, FLANES), 0)
    by_rows = [(o_ref, o_hbm, 0)]
    by_lanes = [(ot_ref, ot_hbm, 1), (qa_ref, qa_hbm, 2)]
    saved = [pltpu.make_async_copy(src, dst, out_sem.at[n])
             for n, (src, dst) in enumerate(((ka_ref, ka_hbm), (va_ref, va_hbm), (kt_ref, kt_hbm)), 3)]
    for copy in saved:
        copy.start()
    qe_s[...] = jnp.zeros(qe_s.shape, BF16)
    count = list_pairs(seg_ref, pad_ref, pat_ref, pairs_s)

    def keep(f):
        for src, dst, n in by_rows:
            pltpu.make_async_copy(src.at[frame_rows(f), :], dst.at[frame_rows(f), :], out_sem.at[n]).start()
        for src, dst, n in by_lanes:
            pltpu.make_async_copy(src.at[:, frame_lanes(f)], dst.at[:, frame_lanes(f)], out_sem.at[n]).start()

    def scores(i, j):
        s = dot(ka_ref[frame_rows(inside(j)), :], qe_s[inside(i)])
        return [s[:, head_lanes(h)] for h in HEADS]

    def gathered(j, ps):
        return [dot(vt_ref[head_rows(h), frame_lanes(inside(j), FROWS)], ps[h]) for h in HEADS]

    def attend(exact):
        def prepare(f):
            qt = qt_ref[:, frame_lanes(f)].astype(F32)
            own = qt * jnp.concatenate([kt_ref[:, frame_lanes(f, FROWS)].astype(F32), zpad], axis=1)
            for h in HEADS:
                if exact:
                    start = jnp.zeros((1, FLANES), F32)
                else:
                    start = jnp.sum(own[head_rows(h)], axis=0, keepdims=True)
                    m_s[f, h] = start
                aug = jnp.where(r32 == 26, 1.0, split_rows(-start, r32))
                qe_s[f, head_rows(h), head_lanes(h)] = (qt[head_rows(h)] + aug).astype(BF16)

        def finalize(i):
            outs, augs = [], []
            for h in HEADS:
                a = acc_s[i, h]
                l = a[24:25, :]
                bad_s[...] = jnp.maximum(bad_s[...], jnp.where(l < 1e30, 0.0, 1.0))
                outs.append(jnp.where(r32 < HEAD_DIM, a * (1.0 / l), 0.0))
                lse = m_s[i, h] + jnp.log2(l)
                q = qe_s[i, head_rows(h), head_lanes(h)].astype(F32)
                augs.append(jnp.where((r32 == 24) | (r32 == 25), split_rows(-lse, r32), q))
            ot = jnp.concatenate(outs, axis=0)
            ot_ref[:, frame_lanes(i)] = ot.astype(BF16)
            qa_ref[:, frame_lanes(i)] = jnp.concatenate(augs, axis=0).astype(BF16)
            o_ref[frame_rows(i), :] = ot.T[:FROWS, :].astype(BF16)

        def attend_pairs(pairs, first):
            ss = [scores(i, j) for i, j in pairs]
            if exact:
                old = [None if first else [m_s[i, h] for h in HEADS] for i, _ in pairs]
                for n, (i, j) in enumerate(pairs):
                    if not first:
                        old[n] = [m_s[i, h] for h in HEADS]
                    top = [jnp.max(ss[n][h], axis=0, keepdims=True) for h in HEADS]
                    if not first:
                        top = [jnp.maximum(old[n][h], top[h]) for h in HEADS]
                    pv = gathered(j, [jnp.exp2(ss[n][h] - top[h]).astype(BF16) for h in HEADS])
                    for h in HEADS:
                        acc_s[i, h] = pv[h] if first else acc_s[i, h] * jnp.exp2(old[n][h] - top[h]) + pv[h]
                        m_s[i, h] = top[h]
                return
            ps = [[jnp.exp2(s[h]).astype(BF16) for h in HEADS] for s in ss]
            pvs = [gathered(j, p) for (_, j), p in zip(pairs, ps)]
            for (i, _), pv in zip(pairs, pvs):
                for h in HEADS:
                    acc_s[i, h] = pv[h] if first else acc_s[i, h] + pv[h]

        bad_s[...] = jnp.zeros(bad_s.shape, F32)
        for k in range(TOGETHER):
            prepare(k)

        def diagonal(n, _):
            attend_pairs([(n * TOGETHER + k,) * 2 for k in range(TOGETHER)], True)
            for k in range(TOGETHER):
                prepare(jnp.minimum((n + 1) * TOGETHER, FRAMES - TOGETHER) + k)
            return 0
        lax.fori_loop(0, FRAMES // TOGETHER, diagonal, 0)
        each_pair(pairs_s, count, lambda pairs: attend_pairs(pairs, False))

        def close(n, _):
            for k in range(TOGETHER):
                finalize(n * TOGETHER + k)
            for k in range(TOGETHER):
                keep(n * TOGETHER + k)
            return 0
        lax.fori_loop(0, FRAMES // TOGETHER, close, 0)
        for src, dst, n in by_rows + by_lanes:
            pltpu.make_async_copy(src, dst, out_sem.at[n]).wait()

    attend(False)

    @pl.when(jnp.max(bad_s[...]) > 0.0)
    def _():
        attend(True)
    for copy in saved:
        copy.wait()


SMEM = pl.BlockSpec(memory_space=pltpu.SMEM)
HBM = pl.BlockSpec(memory_space=pltpu.HBM)


def in_hbm(value):
    return pltpu.with_memory_space_constraint(value, pltpu.HBM)
VM = pl.BlockSpec(memory_space=pltpu.VMEM)


def attn_fwd(seg, pad, pat, qt, ka, va, kt, vt):
    V = pltpu.VMEM
    rows, lanes = (FRAMES * FROWS, WIDE), (WIDE, FRAMES * FLANES)
    return pl.pallas_call(
        fwd_kernel,
        out_shape=tuple(pltpu.HBM(shape, BF16) for shape in (rows, lanes, lanes, rows, rows, lanes))
        + (jax.ShapeDtypeStruct((LISTED,), jnp.int32),),
        in_specs=[SMEM] * 3 + [VM] * 5,
        out_specs=(HBM,) * 6 + (SMEM,),
        scratch_shapes=[V(rows, BF16), V(lanes, BF16), V(lanes, BF16), V((FRAMES, WIDE, HEADS_LOCAL * FLANES), BF16),
                        V((FRAMES + 1, HEADS_LOCAL, 1, FLANES), F32), V((FRAMES + 1, HEADS_LOCAL, HW, FLANES), F32),
                        V((1, FLANES), F32), pltpu.SemaphoreType.DMA((6,))],
        compiler_params=pltpu.CompilerParams(vmem_limit_bytes=26 << 20),
        cost_estimate=pl.CostEstimate(flops=int(2.5e10), bytes_accessed=8 << 20, transcendentals=0),
        name="attend_forward",
    )(seg, pad, pat, qt, ka, va, kt, vt)


def bwd_kernel(pairs_s, qa_ref, ka_ref, va_ref, kt_ref, ot_ref, do_ref, h_ref, w_ref, res_ref,
               dh_ref, early_ref, res_hbm, qe_s, oe_s, dq_s, dk_s, dv_s, dw_s, turn_s, blk_s, res_sem):
    carried = pltpu.make_async_copy(res_ref, res_hbm, res_sem.at[0])
    carried.start()
    scale = HEAD_DIM ** -0.5
    for s in (qe_s, oe_s):
        s[...] = jnp.zeros(s.shape, BF16)
    count = pairs_s[LISTED - 1]
    dw_s[...] = jnp.zeros(dw_s.shape, F32)
    real = lax.broadcasted_iota(jnp.int32, (WIDE, FROWS), 0) % HW < HEAD_DIM
    r32 = lax.broadcasted_iota(jnp.int32, (HW, FLANES), 0)
    zpad = jnp.zeros((WIDE, FLANES - FROWS), F32)

    def prepare(i):
        t = i
        qt = qa_ref[:, frame_lanes(i)]
        dot_ = jnp.concatenate([do_ref[frame_rows(i), :].astype(F32).T, zpad], axis=1)
        prod = dot_ * ot_ref[:, frame_lanes(i)].astype(F32)
        for h in HEADS:
            d = -jnp.sum(prod[head_rows(h)], axis=0, keepdims=True)
            qe_s[t, head_rows(h), head_lanes(h)] = qt[head_rows(h)]
            oe_s[t, head_rows(h), head_lanes(h)] = (dot_[head_rows(h)] + split_rows(d, r32)).astype(BF16)

    def scores(i, j):
        t, u = inside(i), inside(j)
        s, dp = dot(ka_ref[frame_rows(u), :], qe_s[t]), dot(va_ref[frame_rows(u), :], oe_s[t])
        ps = [jnp.exp2(s[:, head_lanes(h)]) for h in HEADS]
        return [p.astype(BF16) for p in ps], [(ps[h] * dp[:, head_lanes(h)]).astype(BF16) for h in HEADS]

    def products(i, j, pb, ds):
        t, u = inside(i), inside(j)
        dq = [dot(kt_ref[head_rows(h), frame_lanes(u, FROWS)], ds[h]) for h in HEADS]
        dv = [dot_nt(oe_s[t, head_rows(h), head_lanes(h)], pb[h]) for h in HEADS]
        dk = [dot_nt(qe_s[t, head_rows(h), head_lanes(h)], ds[h]) for h in HEADS]
        return [jnp.concatenate(value, axis=0) for value in (dq, dk, dv)]

    def attend_pairs(pairs, first):
        made = [scores(i, j) for i, j in pairs]
        values = [products(i, j, pb, ds) for (i, j), (pb, ds) in zip(pairs, made)]
        for (i, j), value in zip(pairs, values):
            for ref, at, part in ((dq_s, frame_lanes(i), 0), (dk_s, frame_lanes(j, FROWS), 1), (dv_s, frame_lanes(j, FROWS), 2)):
                ref[:, at] = value[part] if first else ref[:, at] + value[part]

    def finish(f):
        parts = (dq_s[:, frame_lanes(f, FROWS)] * scale, dk_s[:, frame_lanes(f, FROWS)] * math.log(2.0), dv_s[:, frame_lanes(f, FROWS)])
        grads = jnp.concatenate([jnp.where(real, part, 0.0).astype(BF16) for part in parts], axis=0)
        dh_ref[frame_rows(f), :] = dot_tn(grads, w_ref[...]).astype(BF16)
        return dot(grads, h_ref[frame_rows(f), :])

    for k in range(TOGETHER):
        prepare(k)

    def diagonal(n, _):
        attend_pairs([(n * TOGETHER + k,) * 2 for k in range(TOGETHER)], True)
        for k in range(TOGETHER):
            prepare(jnp.minimum((n + 1) * TOGETHER, FRAMES - TOGETHER) + k)
        return 0
    lax.fori_loop(0, FRAMES // TOGETHER, diagonal, 0)
    each_pair(pairs_s, count, lambda pairs: attend_pairs(pairs, False))

    def close(n, _):
        dw = [finish(n * TOGETHER + k) for k in range(TOGETHER)]
        dw_s[...] += functools.reduce(jnp.add, dw)
        return 0
    lax.fori_loop(0, FRAMES // TOGETHER, close, 0)
    for b in range(3):
        turned = dw_s[b * WIDE:(b + 1) * WIDE, :].T
        turn_s[:, 0:96] = jnp.concatenate([turned[:, HW * h:HW * h + HEAD_DIM] for h in HEADS], axis=1)
        line = [turn_s[pl.ds(k, 96, stride=4), :][:, 0:96] for k in range(4)]
        blk_s[pl.ds(0, 96, stride=3), :] = jnp.concatenate([line[0], line[1][:, :32]], axis=1)
        blk_s[pl.ds(1, 96, stride=3), :] = jnp.concatenate([line[1][:, 32:], line[2][:, :64]], axis=1)
        blk_s[pl.ds(2, 96, stride=3), :] = jnp.concatenate([line[2][:, 64:], line[3]], axis=1)
        early_ref[288 * b:288 * (b + 1), :] = blk_s[...].astype(BF16)
    carried.wait()


def attn_bwd(pairs, qa, ka, va, kt, ot, do, h, w, result):
    sd = jax.ShapeDtypeStruct
    V = pltpu.VMEM
    return pl.pallas_call(
        bwd_kernel,
        out_shape=(sd((FRAMES * FROWS, D), BF16), sd((3 * 288, 128), BF16), pltpu.HBM(result.shape, BF16)),
        in_specs=[SMEM] + [VM] * 9,
        out_specs=(VM,) * 2 + (HBM,),
        scratch_shapes=[V((FRAMES, WIDE, HEADS_LOCAL * FLANES), BF16), V((FRAMES, WIDE, HEADS_LOCAL * FLANES), BF16)]
        + [V((WIDE, (FRAMES + 1) * FLANES), F32)] * 3
        + [V((3 * WIDE, D), F32), V((D, 128), F32), V((288, 128), F32),
           pltpu.SemaphoreType.DMA((1,))],
        compiler_params=pltpu.CompilerParams(vmem_limit_bytes=42 << 20),
        cost_estimate=pl.CostEstimate(flops=int(5e10), bytes_accessed=12 << 20, transcendentals=0),
        name="attend_backward",
    )(pairs, qa, ka, va, kt, ot, do, h, w, result)


MESH = pl.DeviceIdType.MESH
OWN_ROWS = 4 * FROWS


def place(d, m):
    return {"dp": d, "mp": m}


def remote(src, dst, send_sem, recv_sem, device):
    return pltpu.make_async_remote_copy(
        src_ref=src, dst_ref=dst, send_sem=send_sem, recv_sem=recv_sem, device_id=device, device_id_type=MESH
    )


def local(src, dst, sem):
    return pltpu.make_async_copy(src, dst, sem)


def greet(devices):
    barrier = pltpu.get_barrier_semaphore()
    for device in devices:
        pl.semaphore_signal(barrier, inc=1, device_id=device, device_id_type=MESH)
    return len(devices)


def met(count):
    pl.semaphore_wait(pltpu.get_barrier_semaphore(), count)


def group_peers():
    me = lax.axis_index("mp")
    return me, me ^ 1, me ^ 2, me ^ 3


def frame_part(device, c):
    return pl.ds(pl.multiple_of(device * OWN_ROWS + c * FROWS, 16), FROWS)


def normalised(v):
    centred = v - jnp.mean(v, axis=-1, keepdims=True)
    inv = lax.rsqrt(jnp.mean(centred * centred, axis=-1, keepdims=True) + NORM_EPS)
    return centred * inv, inv


def norm_pull(dy, hat, inv, gain):
    dg = dy * gain
    lead = jnp.mean(dg, axis=-1, keepdims=True)
    along = jnp.mean(dg * hat, axis=-1, keepdims=True)
    return inv * (dg - lead - hat * along)


def col_sum(v):
    return jnp.sum(v, axis=0, keepdims=True)


def load_frame(ref, c):
    base = c * PATCHES // 16 * 16
    rows = ref[base:base + FROWS, :].astype(F32)
    shift = c * PATCHES - base
    return pltpu.roll(rows, FROWS - shift, 0) if shift else rows


def live_rows():
    return lax.broadcasted_iota(jnp.int32, (FROWS, 1), 0) < PATCHES


def dp_peers(count):
    d = lax.axis_index("dp")
    side, line = d % 2, d // 2
    return side, line, {"dp": d ^ 1}, [lax.rem(line + n, count) for n in range(count)]


def start_kernel(count, x_hbm, np_hbm, w_hbm, m_hbm, v_hbm,
                 h_ref, qt_ref, ka_ref, va_ref, kt_ref, vt_ref, wa_ref, ws_ref, ma_ref, mb_ref,
                 x_ref, np_ref, w_ref, m_ref, v_ref, mo_s, w_s, load_x, load_w, keep_m,
                 send_x, recv_x, send_p, recv_p, send_f, recv_f, send_t, recv_t, send_l, recv_l):
    me, near, far, _ = group_peers()
    side, line, twin, around = dp_peers(count)
    frames = range(OWN_ROWS // FROWS)
    cuts = [0, 208, 400, 592, 784]
    loads = [local(x_hbm.at[a:b, :], x_ref.at[a:b, :], load_x.at[c]) for c, (a, b) in enumerate(zip(cuts, cuts[1:]))]
    others = [local(m_hbm, m_ref, load_w.at[0]), local(v_hbm, v_ref, load_w.at[1]), local(w_hbm, w_ref, load_w.at[2])]
    gains = local(np_hbm, np_ref, load_w.at[3])
    greeted = greet([{"mp": near}, {"mp": far}, twin] + [{"dp": q * 2 + side} for q in around[1:]])
    for copy in [gains] + loads + others:
        copy.start()
    live = live_rows()
    to_far, to_near, moments = [], [], []
    gains.wait()
    for c in frames:
        loads[c].wait()
        hat, _ = normalised(load_frame(x_ref, c))
        h_ref[frame_part(me, c), :] = jnp.where(live, hat * np_ref[0:1, :] + np_ref[1:2, :], 0.0).astype(BF16)
        rows = h_ref.at[frame_part(me, c), :]
        to_far.append(remote(rows, rows, send_x.at[c], recv_x.at[c], {"mp": far}))
        to_near.append(remote(rows, rows, send_p.at[c], recv_p.at[c], {"mp": near}))
        if c == 0:
            met(greeted)
        to_far[c].start()
        to_near[c].start()

    slots, rows = m_ref.shape[0], m_ref.shape[1]
    others[0].wait()
    others[1].wait()
    for r in range(2 * slots):
        mo_s[r // slots, pl.ds((r % slots) * rows, rows), :] = (v_ref if r % 2 else m_ref)[r // 2].astype(BF16)
    first, second = ma_ref.at[side, line], mb_ref.at[side]
    kept = [local(mo_s.at[0], first, keep_m.at[0]), local(mo_s.at[1], second, keep_m.at[1])]
    for n, q in enumerate(around[1:]):
        moments.append(remote(mo_s.at[0], first, send_l.at[n], recv_l.at[n], {"dp": q * 2 + side}))
    moments.append(remote(mo_s.at[0], first, send_t.at[0], recv_t.at[0], twin))
    moments.append(remote(mo_s.at[1], second, send_t.at[1], recv_t.at[1], twin))
    for copy in moments + kept:
        copy.start()

    def incoming(device, sends, recvs, c):
        rows = h_ref.at[frame_part(device, c), :]
        return remote(rows, rows, sends.at[c], recvs.at[c], {"mp": near})

    def forward(c):
        incoming(far, send_x, recv_x, c).wait_recv()
        copy = incoming(far, send_f, recv_f, c)
        copy.start()
        return copy

    others[2].wait()
    for b in range(3):
        a = [w_ref[b, pl.ds(k, 96, stride=3), :] for k in range(3)]
        lines = [a[0][:, :96], jnp.concatenate([a[0][:, 96:], a[1][:, :64]], axis=1),
                 jnp.concatenate([a[1][:, 64:], a[2][:, :32]], axis=1), a[2][:, 32:]]
        gap = jnp.zeros((96, HW - HEAD_DIM), F32)
        for k in range(4):
            parts = []
            for h in HEADS:
                parts += [lines[k][:, HEAD_DIM * h:HEAD_DIM * (h + 1)], gap]
            w_s[pl.ds(k, 96, stride=4), :] = jnp.concatenate(parts, axis=1)
        wa_ref[b * WIDE:(b + 1) * WIDE, :] = w_s[...].T.astype(BF16)

    col = lax.broadcasted_iota(jnp.int32, (FROWS, WIDE), 1) % HW
    ones = jnp.where((col == 24) | (col == 25), 1.0, 0.0)
    kadd = ones + jnp.where((col == 26) & jnp.logical_not(live), MASKED, 0.0)
    vtadd = jnp.where(lax.broadcasted_iota(jnp.int32, (WIDE, FROWS), 0) % HW == 24, 1.0, 0.0)
    zpad = jnp.zeros((WIDE, FLANES - FROWS), BF16)

    def project(devices, c):
        made = []
        for device in devices:
            hf = h_ref[frame_part(device, c), :]
            made.append((dot_nt(wa_ref[...], hf), dot_nt(hf, wa_ref[WIDE:3 * WIDE, :])))
        for device, (turned, lined) in zip(devices, made):
            f = device * (OWN_ROWS // FROWS) + c
            qt_ref[:, frame_lanes(f)] = jnp.concatenate([(turned[0:WIDE] * QSCALE).astype(BF16), zpad], axis=1)
            kt_ref[:, frame_lanes(f, FROWS)] = turned[WIDE:2 * WIDE].astype(BF16)
            vt_ref[:, frame_lanes(f, FROWS)] = (turned[2 * WIDE:3 * WIDE] + vtadd).astype(BF16)
            ka_ref[frame_rows(f), :] = (lined[:, 0:WIDE] + kadd).astype(BF16)
            va_ref[frame_rows(f), :] = (lined[:, WIDE:2 * WIDE] + ones).astype(BF16)

    copies = [forward(0)]
    for c in frames:
        incoming(near, send_p, recv_p, c).wait_recv()
        project((me, near), c)
    copies.append(forward(1))
    for b in range(3, w_ref.shape[0]):
        for k in range(3):
            lanes = slice(128 * k, 128 * (k + 1))
            part = w_ref[b, pl.ds(k, 96, stride=3), :]
            if b == 3:
                gap = jnp.zeros((HW - HEAD_DIM, 128), F32)
                parts = []
                for h in HEADS:
                    parts += [part[HEAD_DIM * h:HEAD_DIM * (h + 1)], gap]
                ws_ref[2 * D:2 * D + WIDE, lanes] = jnp.concatenate(parts, axis=0).astype(BF16)
            else:
                ws_ref[96 * (b - 4):96 * (b - 3), lanes] = part.astype(BF16)
    for c in frames:
        incoming(near ^ 2, send_f, recv_f, c).wait_recv()
        project((far, near ^ 2), c)
        if c + 2 < len(frames):
            copies.append(forward(c + 2))
    for n in range(1, count):
        part = ma_ref.at[side, around[count - n]]
        remote(part, part, send_l.at[n - 1], recv_l.at[n - 1], twin).wait_recv()
    part = ma_ref.at[1 - side, line]
    remote(part, part, send_t.at[0], recv_t.at[0], twin).wait_recv()
    part = mb_ref.at[1 - side]
    remote(part, part, send_t.at[1], recv_t.at[1], twin).wait_recv()
    for copy in kept:
        copy.wait()
    for copy in to_far + to_near + copies + moments:
        copy.wait_send()


def start_call(dp, x, norm_params, weights, first_moments, second_moments):
    sd, V, S = jax.ShapeDtypeStruct, pltpu.VMEM, pltpu.SemaphoreType.DMA
    blocks, count = weights.shape[0], dp // 2
    half = first_moments.shape[0] * first_moments.shape[1]
    rows, lanes = sd((FRAMES * FROWS, WIDE), BF16), sd((WIDE, FRAMES * FLANES), BF16)
    return pl.pallas_call(
        functools.partial(start_kernel, count),
        out_shape=(sd((FRAMES * FROWS, D), BF16), lanes, rows, rows, lanes, lanes, sd((3 * WIDE, D), BF16),
                   sd((WIDE + 96 * (blocks - 4), D), BF16),
                   pltpu.HBM((2, count, half, 128), BF16), pltpu.HBM((2, half, 128), BF16)),
        in_specs=[HBM] * 5,
        out_specs=(VM,) * 8 + (HBM,) * 2,
        scratch_shapes=[V(x.shape, BF16), V(norm_params.shape, F32), V(weights.shape, F32), V(first_moments.shape, F32),
                        V(first_moments.shape, F32), V((2, half, 128), BF16), V((D, WIDE), F32),
                        S((4,)), S((4,)), S((2,))] + [S((4,))] * 6 + [S((2,))] * 2 + [S((count,))] * 2,
        compiler_params=pltpu.CompilerParams(vmem_limit_bytes=24 << 20, collective_id=1, has_side_effects=True),
        name="norm_and_gather",
    )(*[in_hbm(value) for value in (x, norm_params, weights, first_moments, second_moments)])


def gelu_parts(u):
    lead = math.sqrt(2.0 / math.pi)
    bend = lead * 0.044715
    square = u * u
    half = 0.5 + 0.5 * jnp.tanh(u * (lead + bend * square))
    slope = half + 2.0 * u * (half - half * half) * (lead + 3.0 * bend * square)
    return u * half, slope


def middle_kernel(count, o_ref, x_hbm, ct_hbm, pad_ref, w0_ref, w1_ref, np_hbm, ma_ref, mb_ref,
                  out_ref, dx2_ref, do_ref, l0_ref, l1_ref, l2_ref, l3_ref, nb_ref, mom_ref,
                  ob_s, dob_s, g_s, a_s, du_s, da_s, h2_s, dxa_s, blk_s, res_s, ut_s, wot_s,
                  x_ref, ct_ref, o_s, w2_ref, w3_ref, np_ref, load_s, send_w, recv_w,
                  send_o, recv_o, send_d, recv_d, send_t, recv_t, send_l, recv_l, send_f, recv_f):
    me, near, far, across = group_peers()
    side, line, twin, around = dp_peers(count)
    peers = (far, across, near)
    mine = pl.ds(pl.multiple_of(me * OWN_ROWS, 16), OWN_ROWS)
    loads = [local(ct_hbm, ct_ref, load_s.at[0]), local(x_hbm, x_ref, load_s.at[1]), local(o_ref.at[mine, :], o_s, load_s.at[2]), local(np_hbm, np_ref, load_s.at[3])]
    greeted = greet([{"mp": p} for p in peers] + [twin] + [{"dp": q * 2 + side} for q in around[1:]])
    for copy in loads:
        copy.start()
    frames = range(OWN_ROWS // FROWS)
    live = live_rows()
    shards_w = (w0_ref, w1_ref, w2_ref, w3_ref)
    late = (l0_ref, l1_ref, l2_ref, l3_ref)
    places = range(len(shards_w))
    loads[0].wait()
    for c in frames:
        rows = slice(c * FROWS, (c + 1) * FROWS)
        g_s[rows, :] = jnp.where(live, load_frame(ct_ref, c) * (1 - pad_ref[0, me * len(frames) + c]).astype(F32), 0.0).astype(BF16)
    met(greeted)
    outgoing = []
    for c in frames:
        for n, p in enumerate(peers):
            outgoing.append(remote(o_ref.at[frame_part(p, c), :], ob_s.at[n, pl.ds(c * FROWS, FROWS), :],
                                   send_o.at[n, c], recv_o.at[n, c], {"mp": p}))
            outgoing[-1].start()
    weights = [remote(w0_ref, w3_ref, send_w.at[0], recv_w.at[0], {"mp": near}),
               remote(w1_ref, w2_ref, send_w.at[1], recv_w.at[1], {"mp": near})]
    for copy in weights:
        copy.start()
    moments = []
    for n, q in enumerate(around[1:]):
        own_half = mb_ref.at[side]
        moments.append(remote(own_half, mom_ref.at[1, side, line], send_l.at[n], recv_l.at[n], {"dp": q * 2 + side}))
        moments.append(remote(ma_ref.at[side, q], mom_ref.at[0, side, q], send_t.at[q], recv_t.at[q], twin))
    for copy in moments:
        copy.start()

    def pass_moments(n):
        q = around[count - n]
        part = mom_ref.at[1, side, q]
        remote(part, part, send_l.at[n - 1], recv_l.at[n - 1], twin).wait_recv()
        moments.append(remote(part, part, send_f.at[q], recv_f.at[q], twin))
        moments[-1].start()

    def w_up(m):
        return shards_w[m][0:D, :]

    def w_down(m):
        return shards_w[m][D:2 * D, :]

    def w_o(m):
        return shards_w[m][2 * D:2 * D + WIDE, :]

    def cols(m):
        return slice(m * D, (m + 1) * D)

    for m in (0, 1, 3, 2):
        if m > 1:
            weights[3 - m].wait_recv()
        da_s[:, cols(m)] = dot_nt(g_s[...], w_down(m))
        ut_s[cols(m), :] = w_up(m).astype(F32).T.astype(BF16)
        wot_s[:, m * WIDE:(m + 1) * WIDE] = w_o(m).astype(F32).T.astype(BF16)
    for copy in loads[1:]:
        copy.wait()
    nb_ref[...] = jnp.zeros(nb_ref.shape, F32)
    down = jnp.concatenate([w_down(m) for m in places], axis=0)
    out_w = jnp.concatenate([w_o(m) for m in places], axis=0)
    sent, left = [], list(range(1, count))
    for both in ((0,), (1, 2), (3,)):
        rows = slice(both[0] * FROWS, (both[-1] + 1) * FROWS)
        for c in both:
            for n, p in enumerate(peers):
                part = ob_s.at[n, pl.ds(c * FROWS, FROWS), :]
                remote(part, part, send_o.at[n, c], recv_o.at[n, c], {"mp": p}).wait_recv()
        own_rows = pl.ds(pl.multiple_of(me * OWN_ROWS + both[0] * FROWS, 16), len(both) * FROWS)
        heads = jnp.concatenate([o_s[rows, :]] + [ob_s[n, rows, :] for n in range(len(peers))], axis=1)
        x2 = jnp.concatenate([load_frame(x_ref, c) for c in both], axis=0) + dot(heads, out_w)
        x2 = jnp.where(jnp.concatenate([live] * len(both), axis=0), x2, 0.0)
        hat, inv = normalised(x2)
        h2 = (hat * np_ref[2:3, :] + np_ref[3:4, :]).astype(BF16)
        h2_s[rows, :] = h2
        for m in places:
            value, slope = gelu_parts(dot(h2, w_up(m)))
            a_s[rows, cols(m)] = value.astype(BF16)
            du_s[rows, cols(m)] = (da_s[rows, cols(m)] * slope).astype(BF16)
        if left and len(both) > 1:
            pass_moments(left.pop(0))
        result = x2 + dot(a_s[rows, :], down)
        for k, c in enumerate(both):
            res_s[pl.ds(c * PATCHES, FROWS), :] = result[k * FROWS:(k + 1) * FROWS]
        dh2 = dot(du_s[rows, :], ut_s[...])
        nb_ref[0:1, :] += col_sum(dh2 * hat)
        nb_ref[1:2, :] += col_sum(dh2)
        dx2 = g_s[rows, :].astype(F32) + norm_pull(dh2, hat, inv, np_ref[2:3, :])
        dx2_ref[rows, :] = dx2
        dxa = dx2.astype(BF16)
        dxa_s[rows, :] = dxa
        d_heads = dot(dxa, wot_s[...]).astype(BF16)
        for n in range(len(peers)):
            dob_s[n, rows, :] = d_heads[:, (n + 1) * WIDE:(n + 2) * WIDE]
        for c in both:
            for n, p in enumerate(peers):
                sent.append(remote(dob_s.at[n, pl.ds(c * FROWS, FROWS), :], do_ref.at[frame_part(me, c), :],
                                   send_d.at[n, c], recv_d.at[n, c], {"mp": p}))
                sent[-1].start()
        do_ref[own_rows, :] = d_heads[:, 0:WIDE]
        if left and both[-1] < 3:
            pass_moments(left.pop(0))
    while left:
        pass_moments(left.pop(0))
    out_ref[...] = res_s[0:out_ref.shape[0], :].astype(BF16)

    def as_block(shard, first, value):
        size = value.shape[0]
        for k in range(3):
            blk_s[pl.ds(k, size, stride=3), :] = value[:, 128 * k:128 * (k + 1)]
        late[shard][first * 288:first * 288 + 3 * size, :] = blk_s[0:3 * size, :].astype(BF16)

    def drop_gaps(value):
        return jnp.concatenate([value[HW * h:HW * h + HEAD_DIM] for h in HEADS], axis=0)

    dw1 = dot_tn(h2_s[...], du_s[...])
    dw2 = dot_tn(g_s[...], a_s[...])
    for m in places:
        as_block(m, 1, dw1[:, cols(m)])
        as_block(m, 5, dw2[:, cols(m)].T)
        o_m = o_s[...] if m == 0 else ob_s[m - 1]
        as_block(m, 0, drop_gaps(dot_tn(o_m, dxa_s[...])))
    for c in frames:
        for n, p in enumerate(peers):
            part = do_ref.at[frame_part(p, c), :]
            remote(part, part, send_d.at[n, c], recv_d.at[n, c], {"mp": p}).wait_recv()
    for q in around[1:]:
        for half, sends, recvs in ((0, send_t, recv_t), (1, send_f, recv_f)):
            part = mom_ref.at[half, 1 - side, q]
            remote(part, part, sends.at[q], recvs.at[q], twin).wait_recv()
    for copy in outgoing + sent + moments + weights:
        copy.wait_send()


def middle_call(dp, o, x, ct, padding, w, norm_params, ma, mb):
    sd = jax.ShapeDtypeStruct
    V, S = pltpu.VMEM, pltpu.SemaphoreType.DMA
    count = dp // 2
    late = sd((9 * 288, 128), BF16)
    return pl.pallas_call(
        functools.partial(middle_kernel, count),
        out_shape=(sd(x.shape, BF16), sd((OWN_ROWS, D), F32), sd((FRAMES * FROWS, WIDE), BF16),
                   late, late, late, late, sd((2, D), F32), pltpu.HBM((2,) + ma.shape, BF16)),
        in_specs=[HBM, HBM, HBM, SMEM] + [VM] * 2 + [HBM] * 3,
        out_specs=(VM,) * 8 + (HBM,),
        scratch_shapes=[V((3, OWN_ROWS, WIDE), BF16), V((3, OWN_ROWS, WIDE), BF16), V((OWN_ROWS, D), BF16),
                        V((OWN_ROWS, FF), BF16), V((OWN_ROWS, FF), BF16), V((OWN_ROWS, FF), F32),
                        V((OWN_ROWS, D), BF16), V((OWN_ROWS, D), BF16), V((1152, 128), F32), V((OWN_ROWS, D), F32),
                        V((FF, D), BF16), V((D, 4 * WIDE), BF16),
                        V(x.shape, BF16), V(x.shape, BF16), V((OWN_ROWS, WIDE), BF16), V(w[0].shape, BF16), V(w[0].shape, BF16), V(norm_params.shape, F32), S((4,)), S((2,)), S((2,)), S((3, 4)), S((3, 4)), S((3, 4)), S((3, 4))] + [S((count,))] * 6,
        compiler_params=pltpu.CompilerParams(vmem_limit_bytes=36 << 20, collective_id=2, has_side_effects=True),
        cost_estimate=pl.CostEstimate(flops=int(6e9), bytes_accessed=12 << 20, transcendentals=0),
        name="feed_forward",
    )(in_hbm(o), in_hbm(x), in_hbm(ct), padding, *w, in_hbm(norm_params), in_hbm(ma), in_hbm(mb))


def reduce_kernel(dp, piece, dh_ref, early_ref, l0_ref, l1_ref, l2_ref, l3_ref, x_ref, dx2_ref, np_ref, nb_ref,
                  gin_ref, gs_ref, tot_ref,
                  res_s, pb_s, xs_s, xb_s, g_s, yb_s, zs_s, zb_s, msg_s, mb_s, dm_s, db_s,
                  send_p, recv_p, send_x, recv_x, send_y, recv_y, send_z, recv_z,
                  send_a, recv_a, send_w, recv_w, send_m, recv_m, send_n, recv_n):
    me, near, far, across = group_peers()
    d = lax.axis_index("dp")
    count = dp // 2
    side, line = d % 2, d // 2
    twin = {"dp": d ^ 1}

    order, top = [], count
    while top > 1:
        top //= 2
        order += range(top, 2 * top)
    turns = [line ^ n for n in order]
    cut = -(-piece // 32) * 16
    halves = [(0, cut), (cut, piece - cut)]

    def line_device(q):
        return {"dp": q * 2 + side}

    frames = range(OWN_ROWS // FROWS)
    greeted = greet([{"mp": near}, {"mp": far}, {"mp": across}] + [{"dp": d ^ n} for n in range(1, dp)])
    total = early_ref.shape[0] + l0_ref.shape[0]
    g_s[0:early_ref.shape[0], :] = early_ref[...]
    g_s[early_ref.shape[0]:total, :] = (l0_ref[...].astype(F32) + l1_ref[...].astype(F32)
                                        + (l2_ref[...].astype(F32) + l3_ref[...].astype(F32))).astype(BF16)
    if g_s.shape[0] > total:
        g_s[total:, :] = jnp.zeros((g_s.shape[0] - total, 128), BF16)
    met(greeted)

    def own(c):
        return pl.ds(c * FROWS, FROWS)

    to_near = []
    for k, target in ((1, across), (0, near)):
        for c in frames:
            to_near.append(remote(dh_ref.at[frame_part(target, c), :], pb_s.at[k, own(c), :],
                                  send_p.at[k, c], recv_p.at[k, c], {"mp": near}))
            to_near[-1].start()

    def at(s, q, k):
        return pl.ds(pl.multiple_of((s * count + q) * piece + halves[k][0], 16), halves[k][1])

    def part(ref, q, k):
        return ref.at[q, pl.ds(*halves[k]), :]

    to_twin = []
    for q in turns + [line]:
        for k in range(2):
            to_twin.append(remote(g_s.at[at(1 - side, q, k), :], part(yb_s, q, k), send_y.at[q, k], recv_y.at[q, k], twin))
            to_twin[-1].start()

    to_far = []
    for c in frames:
        remote(pb_s.at[1, own(c), :], pb_s.at[1, own(c), :], send_p.at[1, c], recv_p.at[1, c], {"mp": near}).wait_recv()
        xs_s[own(c), :] = (dh_ref[frame_part(far, c), :].astype(F32) + pb_s[1, own(c), :].astype(F32)).astype(BF16)
        to_far.append(remote(xs_s.at[own(c), :], xb_s.at[own(c), :], send_x.at[c], recv_x.at[c], {"mp": far}))
        to_far[-1].start()

    to_line = []
    for q in turns + [line]:
        for k in range(2):
            got = part(yb_s, q, k)
            remote(got, got, send_y.at[q, k], recv_y.at[q, k], twin).wait_recv()
            rows = pl.ds(*halves[k])
            zs_s[q, rows, :] = (g_s[at(side, q, k), :].astype(F32) + yb_s[q, rows, :].astype(F32)).astype(BF16)
            if q is not line:
                to_line.append(remote(part(zs_s, q, k), part(zb_s, line, k), send_z.at[q, k], recv_z.at[line, k], line_device(q)))
                to_line[-1].start()
    live = live_rows()
    norm_sums = [jnp.zeros((1, D), F32), jnp.zeros((1, D), F32)]

    def norm_frame(c):
        remote(pb_s.at[0, own(c), :], pb_s.at[0, own(c), :], send_p.at[0, c], recv_p.at[0, c], {"mp": near}).wait_recv()
        remote(xb_s.at[own(c), :], xb_s.at[own(c), :], send_x.at[c], recv_x.at[c], {"mp": far}).wait_recv()
        dy = dh_ref[frame_part(me, c), :].astype(F32) + pb_s[0, own(c), :].astype(F32) + xb_s[own(c), :].astype(F32)
        dy = jnp.where(live, dy, 0.0)
        hat, inv = normalised(load_frame(x_ref, c))
        norm_sums[0] = norm_sums[0] + col_sum(dy * hat)
        norm_sums[1] = norm_sums[1] + col_sum(dy)
        res_s[pl.ds(c * PATCHES, FROWS), :] = dx2_ref[own(c), :] + norm_pull(dy, hat, inv, np_ref[0:1, :])

    norm_frame(0)
    norm_frame(1)
    spread, passed = [], []
    squares = jnp.zeros((1, 128), F32)
    for k in range(2):
        rows = pl.ds(*halves[k])
        mine = zs_s[line, rows, :].astype(F32)
        for q in turns:
            got = part(zb_s, q, k)
            remote(got, got, send_z.at[q, k], recv_z.at[q, k], line_device(q)).wait_recv()
            mine = mine + zb_s[q, rows, :].astype(F32)
        mine = mine.astype(BF16)
        gs_ref[at(side, line, k), :] = mine
        whole = gs_ref.at[at(side, line, k), :]
        for q in turns:
            spread.append(remote(whole, whole, send_a.at[q, k], recv_a.at[line, k], line_device(q)))
        passed.append(remote(whole, whole, send_w.at[line, k], recv_w.at[line, k], twin))
        for copy in spread[-len(turns):] + passed[-1:]:
            copy.start()
        mine = mine.astype(F32)
        squares = squares + col_sum(mine * mine)
        norm_frame(2 + k)

    msg_s[...] = jnp.zeros(msg_s.shape, F32)
    msg_s[0:1, :] = norm_sums[0]
    msg_s[1:2, :] = norm_sums[1]
    msg_s[2:4, :] = nb_ref[...]
    msg_s[4:5, 0:128] = squares
    small = []
    for n, p in enumerate((near, far, across)):
        small.append(remote(msg_s, mb_s.at[n], send_m.at[n], recv_m.at[n], {"mp": p}))
        small[-1].start()

    def pass_on(q, k):
        piece_at = gs_ref.at[at(side, q, k), :]
        remote(piece_at, piece_at, send_a.at[q, k], recv_a.at[q, k], line_device(q)).wait_recv()
        passed.append(remote(piece_at, piece_at, send_w.at[q, k], recv_w.at[q, k], twin))
        passed[-1].start()

    pass_on(turns[0], 0)
    add = msg_s[...]
    for n, p in enumerate((near, far, across)):
        remote(mb_s.at[n], mb_s.at[n], send_m.at[n], recv_m.at[n], {"mp": p}).wait_recv()
        add = add + mb_s[n]
    dm_s[...] = add
    for n in range(1, dp):
        small.append(remote(dm_s, db_s.at[n], send_n.at[n], recv_n.at[n], {"dp": d ^ n}))
        small[-1].start()
    for k in range(2):
        for q in turns[1 - k:]:
            pass_on(q, k)
    gin_ref[...] = res_s[0:gin_ref.shape[0], :].astype(BF16)
    for n in range(1, dp):
        remote(db_s.at[n], db_s.at[n], send_n.at[n], recv_n.at[n], {"dp": d ^ n}).wait_recv()
        add = add + db_s[n]
    tot_ref[...] = add
    for k in range(2):
        for q in turns + [line]:
            piece_at = gs_ref.at[at(1 - side, q, k), :]
            remote(piece_at, piece_at, send_w.at[q, k], recv_w.at[q, k], twin).wait_recv()
    for copy in to_near + to_twin + to_far + to_line + spread + passed + small:
        copy.wait_send()


def reduce_call(dp, dh, early, late, x, dx2, norm_params, nb):
    sd = jax.ShapeDtypeStruct
    V, S = pltpu.VMEM, pltpu.SemaphoreType.DMA
    rows = early.shape[0] + late[0].shape[0]
    count = dp // 2
    piece = -(-rows // (2 * count * 16)) * 16
    held = 2 * count * piece
    return pl.pallas_call(
        functools.partial(reduce_kernel, dp, piece),
        out_shape=(sd(x.shape, BF16), sd((held, 128), BF16), sd((8, D), F32)),
        in_specs=[VM] * 10,
        out_specs=(VM,) * 3,
        scratch_shapes=[V((OWN_ROWS, D), F32), V((2, OWN_ROWS, D), BF16), V((OWN_ROWS, D), BF16), V((OWN_ROWS, D), BF16), V((held, 128), BF16),
                        V((count, piece, 128), BF16), V((count, piece, 128), BF16), V((count, piece, 128), BF16),
                        V((8, D), F32), V((3, 8, D), F32), V((8, D), F32), V((dp, 8, D), F32),
                        S((2, 4)), S((2, 4)), S((4,)), S((4,))] + [S((count, 2))] * 8 + [S((3,)), S((3,)), S((dp,)), S((dp,))],
        compiler_params=pltpu.CompilerParams(vmem_limit_bytes=22 << 20, collective_id=3, has_side_effects=True),
        name="reduce_gradients",
    )(dh, early, *late, x, dx2, norm_params, nb)


def update_kernel(slot_ref, dev_ref, gin_ref, tot_ref, gs_ref, w_ref, m_ref, v_ref, ma_ref, mb_ref, mom_ref, np_ref, nm_ref, nv_ref,
                  gout_ref, norm_ref, nw_hbm, nf_hbm, ns_hbm, nn_ref, nnf_ref, nns_ref, nw_ref, nf_ref, ns_ref, sem_s):
    carried = [local(gin_ref, gout_ref, sem_s.at[0])]
    for copy in carried:
        copy.start()
    blocks, rows, _ = w_ref.shape
    slots = m_ref.shape[0]
    tot = tot_ref[...]
    grads = tot[0:4, :]
    norm = jnp.sqrt(jnp.sum(grads * grads, keepdims=True) + jnp.sum(tot[4:5, 0:128], keepdims=True))
    norm_ref[...] = norm
    clip_level = 0.5 * (4 * D * D + 2 * D * FF + 4 * D) ** 0.5
    factor = jnp.minimum(1.0, clip_level / norm)
    nn_ref[...], nnf_ref[...], nns_ref[...] = adam_update(
        np_ref[...], grads * factor, nm_ref[...], nv_ref[...], 0.0, NORM_RATE)

    def block(b):
        return gs_ref[pl.ds(pl.multiple_of(b * rows, 16), rows), :].astype(F32) * factor

    for s in range(slots):
        owned = jnp.int32(-1)
        for b in range(blocks):
            owned = jnp.where(slot_ref[b] == dev_ref[0] * slots + s, b, owned)
        _, first, second = adam_update(0.0, block(jnp.maximum(owned, 0)), m_ref[s], v_ref[s], 0.0, LEARN_RATE)
        nf_ref[s] = jnp.where(owned >= 0, first, m_ref[s])
        ns_ref[s] = jnp.where(owned >= 0, second, v_ref[s])
    leaving = [local(nf_ref, nf_hbm, sem_s.at[2]), local(ns_ref, ns_hbm, sem_s.at[3])]
    for copy in leaving:
        copy.start()

    def step(b, _):
        holder, first = slot_ref[b] // slots, slot_ref[b] % slots * 2
        side, line = holder % 2, holder // 2
        on_side, on_line = side == dev_ref[0] % 2, line == dev_ref[0] // 2

        def moment(r):
            at = pl.ds(pl.multiple_of(r % slots * rows, 16), rows)
            late = mom_ref[r // slots, side, line, at, :]
            lead = jnp.where(on_side | on_line, ma_ref[side, line, at, :], late)
            rest = jnp.where(on_line, mb_ref[side, at, :], late)
            return jnp.where(r < slots, lead, rest).astype(F32)

        old = [moment(first), moment(first + 1)]
        nw_ref[b], _, _ = adam_update(w_ref[b], block(b), old[0], old[1], WEIGHT_DECAY, LEARN_RATE)
        local(nw_ref.at[b], nw_hbm.at[b], sem_s.at[4]).start()
        return 0
    lax.fori_loop(0, blocks, step, 0)
    for copy in carried + leaving + [local(nw_ref, nw_hbm, sem_s.at[4])]:
        copy.wait()


def update_call(owner_slot, grad_in, tot, gs, weights, first, second, ma, mb, moments, norm_params, norm_first, norm_second):
    sd = jax.ShapeDtypeStruct
    small = sd((4, D), F32)
    device = lax.axis_index("dp").reshape(1)
    return pl.pallas_call(
        update_kernel,
        out_shape=(pltpu.HBM(grad_in.shape, BF16), sd((1, 1), F32), pltpu.HBM(weights.shape, F32),
                   pltpu.HBM(first.shape, F32), pltpu.HBM(first.shape, F32), small, small, small),
        in_specs=[SMEM] * 2 + [VM] * 12,
        out_specs=(HBM, VM) + (HBM,) * 3 + (VM,) * 3,
        scratch_shapes=[pltpu.VMEM(weights.shape, F32), pltpu.VMEM(first.shape, F32), pltpu.VMEM(first.shape, F32),
                        pltpu.SemaphoreType.DMA((5,))],
        compiler_params=pltpu.CompilerParams(vmem_limit_bytes=16 << 20),
        name="clipped_update",
    )(owner_slot, device, grad_in, tot, gs, weights, first, second, ma, mb, moments, norm_params, norm_first, norm_second)


def adam_update(current, gradient, first_moment, second_moment, decay_rate, step_rate):
    first_new = BETA_ONE * first_moment + (1.0 - BETA_ONE) * gradient
    second_new = BETA_TWO * second_moment + (1.0 - BETA_TWO) * gradient * gradient
    first_fix = 1.0 / (1.0 - BETA_ONE**STEP)
    second_fix = 1.0 / (1.0 - BETA_TWO**STEP)
    direction = first_new * (step_rate * first_fix) / (jnp.sqrt(second_new * second_fix) + ADAM_EPS)
    return (current * (1.0 - step_rate * decay_rate) - direction, first_new, second_new)


def from_peer(value, distance):
    return lax.ppermute(value, "mp", [(i, i ^ distance) for i in range(lax.axis_size("mp"))])


def shards(tokens, cotangent, segment_ids, padding, pattern, owner_slot, weights, first_moments, second_moments,
           norm_params, norm_first, norm_second):
    dp = lax.axis_size("dp")
    x, ct = tokens[0], cotangent[0]
    h1, qt, ka, va, kt, vt, wa, own_shared, ma, mb = start_call(dp, x, norm_params, weights, first_moments, second_moments)
    shared = [own_shared, from_peer(own_shared, 2)]
    o, ot, qa, ka, va, kt, pairs = attn_fwd(segment_ids, padding, pattern, qt, ka, va, kt, vt)
    result, dx2, do, *late, nb, moments = middle_call(dp, o, x, ct, padding, shared, norm_params, ma, mb)
    late = [late[0], from_peer(late[1], 2), from_peer(late[2], 3), from_peer(late[3], 1)]
    dh, early, result = attn_bwd(pairs, qa, ka, va, kt, ot, do, h1, wa, result)
    grad_in, gs, tot = reduce_call(dp, dh, early, late, x, dx2, norm_params, nb)
    grad_in, grad_norm, new_weights, new_first, new_second, new_norm, new_norm_first, new_norm_second = update_call(
        owner_slot, grad_in, tot, gs, weights, first_moments, second_moments, ma, mb, moments, norm_params, norm_first, norm_second)
    return (result[None], grad_in[None], grad_norm[0, 0], new_weights, new_first, new_second,
            new_norm, new_norm_first, new_norm_second)


def solution(mesh):
    rows, blocks, slots = P("dp", "mp", None), P(None, "mp", None), P("dp", "mp", None)
    return jax.shard_map(
        shards,
        mesh=mesh,
        in_specs=(rows, rows, P("dp", None), P("dp", None), P(), P(), blocks, slots, slots, P(), P(), P()),
        out_specs=(rows, rows, P(), blocks, slots, slots, P(), P(), P()),
        check_vma=False,
    )
```

```python
import functools
import math

import jax
import jax.numpy as jnp
from jax import lax
from jax.experimental import pallas as pl
from jax.experimental.pallas import tpu as pltpu
from jax.sharding import PartitionSpec as P

FF = 1536
STEP = 10
NORM_EPS = 1e-05
BETA_ONE = 0.9
BETA_TWO = 0.95
ADAM_EPS = 1e-08
LEARN_RATE = 0.15
NORM_RATE = 0.6
WEIGHT_DECAY = 0.05

D = 384
HEAD_DIM = 24
FRAMES = 16
PATCHES = 196
FROWS = 208
FLANES = 256
HW = 32
HEADS_LOCAL = 4
WIDE = HEADS_LOCAL * HW
MASKED = -1e30
QSCALE = math.log2(math.e) / math.sqrt(HEAD_DIM)
F32 = jnp.float32
BF16 = jnp.bfloat16
NT = (((1,), (1,)), ((), ()))
TN = (((0,), (0,)), ((), ()))
HEADS = range(HEADS_LOCAL)
UNROLL = 6
LISTED = 136
TOGETHER = 4


def dot(a, b):
    return jnp.dot(a, b, preferred_element_type=F32)


def dot_nt(a, b):
    return lax.dot_general(a, b, NT, preferred_element_type=F32)


def dot_tn(a, b):
    return lax.dot_general(a, b, TN, preferred_element_type=F32)


def frame_rows(f):
    return pl.ds(pl.multiple_of(f * FROWS, 16), FROWS)


def frame_lanes(f, size=FLANES):
    return pl.ds(pl.multiple_of(f * FLANES, 128), size)


def head_rows(h):
    return slice(HW * h, HW * (h + 1))


def head_lanes(h):
    return slice(FLANES * h, FLANES * (h + 1))


def list_pairs(seg_ref, pad_ref, pat_ref, pairs_s):
    def rows(i, carry):
        start, count = carry
        start = jnp.where(seg_ref[0, i] == seg_ref[0, jnp.maximum(i - 1, 0)], start, i)

        def cols(j, count):
            pairs_s[count] = i * 32 + j
            return count + jnp.where((pat_ref[i, j] == 1) & (pad_ref[0, j] == 0), 1, 0)
        return start, lax.fori_loop(start, i, cols, count)
    _, count = lax.fori_loop(0, FRAMES, rows, (jnp.int32(0), jnp.int32(0)))
    for n in range(UNROLL):
        pairs_s[count + n] = FRAMES * 33
    pairs_s[LISTED - 1] = count
    return count


def each_pair(pairs_s, count, work):
    def step(first, size):
        def body(n, _):
            codes = [pairs_s[first + n * size + u] for u in range(size)]
            work([(code // 32, code % 32) for code in codes])
            return 0
        return body
    whole = count // UNROLL
    lax.fori_loop(0, whole, step(0, UNROLL), 0)
    lax.fori_loop(0, (count - whole * UNROLL + 1) // 2, step(whole * UNROLL, 2), 0)


def inside(f):
    return jnp.minimum(f, FRAMES - 1)


def split_rows(value, r32):
    high = value.astype(BF16).astype(F32)
    return jnp.where(r32 == 24, high, jnp.where(r32 == 25, value - high, 0.0))


def fwd_kernel(seg_ref, pad_ref, pat_ref, qt_ref, ka_ref, va_ref, kt_ref, vt_ref,
               o_hbm, ot_hbm, qa_hbm, ka_hbm, va_hbm, kt_hbm, pairs_s,
               o_ref, ot_ref, qa_ref, qe_s, m_s, acc_s, bad_s, out_sem):
    zpad = jnp.zeros((WIDE, FLANES - FROWS), F32)
    r32 = lax.broadcasted_iota(jnp.int32, (HW, FLANES), 0)
    by_rows = [(o_ref, o_hbm, 0)]
    by_lanes = [(ot_ref, ot_hbm, 1), (qa_ref, qa_hbm, 2)]
    saved = [pltpu.make_async_copy(src, dst, out_sem.at[n])
             for n, (src, dst) in enumerate(((ka_ref, ka_hbm), (va_ref, va_hbm), (kt_ref, kt_hbm)), 3)]
    for copy in saved:
        copy.start()
    qe_s[...] = jnp.zeros(qe_s.shape, BF16)
    count = list_pairs(seg_ref, pad_ref, pat_ref, pairs_s)

    def keep(f):
        for src, dst, n in by_rows:
            pltpu.make_async_copy(src.at[frame_rows(f), :], dst.at[frame_rows(f), :], out_sem.at[n]).start()
        for src, dst, n in by_lanes:
            pltpu.make_async_copy(src.at[:, frame_lanes(f)], dst.at[:, frame_lanes(f)], out_sem.at[n]).start()

    def scores(i, j):
        s = dot(ka_ref[frame_rows(inside(j)), :], qe_s[inside(i)])
        return [s[:, head_lanes(h)] for h in HEADS]

    def gathered(j, ps):
        return [dot(vt_ref[head_rows(h), frame_lanes(inside(j), FROWS)], ps[h]) for h in HEADS]

    def attend(exact):
        def prepare(f):
            qt = qt_ref[:, frame_lanes(f)].astype(F32)
            own = qt * jnp.concatenate([kt_ref[:, frame_lanes(f, FROWS)].astype(F32), zpad], axis=1)
            for h in HEADS:
                if exact:
                    start = jnp.zeros((1, FLANES), F32)
                else:
                    start = jnp.sum(own[head_rows(h)], axis=0, keepdims=True)
                    m_s[f, h] = start
                aug = jnp.where(r32 == 26, 1.0, split_rows(-start, r32))
                qe_s[f, head_rows(h), head_lanes(h)] = (qt[head_rows(h)] + aug).astype(BF16)

        def finalize(i):
            outs, augs = [], []
            for h in HEADS:
                a = acc_s[i, h]
                l = a[24:25, :]
                bad_s[...] = jnp.maximum(bad_s[...], jnp.where(l < 1e30, 0.0, 1.0))
                outs.append(jnp.where(r32 < HEAD_DIM, a * (1.0 / l), 0.0))
                lse = m_s[i, h] + jnp.log2(l)
                q = qe_s[i, head_rows(h), head_lanes(h)].astype(F32)
                augs.append(jnp.where((r32 == 24) | (r32 == 25), split_rows(-lse, r32), q))
            ot = jnp.concatenate(outs, axis=0)
            ot_ref[:, frame_lanes(i)] = ot.astype(BF16)
            qa_ref[:, frame_lanes(i)] = jnp.concatenate(augs, axis=0).astype(BF16)
            o_ref[frame_rows(i), :] = ot.T[:FROWS, :].astype(BF16)

        def attend_pairs(pairs, first):
            ss = [scores(i, j) for i, j in pairs]
            if exact:
                old = [None if first else [m_s[i, h] for h in HEADS] for i, _ in pairs]
                for n, (i, j) in enumerate(pairs):
                    if not first:
                        old[n] = [m_s[i, h] for h in HEADS]
                    top = [jnp.max(ss[n][h], axis=0, keepdims=True) for h in HEADS]
                    if not first:
                        top = [jnp.maximum(old[n][h], top[h]) for h in HEADS]
                    pv = gathered(j, [jnp.exp2(ss[n][h] - top[h]).astype(BF16) for h in HEADS])
                    for h in HEADS:
                        acc_s[i, h] = pv[h] if first else acc_s[i, h] * jnp.exp2(old[n][h] - top[h]) + pv[h]
                        m_s[i, h] = top[h]
                return
            ps = [[jnp.exp2(s[h]).astype(BF16) for h in HEADS] for s in ss]
            pvs = [gathered(j, p) for (_, j), p in zip(pairs, ps)]
            for (i, _), pv in zip(pairs, pvs):
                for h in HEADS:
                    acc_s[i, h] = pv[h] if first else acc_s[i, h] + pv[h]

        bad_s[...] = jnp.zeros(bad_s.shape, F32)
        for k in range(TOGETHER):
            prepare(k)

        def diagonal(n, _):
            attend_pairs([(n * TOGETHER + k,) * 2 for k in range(TOGETHER)], True)
            for k in range(TOGETHER):
                prepare(jnp.minimum((n + 1) * TOGETHER, FRAMES - TOGETHER) + k)
            return 0
        lax.fori_loop(0, FRAMES // TOGETHER, diagonal, 0)
        each_pair(pairs_s, count, lambda pairs: attend_pairs(pairs, False))

        def close(n, _):
            for k in range(TOGETHER):
                finalize(n * TOGETHER + k)
            for k in range(TOGETHER):
                keep(n * TOGETHER + k)
            return 0
        lax.fori_loop(0, FRAMES // TOGETHER, close, 0)
        for src, dst, n in by_rows + by_lanes:
            pltpu.make_async_copy(src, dst, out_sem.at[n]).wait()

    attend(False)

    @pl.when(jnp.max(bad_s[...]) > 0.0)
    def _():
        attend(True)
    for copy in saved:
        copy.wait()


SMEM = pl.BlockSpec(memory_space=pltpu.SMEM)
HBM = pl.BlockSpec(memory_space=pltpu.HBM)


def in_hbm(value):
    return pltpu.with_memory_space_constraint(value, pltpu.HBM)
VM = pl.BlockSpec(memory_space=pltpu.VMEM)


def attn_fwd(seg, pad, pat, qt, ka, va, kt, vt):
    V = pltpu.VMEM
    rows, lanes = (FRAMES * FROWS, WIDE), (WIDE, FRAMES * FLANES)
    return pl.pallas_call(
        fwd_kernel,
        out_shape=tuple(pltpu.HBM(shape, BF16) for shape in (rows, lanes, lanes, rows, rows, lanes))
        + (jax.ShapeDtypeStruct((LISTED,), jnp.int32),),
        in_specs=[SMEM] * 3 + [VM] * 5,
        out_specs=(HBM,) * 6 + (SMEM,),
        scratch_shapes=[V(rows, BF16), V(lanes, BF16), V(lanes, BF16), V((FRAMES, WIDE, HEADS_LOCAL * FLANES), BF16),
                        V((FRAMES + 1, HEADS_LOCAL, 1, FLANES), F32), V((FRAMES + 1, HEADS_LOCAL, HW, FLANES), F32),
                        V((1, FLANES), F32), pltpu.SemaphoreType.DMA((6,))],
        compiler_params=pltpu.CompilerParams(vmem_limit_bytes=26 << 20),
        cost_estimate=pl.CostEstimate(flops=int(2.5e10), bytes_accessed=8 << 20, transcendentals=0),
        name="attend_forward",
    )(seg, pad, pat, qt, ka, va, kt, vt)


def bwd_kernel(pairs_s, qa_ref, ka_ref, va_ref, kt_ref, ot_ref, do_ref, h_ref, w_ref, res_ref,
               dh_ref, early_ref, res_hbm, qe_s, oe_s, dq_s, dk_s, dv_s, dw_s, turn_s, blk_s, res_sem):
    carried = pltpu.make_async_copy(res_ref, res_hbm, res_sem.at[0])
    carried.start()
    scale = HEAD_DIM ** -0.5
    for s in (qe_s, oe_s):
        s[...] = jnp.zeros(s.shape, BF16)
    count = pairs_s[LISTED - 1]
    dw_s[...] = jnp.zeros(dw_s.shape, F32)
    real = lax.broadcasted_iota(jnp.int32, (WIDE, FROWS), 0) % HW < HEAD_DIM
    r32 = lax.broadcasted_iota(jnp.int32, (HW, FLANES), 0)
    zpad = jnp.zeros((WIDE, FLANES - FROWS), F32)

    def prepare(i):
        t = i
        qt = qa_ref[:, frame_lanes(i)]
        dot_ = jnp.concatenate([do_ref[frame_rows(i), :].astype(F32).T, zpad], axis=1)
        prod = dot_ * ot_ref[:, frame_lanes(i)].astype(F32)
        for h in HEADS:
            d = -jnp.sum(prod[head_rows(h)], axis=0, keepdims=True)
            qe_s[t, head_rows(h), head_lanes(h)] = qt[head_rows(h)]
            oe_s[t, head_rows(h), head_lanes(h)] = (dot_[head_rows(h)] + split_rows(d, r32)).astype(BF16)

    def scores(i, j):
        t, u = inside(i), inside(j)
        s, dp = dot(ka_ref[frame_rows(u), :], qe_s[t]), dot(va_ref[frame_rows(u), :], oe_s[t])
        ps = [jnp.exp2(s[:, head_lanes(h)]) for h in HEADS]
        return [p.astype(BF16) for p in ps], [(ps[h] * dp[:, head_lanes(h)]).astype(BF16) for h in HEADS]

    def products(i, j, pb, ds):
        t, u = inside(i), inside(j)
        dq = [dot(kt_ref[head_rows(h), frame_lanes(u, FROWS)], ds[h]) for h in HEADS]
        dv = [dot_nt(oe_s[t, head_rows(h), head_lanes(h)], pb[h]) for h in HEADS]
        dk = [dot_nt(qe_s[t, head_rows(h), head_lanes(h)], ds[h]) for h in HEADS]
        return [jnp.concatenate(value, axis=0) for value in (dq, dk, dv)]

    def attend_pairs(pairs, first):
        made = [scores(i, j) for i, j in pairs]
        values = [products(i, j, pb, ds) for (i, j), (pb, ds) in zip(pairs, made)]
        for (i, j), value in zip(pairs, values):
            for ref, at, part in ((dq_s, frame_lanes(i), 0), (dk_s, frame_lanes(j, FROWS), 1), (dv_s, frame_lanes(j, FROWS), 2)):
                ref[:, at] = value[part] if first else ref[:, at] + value[part]

    def finish(f):
        parts = (dq_s[:, frame_lanes(f, FROWS)] * scale, dk_s[:, frame_lanes(f, FROWS)] * math.log(2.0), dv_s[:, frame_lanes(f, FROWS)])
        grads = jnp.concatenate([jnp.where(real, part, 0.0).astype(BF16) for part in parts], axis=0)
        dh_ref[frame_rows(f), :] = dot_tn(grads, w_ref[...]).astype(BF16)
        return dot(grads, h_ref[frame_rows(f), :])

    for k in range(TOGETHER):
        prepare(k)

    def diagonal(n, _):
        attend_pairs([(n * TOGETHER + k,) * 2 for k in range(TOGETHER)], True)
        for k in range(TOGETHER):
            prepare(jnp.minimum((n + 1) * TOGETHER, FRAMES - TOGETHER) + k)
        return 0
    lax.fori_loop(0, FRAMES // TOGETHER, diagonal, 0)
    each_pair(pairs_s, count, lambda pairs: attend_pairs(pairs, False))

    def close(n, _):
        dw = [finish(n * TOGETHER + k) for k in range(TOGETHER)]
        dw_s[...] += functools.reduce(jnp.add, dw)
        return 0
    lax.fori_loop(0, FRAMES // TOGETHER, close, 0)
    for b in range(3):
        turned = dw_s[b * WIDE:(b + 1) * WIDE, :].T
        turn_s[:, 0:96] = jnp.concatenate([turned[:, HW * h:HW * h + HEAD_DIM] for h in HEADS], axis=1)
        line = [turn_s[pl.ds(k, 96, stride=4), :][:, 0:96] for k in range(4)]
        blk_s[pl.ds(0, 96, stride=3), :] = jnp.concatenate([line[0], line[1][:, :32]], axis=1)
        blk_s[pl.ds(1, 96, stride=3), :] = jnp.concatenate([line[1][:, 32:], line[2][:, :64]], axis=1)
        blk_s[pl.ds(2, 96, stride=3), :] = jnp.concatenate([line[2][:, 64:], line[3]], axis=1)
        early_ref[288 * b:288 * (b + 1), :] = blk_s[...].astype(BF16)
    carried.wait()


def attn_bwd(pairs, qa, ka, va, kt, ot, do, h, w, result):
    sd = jax.ShapeDtypeStruct
    V = pltpu.VMEM
    return pl.pallas_call(
        bwd_kernel,
        out_shape=(sd((FRAMES * FROWS, D), BF16), sd((3 * 288, 128), BF16), pltpu.HBM(result.shape, BF16)),
        in_specs=[SMEM] + [VM] * 9,
        out_specs=(VM,) * 2 + (HBM,),
        scratch_shapes=[V((FRAMES, WIDE, HEADS_LOCAL * FLANES), BF16), V((FRAMES, WIDE, HEADS_LOCAL * FLANES), BF16)]
        + [V((WIDE, (FRAMES + 1) * FLANES), F32)] * 3
        + [V((3 * WIDE, D), F32), V((D, 128), F32), V((288, 128), F32),
           pltpu.SemaphoreType.DMA((1,))],
        compiler_params=pltpu.CompilerParams(vmem_limit_bytes=42 << 20),
        cost_estimate=pl.CostEstimate(flops=int(5e10), bytes_accessed=12 << 20, transcendentals=0),
        name="attend_backward",
    )(pairs, qa, ka, va, kt, ot, do, h, w, result)


MESH = pl.DeviceIdType.MESH
OWN_ROWS = 4 * FROWS


def place(d, m):
    return {"dp": d, "mp": m}


def remote(src, dst, send_sem, recv_sem, device):
    return pltpu.make_async_remote_copy(
        src_ref=src, dst_ref=dst, send_sem=send_sem, recv_sem=recv_sem, device_id=device, device_id_type=MESH
    )


def local(src, dst, sem):
    return pltpu.make_async_copy(src, dst, sem)


def greet(devices):
    barrier = pltpu.get_barrier_semaphore()
    for device in devices:
        pl.semaphore_signal(barrier, inc=1, device_id=device, device_id_type=MESH)
    return len(devices)


def met(count):
    pl.semaphore_wait(pltpu.get_barrier_semaphore(), count)


def group_peers():
    me = lax.axis_index("mp")
    return me, me ^ 1, me ^ 2, me ^ 3


def frame_part(device, c):
    return pl.ds(pl.multiple_of(device * OWN_ROWS + c * FROWS, 16), FROWS)


def normalised(v):
    centred = v - jnp.mean(v, axis=-1, keepdims=True)
    inv = lax.rsqrt(jnp.mean(centred * centred, axis=-1, keepdims=True) + NORM_EPS)
    return centred * inv, inv


def norm_pull(dy, hat, inv, gain):
    dg = dy * gain
    lead = jnp.mean(dg, axis=-1, keepdims=True)
    along = jnp.mean(dg * hat, axis=-1, keepdims=True)
    return inv * (dg - lead - hat * along)


def col_sum(v):
    return jnp.sum(v, axis=0, keepdims=True)


def load_frame(ref, c):
    base = c * PATCHES // 16 * 16
    rows = ref[base:base + FROWS, :].astype(F32)
    shift = c * PATCHES - base
    return pltpu.roll(rows, FROWS - shift, 0) if shift else rows


def live_rows():
    return lax.broadcasted_iota(jnp.int32, (FROWS, 1), 0) < PATCHES


def dp_peers(count):
    d = lax.axis_index("dp")
    side, line = d % 2, d // 2
    return side, line, {"dp": d ^ 1}, [lax.rem(line + n, count) for n in range(count)]


def start_kernel(count, x_hbm, np_hbm, w_hbm, m_hbm, v_hbm,
                 h_ref, qt_ref, ka_ref, va_ref, kt_ref, vt_ref, wa_ref, ws_ref, ma_ref, mb_ref,
                 x_ref, np_ref, w_ref, m_ref, v_ref, mo_s, w_s, load_x, load_w, keep_m,
                 send_x, recv_x, send_p, recv_p, send_f, recv_f, send_t, recv_t, send_l, recv_l):
    me, near, far, _ = group_peers()
    side, line, twin, around = dp_peers(count)
    frames = range(OWN_ROWS // FROWS)
    cuts = [0, 208, 400, 592, 784]
    loads = [local(x_hbm.at[a:b, :], x_ref.at[a:b, :], load_x.at[c]) for c, (a, b) in enumerate(zip(cuts, cuts[1:]))]
    others = [local(m_hbm, m_ref, load_w.at[0]), local(v_hbm, v_ref, load_w.at[1]), local(w_hbm, w_ref, load_w.at[2])]
    gains = local(np_hbm, np_ref, load_w.at[3])
    greeted = greet([{"mp": near}, {"mp": far}, twin] + [{"dp": q * 2 + side} for q in around[1:]])
    for copy in [gains] + loads + others:
        copy.start()
    live = live_rows()
    to_far, to_near, moments = [], [], []
    gains.wait()
    for c in frames:
        loads[c].wait()
        hat, _ = normalised(load_frame(x_ref, c))
        h_ref[frame_part(me, c), :] = jnp.where(live, hat * np_ref[0:1, :] + np_ref[1:2, :], 0.0).astype(BF16)
        rows = h_ref.at[frame_part(me, c), :]
        to_far.append(remote(rows, rows, send_x.at[c], recv_x.at[c], {"mp": far}))
        to_near.append(remote(rows, rows, send_p.at[c], recv_p.at[c], {"mp": near}))
        if c == 0:
            met(greeted)
        to_far[c].start()
        to_near[c].start()

    slots, rows = m_ref.shape[0], m_ref.shape[1]
    others[0].wait()
    others[1].wait()
    for r in range(2 * slots):
        mo_s[r // slots, pl.ds((r % slots) * rows, rows), :] = (v_ref if r % 2 else m_ref)[r // 2].astype(BF16)
    first, second = ma_ref.at[side, line], mb_ref.at[side]
    kept = [local(mo_s.at[0], first, keep_m.at[0]), local(mo_s.at[1], second, keep_m.at[1])]
    for n, q in enumerate(around[1:]):
        moments.append(remote(mo_s.at[0], first, send_l.at[n], recv_l.at[n], {"dp": q * 2 + side}))
    moments.append(remote(mo_s.at[0], first, send_t.at[0], recv_t.at[0], twin))
    moments.append(remote(mo_s.at[1], second, send_t.at[1], recv_t.at[1], twin))
    for copy in moments + kept:
        copy.start()

    def incoming(device, sends, recvs, c):
        rows = h_ref.at[frame_part(device, c), :]
        return remote(rows, rows, sends.at[c], recvs.at[c], {"mp": near})

    def forward(c):
        incoming(far, send_x, recv_x, c).wait_recv()
        copy = incoming(far, send_f, recv_f, c)
        copy.start()
        return copy

    others[2].wait()
    for b in range(3):
        a = [w_ref[b, pl.ds(k, 96, stride=3), :] for k in range(3)]
        lines = [a[0][:, :96], jnp.concatenate([a[0][:, 96:], a[1][:, :64]], axis=1),
                 jnp.concatenate([a[1][:, 64:], a[2][:, :32]], axis=1), a[2][:, 32:]]
        gap = jnp.zeros((96, HW - HEAD_DIM), F32)
        for k in range(4):
            parts = []
            for h in HEADS:
                parts += [lines[k][:, HEAD_DIM * h:HEAD_DIM * (h + 1)], gap]
            w_s[pl.ds(k, 96, stride=4), :] = jnp.concatenate(parts, axis=1)
        wa_ref[b * WIDE:(b + 1) * WIDE, :] = w_s[...].T.astype(BF16)

    col = lax.broadcasted_iota(jnp.int32, (FROWS, WIDE), 1) % HW
    ones = jnp.where((col == 24) | (col == 25), 1.0, 0.0)
    kadd = ones + jnp.where((col == 26) & jnp.logical_not(live), MASKED, 0.0)
    vtadd = jnp.where(lax.broadcasted_iota(jnp.int32, (WIDE, FROWS), 0) % HW == 24, 1.0, 0.0)
    zpad = jnp.zeros((WIDE, FLANES - FROWS), BF16)

    def project(devices, c):
        made = []
        for device in devices:
            hf = h_ref[frame_part(device, c), :]
            made.append((dot_nt(wa_ref[...], hf), dot_nt(hf, wa_ref[WIDE:3 * WIDE, :])))
        for device, (turned, lined) in zip(devices, made):
            f = device * (OWN_ROWS // FROWS) + c
            qt_ref[:, frame_lanes(f)] = jnp.concatenate([(turned[0:WIDE] * QSCALE).astype(BF16), zpad], axis=1)
            kt_ref[:, frame_lanes(f, FROWS)] = turned[WIDE:2 * WIDE].astype(BF16)
            vt_ref[:, frame_lanes(f, FROWS)] = (turned[2 * WIDE:3 * WIDE] + vtadd).astype(BF16)
            ka_ref[frame_rows(f), :] = (lined[:, 0:WIDE] + kadd).astype(BF16)
            va_ref[frame_rows(f), :] = (lined[:, WIDE:2 * WIDE] + ones).astype(BF16)

    copies = [forward(0)]
    for c in frames:
        incoming(near, send_p, recv_p, c).wait_recv()
        project((me, near), c)
    copies.append(forward(1))
    for b in range(3, w_ref.shape[0]):
        for k in range(3):
            lanes = slice(128 * k, 128 * (k + 1))
            part = w_ref[b, pl.ds(k, 96, stride=3), :]
            if b == 3:
                gap = jnp.zeros((HW - HEAD_DIM, 128), F32)
                parts = []
                for h in HEADS:
                    parts += [part[HEAD_DIM * h:HEAD_DIM * (h + 1)], gap]
                ws_ref[2 * D:2 * D + WIDE, lanes] = jnp.concatenate(parts, axis=0).astype(BF16)
            else:
                ws_ref[96 * (b - 4):96 * (b - 3), lanes] = part.astype(BF16)
    for c in frames:
        incoming(near ^ 2, send_f, recv_f, c).wait_recv()
        project((far, near ^ 2), c)
        if c + 2 < len(frames):
            copies.append(forward(c + 2))
    for n in range(1, count):
        part = ma_ref.at[side, around[count - n]]
        remote(part, part, send_l.at[n - 1], recv_l.at[n - 1], twin).wait_recv()
    part = ma_ref.at[1 - side, line]
    remote(part, part, send_t.at[0], recv_t.at[0], twin).wait_recv()
    part = mb_ref.at[1 - side]
    remote(part, part, send_t.at[1], recv_t.at[1], twin).wait_recv()
    for copy in kept:
        copy.wait()
    for copy in to_far + to_near + copies + moments:
        copy.wait_send()


def start_call(dp, x, norm_params, weights, first_moments, second_moments):
    sd, V, S = jax.ShapeDtypeStruct, pltpu.VMEM, pltpu.SemaphoreType.DMA
    blocks, count = weights.shape[0], dp // 2
    half = first_moments.shape[0] * first_moments.shape[1]
    rows, lanes = sd((FRAMES * FROWS, WIDE), BF16), sd((WIDE, FRAMES * FLANES), BF16)
    return pl.pallas_call(
        functools.partial(start_kernel, count),
        out_shape=(sd((FRAMES * FROWS, D), BF16), lanes, rows, rows, lanes, lanes, sd((3 * WIDE, D), BF16),
                   sd((WIDE + 96 * (blocks - 4), D), BF16),
                   pltpu.HBM((2, count, half, 128), BF16), pltpu.HBM((2, half, 128), BF16)),
        in_specs=[HBM] * 5,
        out_specs=(VM,) * 8 + (HBM,) * 2,
        scratch_shapes=[V(x.shape, BF16), V(norm_params.shape, F32), V(weights.shape, F32), V(first_moments.shape, F32),
                        V(first_moments.shape, F32), V((2, half, 128), BF16), V((D, WIDE), F32),
                        S((4,)), S((4,)), S((2,))] + [S((4,))] * 6 + [S((2,))] * 2 + [S((count,))] * 2,
        compiler_params=pltpu.CompilerParams(vmem_limit_bytes=24 << 20, collective_id=1, has_side_effects=True),
        name="norm_and_gather",
    )(*[in_hbm(value) for value in (x, norm_params, weights, first_moments, second_moments)])


def gelu_parts(u):
    lead = math.sqrt(2.0 / math.pi)
    bend = lead * 0.044715
    square = u * u
    half = 0.5 + 0.5 * jnp.tanh(u * (lead + bend * square))
    slope = half + 2.0 * u * (half - half * half) * (lead + 3.0 * bend * square)
    return u * half, slope


def middle_kernel(count, o_ref, x_hbm, ct_hbm, pad_ref, w0_ref, w1_ref, np_hbm, ma_ref, mb_ref,
                  out_ref, dx2_ref, do_ref, l0_ref, l1_ref, l2_ref, l3_ref, nb_ref, mom_ref,
                  ob_s, dob_s, g_s, a_s, du_s, da_s, h2_s, dxa_s, blk_s, res_s, ut_s, wot_s,
                  x_ref, ct_ref, o_s, w2_ref, w3_ref, np_ref, load_s, send_w, recv_w,
                  send_o, recv_o, send_d, recv_d, send_t, recv_t, send_l, recv_l, send_f, recv_f):
    me, near, far, across = group_peers()
    side, line, twin, around = dp_peers(count)
    peers = (far, across, near)
    mine = pl.ds(pl.multiple_of(me * OWN_ROWS, 16), OWN_ROWS)
    loads = [local(ct_hbm, ct_ref, load_s.at[0]), local(x_hbm, x_ref, load_s.at[1]), local(o_ref.at[mine, :], o_s, load_s.at[2]), local(np_hbm, np_ref, load_s.at[3])]
    greeted = greet([{"mp": p} for p in peers] + [twin] + [{"dp": q * 2 + side} for q in around[1:]])
    for copy in loads:
        copy.start()
    frames = range(OWN_ROWS // FROWS)
    live = live_rows()
    shards_w = (w0_ref, w1_ref, w2_ref, w3_ref)
    late = (l0_ref, l1_ref, l2_ref, l3_ref)
    places = range(len(shards_w))
    loads[0].wait()
    for c in frames:
        rows = slice(c * FROWS, (c + 1) * FROWS)
        g_s[rows, :] = jnp.where(live, load_frame(ct_ref, c) * (1 - pad_ref[0, me * len(frames) + c]).astype(F32), 0.0).astype(BF16)
    met(greeted)
    outgoing = []
    for c in frames:
        for n, p in enumerate(peers):
            outgoing.append(remote(o_ref.at[frame_part(p, c), :], ob_s.at[n, pl.ds(c * FROWS, FROWS), :],
                                   send_o.at[n, c], recv_o.at[n, c], {"mp": p}))
            outgoing[-1].start()
    weights = [remote(w0_ref, w3_ref, send_w.at[0], recv_w.at[0], {"mp": near}),
               remote(w1_ref, w2_ref, send_w.at[1], recv_w.at[1], {"mp": near})]
    for copy in weights:
        copy.start()
    moments = []
    for n, q in enumerate(around[1:]):
        own_half = mb_ref.at[side]
        moments.append(remote(own_half, mom_ref.at[1, side, line], send_l.at[n], recv_l.at[n], {"dp": q * 2 + side}))
        moments.append(remote(ma_ref.at[side, q], mom_ref.at[0, side, q], send_t.at[q], recv_t.at[q], twin))
    for copy in moments:
        copy.start()

    def pass_moments(n):
        q = around[count - n]
        part = mom_ref.at[1, side, q]
        remote(part, part, send_l.at[n - 1], recv_l.at[n - 1], twin).wait_recv()
        moments.append(remote(part, part, send_f.at[q], recv_f.at[q], twin))
        moments[-1].start()

    def w_up(m):
        return shards_w[m][0:D, :]

    def w_down(m):
        return shards_w[m][D:2 * D, :]

    def w_o(m):
        return shards_w[m][2 * D:2 * D + WIDE, :]

    def cols(m):
        return slice(m * D, (m + 1) * D)

    for m in (0, 1, 3, 2):
        if m > 1:
            weights[3 - m].wait_recv()
        da_s[:, cols(m)] = dot_nt(g_s[...], w_down(m))
        ut_s[cols(m), :] = w_up(m).astype(F32).T.astype(BF16)
        wot_s[:, m * WIDE:(m + 1) * WIDE] = w_o(m).astype(F32).T.astype(BF16)
    for copy in loads[1:]:
        copy.wait()
    nb_ref[...] = jnp.zeros(nb_ref.shape, F32)
    down = jnp.concatenate([w_down(m) for m in places], axis=0)
    out_w = jnp.concatenate([w_o(m) for m in places], axis=0)
    sent, left = [], list(range(1, count))
    for both in ((0,), (1, 2), (3,)):
        rows = slice(both[0] * FROWS, (both[-1] + 1) * FROWS)
        for c in both:
            for n, p in enumerate(peers):
                part = ob_s.at[n, pl.ds(c * FROWS, FROWS), :]
                remote(part, part, send_o.at[n, c], recv_o.at[n, c], {"mp": p}).wait_recv()
        own_rows = pl.ds(pl.multiple_of(me * OWN_ROWS + both[0] * FROWS, 16), len(both) * FROWS)
        heads = jnp.concatenate([o_s[rows, :]] + [ob_s[n, rows, :] for n in range(len(peers))], axis=1)
        x2 = jnp.concatenate([load_frame(x_ref, c) for c in both], axis=0) + dot(heads, out_w)
        x2 = jnp.where(jnp.concatenate([live] * len(both), axis=0), x2, 0.0)
        hat, inv = normalised(x2)
        h2 = (hat * np_ref[2:3, :] + np_ref[3:4, :]).astype(BF16)
        h2_s[rows, :] = h2
        for m in places:
            value, slope = gelu_parts(dot(h2, w_up(m)))
            a_s[rows, cols(m)] = value.astype(BF16)
            du_s[rows, cols(m)] = (da_s[rows, cols(m)] * slope).astype(BF16)
        if left and len(both) > 1:
            pass_moments(left.pop(0))
        result = x2 + dot(a_s[rows, :], down)
        for k, c in enumerate(both):
            res_s[pl.ds(c * PATCHES, FROWS), :] = result[k * FROWS:(k + 1) * FROWS]
        dh2 = dot(du_s[rows, :], ut_s[...])
        nb_ref[0:1, :] += col_sum(dh2 * hat)
        nb_ref[1:2, :] += col_sum(dh2)
        dx2 = g_s[rows, :].astype(F32) + norm_pull(dh2, hat, inv, np_ref[2:3, :])
        dx2_ref[rows, :] = dx2
        dxa = dx2.astype(BF16)
        dxa_s[rows, :] = dxa
        d_heads = dot(dxa, wot_s[...]).astype(BF16)
        for n in range(len(peers)):
            dob_s[n, rows, :] = d_heads[:, (n + 1) * WIDE:(n + 2) * WIDE]
        for c in both:
            for n, p in enumerate(peers):
                sent.append(remote(dob_s.at[n, pl.ds(c * FROWS, FROWS), :], do_ref.at[frame_part(me, c), :],
                                   send_d.at[n, c], recv_d.at[n, c], {"mp": p}))
                sent[-1].start()
        do_ref[own_rows, :] = d_heads[:, 0:WIDE]
        if left and both[-1] < 3:
            pass_moments(left.pop(0))
    while left:
        pass_moments(left.pop(0))
    out_ref[...] = res_s[0:out_ref.shape[0], :].astype(BF16)

    def as_block(shard, first, value):
        size = value.shape[0]
        for k in range(3):
            blk_s[pl.ds(k, size, stride=3), :] = value[:, 128 * k:128 * (k + 1)]
        late[shard][first * 288:first * 288 + 3 * size, :] = blk_s[0:3 * size, :].astype(BF16)

    def drop_gaps(value):
        return jnp.concatenate([value[HW * h:HW * h + HEAD_DIM] for h in HEADS], axis=0)

    dw1 = dot_tn(h2_s[...], du_s[...])
    dw2 = dot_tn(g_s[...], a_s[...])
    for m in places:
        as_block(m, 1, dw1[:, cols(m)])
        as_block(m, 5, dw2[:, cols(m)].T)
        o_m = o_s[...] if m == 0 else ob_s[m - 1]
        as_block(m, 0, drop_gaps(dot_tn(o_m, dxa_s[...])))
    for c in frames:
        for n, p in enumerate(peers):
            part = do_ref.at[frame_part(p, c), :]
            remote(part, part, send_d.at[n, c], recv_d.at[n, c], {"mp": p}).wait_recv()
    for q in around[1:]:
        for half, sends, recvs in ((0, send_t, recv_t), (1, send_f, recv_f)):
            part = mom_ref.at[half, 1 - side, q]
            remote(part, part, sends.at[q], recvs.at[q], twin).wait_recv()
    for copy in outgoing + sent + moments + weights:
        copy.wait_send()


def middle_call(dp, o, x, ct, padding, w, norm_params, ma, mb):
    sd = jax.ShapeDtypeStruct
    V, S = pltpu.VMEM, pltpu.SemaphoreType.DMA
    count = dp // 2
    late = sd((9 * 288, 128), BF16)
    return pl.pallas_call(
        functools.partial(middle_kernel, count),
        out_shape=(sd(x.shape, BF16), sd((OWN_ROWS, D), F32), sd((FRAMES * FROWS, WIDE), BF16),
                   late, late, late, late, sd((2, D), F32), pltpu.HBM((2,) + ma.shape, BF16)),
        in_specs=[HBM, HBM, HBM, SMEM] + [VM] * 2 + [HBM] * 3,
        out_specs=(VM,) * 8 + (HBM,),
        scratch_shapes=[V((3, OWN_ROWS, WIDE), BF16), V((3, OWN_ROWS, WIDE), BF16), V((OWN_ROWS, D), BF16),
                        V((OWN_ROWS, FF), BF16), V((OWN_ROWS, FF), BF16), V((OWN_ROWS, FF), F32),
                        V((OWN_ROWS, D), BF16), V((OWN_ROWS, D), BF16), V((1152, 128), F32), V((OWN_ROWS, D), F32),
                        V((FF, D), BF16), V((D, 4 * WIDE), BF16),
                        V(x.shape, BF16), V(x.shape, BF16), V((OWN_ROWS, WIDE), BF16), V(w[0].shape, BF16), V(w[0].shape, BF16), V(norm_params.shape, F32), S((4,)), S((2,)), S((2,)), S((3, 4)), S((3, 4)), S((3, 4)), S((3, 4))] + [S((count,))] * 6,
        compiler_params=pltpu.CompilerParams(vmem_limit_bytes=36 << 20, collective_id=2, has_side_effects=True),
        cost_estimate=pl.CostEstimate(flops=int(6e9), bytes_accessed=12 << 20, transcendentals=0),
        name="feed_forward",
    )(in_hbm(o), in_hbm(x), in_hbm(ct), padding, *w, in_hbm(norm_params), in_hbm(ma), in_hbm(mb))


def reduce_kernel(dp, piece, dh_ref, early_ref, l0_ref, l1_ref, l2_ref, l3_ref, x_ref, dx2_ref, np_ref, nb_ref,
                  gin_ref, gs_ref, tot_ref,
                  res_s, pb_s, xs_s, xb_s, g_s, yb_s, zs_s, zb_s, msg_s, mb_s, dm_s, db_s,
                  send_p, recv_p, send_x, recv_x, send_y, recv_y, send_z, recv_z,
                  send_a, recv_a, send_w, recv_w, send_m, recv_m, send_n, recv_n):
    me, near, far, across = group_peers()
    d = lax.axis_index("dp")
    count = dp // 2
    side, line = d % 2, d // 2
    twin = {"dp": d ^ 1}

    order, top = [], count
    while top > 1:
        top //= 2
        order += range(top, 2 * top)
    turns = [line ^ n for n in order]
    cut = -(-piece // 32) * 16
    halves = [(0, cut), (cut, piece - cut)]

    def line_device(q):
        return {"dp": q * 2 + side}

    frames = range(OWN_ROWS // FROWS)
    greeted = greet([{"mp": near}, {"mp": far}, {"mp": across}] + [{"dp": d ^ n} for n in range(1, dp)])
    total = early_ref.shape[0] + l0_ref.shape[0]
    g_s[0:early_ref.shape[0], :] = early_ref[...]
    g_s[early_ref.shape[0]:total, :] = (l0_ref[...].astype(F32) + l1_ref[...].astype(F32)
                                        + (l2_ref[...].astype(F32) + l3_ref[...].astype(F32))).astype(BF16)
    if g_s.shape[0] > total:
        g_s[total:, :] = jnp.zeros((g_s.shape[0] - total, 128), BF16)
    met(greeted)

    def own(c):
        return pl.ds(c * FROWS, FROWS)

    to_near = []
    def to_partner(k, target):
        for c in frames:
            to_near.append(remote(dh_ref.at[frame_part(target, c), :], pb_s.at[k, own(c), :],
                                  send_p.at[k, c], recv_p.at[k, c], {"mp": near}))
            to_near[-1].start()

    to_partner(1, across)

    def at(s, q, k):
        return pl.ds(pl.multiple_of((s * count + q) * piece + halves[k][0], 16), halves[k][1])

    def part(ref, q, k):
        return ref.at[q, pl.ds(*halves[k]), :]

    to_twin = []
    for q in turns + [line]:
        for k in range(2):
            to_twin.append(remote(g_s.at[at(1 - side, q, k), :], part(yb_s, q, k), send_y.at[q, k], recv_y.at[q, k], twin))
            to_twin[-1].start()
    to_partner(0, near)

    to_far = []
    for c in frames:
        remote(pb_s.at[1, own(c), :], pb_s.at[1, own(c), :], send_p.at[1, c], recv_p.at[1, c], {"mp": near}).wait_recv()
        xs_s[own(c), :] = (dh_ref[frame_part(far, c), :].astype(F32) + pb_s[1, own(c), :].astype(F32)).astype(BF16)
        to_far.append(remote(xs_s.at[own(c), :], xb_s.at[own(c), :], send_x.at[c], recv_x.at[c], {"mp": far}))
        to_far[-1].start()

    to_line = []
    for q in turns + [line]:
        for k in range(2):
            got = part(yb_s, q, k)
            remote(got, got, send_y.at[q, k], recv_y.at[q, k], twin).wait_recv()
            rows = pl.ds(*halves[k])
            zs_s[q, rows, :] = (g_s[at(side, q, k), :].astype(F32) + yb_s[q, rows, :].astype(F32)).astype(BF16)
            if q is not line:
                to_line.append(remote(part(zs_s, q, k), part(zb_s, line, k), send_z.at[q, k], recv_z.at[line, k], line_device(q)))
                to_line[-1].start()
    live = live_rows()
    norm_sums = [jnp.zeros((1, D), F32), jnp.zeros((1, D), F32)]

    def norm_frame(c):
        remote(pb_s.at[0, own(c), :], pb_s.at[0, own(c), :], send_p.at[0, c], recv_p.at[0, c], {"mp": near}).wait_recv()
        remote(xb_s.at[own(c), :], xb_s.at[own(c), :], send_x.at[c], recv_x.at[c], {"mp": far}).wait_recv()
        dy = dh_ref[frame_part(me, c), :].astype(F32) + pb_s[0, own(c), :].astype(F32) + xb_s[own(c), :].astype(F32)
        dy = jnp.where(live, dy, 0.0)
        hat, inv = normalised(load_frame(x_ref, c))
        norm_sums[0] = norm_sums[0] + col_sum(dy * hat)
        norm_sums[1] = norm_sums[1] + col_sum(dy)
        res_s[pl.ds(c * PATCHES, FROWS), :] = dx2_ref[own(c), :] + norm_pull(dy, hat, inv, np_ref[0:1, :])

    norm_frame(0)
    norm_frame(1)
    spread, passed = [], []
    squares = jnp.zeros((1, 128), F32)
    for k in range(2):
        rows = pl.ds(*halves[k])
        mine = zs_s[line, rows, :].astype(F32)
        for q in turns:
            got = part(zb_s, q, k)
            remote(got, got, send_z.at[q, k], recv_z.at[q, k], line_device(q)).wait_recv()
            mine = mine + zb_s[q, rows, :].astype(F32)
        mine = mine.astype(BF16)
        gs_ref[at(side, line, k), :] = mine
        whole = gs_ref.at[at(side, line, k), :]
        for q in turns:
            spread.append(remote(whole, whole, send_a.at[q, k], recv_a.at[line, k], line_device(q)))
        passed.append(remote(whole, whole, send_w.at[line, k], recv_w.at[line, k], twin))
        for copy in spread[-len(turns):] + passed[-1:]:
            copy.start()
        mine = mine.astype(F32)
        squares = squares + col_sum(mine * mine)
        norm_frame(2 + k)

    msg_s[...] = jnp.zeros(msg_s.shape, F32)
    msg_s[0:1, :] = norm_sums[0]
    msg_s[1:2, :] = norm_sums[1]
    msg_s[2:4, :] = nb_ref[...]
    msg_s[4:5, 0:128] = squares
    small = []
    for n, p in enumerate((near, far, across)):
        small.append(remote(msg_s, mb_s.at[n], send_m.at[n], recv_m.at[n], {"mp": p}))
        small[-1].start()

    def pass_on(q, k):
        piece_at = gs_ref.at[at(side, q, k), :]
        remote(piece_at, piece_at, send_a.at[q, k], recv_a.at[q, k], line_device(q)).wait_recv()
        passed.append(remote(piece_at, piece_at, send_w.at[q, k], recv_w.at[q, k], twin))
        passed[-1].start()

    pass_on(turns[0], 0)
    add = msg_s[...]
    for n, p in enumerate((near, far, across)):
        remote(mb_s.at[n], mb_s.at[n], send_m.at[n], recv_m.at[n], {"mp": p}).wait_recv()
        add = add + mb_s[n]
    dm_s[...] = add
    for n in range(1, dp):
        small.append(remote(dm_s, db_s.at[n], send_n.at[n], recv_n.at[n], {"dp": d ^ n}))
        small[-1].start()
    for k in range(2):
        for q in turns[1 - k:]:
            pass_on(q, k)
    gin_ref[...] = res_s[0:gin_ref.shape[0], :].astype(BF16)
    for n in range(1, dp):
        remote(db_s.at[n], db_s.at[n], send_n.at[n], recv_n.at[n], {"dp": d ^ n}).wait_recv()
        add = add + db_s[n]
    tot_ref[...] = add
    for k in range(2):
        for q in turns + [line]:
            piece_at = gs_ref.at[at(1 - side, q, k), :]
            remote(piece_at, piece_at, send_w.at[q, k], recv_w.at[q, k], twin).wait_recv()
    for copy in to_near + to_twin + to_far + to_line + spread + passed + small:
        copy.wait_send()


def reduce_call(dp, dh, early, late, x, dx2, norm_params, nb):
    sd = jax.ShapeDtypeStruct
    V, S = pltpu.VMEM, pltpu.SemaphoreType.DMA
    rows = early.shape[0] + late[0].shape[0]
    count = dp // 2
    piece = -(-rows // (2 * count * 16)) * 16
    held = 2 * count * piece
    return pl.pallas_call(
        functools.partial(reduce_kernel, dp, piece),
        out_shape=(sd(x.shape, BF16), sd((held, 128), BF16), sd((8, D), F32)),
        in_specs=[VM] * 10,
        out_specs=(VM,) * 3,
        scratch_shapes=[V((OWN_ROWS, D), F32), V((2, OWN_ROWS, D), BF16), V((OWN_ROWS, D), BF16), V((OWN_ROWS, D), BF16), V((held, 128), BF16),
                        V((count, piece, 128), BF16), V((count, piece, 128), BF16), V((count, piece, 128), BF16),
                        V((8, D), F32), V((3, 8, D), F32), V((8, D), F32), V((dp, 8, D), F32),
                        S((2, 4)), S((2, 4)), S((4,)), S((4,))] + [S((count, 2))] * 8 + [S((3,)), S((3,)), S((dp,)), S((dp,))],
        compiler_params=pltpu.CompilerParams(vmem_limit_bytes=22 << 20, collective_id=3, has_side_effects=True),
        name="reduce_gradients",
    )(dh, early, *late, x, dx2, norm_params, nb)


def update_kernel(slot_ref, dev_ref, gin_ref, tot_ref, gs_ref, w_ref, m_ref, v_ref, ma_ref, mb_ref, mom_ref, np_ref, nm_ref, nv_ref,
                  gout_ref, norm_ref, nw_hbm, nf_hbm, ns_hbm, nn_ref, nnf_ref, nns_ref, nw_ref, nf_ref, ns_ref, sem_s):
    carried = [local(gin_ref, gout_ref, sem_s.at[0])]
    for copy in carried:
        copy.start()
    blocks, rows, _ = w_ref.shape
    slots = m_ref.shape[0]
    tot = tot_ref[...]
    grads = tot[0:4, :]
    norm = jnp.sqrt(jnp.sum(grads * grads, keepdims=True) + jnp.sum(tot[4:5, 0:128], keepdims=True))
    norm_ref[...] = norm
    clip_level = 0.5 * (4 * D * D + 2 * D * FF + 4 * D) ** 0.5
    factor = jnp.minimum(1.0, clip_level / norm)
    nn_ref[...], nnf_ref[...], nns_ref[...] = adam_update(
        np_ref[...], grads * factor, nm_ref[...], nv_ref[...], 0.0, NORM_RATE)

    def block(b):
        return gs_ref[pl.ds(pl.multiple_of(b * rows, 16), rows), :].astype(F32) * factor

    for s in range(slots):
        owned = jnp.int32(-1)
        for b in range(blocks):
            owned = jnp.where(slot_ref[b] == dev_ref[0] * slots + s, b, owned)
        _, first, second = adam_update(0.0, block(jnp.maximum(owned, 0)), m_ref[s], v_ref[s], 0.0, LEARN_RATE)
        nf_ref[s] = jnp.where(owned >= 0, first, m_ref[s])
        ns_ref[s] = jnp.where(owned >= 0, second, v_ref[s])
    leaving = [local(nf_ref, nf_hbm, sem_s.at[2]), local(ns_ref, ns_hbm, sem_s.at[3])]
    for copy in leaving:
        copy.start()

    def step(b, _):
        holder, first = slot_ref[b] // slots, slot_ref[b] % slots * 2
        side, line = holder % 2, holder // 2
        on_side, on_line = side == dev_ref[0] % 2, line == dev_ref[0] // 2

        def moment(r):
            at = pl.ds(pl.multiple_of(r % slots * rows, 16), rows)
            late = mom_ref[r // slots, side, line, at, :]
            lead = jnp.where(on_side | on_line, ma_ref[side, line, at, :], late)
            rest = jnp.where(on_line, mb_ref[side, at, :], late)
            return jnp.where(r < slots, lead, rest).astype(F32)

        old = [moment(first), moment(first + 1)]
        nw_ref[b], _, _ = adam_update(w_ref[b], block(b), old[0], old[1], WEIGHT_DECAY, LEARN_RATE)
        local(nw_ref.at[b], nw_hbm.at[b], sem_s.at[4]).start()
        return 0
    lax.fori_loop(0, blocks, step, 0)
    for copy in carried + leaving + [local(nw_ref, nw_hbm, sem_s.at[4])]:
        copy.wait()


def update_call(owner_slot, grad_in, tot, gs, weights, first, second, ma, mb, moments, norm_params, norm_first, norm_second):
    sd = jax.ShapeDtypeStruct
    small = sd((4, D), F32)
    device = lax.axis_index("dp").reshape(1)
    return pl.pallas_call(
        update_kernel,
        out_shape=(pltpu.HBM(grad_in.shape, BF16), sd((1, 1), F32), pltpu.HBM(weights.shape, F32),
                   pltpu.HBM(first.shape, F32), pltpu.HBM(first.shape, F32), small, small, small),
        in_specs=[SMEM] * 2 + [VM] * 12,
        out_specs=(HBM, VM) + (HBM,) * 3 + (VM,) * 3,
        scratch_shapes=[pltpu.VMEM(weights.shape, F32), pltpu.VMEM(first.shape, F32), pltpu.VMEM(first.shape, F32),
                        pltpu.SemaphoreType.DMA((5,))],
        compiler_params=pltpu.CompilerParams(vmem_limit_bytes=16 << 20),
        name="clipped_update",
    )(owner_slot, device, grad_in, tot, gs, weights, first, second, ma, mb, moments, norm_params, norm_first, norm_second)


def adam_update(current, gradient, first_moment, second_moment, decay_rate, step_rate):
    first_new = BETA_ONE * first_moment + (1.0 - BETA_ONE) * gradient
    second_new = BETA_TWO * second_moment + (1.0 - BETA_TWO) * gradient * gradient
    first_fix = 1.0 / (1.0 - BETA_ONE**STEP)
    second_fix = 1.0 / (1.0 - BETA_TWO**STEP)
    direction = first_new * (step_rate * first_fix) / (jnp.sqrt(second_new * second_fix) + ADAM_EPS)
    return (current * (1.0 - step_rate * decay_rate) - direction, first_new, second_new)


def from_peer(value, distance):
    return lax.ppermute(value, "mp", [(i, i ^ distance) for i in range(lax.axis_size("mp"))])


def shards(tokens, cotangent, segment_ids, padding, pattern, owner_slot, weights, first_moments, second_moments,
           norm_params, norm_first, norm_second):
    dp = lax.axis_size("dp")
    x, ct = tokens[0], cotangent[0]
    h1, qt, ka, va, kt, vt, wa, own_shared, ma, mb = start_call(dp, x, norm_params, weights, first_moments, second_moments)
    shared = [own_shared, from_peer(own_shared, 2)]
    o, ot, qa, ka, va, kt, pairs = attn_fwd(segment_ids, padding, pattern, qt, ka, va, kt, vt)
    result, dx2, do, *late, nb, moments = middle_call(dp, o, x, ct, padding, shared, norm_params, ma, mb)
    late = [late[0], from_peer(late[1], 2), from_peer(late[2], 3), from_peer(late[3], 1)]
    dh, early, result = attn_bwd(pairs, qa, ka, va, kt, ot, do, h1, wa, result)
    grad_in, gs, tot = reduce_call(dp, dh, early, late, x, dx2, norm_params, nb)
    grad_in, grad_norm, new_weights, new_first, new_second, new_norm, new_norm_first, new_norm_second = update_call(
        owner_slot, grad_in, tot, gs, weights, first_moments, second_moments, ma, mb, moments, norm_params, norm_first, norm_second)
    return (result[None], grad_in[None], grad_norm[0, 0], new_weights, new_first, new_second,
            new_norm, new_norm_first, new_norm_second)


def solution(mesh):
    rows, blocks, slots = P("dp", "mp", None), P(None, "mp", None), P("dp", "mp", None)
    return jax.shard_map(
        shards,
        mesh=mesh,
        in_specs=(rows, rows, P("dp", None), P("dp", None), P(), P(), blocks, slots, slots, P(), P(), P()),
        out_specs=(rows, rows, P(), blocks, slots, slots, P(), P(), P()),
        check_vma=False,
    )
```
